32 devices in a mesh: dp: 16 (over z, y, core), tensor: 2 (over x).
Axes of the slice: x: 2, y: 2, z: 4, core: 2. Of those that a mesh axis runs over, the one named last changes fastest.
Arguments:
- tokens: bfloat16 [16384, 1024], P(('dp', 'tensor')), may hold values from -6 to 6
- cotangent: bfloat16 [16384, 1024], P(('dp', 'tensor')), may hold values from -6 to 6
- lengths: int32 [16], P('dp'), may hold values from 256 to 1024, as said below
- expert_ids: int32 [16384, 8], P(('dp', 'tensor')), may hold values from 0 to 31, all different within a row; in each aligned block of 1024 rows (0 to 1023, 1024 to 2047, ...) at most 288 rows name the same one
- gate_values: bfloat16 [16384, 8], P(('dp', 'tensor')), may hold values from 0.049804688 to 0.29882812
- first_gain: float32 [1024], replicated, may hold values from 0.5 to 1.5
- qkv_weight: bfloat16 [1024, 8, 256], P('dp', 'tensor'), may hold values from -0.1875 to 0.1875
- attn_out_weight: bfloat16 [1024, 1024], P('tensor', 'dp'), may hold values from -0.75 to 0.75
- second_gain: float32 [1024], replicated, may hold values from 0.5 to 1.5
- expert_in_weight: bfloat16 [32, 1024, 1024], P('tensor', 'dp'), may hold values from -0.1875 to 0.1875
- expert_out_weight: bfloat16 [32, 512, 1024], P('tensor', 'dp'), may hold values from -0.25 to 0.25
Outputs:
- output: bfloat16 [16384, 1024], P(('dp', 'tensor'))
- tokens_grad: float32 [16384, 1024], P(('dp', 'tensor'))
- first_gain_grad: float32 [1024], replicated
- qkv_grad: float32 [1024, 8, 256], P('dp', 'tensor')
- attn_out_grad: float32 [1024, 1024], P('tensor', 'dp')
- second_gain_grad: float32 [1024], replicated
- expert_in_grad: float32 [32, 1024, 1024], P('tensor', 'dp')
- expert_out_grad: float32 [32, 512, 1024], P('tensor', 'dp')
The draws below stay inside these ranges and needn't reach their ends.
Inputs may be any that keep to these rules, and one draw needn't show every extreme that they name: Each slot holds one sequence of lengths[s] tokens from its first position on; the rest of its 1024 positions is padding. `expert_ids`: each row names 8 different experts; within each aligned block of 1024 rows (one slot) no expert is named by more than 288 rows.
All inputs are finite; a program needn't handle non-finite values.
Results may differ from the reference program's by a relative error of at most 0.018.
Values may be sent and summed in bfloat16 or wider, within the bound.
A program may use at most 256 MiB of HBM per device.

```python
import math
import jax
import jax.numpy as jnp
import numpy as np
from jax import lax

D = 1024
H = 16
KV = 8
HD = 64
FF = 512
EXPERTS = 32
TOP = 8
SLOT = 1024
G = 2
QKV_W = 256
CAP = 288
SEQS = 16
TOKENS = 16384


def draw_lengths(key, part):
    base_lengths = jax.random.randint(key, (SEQS,), SLOT // 4, SLOT + 1)
    longest = jax.random.randint(jax.random.fold_in(key, 1), (), 0, SEQS)
    shortest = (longest + 1 + jax.random.randint(jax.random.fold_in(key, 2), (), 0, SEQS - 1)) % SEQS
    return base_lengths.at[longest].set(SLOT).at[shortest].set(SLOT // 4).astype(jnp.int32)


def levels(rng, shape, pieces, least, high):
    def one(axis_at, blocks):
        steps = jax.random.uniform(jax.random.fold_in(jax.random.fold_in(rng, 6), axis_at), (blocks,), jnp.float32, least / len(pieces), high / len(pieces))
        return jnp.repeat(jnp.exp(steps), shape[axis_at] // blocks).reshape((-1,) + (1,) * (len(shape) - axis_at - 1))

    level = one(*pieces[0])
    for cut in pieces[1:]:
        level = level * one(*cut)
    return level


def deal_out(own_key, own, number, rows, number_of, top, bound, lean):
    ranking = jax.random.permutation(own_key, number_of)
    packed, common = portions_of(number_of, rows * top, bound, lean, True), portions_of(number_of, rows * top, bound, lean, False)
    places = jnp.arange(number_of)

    def named(sizes, offset_by):
        used = int((sizes > 0).sum())
        fixed = max(1, used // 4)
        moved = fixed + (places - fixed + offset_by * (used - fixed)) % max(1, number_of - fixed)
        return jnp.zeros((number_of,), jnp.int32).at[ranking[jnp.where(places < fixed, places, moved)]].set(jnp.asarray(sizes, jnp.int32))

    sizes = jnp.where(number % 4 == 0, named(packed, number // 4), named(common, number - number // 4 - 1))
    mixed = jax.random.permutation(jax.random.fold_in(own, 3), number_of)
    source_of, receiver = mixed[0:number_of // 2 * 2:2], mixed[1:number_of // 2 * 2:2]
    room = jnp.minimum(sizes[source_of] - 1, bound - sizes[receiver]) // 2
    room = jnp.where((source_of == ranking[0]) | (receiver == ranking[0]) | (sizes[receiver] == 0), 0, jnp.maximum(room, 0))
    moved = jax.random.randint(jax.random.fold_in(own, 4), (number_of // 2,), 0, 1 << 20) % (room + 1)
    sizes = sizes.at[source_of].add(-moved).at[receiver].add(moved)
    items = jnp.searchsorted(jnp.cumsum(sizes), jnp.arange(rows * top), side="right").astype(jnp.int32)
    table = items.reshape(top, rows).T
    table = table[jax.random.permutation(jax.random.fold_in(own, 1), rows)]
    offset_by = jax.random.randint(jax.random.fold_in(own, 2), (rows, 1), 0, top)
    return jnp.take_along_axis(table, (jnp.arange(top)[None, :] + offset_by) % top, axis=1)


def portions_of(amount, total, limit, skew, full):
    portions = [(1 << 20) // math.isqrt(grade ** skew) + 1 for grade in range(1, amount + 1)]
    largest = limit if full else min(limit, max(-(-total // amount), total * portions[0] // sum(portions)))
    least = 1 if total - largest >= amount - 1 else 0
    counts, spare = [largest] + [least] * (amount - 1), total - largest - least * (amount - 1)
    while spare > 0:
        movable = [i for i in range(1, amount) if counts[i] < largest] or [i for i in range(1, amount) if counts[i] < limit]
        mass, budget = sum([portions[i] for i in movable]), spare
        for i in movable:
            addition = min(limit - counts[i], max(1, budget * portions[i] // mass), spare)
            counts[i] = counts[i] + addition
            spare = spare - addition
    return np.array(counts)


def gaussian(key, shape, deviation, most, shards=(), held_as=jnp.bfloat16):
    factor_of = levels(key, shape, shards, -0.22, 0.18) if shards else 1.0
    drawn = jax.random.normal(key, shape, jnp.float32) * deviation * factor_of
    return jnp.minimum(jnp.maximum(drawn, -most), most).astype(held_as)


def setup_inputs(seed: int = 0) -> dict:
    key_of = jax.random.split(jax.random.key(seed), 12)
    tokens = gaussian(key_of[0], (TOKENS, D), 1.0, 6.0, ((0, 32),))
    cotangent = gaussian(key_of[1], (TOKENS, D), 1.0, 6.0, ((0, 32),))
    lengths = draw_lengths(jax.random.fold_in(key_of[11], 71), 0)
    expert_ids_keys = jax.random.split(jax.random.fold_in(key_of[3], 1), TOKENS // SLOT)
    expert_ids_turns = jax.random.permutation(jax.random.fold_in(key_of[3], 3), TOKENS // SLOT)
    expert_ids = jax.vmap(lambda own, number: deal_out(jax.random.fold_in(key_of[3], 2), own, number, SLOT, EXPERTS, TOP, CAP, 1))(expert_ids_keys, expert_ids_turns).reshape((TOKENS, TOP))
    gate_values = jnp.clip(jnp.exp(math.log(0.29882812) - 1.7917595 * jax.random.uniform(key_of[4], (TOKENS, TOP), jnp.float32) ** levels(key_of[4], (TOKENS, TOP), ((0, 32),), -0.2, 0.2)), 0.049804688, 0.29882812).astype(jnp.bfloat16)
    first_gain = jnp.clip(1.0 + 0.1 * jax.random.normal(key_of[5], (D,), jnp.float32), 0.5, 1.5)
    qkv_weight = gaussian(key_of[6], (D, KV, QKV_W), D ** -0.5, 0.1875, ((0, 16), (1, 2)))
    attn_out_weight = gaussian(key_of[7], (H * HD, D), (H * HD // 16) ** -0.5, 0.75, ((0, 2), (1, 16)))
    second_gain = jnp.clip(1.0 + 0.1 * jax.random.normal(key_of[8], (D,), jnp.float32), 0.5, 1.5)
    expert_in_weight = gaussian(key_of[9], (EXPERTS, D, 2 * FF), D ** -0.5, 0.1875, ((0, 2), (1, 16)))
    expert_out_weight = gaussian(key_of[10], (EXPERTS, FF, D), FF ** -0.5, 0.25, ((0, 2), (1, 16)))
    return dict(tokens=tokens, cotangent=cotangent, lengths=lengths, expert_ids=expert_ids, gate_values=gate_values, first_gain=first_gain, qkv_weight=qkv_weight, attn_out_weight=attn_out_weight, second_gain=second_gain, expert_in_weight=expert_in_weight, expert_out_weight=expert_out_weight)


EPSILON = 1e-06
THETA = 10000.0
NEGATIVE = -1e+30
HIGHEST = lax.Precision.HIGHEST

@jax.custom_vjp
def low(v):
    return lax.optimization_barrier(v.astype(jnp.bfloat16)).astype(jnp.float32)

@jax.custom_vjp
def low_back(v):
    return v

def low_keep(v):
    return (low(v), None)

def low_pass(kept, grad):
    return (grad,)

def back_keep(v):
    return (v, None)

def back_low(kept, grad):
    return (low(grad),)
low.defvjp(low_keep, low_pass)
low_back.defvjp(back_keep, back_low)

def rope_tables(total_rows, head_size):
    half_size = head_size // 2
    positions = jnp.arange(total_rows).astype(jnp.float32)
    frequency = THETA ** (-(jnp.arange(half_size).astype(jnp.float32) * 2.0 / head_size))
    angles = positions[:, None] * frequency[None, :]
    return (jnp.cos(angles), jnp.sin(angles))

def rotate(tensor_in, cosine_table, sine_table):
    half_size = tensor_in.shape[-1] // 2
    shape_out = (tensor_in.shape[0],) + (1,) * (tensor_in.ndim - 2) + (half_size,)
    cos_part = cosine_table.reshape(shape_out)
    sin_part = sine_table.reshape(shape_out)
    first_half = tensor_in[..., :half_size]
    second_half = tensor_in[..., half_size:]
    return jnp.concatenate([first_half * cos_part - second_half * sin_part, second_half * cos_part + first_half * sin_part], axis=-1)

def dispatch(routes, route_gates, first_expert, expert_count, capacity, total_rows):
    flat_routes = routes.reshape(-1).astype(jnp.int32) - first_expert
    inside = (flat_routes >= 0) & (flat_routes < expert_count)
    one_hot = (flat_routes[:, None] == jnp.arange(expert_count, dtype=jnp.int32)[None, :]).astype(jnp.int32)
    before = jnp.cumsum(one_hot, axis=0, dtype=jnp.int32) - one_hot
    position = lax.optimization_barrier(jnp.sum(before * one_hot, axis=1, dtype=jnp.int32))
    target = jnp.where(inside, flat_routes * capacity + position, expert_count * capacity).astype(jnp.int32)
    owner = (jnp.arange(flat_routes.shape[0], dtype=jnp.int32) // routes.shape[1]).astype(jnp.int32)
    slot_token = jnp.full((expert_count * capacity + 1,), total_rows, jnp.int32).at[target].set(owner)[:expert_count * capacity]
    slot_gate = jnp.zeros((expert_count * capacity + 1,), jnp.float32).at[target].set(route_gates.reshape(-1).astype(jnp.float32))[:expert_count * capacity]
    return (slot_token, slot_gate)

def layer(inputs_f, first_gain, qkv_weight, attn_out_weight, second_gain, expert_in_weight, expert_out_weight, slot_token, slot_gate, length):
    total_rows = inputs_f.shape[0]
    inverse_one = lax.rsqrt(lax.optimization_barrier(jnp.mean(inputs_f * inputs_f, axis=-1, keepdims=True)) + EPSILON)
    normed_one = low(inputs_f * inverse_one * first_gain)
    projected = low_back(jnp.dot(normed_one, qkv_weight.reshape(D, -1), precision=HIGHEST)).reshape(total_rows, KV, G + 2, HD)
    cosine_table, sine_table = rope_tables(total_rows, HD)
    queries = low(rotate(projected[:, :, :G], cosine_table, sine_table))
    key_heads = low(rotate(projected[:, :, G], cosine_table, sine_table))
    value_heads = low(projected[:, :, G + 1])
    block_rows = min(512, total_rows)
    score_scale = 1.0 / math.sqrt(HD)

    def attend(block_start):
        query_block = lax.dynamic_slice_in_dim(queries, block_start, block_rows, 0)
        scores = low_back(jnp.einsum('qkgd,tkd->kgqt', query_block, key_heads, precision=HIGHEST) * score_scale)
        query_pos = block_start + jnp.arange(block_rows, dtype=jnp.int32)
        key_pos = jnp.arange(total_rows, dtype=jnp.int32)
        allowed = (key_pos[None, :] <= query_pos[:, None]) & (key_pos[None, :] < length)
        probabilities = jax.nn.softmax(jnp.where(allowed, scores, NEGATIVE), axis=-1)
        return jnp.einsum('kgqt,tkd->qkgd', low(probabilities), value_heads, precision=HIGHEST)
    block_starts = jnp.arange(total_rows // block_rows, dtype=jnp.int32) * block_rows
    attended = lax.map(jax.checkpoint(attend), block_starts).reshape(total_rows, H * HD)
    attended = low(low_back(attended))
    branch = low_back(jnp.dot(attended, attn_out_weight, precision=HIGHEST))
    hidden = inputs_f + branch
    inverse_two = lax.rsqrt(lax.optimization_barrier(jnp.mean(hidden * hidden, axis=-1, keepdims=True)) + EPSILON)
    normed_two = low(hidden * inverse_two * second_gain)
    padded = jnp.concatenate([normed_two, jnp.zeros((1, D), jnp.float32)], axis=0)
    expert_rows = padded[slot_token].reshape(EXPERTS, CAP, D)
    gate_up = low_back(jnp.einsum('ecd,edf->ecf', expert_rows, expert_in_weight, precision=HIGHEST))
    activated = low(jax.nn.silu(gate_up[..., :FF]) * gate_up[..., FF:])
    expert_out = low_back(jnp.einsum('ecf,efd->ecd', activated, expert_out_weight, precision=HIGHEST))
    weighted = expert_out * slot_gate.reshape(EXPERTS, CAP, 1)
    mixture = jnp.zeros((total_rows + 1, D), jnp.float32).at[slot_token].add(weighted.reshape(-1, D))[:total_rows]
    valid_rows = jnp.arange(total_rows, dtype=jnp.int32) < length
    return jnp.where(valid_rows[:, None], hidden + mixture, 0.0)

def reference(tokens, cotangent, lengths, expert_ids, gate_values, first_gain, qkv_weight, attn_out_weight, second_gain, expert_in_weight, expert_out_weight):
    weights_f = (first_gain.astype(jnp.float32), qkv_weight.astype(jnp.float32), attn_out_weight.astype(jnp.float32), second_gain.astype(jnp.float32), expert_in_weight.astype(jnp.float32), expert_out_weight.astype(jnp.float32))

    def per_slot(totals, items):
        slot_inputs, slot_cotangent, slot_length, slot_routes, slot_gates = items
        slot_token, slot_gate = dispatch(slot_routes, slot_gates, 0, EXPERTS, CAP, SLOT)

        def layer_of(inputs_f, gain_one, qkv_f, out_f, gain_two, in_f, down_f):
            return layer(inputs_f, gain_one, qkv_f, out_f, gain_two, in_f, down_f, slot_token, slot_gate, slot_length)
        outputs, pullback = jax.vjp(layer_of, slot_inputs.astype(jnp.float32), *weights_f)
        grads = pullback(slot_cotangent.astype(jnp.float32))
        new_totals = tuple((total_item + grad_item for total_item, grad_item in zip(totals, grads[1:])))
        return (new_totals, (outputs.astype(jnp.bfloat16), grads[0]))
    totals_init = tuple((jnp.zeros_like(weight_item) for weight_item in weights_f))
    totals, (outputs, input_grads) = lax.scan(per_slot, totals_init, (tokens.reshape(SEQS, SLOT, D), cotangent.reshape(SEQS, SLOT, D), lengths, expert_ids.reshape(SEQS, SLOT, TOP), gate_values.reshape(SEQS, SLOT, TOP)))
    return (outputs.reshape(TOKENS, D), input_grads.reshape(TOKENS, D), totals[0], totals[1], totals[2], totals[3], totals[4], totals[5])
```

```python
import functools
import math

import jax
import jax.numpy as jnp
from jax import lax
from jax.experimental import pallas as pl
from jax.experimental.pallas import tpu as pltpu
from jax.sharding import PartitionSpec as P

D = 1024
HD = 64
FF = 512
G = 2
CAP = 288
GROUP = 4
LANES = 128

EPSILON = 1e-06
THETA = 10000.0
NEGATIVE = -1e30
BF = jnp.bfloat16
F32 = jnp.float32
VMEM_LIMIT = 60 * 1024 * 1024

ANY = pl.BlockSpec(memory_space=pl.ANY)
SMEM = pl.BlockSpec(memory_space=pltpu.SMEM)
VM = pl.BlockSpec(memory_space=pltpu.VMEM)


def mm(a, b):
    return lax.dot_general(a, b, (((1,), (0,)), ((), ())), preferred_element_type=F32)


def mm_nt(a, b):
    return lax.dot_general(a, b, (((1,), (1,)), ((), ())), preferred_element_type=F32)


def mm_tn(a, b):
    return lax.dot_general(a, b, (((0,), (0,)), ((), ())), preferred_element_type=F32)


def call(kernel, name, out_shape, in_specs, out_specs, args, scratch=(), flops=0, moved=0, **more):
    return pl.pallas_call(
        kernel,
        name=name,
        out_shape=out_shape,
        in_specs=in_specs,
        out_specs=out_specs,
        scratch_shapes=list(scratch),
        compiler_params=pltpu.CompilerParams(vmem_limit_bytes=VMEM_LIMIT),
        cost_estimate=pl.CostEstimate(flops=flops, bytes_accessed=moved, transcendentals=0),
        **more,
    )(*args)


def rope_tables(total_rows):
    half = HD // 2
    positions = jnp.arange(total_rows).astype(F32)
    frequency = THETA ** (-(jnp.arange(half).astype(F32) * 2.0 / HD))
    angles = positions[:, None] * frequency[None, :]
    cosine, sine = jnp.cos(angles), jnp.sin(angles)
    return (
        jnp.concatenate([cosine] * 4, axis=1),
        jnp.concatenate([-sine, sine, -sine, sine], axis=1),
    )


def swap_halves(v):
    lane = lax.broadcasted_iota(jnp.int32, v.shape, 1)
    return jnp.where(lane % HD < HD // 2, pltpu.roll(v, LANES - HD // 2, 1), pltpu.roll(v, HD // 2, 1))


def qkv_kernel(n_ref, w_ref, cos_ref, sin_ref, out_ref):
    projected = mm(n_ref[...], w_ref[...])
    cosine, sine = cos_ref[...], sin_ref[...]
    key_lanes = lax.broadcasted_iota(jnp.int32, cosine.shape, 1) < HD
    for g in range(projected.shape[1] // (2 * LANES)):
        q = projected[:, g * 2 * LANES : g * 2 * LANES + LANES]
        kv = projected[:, g * 2 * LANES + LANES : (g + 1) * 2 * LANES]
        q = q * cosine + swap_halves(q) * sine
        kv = jnp.where(key_lanes, kv * cosine + swap_halves(kv) * sine, kv)
        out_ref[:, g * 2 * LANES : g * 2 * LANES + LANES] = q.astype(BF)
        out_ref[:, g * 2 * LANES + LANES : (g + 1) * 2 * LANES] = kv.astype(BF)


def qkv_project(normed, weight, cosine, sine):
    rows, width = normed.shape[0], weight.shape[1]
    block = 256
    return pl.pallas_call(
        qkv_kernel,
        name="qkv_rope",
        grid=(rows // block,),
        out_shape=jax.ShapeDtypeStruct((rows, width), BF),
        in_specs=[
            pl.BlockSpec((block, D), lambda b: (b, 0)),
            pl.BlockSpec((D, width), lambda b: (0, 0)),
            pl.BlockSpec((block, LANES), lambda b: (b, 0)),
            pl.BlockSpec((block, LANES), lambda b: (b, 0)),
        ],
        out_specs=pl.BlockSpec((block, width), lambda b: (b, 0)),
        compiler_params=pltpu.CompilerParams(vmem_limit_bytes=VMEM_LIMIT),
        cost_estimate=pl.CostEstimate(flops=2 * rows * D * width, bytes_accessed=6 << 20, transcendentals=0),
    )(normed, weight, cosine, sine)


def head_pair(v):
    first = lax.broadcasted_iota(jnp.int32, v.shape, 1) < HD
    zero = jnp.zeros_like(v)
    return jnp.concatenate([jnp.where(first, v, zero), jnp.where(first, zero, v)], axis=0)


def head_join(v):
    n = v.shape[0] // 2
    first = lax.broadcasted_iota(jnp.int32, (n, LANES), 1) < HD
    return jnp.where(first, v[:n], v[n:])


def doubled(kv):
    first = lax.broadcasted_iota(jnp.int32, kv.shape, 1) < HD
    other = pltpu.roll(kv.astype(F32), HD, 1).astype(BF)
    return jnp.where(first, kv, other), jnp.where(first, other, kv)


def allowed(n_keys, q_block, q_start, length):
    key = lax.broadcasted_iota(jnp.int32, (n_keys, 2 * q_block), 0)
    lane = lax.broadcasted_iota(jnp.int32, (n_keys, 2 * q_block), 1)
    query = q_start + jnp.where(lane < q_block, lane, lane - q_block)
    return (key <= query) & (key < length)


def attend_kernel(q_block, idx_ref, qkv_ref, *out_refs):
    outs, lse_ref = out_refs[:-1], out_refs[-1]
    rows = qkv_ref.shape[0]
    length = idx_ref[3]
    keys, values = doubled(qkv_ref[:, LANES:])
    for b in range(rows // q_block):
        start, n_keys = b * q_block, (b + 1) * q_block
        q = head_pair(qkv_ref[start : start + q_block, :LANES])
        scores = mm_nt(keys[:n_keys], q) * (1.0 / math.sqrt(HD))
        scores = jnp.where(allowed(n_keys, q_block, start, length), scores, NEGATIVE)
        largest = jnp.max(scores, axis=0, keepdims=True)
        expon = jnp.exp(scores - largest)
        totals = jnp.sum(expon, axis=0, keepdims=True)
        probs = (expon * (1.0 / totals)).astype(BF)
        mixed = head_join(mm_tn(probs, values[:n_keys])).astype(BF)
        lse_ref[0, b : b + 1, :] = largest + jnp.log(totals)
        if len(outs) == 1:
            outs[0][start : start + q_block] = mixed
        else:
            own_rows = rows // 2
            half, at = start // own_rows, start % own_rows
            mine = idx_ref[2] == half

            @pl.when(mine)
            def _():
                outs[0][at : at + q_block] = mixed

            @pl.when(jnp.logical_not(mine))
            def _():
                outs[1][at : at + q_block] = mixed


def attend(idx, qkv, parts, q_block):
    rows, groups = qkv.shape[0], qkv.shape[1] // (2 * LANES)
    out = jax.ShapeDtypeStruct((rows // parts, groups * LANES), BF)
    return pl.pallas_call(
        functools.partial(attend_kernel, q_block),
        name="attend",
        grid=(groups,),
        out_shape=[out] * parts + [jax.ShapeDtypeStruct((groups, rows // q_block, 2 * q_block), F32)],
        in_specs=[SMEM, pl.BlockSpec((rows, 2 * LANES), lambda g: (0, g))],
        out_specs=[pl.BlockSpec((rows // parts, LANES), lambda g: (0, g))] * parts
        + [pl.BlockSpec((1, rows // q_block, 2 * q_block), lambda g: (g, 0, 0))],
        compiler_params=pltpu.CompilerParams(vmem_limit_bytes=VMEM_LIMIT),
        cost_estimate=pl.CostEstimate(flops=14 << 30, bytes_accessed=4 << 20, transcendentals=0),
    )(idx, qkv)


def attend_back_kernel(q_block, n_grads, idx_ref, qkv_ref, lse_ref, cos_ref, sin_ref, *refs):
    grads, outs = refs[:n_grads], refs[n_grads : 2 * n_grads]
    do_ref, dq_ref, dk_ref, dv_ref = refs[2 * n_grads :]
    rows = qkv_ref.shape[0]
    own_rows = rows // n_grads
    length = idx_ref[3]
    for p in range(n_grads):
        at = pl.multiple_of((p ^ idx_ref[2] if n_grads == 2 else 0) * own_rows, own_rows)
        do_ref[pl.ds(at, own_rows), :] = grads[p][...]
    keys, values = doubled(qkv_ref[:, LANES:])
    dk_ref[...] = jnp.zeros_like(dk_ref)
    dv_ref[...] = jnp.zeros_like(dv_ref)
    scale = 1.0 / math.sqrt(HD)
    for b in range(rows // q_block):
        start, n_keys = b * q_block, (b + 1) * q_block
        q = head_pair(qkv_ref[start : start + q_block, :LANES])
        grad = head_pair(do_ref[start : start + q_block, :])
        scores = mm_nt(keys[:n_keys], q) * scale
        probs = jnp.where(
            allowed(n_keys, q_block, start, length), jnp.exp(scores - lse_ref[0, b : b + 1, :]), 0.0
        )
        prob_grad = mm_nt(values[:n_keys], grad)
        center = jnp.sum(probs * prob_grad, axis=0, keepdims=True)
        score_grad = (probs * (prob_grad - center)).astype(BF)
        dq_ref[start : start + q_block, :] = head_join(mm_tn(score_grad, keys[:n_keys])) * scale
        dk_ref[:n_keys, :] += mm(score_grad, q)
        dv_ref[:n_keys, :] += mm(probs.astype(BF), grad)
    cosine, sine = cos_ref[...], sin_ref[...]
    dq = dq_ref[...]
    dq = (dq * cosine - swap_halves(dq) * sine).astype(BF)
    dk, dv = dk_ref[...] * scale, dv_ref[...]
    dk = dk + pltpu.roll(dk, HD, 1)
    dv = dv + pltpu.roll(dv, HD, 1)
    dk = dk * cosine - swap_halves(dk) * sine
    first = lax.broadcasted_iota(jnp.int32, dk.shape, 1) < HD
    dkv = jnp.where(first, dk, dv).astype(BF)
    if n_grads == 1:
        outs[0][:, :LANES] = dq
        outs[0][:, LANES:] = dkv
    else:
        do_ref[...] = dq
        for p in range(2):
            at = pl.multiple_of((p ^ idx_ref[2]) * own_rows, own_rows)
            outs[p][:, :LANES] = do_ref[pl.ds(at, own_rows), :]
        do_ref[...] = dkv
        for p in range(2):
            at = pl.multiple_of((p ^ idx_ref[2]) * own_rows, own_rows)
            outs[p][:, LANES:] = do_ref[pl.ds(at, own_rows), :]


def attend_back(idx, qkv, lse, cosine, sine, grads, q_block):
    rows, groups, parts = qkv.shape[0], qkv.shape[1] // (2 * LANES), len(grads)
    return pl.pallas_call(
        functools.partial(attend_back_kernel, q_block, parts),
        name="attend_back",
        grid=(groups,),
        out_shape=[jax.ShapeDtypeStruct((rows // parts, groups * 2 * LANES), BF)] * parts,
        in_specs=[
            SMEM,
            pl.BlockSpec((rows, 2 * LANES), lambda g: (0, g)),
            pl.BlockSpec((1, rows // q_block, 2 * q_block), lambda g: (g, 0, 0)),
            pl.BlockSpec((rows, LANES), lambda g: (0, 0)),
            pl.BlockSpec((rows, LANES), lambda g: (0, 0)),
        ]
        + [pl.BlockSpec((rows // parts, LANES), lambda g: (0, g))] * parts,
        out_specs=[pl.BlockSpec((rows // parts, 2 * LANES), lambda g: (0, g))] * parts,
        scratch_shapes=[pltpu.VMEM((rows, LANES), BF)] + [pltpu.VMEM((rows, LANES), F32)] * 3,
        compiler_params=pltpu.CompilerParams(vmem_limit_bytes=VMEM_LIMIT),
        cost_estimate=pl.CostEstimate(flops=30 << 30, bytes_accessed=6 << 20, transcendentals=0),
    )(idx, qkv, lse, cosine, sine, *grads)


def project_out_kernel(n_parts, pieces, x_ref, gain_ref, *refs):
    attns, weights = refs[:n_parts], refs[n_parts : 2 * n_parts]
    hidden_ref, normed_refs = refs[2 * n_parts], refs[2 * n_parts + 1 :]
    rows = x_ref.shape[0] // pieces
    for p in range(pieces):
        at = slice(p * rows, (p + 1) * rows)
        hidden = x_ref[at].astype(F32)
        for a, w in zip(attns, weights, strict=True):
            hidden = hidden + mm_nt(a[at], w[...])
        inverse = lax.rsqrt(jnp.mean(hidden * hidden, axis=-1, keepdims=True) + EPSILON)
        hidden_ref[at] = hidden
        normed_refs[p][...] = (hidden * inverse * gain_ref[...]).astype(BF)


def project_out(x, gain, attns, weights, pieces):
    rows = x.shape[0]
    n = len(attns)
    return call(
        functools.partial(project_out_kernel, n, pieces),
        "project_out",
        [jax.ShapeDtypeStruct((rows, D), F32)] + [jax.ShapeDtypeStruct((rows // pieces, D), BF)] * pieces,
        [VM] * (2 + 2 * n),
        [VM] * (1 + pieces),
        (x, gain.reshape(1, D), *attns, *weights),
        flops=2 * rows * D * D,
        moved=7 << 20,
    )


def hidden_back_kernel(n_parts, pieces, n_sums, valid_ref, hidden_ref, cot_ref, gain_ref, *refs):
    sums, refs = refs[: pieces * n_sums], refs[pieces * n_sums :]
    weights, refs = refs[:n_parts], refs[n_parts:]
    grad_ref, low_ref, gain_grad_ref, attn_refs = refs[0], refs[1], refs[2], refs[3:]
    rows = hidden_ref.shape[0] // pieces
    gain = gain_ref[...]
    gain_grad = jnp.zeros((1, D), F32)
    for p in range(pieces):
        at = slice(p * rows, (p + 1) * rows)
        hidden = hidden_ref[at]
        normed_grad = sums[p * n_sums][...].astype(F32)
        for s in sums[p * n_sums + 1 : (p + 1) * n_sums]:
            normed_grad = normed_grad + s[...].astype(F32)
        inverse = lax.rsqrt(jnp.mean(hidden * hidden, axis=-1, keepdims=True) + EPSILON)
        gain_grad = gain_grad + jnp.sum(normed_grad * (hidden * inverse), axis=0, keepdims=True)
        scaled = normed_grad * gain
        back = inverse * scaled - hidden * (
            inverse * inverse * inverse * jnp.mean(scaled * hidden, axis=-1, keepdims=True)
        )
        dy = jnp.where(valid_ref[at] > 0, cot_ref[at].astype(F32), 0.0)
        total = dy + back
        grad_ref[at] = total
        low = total.astype(BF)
        low_ref[at] = low
        for a, w in zip(attn_refs, weights, strict=True):
            a[at] = mm(low, w[...]).astype(BF)
    gain_grad_ref[...] = gain_grad


def hidden_back(valid, hidden, cotangent, gain, sums, weights):
    rows, pieces, n_sums, n = hidden.shape[0], len(sums), len(sums[0]), len(weights)
    heads = weights[0].shape[1]
    return call(
        functools.partial(hidden_back_kernel, n, pieces, n_sums),
        "hidden_back",
        [
            jax.ShapeDtypeStruct((rows, D), F32),
            jax.ShapeDtypeStruct((rows, D), BF),
            jax.ShapeDtypeStruct((1, D), F32),
        ]
        + [jax.ShapeDtypeStruct((rows, heads), BF)] * n,
        [VM] * (4 + pieces * n_sums + n),
        [VM] * (3 + n),
        (valid, hidden, cotangent, gain.reshape(1, D), *[s for piece in sums for s in piece], *weights),
        flops=2 * rows * D * D,
        moved=10 << 20,
    )


def dispatch_kernel(n_pieces, scaled, pos_ref, gate_ref, *refs):
    pieces, out_ref, rows_ref, sems = refs[:n_pieces], refs[n_pieces], refs[n_pieces + 1], refs[n_pieces + 2]
    height = rows_ref.shape[0] // n_pieces
    copies = [
        pltpu.make_async_copy(piece, rows_ref.at[pl.ds(p * height, height)], sems.at[p])
        for p, piece in enumerate(pieces)
    ]
    for c in copies:
        c.start()
    rank = lax.broadcasted_iota(jnp.int32, (CAP, rows_ref.shape[0]), 0)
    for c in copies:
        c.wait()
    for j in range(out_ref.shape[0]):
        chosen = rank == pos_ref[j : j + 1, :]
        value = gate_ref[j : j + 1, :] if scaled else 1.0
        one_hot = jnp.where(chosen, value, 0.0).astype(BF)
        out_ref[j] = mm(one_hot, rows_ref[...]).astype(BF)


def dispatch(pos, gate, pieces, scaled):
    experts, rows = pos.shape
    return call(
        functools.partial(dispatch_kernel, len(pieces), scaled),
        "dispatch_scaled" if scaled else "dispatch",
        jax.ShapeDtypeStruct((experts, CAP, D), BF),
        [VM, VM] + [ANY] * len(pieces),
        VM,
        (pos, gate, *pieces),
        scratch=[pltpu.VMEM((rows, D), BF), pltpu.SemaphoreType.DMA((len(pieces),))],
        flops=2 * experts * CAP * rows * D,
        moved=5 << 20,
    )


def combine_kernel(n_experts, slot, scaled, n_adds, n_outs, pos_ref, gate_ref, *refs):
    sources, refs = refs[:n_experts], refs[n_experts:]
    adds, outs, (held, sems) = refs[:n_adds], refs[n_adds : n_adds + n_outs], refs[n_adds + n_outs :]
    copies = [
        pltpu.make_async_copy(source.at[slot], held.at[pl.ds(j * CAP, CAP)], sems.at[j])
        for j, source in enumerate(sources)
    ]
    for c in copies:
        c.start()
    for c in copies:
        c.wait()
    width = n_experts * CAP
    rows = pos_ref.shape[0]
    block = 256
    per_out = rows // n_outs
    for b in range(rows // block):
        at = slice(b * block, (b + 1) * block)
        tiles = []
        for first in range(0, width, LANES):
            size = min(LANES, width - first)
            lane = first + lax.broadcasted_iota(jnp.int32, (block, size), 1)
            tile = jnp.zeros((block, size), F32)
            for j in range(first // CAP, (first + size - 1) // CAP + 1):
                target = pos_ref[at, j : j + 1]
                target = jnp.where(target >= 0, target + j * CAP, -1)
                tile = jnp.where(lane == target, gate_ref[at, j : j + 1] if scaled else 1.0, tile)
            tiles.append(tile.astype(BF))
        total = mm(jnp.concatenate(tiles, axis=1), held[...])
        out, inner = outs[b * block // per_out], slice(b * block % per_out, b * block % per_out + block)
        if n_adds:
            total = total + adds[0][at].astype(F32)
        out[inner] = total.astype(BF)


def combine(pos, gate, sources, slot, scaled, add, n_outs):
    rows, n_experts = pos.shape
    adds = [] if add is None else [add]
    return call(
        functools.partial(combine_kernel, n_experts, slot, scaled, len(adds), n_outs),
        "combine_scaled" if scaled else "combine",
        [jax.ShapeDtypeStruct((rows // n_outs, D), BF)] * n_outs,
        [VM, VM] + [ANY] * n_experts + [VM] * len(adds),
        [VM] * n_outs,
        (pos, gate, *sources, *adds),
        scratch=[pltpu.VMEM((n_experts * CAP, D), BF), pltpu.SemaphoreType.DMA((n_experts,))],
        flops=2 * n_experts * CAP * rows * D,
        moved=5 << 20,
    )


def expert_kernel(j, outer, in_rows, down_rows, idx_ref, *refs):
    n_hops = outer - 1
    xs, refs = refs[:GROUP], refs[GROUP:]
    gs, refs = refs[:GROUP], refs[GROUP:]
    own, refs = refs[0], refs[1:]
    lefts, refs = refs[:n_hops], refs[n_hops:]
    rights, refs = refs[:n_hops], refs[n_hops:]
    y_ref, dx_ref, dw_ref = refs[:3]
    x_all, g_all, w_in, w_down, act_all, gug_all, sem_x, sem_g, sem_w, sem_d = refs[3:]
    o, i = idx_ref[0], idx_ref[1]

    def rows_of(sources, held, sems):
        return [
            pltpu.make_async_copy(s.at[j], held.at[pl.ds(n * CAP, CAP)], sems.at[n])
            for n, s in enumerate(sources)
        ]

    def weight_copies(source, at, slot):
        made = []
        for m in range(GROUP):
            place = at * GROUP + (i ^ m)
            made.append(
                pltpu.make_async_copy(
                    source.at[m, pl.ds(0, in_rows)],
                    w_in.at[pl.ds(pl.multiple_of(place * in_rows, in_rows), in_rows)],
                    sem_w.at[slot * GROUP + m],
                )
            )
            made.append(
                pltpu.make_async_copy(
                    source.at[m, pl.ds(in_rows, down_rows)],
                    w_down.at[pl.ds(pl.multiple_of(place * down_rows, down_rows), down_rows)],
                    sem_d.at[slot * GROUP + m],
                )
            )
        return made

    def each_weight(act):
        act(weight_copies(own, o, 0))
        for k in range(1, outer):

            @pl.when(o >= k)
            def _():
                act(weight_copies(lefts[k - 1], o - k, k))

            @pl.when(o + k < outer)
            def _():
                act(weight_copies(rights[k - 1], o + k, n_hops + k))

    def start(made):
        for c in made:
            c.start()

    def wait(made):
        for c in made:
            c.wait()

    each_weight(start)
    copy_x, copy_g = rows_of(xs, x_all, sem_x), rows_of(gs, g_all, sem_g)
    start(copy_x)
    start(copy_g)
    each_weight(wait)
    wait(copy_x)
    wait(copy_g)

    def per_slot(s, carry):
        at = pl.ds(pl.multiple_of(s * CAP, CAP), CAP)
        gate_up = mm(x_all[at, :], w_in[...])
        g, u = gate_up[:, :FF], gate_up[:, FF:]
        sigma = 1.0 / (1.0 + jnp.exp(-g))
        silu = g * sigma
        act = (silu * u).astype(BF)
        act_all[at, :] = act
        y_ref[s] = mm(act, w_down[...]).astype(BF)
        act_grad = mm_nt(g_all[at, :], w_down[...])
        gug_all[at, :FF] = (act_grad * u * sigma * (1.0 + g * (1.0 - sigma))).astype(BF)
        gug_all[at, FF:] = (act_grad * silu).astype(BF)
        dx_ref[s] = mm_nt(gug_all[at, :], w_in[...]).astype(BF)
        return carry

    lax.fori_loop(0, GROUP, per_slot, 0)
    for c in range(outer):
        part = mm_tn(x_all[:, c * GROUP * in_rows : (c + 1) * GROUP * in_rows], gug_all[...]).astype(BF)
        for r in range(GROUP):
            dw_ref[c, i ^ r, :in_rows, :] = part[r * in_rows : (r + 1) * in_rows]
        part = mm_tn(act_all[:, c * GROUP * down_rows : (c + 1) * GROUP * down_rows], g_all[...]).astype(BF)
        for r in range(GROUP):
            dw_ref[c, i ^ r, in_rows:, :] = part[r * down_rows : (r + 1) * down_rows]


def expert(idx, j, outer, in_rows, down_rows, xs, gs, own, lefts, rights):
    n_hops = outer - 1
    total = GROUP * CAP
    packed = in_rows + down_rows
    return call(
        functools.partial(expert_kernel, j, outer, in_rows, down_rows),
        "expert",
        [
            jax.ShapeDtypeStruct((GROUP, CAP, D), BF),
            jax.ShapeDtypeStruct((GROUP, CAP, D), BF),
            jax.ShapeDtypeStruct((outer, GROUP, packed, D), BF),
        ],
        [SMEM] + [ANY] * (2 * GROUP + 1 + 2 * n_hops),
        [VM] * 3,
        (idx, *xs, *gs, own, *lefts, *rights),
        scratch=[
            pltpu.VMEM((total, D), BF),
            pltpu.VMEM((total, D), BF),
            pltpu.VMEM((D, 2 * FF), BF),
            pltpu.VMEM((FF, D), BF),
            pltpu.VMEM((total, FF), BF),
            pltpu.VMEM((total, 2 * FF), BF),
            pltpu.SemaphoreType.DMA((GROUP,)),
            pltpu.SemaphoreType.DMA((GROUP,)),
            pltpu.SemaphoreType.DMA(((1 + 2 * n_hops) * GROUP,)),
            pltpu.SemaphoreType.DMA(((1 + 2 * n_hops) * GROUP,)),
        ],
        flops=18 * total * D * FF,
        moved=15 << 20,
    )


def pack_kernel(n_experts, in_rows, down_rows, idx_ref, in_ref, down_ref, *refs):
    outs, sems = refs[:-1], refs[-1]
    i = idx_ref[1]
    copies = []
    for j in range(n_experts):
        for m in range(GROUP):
            n = j * GROUP + m
            source = (i ^ m) * n_experts + j
            copies.append(pltpu.make_async_copy(in_ref.at[source], outs[n].at[pl.ds(0, in_rows)], sems.at[2 * n]))
            copies.append(
                pltpu.make_async_copy(down_ref.at[source], outs[n].at[pl.ds(in_rows, down_rows)], sems.at[2 * n + 1])
            )
    for c in copies:
        c.start()
    for c in copies:
        c.wait()


def pack_weights(idx, expert_in, expert_down):
    experts, in_rows, _ = expert_in.shape
    down_rows = expert_down.shape[1]
    n = experts // GROUP
    flat = call(
        functools.partial(pack_kernel, n, in_rows, down_rows),
        "pack_weights",
        [jax.ShapeDtypeStruct((in_rows + down_rows, D), BF)] * experts,
        [SMEM, ANY, ANY],
        [VM] * experts,
        (idx, expert_in, expert_down),
        scratch=[pltpu.SemaphoreType.DMA((2 * experts,))],
        moved=6 << 20,
    )
    return [[flat[j * GROUP + m] for m in range(GROUP)] for j in range(n)]


def body(
    tokens,
    cotangent,
    lengths,
    expert_ids,
    gate_values,
    first_gain,
    qkv_weight,
    attn_out_weight,
    second_gain,
    expert_in_weight,
    expert_out_weight,
):
    rows = tokens.shape[0]
    n_tensor, n_dp = lax.axis_size("tensor"), lax.axis_size("dp")
    outer = n_dp // GROUP
    slot_rows = rows * n_tensor
    d, t = lax.axis_index("dp"), lax.axis_index("tensor")
    o, i = d // GROUP, d % GROUP
    length = lengths[0]
    idx = jnp.stack([o, i, t, length]).astype(jnp.int32)
    width = qkv_weight.shape[1] * qkv_weight.shape[2]
    experts_local, in_rows, _ = expert_in_weight.shape
    down_rows = expert_out_weight.shape[1]
    own_experts = experts_local // GROUP
    pair = n_tensor == 2
    q_block = 256
    half = rows // 2

    def across(v, m):
        return lax.ppermute(v, "dp", [(a, a ^ m) for a in range(n_dp)])

    def beside(v):
        return lax.ppermute(v, "tensor", [(0, 1), (1, 0)])

    def chain(v):
        up = [(a, a + GROUP) for a in range(n_dp - GROUP)]
        down = [(b, a) for a, b in up]
        lefts, rights = [], []
        a = b = v
        for _ in range(outer - 1):
            a, b = lax.ppermute(a, "dp", up), lax.ppermute(b, "dp", down)
            lefts.append(a)
            rights.append(b)
        return lefts, rights

    def gather_group(pieces):
        if pair:
            a, b = pieces
            ax, by, ay, bx = beside(a), across(b, 2), across(a, 2), beside(b)
            axy, bxy = across(ax, 2), beside(by)
            slots = [[a, ax, b, bx], [ay, axy, by, bxy]]
        else:
            slot = lax.all_gather(pieces[0], "tensor", axis=0, tiled=True)
            slots = [[slot], [across(slot, 2)]]
        return slots + [[across(p, 1) for p in s] for s in slots]

    qkv_full = lax.all_gather(qkv_weight.reshape(qkv_weight.shape[0], width), "dp", axis=0, tiled=True)
    out_full = lax.all_gather(attn_out_weight.T, "dp", axis=0, tiled=True)
    blocks = pack_weights(idx, expert_in_weight, expert_out_weight)
    moved_weights = []
    for per_expert in blocks:
        own = jnp.stack([per_expert[0]] + [across(per_expert[m], m) for m in range(1, GROUP)])
        moved_weights.append((own, *chain(own)))
    if pair:
        out_parts = [out_full, beside(out_full)]
    else:
        gathered = lax.all_gather(out_full, "tensor", axis=0)
        out_parts = [gathered[k] for k in range(n_tensor)]

    x = tokens.astype(F32)
    inverse_one = lax.rsqrt(jnp.mean(x * x, axis=-1, keepdims=True) + EPSILON)
    normed_one = (x * inverse_one * first_gain).astype(BF)
    if pair:
        other = beside(normed_one)
        normed_all = jnp.where(
            t == 0,
            jnp.concatenate([normed_one, other], axis=0),
            jnp.concatenate([other, normed_one], axis=0),
        )
    else:
        normed_all = lax.all_gather(normed_one, "tensor", axis=0, tiled=True)
    cosine, sine = rope_tables(slot_rows)
    qkv = qkv_project(normed_all, qkv_full, cosine, sine)
    *attended, lse = attend(idx, qkv, 2 if pair else 1, q_block)
    if pair:
        attn_parts = [attended[0], beside(attended[1])]
    else:
        heads = attended[0].shape[1]
        exchanged = lax.all_to_all(attended[0].reshape(n_tensor, rows, heads), "tensor", 0, 0)
        attn_parts = [exchanged[k] for k in range(n_tensor)]
    hidden, *normed_two = project_out(tokens, second_gain, attn_parts, out_parts, 2 if pair else 1)

    positions = t * rows + jnp.arange(rows, dtype=jnp.int32)
    valid_rows = positions < length
    n_experts = experts_local * n_tensor
    chosen = expert_ids.T[None] == jnp.arange(n_experts, dtype=jnp.int32)[:, None, None]
    gates = jnp.sum(jnp.where(chosen, gate_values.T[None].astype(F32), 0.0), axis=1)
    gates = jnp.where(valid_rows[None, :], gates, 0.0).astype(BF)
    if pair:
        gates_x = beside(gates)
        slot_gates = jnp.concatenate(
            [gates[:, :half], gates_x[:, :half], gates[:, half:], gates_x[:, half:]], axis=1
        )
    else:
        slot_gates = lax.all_gather(gates, "tensor", axis=1, tiled=True)
    gates_y = across(slot_gates, 2)
    all_gates = jnp.stack([slot_gates, gates_y, across(slot_gates, 1), across(gates_y, 1)])
    own_gates = lax.dynamic_slice_in_dim(
        all_gates, t * experts_local + i * own_experts, own_experts, axis=1
    ).astype(F32)
    named = own_gates > 0
    before = (
        lax.broadcasted_iota(jnp.int32, (slot_rows, slot_rows), 0)
        < lax.broadcasted_iota(jnp.int32, (slot_rows, slot_rows), 1)
    ).astype(BF)
    ranks = jnp.dot(
        named.astype(BF).reshape(GROUP * own_experts, slot_rows), before, preferred_element_type=F32
    ).reshape(GROUP, own_experts, slot_rows)
    pos = jnp.where(named, ranks, -1.0).astype(jnp.int32)
    pos_columns, gate_columns = jnp.swapaxes(pos, 1, 2), jnp.swapaxes(own_gates, 1, 2)

    dy = jnp.where(valid_rows[:, None], cotangent, jnp.zeros_like(cotangent))
    dy_slots = gather_group([dy[:half], dy[half:]] if pair else [dy])
    out_grads = [dispatch(pos[s], own_gates[s], dy_slots[s], True) for s in range(GROUP)]
    normed_slots = gather_group(normed_two)
    expert_rows = [dispatch(pos[s], own_gates[s], normed_slots[s], False) for s in range(GROUP)]

    expert_outs, row_grads, weight_grads = [], [], []
    for j in range(own_experts):
        own, lefts, rights = moved_weights[j]
        y, dx, dw = expert(
            idx, j, outer, in_rows, down_rows, expert_rows, out_grads, own, lefts, rights
        )
        expert_outs.append(y)
        row_grads.append(dx)
        weight_grads.append(dw)

    def sum_group(sources, scaled):
        def part(s, add, n_outs):
            return combine(pos_columns[s], gate_columns[s], sources, s, scaled, add, n_outs)

        far = [part(2, None, 1)[0], part(3, None, 1)[0]]
        near = [across(v, 1) for v in far]
        if pair:
            ay, axy, by, bxy = part(1, near[1], 4)
            a, ax, b, bx = part(0, near[0], 4)

            def add(p, q):
                return (p.astype(F32) + q.astype(F32)).astype(BF)

            a, ax = add(a, across(ay, 2)), add(ax, across(axy, 2))
            b, by = add(b, beside(bx)), add(by, beside(bxy))
            return [[a, beside(ax)], [b, across(by, 2)]]
        (y,) = part(1, near[1], 1)
        (v,) = part(0, near[0], 1)
        v = (v.astype(F32) + across(y, 2).astype(F32)).astype(BF)
        return [[lax.psum_scatter(v, "tensor", scatter_dimension=0, tiled=True)]]

    valid_column = valid_rows.astype(F32)[:, None]
    normed_two_grad = sum_group(row_grads, False)
    hidden_grad, branch_grad, second_gain_part, *attn_grads = hidden_back(
        valid_column, hidden, cotangent, second_gain, normed_two_grad, out_parts
    )
    if pair:
        attn_grads = [attn_grads[0], beside(attn_grads[1])]
    else:
        attn_grads = [
            lax.all_to_all(jnp.stack(attn_grads), "tensor", 0, 0).reshape(slot_rows, attn_grads[0].shape[1])
        ]
    projected_grads = attend_back(idx, qkv, lse, cosine, sine, attn_grads, q_block)

    def first_norm_part(v):
        return lax.dot_general(v, qkv_full, (((1,), (1,)), ((), ())), preferred_element_type=F32).astype(BF)

    if pair:
        theirs = beside(first_norm_part(projected_grads[1]))
        normed_one_grad = first_norm_part(projected_grads[0]).astype(F32) + theirs.astype(F32)
        qkv_part = mm_tn(normed_one, projected_grads[0]) + mm_tn(other, projected_grads[1])
    else:
        normed_one_grad = lax.psum_scatter(
            first_norm_part(projected_grads[0]), "tensor", scatter_dimension=0, tiled=True
        ).astype(F32)
        qkv_part = mm_tn(normed_all, projected_grads[0])
    first_gain_part = jnp.sum(normed_one_grad * (x * inverse_one), axis=0)
    scaled = normed_one_grad * first_gain
    tokens_grad = (
        hidden_grad
        + inverse_one * scaled
        - x * (inverse_one * inverse_one * inverse_one * jnp.mean(scaled * x, axis=-1, keepdims=True))
    )

    mixture = sum_group(expert_outs, True)
    mixture = jnp.concatenate([sum(v.astype(F32) for v in terms) for terms in mixture], axis=0)
    output = jnp.where(valid_rows[:, None], hidden + mixture, 0.0).astype(BF)

    outer_groups = [[a * GROUP + b for a in range(outer)] for b in range(GROUP)]
    received = [[] for _ in range(GROUP)]
    for dw in weight_grads:
        mine = lax.psum_scatter(dw, "dp", scatter_dimension=0, tiled=True, axis_index_groups=outer_groups)
        for m in range(GROUP):
            block = mine[0, m]
            received[m].append(block if m == 0 else across(block, m))
    by_distance = jnp.stack([jnp.stack(v) for v in received])
    by_source = jnp.take(by_distance, jnp.arange(GROUP) ^ i, axis=0).reshape(
        experts_local, in_rows + down_rows, D
    )
    expert_in_grad = by_source[:, :in_rows].astype(F32)
    expert_out_grad = by_source[:, in_rows:].astype(F32)

    attn_out_parts = [mm_tn(branch_grad, part).astype(BF) for part in attn_parts]
    if pair:
        attn_out_part = (attn_out_parts[0].astype(F32) + beside(attn_out_parts[1]).astype(F32)).astype(BF)
    else:
        attn_out_part = lax.psum_scatter(jnp.stack(attn_out_parts), "tensor", scatter_dimension=0, tiled=True)[0]
    qkv_grad = lax.psum_scatter(qkv_part.astype(BF), "dp", scatter_dimension=0, tiled=True).astype(F32)
    attn_out_grad = lax.psum_scatter(attn_out_part, "dp", scatter_dimension=0, tiled=True).astype(F32).T

    gains = jnp.stack([first_gain_part, second_gain_part[0]])
    if pair:
        gains = gains + beside(gains)
    else:
        gains = lax.psum(gains, "tensor")
    step = 1
    while step < n_dp:
        gains = gains + across(gains, step)
        step *= 2
    return (
        output,
        tokens_grad,
        gains[0],
        qkv_grad.reshape(qkv_weight.shape),
        attn_out_grad,
        gains[1],
        expert_in_grad,
        expert_out_grad,
    )


def solution(mesh):
    placed = (
        P(("dp", "tensor"), None),
        P(("dp", "tensor"), None),
        P("dp"),
        P(("dp", "tensor"), None),
        P(("dp", "tensor"), None),
        P(),
        P("dp", "tensor", None),
        P("tensor", "dp"),
        P(),
        P("tensor", "dp", None),
        P("tensor", "dp", None),
    )
    return jax.shard_map(
        body,
        mesh=mesh,
        in_specs=placed,
        out_specs=(
            P(("dp", "tensor"), None),
            P(("dp", "tensor"), None),
            P(),
            P("dp", "tensor", None),
            P("tensor", "dp"),
            P(),
            P("tensor", "dp", None),
            P("tensor", "dp", None),
        ),
        check_vma=False,
    )
```

```python
import functools
import math

import jax
import jax.numpy as jnp
from jax import lax
from jax.experimental import pallas as pl
from jax.experimental.pallas import tpu as pltpu
from jax.sharding import PartitionSpec as P

D = 1024
HD = 64
FF = 512
G = 2
CAP = 288
GROUP = 4
LANES = 128

EPSILON = 1e-06
THETA = 10000.0
NEGATIVE = -1e30
BF = jnp.bfloat16
F32 = jnp.float32
VMEM_LIMIT = 60 * 1024 * 1024
MESH = pl.DeviceIdType.MESH

ANY = pl.BlockSpec(memory_space=pl.ANY)
SMEM = pl.BlockSpec(memory_space=pltpu.SMEM)
VM = pl.BlockSpec(memory_space=pltpu.VMEM)


def mm(a, b):
    return lax.dot_general(a, b, (((1,), (0,)), ((), ())), preferred_element_type=F32)


def mm_nt(a, b):
    return lax.dot_general(a, b, (((1,), (1,)), ((), ())), preferred_element_type=F32)


def mm_tn(a, b):
    return lax.dot_general(a, b, (((0,), (0,)), ((), ())), preferred_element_type=F32)


def call(kernel, name, out_shape, in_specs, out_specs, args, scratch=(), flops=0, moved=0, **more):
    return pl.pallas_call(
        kernel,
        name=name,
        out_shape=out_shape,
        in_specs=in_specs,
        out_specs=out_specs,
        scratch_shapes=list(scratch),
        compiler_params=pltpu.CompilerParams(vmem_limit_bytes=VMEM_LIMIT),
        cost_estimate=pl.CostEstimate(flops=flops, bytes_accessed=moved, transcendentals=0),
        **more,
    )(*args)


def rope_tables(total_rows):
    half = HD // 2
    positions = jnp.arange(total_rows).astype(F32)
    frequency = THETA ** (-(jnp.arange(half).astype(F32) * 2.0 / HD))
    angles = positions[:, None] * frequency[None, :]
    cosine, sine = jnp.cos(angles), jnp.sin(angles)
    return (
        jnp.concatenate([cosine] * 4, axis=1),
        jnp.concatenate([-sine, sine, -sine, sine], axis=1),
    )


def swap_halves(v):
    lane = lax.broadcasted_iota(jnp.int32, v.shape, 1)
    return jnp.where(lane % HD < HD // 2, pltpu.roll(v, LANES - HD // 2, 1), pltpu.roll(v, HD // 2, 1))


def qkv_kernel(n_ref, w_ref, cos_ref, sin_ref, out_ref):
    projected = mm(n_ref[...], w_ref[...])
    cosine, sine = cos_ref[...], sin_ref[...]
    key_lanes = lax.broadcasted_iota(jnp.int32, cosine.shape, 1) < HD
    for g in range(projected.shape[1] // (2 * LANES)):
        q = projected[:, g * 2 * LANES : g * 2 * LANES + LANES]
        kv = projected[:, g * 2 * LANES + LANES : (g + 1) * 2 * LANES]
        q = q * cosine + swap_halves(q) * sine
        kv = jnp.where(key_lanes, kv * cosine + swap_halves(kv) * sine, kv)
        out_ref[:, g * 2 * LANES : g * 2 * LANES + LANES] = q.astype(BF)
        out_ref[:, g * 2 * LANES + LANES : (g + 1) * 2 * LANES] = kv.astype(BF)


def qkv_project(normed, weight, cosine, sine):
    rows, width = normed.shape[0], weight.shape[1]
    block = 256
    return pl.pallas_call(
        qkv_kernel,
        name="qkv_rope",
        grid=(rows // block,),
        out_shape=jax.ShapeDtypeStruct((rows, width), BF),
        in_specs=[
            pl.BlockSpec((block, D), lambda b: (b, 0)),
            pl.BlockSpec((D, width), lambda b: (0, 0)),
            pl.BlockSpec((block, LANES), lambda b: (b, 0)),
            pl.BlockSpec((block, LANES), lambda b: (b, 0)),
        ],
        out_specs=pl.BlockSpec((block, width), lambda b: (b, 0)),
        compiler_params=pltpu.CompilerParams(vmem_limit_bytes=VMEM_LIMIT),
        cost_estimate=pl.CostEstimate(flops=2 * rows * D * width, bytes_accessed=6 << 20, transcendentals=0),
    )(normed, weight, cosine, sine)


def head_pair(v):
    first = lax.broadcasted_iota(jnp.int32, v.shape, 1) < HD
    zero = jnp.zeros_like(v)
    return jnp.concatenate([jnp.where(first, v, zero), jnp.where(first, zero, v)], axis=0)


def head_join(v):
    n = v.shape[0] // 2
    first = lax.broadcasted_iota(jnp.int32, (n, LANES), 1) < HD
    return jnp.where(first, v[:n], v[n:])


def doubled(kv):
    first = lax.broadcasted_iota(jnp.int32, kv.shape, 1) < HD
    other = pltpu.roll(kv.astype(F32), HD, 1).astype(BF)
    return jnp.where(first, kv, other), jnp.where(first, other, kv)


def allowed(n_keys, q_block, q_start, length):
    key = lax.broadcasted_iota(jnp.int32, (n_keys, 2 * q_block), 0)
    lane = lax.broadcasted_iota(jnp.int32, (n_keys, 2 * q_block), 1)
    query = q_start + jnp.where(lane < q_block, lane, lane - q_block)
    return (key <= query) & (key < length)


def attend_kernel(q_block, idx_ref, qkv_ref, *out_refs):
    outs, lse_ref = out_refs[:-1], out_refs[-1]
    rows = qkv_ref.shape[0]
    length = idx_ref[3]
    keys, values = doubled(qkv_ref[:, LANES:])
    for b in range(rows // q_block):
        start, n_keys = b * q_block, (b + 1) * q_block
        q = head_pair(qkv_ref[start : start + q_block, :LANES])
        scores = mm_nt(keys[:n_keys], q) * (1.0 / math.sqrt(HD))
        scores = jnp.where(allowed(n_keys, q_block, start, length), scores, NEGATIVE)
        largest = jnp.max(scores, axis=0, keepdims=True)
        expon = jnp.exp(scores - largest)
        totals = jnp.sum(expon, axis=0, keepdims=True)
        probs = (expon * (1.0 / totals)).astype(BF)
        mixed = head_join(mm_tn(probs, values[:n_keys])).astype(BF)
        lse_ref[0, b : b + 1, :] = largest + jnp.log(totals)
        if len(outs) == 1:
            outs[0][start : start + q_block] = mixed
        else:
            own_rows = rows // 2
            half, at = start // own_rows, start % own_rows
            mine = idx_ref[2] == half

            @pl.when(mine)
            def _():
                outs[0][at : at + q_block] = mixed

            @pl.when(jnp.logical_not(mine))
            def _():
                outs[1][at : at + q_block] = mixed


def attend(idx, qkv, parts, q_block):
    rows, groups = qkv.shape[0], qkv.shape[1] // (2 * LANES)
    out = jax.ShapeDtypeStruct((rows // parts, groups * LANES), BF)
    return pl.pallas_call(
        functools.partial(attend_kernel, q_block),
        name="attend",
        grid=(groups,),
        out_shape=[out] * parts + [jax.ShapeDtypeStruct((groups, rows // q_block, 2 * q_block), F32)],
        in_specs=[SMEM, pl.BlockSpec((rows, 2 * LANES), lambda g: (0, g))],
        out_specs=[pl.BlockSpec((rows // parts, LANES), lambda g: (0, g))] * parts
        + [pl.BlockSpec((1, rows // q_block, 2 * q_block), lambda g: (g, 0, 0))],
        compiler_params=pltpu.CompilerParams(vmem_limit_bytes=VMEM_LIMIT),
        cost_estimate=pl.CostEstimate(flops=14 << 30, bytes_accessed=4 << 20, transcendentals=0),
    )(idx, qkv)


def attend_back_kernel(q_block, n_grads, idx_ref, qkv_ref, lse_ref, cos_ref, sin_ref, *refs):
    grads, outs = refs[:n_grads], refs[n_grads : 2 * n_grads]
    do_ref, dq_ref, dk_ref, dv_ref = refs[2 * n_grads :]
    rows = qkv_ref.shape[0]
    own_rows = rows // n_grads
    length = idx_ref[3]
    for p in range(n_grads):
        at = pl.multiple_of((p ^ idx_ref[2] if n_grads == 2 else 0) * own_rows, own_rows)
        do_ref[pl.ds(at, own_rows), :] = grads[p][...]
    keys, values = doubled(qkv_ref[:, LANES:])
    dk_ref[...] = jnp.zeros_like(dk_ref)
    dv_ref[...] = jnp.zeros_like(dv_ref)
    scale = 1.0 / math.sqrt(HD)
    for b in range(rows // q_block):
        start, n_keys = b * q_block, (b + 1) * q_block
        q = head_pair(qkv_ref[start : start + q_block, :LANES])
        grad = head_pair(do_ref[start : start + q_block, :])
        scores = mm_nt(keys[:n_keys], q) * scale
        probs = jnp.where(
            allowed(n_keys, q_block, start, length), jnp.exp(scores - lse_ref[0, b : b + 1, :]), 0.0
        )
        prob_grad = mm_nt(values[:n_keys], grad)
        center = jnp.sum(probs * prob_grad, axis=0, keepdims=True)
        score_grad = (probs * (prob_grad - center)).astype(BF)
        dq_ref[start : start + q_block, :] = head_join(mm_tn(score_grad, keys[:n_keys])) * scale
        dk_ref[:n_keys, :] += mm(score_grad, q)
        dv_ref[:n_keys, :] += mm(probs.astype(BF), grad)
    cosine, sine = cos_ref[...], sin_ref[...]
    dq = dq_ref[...]
    dq = (dq * cosine - swap_halves(dq) * sine).astype(BF)
    dk, dv = dk_ref[...] * scale, dv_ref[...]
    dk = dk + pltpu.roll(dk, HD, 1)
    dv = dv + pltpu.roll(dv, HD, 1)
    dk = dk * cosine - swap_halves(dk) * sine
    first = lax.broadcasted_iota(jnp.int32, dk.shape, 1) < HD
    dkv = jnp.where(first, dk, dv).astype(BF)
    if n_grads == 1:
        outs[0][:, :LANES] = dq
        outs[0][:, LANES:] = dkv
    else:
        do_ref[...] = dq
        for p in range(2):
            at = pl.multiple_of((p ^ idx_ref[2]) * own_rows, own_rows)
            outs[p][:, :LANES] = do_ref[pl.ds(at, own_rows), :]
        do_ref[...] = dkv
        for p in range(2):
            at = pl.multiple_of((p ^ idx_ref[2]) * own_rows, own_rows)
            outs[p][:, LANES:] = do_ref[pl.ds(at, own_rows), :]


def attend_back(idx, qkv, lse, cosine, sine, grads, q_block):
    rows, groups, parts = qkv.shape[0], qkv.shape[1] // (2 * LANES), len(grads)
    return pl.pallas_call(
        functools.partial(attend_back_kernel, q_block, parts),
        name="attend_back",
        grid=(groups,),
        out_shape=[jax.ShapeDtypeStruct((rows // parts, groups * 2 * LANES), BF)] * parts,
        in_specs=[
            SMEM,
            pl.BlockSpec((rows, 2 * LANES), lambda g: (0, g)),
            pl.BlockSpec((1, rows // q_block, 2 * q_block), lambda g: (g, 0, 0)),
            pl.BlockSpec((rows, LANES), lambda g: (0, 0)),
            pl.BlockSpec((rows, LANES), lambda g: (0, 0)),
        ]
        + [pl.BlockSpec((rows // parts, LANES), lambda g: (0, g))] * parts,
        out_specs=[pl.BlockSpec((rows // parts, 2 * LANES), lambda g: (0, g))] * parts,
        scratch_shapes=[pltpu.VMEM((rows, LANES), BF)] + [pltpu.VMEM((rows, LANES), F32)] * 3,
        compiler_params=pltpu.CompilerParams(vmem_limit_bytes=VMEM_LIMIT),
        cost_estimate=pl.CostEstimate(flops=30 << 30, bytes_accessed=6 << 20, transcendentals=0),
    )(idx, qkv, lse, cosine, sine, *grads)


def project_out_kernel(n_parts, pieces, x_ref, gain_ref, *refs):
    attns, weights = refs[:n_parts], refs[n_parts : 2 * n_parts]
    hidden_ref, normed_refs = refs[2 * n_parts], refs[2 * n_parts + 1 :]
    rows = x_ref.shape[0] // pieces
    for p in range(pieces):
        at = slice(p * rows, (p + 1) * rows)
        hidden = x_ref[at].astype(F32)
        for a, w in zip(attns, weights, strict=True):
            hidden = hidden + mm_nt(a[at], w[...])
        inverse = lax.rsqrt(jnp.mean(hidden * hidden, axis=-1, keepdims=True) + EPSILON)
        hidden_ref[at] = hidden
        normed_refs[p][...] = (hidden * inverse * gain_ref[...]).astype(BF)


def project_out(x, gain, attns, weights, pieces):
    rows = x.shape[0]
    n = len(attns)
    return call(
        functools.partial(project_out_kernel, n, pieces),
        "project_out",
        [jax.ShapeDtypeStruct((rows, D), F32)] + [jax.ShapeDtypeStruct((rows // pieces, D), BF)] * pieces,
        [VM] * (2 + 2 * n),
        [VM] * (1 + pieces),
        (x, gain.reshape(1, D), *attns, *weights),
        flops=2 * rows * D * D,
        moved=7 << 20,
    )


def hidden_back_kernel(n_parts, pieces, n_sums, valid_ref, hidden_ref, cot_ref, gain_ref, *refs):
    sums, refs = refs[: pieces * n_sums], refs[pieces * n_sums :]
    weights, refs = refs[:n_parts], refs[n_parts:]
    grad_ref, low_ref, gain_grad_ref, attn_refs = refs[0], refs[1], refs[2], refs[3:]
    rows = hidden_ref.shape[0] // pieces
    gain = gain_ref[...]
    gain_grad = jnp.zeros((1, D), F32)
    for p in range(pieces):
        at = slice(p * rows, (p + 1) * rows)
        hidden = hidden_ref[at]
        normed_grad = sums[p * n_sums][...].astype(F32)
        for s in sums[p * n_sums + 1 : (p + 1) * n_sums]:
            normed_grad = normed_grad + s[...].astype(F32)
        inverse = lax.rsqrt(jnp.mean(hidden * hidden, axis=-1, keepdims=True) + EPSILON)
        gain_grad = gain_grad + jnp.sum(normed_grad * (hidden * inverse), axis=0, keepdims=True)
        scaled = normed_grad * gain
        back = inverse * scaled - hidden * (
            inverse * inverse * inverse * jnp.mean(scaled * hidden, axis=-1, keepdims=True)
        )
        dy = jnp.where(valid_ref[at] > 0, cot_ref[at].astype(F32), 0.0)
        total = dy + back
        grad_ref[at] = total
        low = total.astype(BF)
        low_ref[at] = low
        for a, w in zip(attn_refs, weights, strict=True):
            a[at] = mm(low, w[...]).astype(BF)
    gain_grad_ref[...] = gain_grad


def hidden_back(valid, hidden, cotangent, gain, sums, weights):
    rows, pieces, n_sums, n = hidden.shape[0], len(sums), len(sums[0]), len(weights)
    heads = weights[0].shape[1]
    return call(
        functools.partial(hidden_back_kernel, n, pieces, n_sums),
        "hidden_back",
        [
            jax.ShapeDtypeStruct((rows, D), F32),
            jax.ShapeDtypeStruct((rows, D), BF),
            jax.ShapeDtypeStruct((1, D), F32),
        ]
        + [jax.ShapeDtypeStruct((rows, heads), BF)] * n,
        [VM] * (4 + pieces * n_sums + n),
        [VM] * (3 + n),
        (valid, hidden, cotangent, gain.reshape(1, D), *[s for piece in sums for s in piece], *weights),
        flops=2 * rows * D * D,
        moved=10 << 20,
    )


def dispatch_kernel(n_pieces, scaled, pos_ref, gate_ref, *refs):
    pieces, out_ref, rows_ref, sems = refs[:n_pieces], refs[n_pieces], refs[n_pieces + 1], refs[n_pieces + 2]
    height = rows_ref.shape[0] // n_pieces
    copies = [
        pltpu.make_async_copy(piece, rows_ref.at[pl.ds(p * height, height)], sems.at[p])
        for p, piece in enumerate(pieces)
    ]
    for c in copies:
        c.start()
    rank = lax.broadcasted_iota(jnp.int32, (CAP, rows_ref.shape[0]), 0)
    for c in copies:
        c.wait()
    for j in range(out_ref.shape[0]):
        chosen = rank == pos_ref[j : j + 1, :]
        value = gate_ref[j : j + 1, :] if scaled else 1.0
        one_hot = jnp.where(chosen, value, 0.0).astype(BF)
        out_ref[j] = mm(one_hot, rows_ref[...]).astype(BF)


def dispatch(pos, gate, pieces, scaled):
    experts, rows = pos.shape
    return call(
        functools.partial(dispatch_kernel, len(pieces), scaled),
        "dispatch_scaled" if scaled else "dispatch",
        jax.ShapeDtypeStruct((experts, CAP, D), BF),
        [VM, VM] + [ANY] * len(pieces),
        VM,
        (pos, gate, *pieces),
        scratch=[pltpu.VMEM((rows, D), BF), pltpu.SemaphoreType.DMA((len(pieces),))],
        flops=2 * experts * CAP * rows * D,
        moved=5 << 20,
    )


def combine_kernel(n_experts, slot, scaled, n_adds, n_outs, pos_ref, gate_ref, *refs):
    sources, refs = refs[:n_experts], refs[n_experts:]
    adds, outs, (held, sems) = refs[:n_adds], refs[n_adds : n_adds + n_outs], refs[n_adds + n_outs :]
    copies = [
        pltpu.make_async_copy(source.at[slot], held.at[pl.ds(j * CAP, CAP)], sems.at[j])
        for j, source in enumerate(sources)
    ]
    for c in copies:
        c.start()
    for c in copies:
        c.wait()
    width = n_experts * CAP
    rows = pos_ref.shape[0]
    block = 256
    per_out = rows // n_outs
    for b in range(rows // block):
        at = slice(b * block, (b + 1) * block)
        tiles = []
        for first in range(0, width, LANES):
            size = min(LANES, width - first)
            lane = first + lax.broadcasted_iota(jnp.int32, (block, size), 1)
            tile = jnp.zeros((block, size), F32)
            for j in range(first // CAP, (first + size - 1) // CAP + 1):
                target = pos_ref[at, j : j + 1]
                target = jnp.where(target >= 0, target + j * CAP, -1)
                tile = jnp.where(lane == target, gate_ref[at, j : j + 1] if scaled else 1.0, tile)
            tiles.append(tile.astype(BF))
        total = mm(jnp.concatenate(tiles, axis=1), held[...])
        out, inner = outs[b * block // per_out], slice(b * block % per_out, b * block % per_out + block)
        if n_adds:
            total = total + adds[0][at].astype(F32)
        out[inner] = total.astype(BF)


def combine(pos, gate, sources, slot, scaled, add, n_outs):
    rows, n_experts = pos.shape
    adds = [] if add is None else [add]
    return call(
        functools.partial(combine_kernel, n_experts, slot, scaled, len(adds), n_outs),
        "combine_scaled" if scaled else "combine",
        [jax.ShapeDtypeStruct((rows // n_outs, D), BF)] * n_outs,
        [VM, VM] + [ANY] * n_experts + [VM] * len(adds),
        [VM] * n_outs,
        (pos, gate, *sources, *adds),
        scratch=[pltpu.VMEM((n_experts * CAP, D), BF), pltpu.SemaphoreType.DMA((n_experts,))],
        flops=2 * n_experts * CAP * rows * D,
        moved=5 << 20,
    )


def expert_kernel(j, outer, in_rows, down_rows, idx_ref, *refs):
    n_hops = outer - 1
    xs, refs = refs[:GROUP], refs[GROUP:]
    gs, refs = refs[:GROUP], refs[GROUP:]
    own, refs = refs[0], refs[1:]
    lefts, refs = refs[:n_hops], refs[n_hops:]
    rights, refs = refs[:n_hops], refs[n_hops:]
    y_ref, dx_ref, dw_ref = refs[:3]
    x_all, g_all, w_in, w_down, act_all, gug_all, sem_x, sem_g, sem_w, sem_d = refs[3:]
    o, i = idx_ref[0], idx_ref[1]

    def rows_of(sources, held, sems):
        return [
            pltpu.make_async_copy(s.at[j], held.at[pl.ds(n * CAP, CAP)], sems.at[n])
            for n, s in enumerate(sources)
        ]

    def weight_copies(source, at, slot):
        made = []
        for m in range(GROUP):
            place = at * GROUP + (i ^ m)
            made.append(
                pltpu.make_async_copy(
                    source.at[m, pl.ds(0, in_rows)],
                    w_in.at[pl.ds(pl.multiple_of(place * in_rows, in_rows), in_rows)],
                    sem_w.at[slot * GROUP + m],
                )
            )
            made.append(
                pltpu.make_async_copy(
                    source.at[m, pl.ds(in_rows, down_rows)],
                    w_down.at[pl.ds(pl.multiple_of(place * down_rows, down_rows), down_rows)],
                    sem_d.at[slot * GROUP + m],
                )
            )
        return made

    def each_weight(act):
        act(weight_copies(own, o, 0))
        for k in range(1, outer):

            @pl.when(o >= k)
            def _():
                act(weight_copies(lefts[k - 1], o - k, k))

            @pl.when(o + k < outer)
            def _():
                act(weight_copies(rights[k - 1], o + k, n_hops + k))

    def start(made):
        for c in made:
            c.start()

    def wait(made):
        for c in made:
            c.wait()

    each_weight(start)
    copy_x, copy_g = rows_of(xs, x_all, sem_x), rows_of(gs, g_all, sem_g)
    start(copy_x)
    start(copy_g)
    each_weight(wait)
    wait(copy_x)
    wait(copy_g)

    def per_slot(s, carry):
        at = pl.ds(pl.multiple_of(s * CAP, CAP), CAP)
        gate_up = mm(x_all[at, :], w_in[...])
        g, u = gate_up[:, :FF], gate_up[:, FF:]
        sigma = 1.0 / (1.0 + jnp.exp(-g))
        silu = g * sigma
        act = (silu * u).astype(BF)
        act_all[at, :] = act
        y_ref[s] = mm(act, w_down[...]).astype(BF)
        act_grad = mm_nt(g_all[at, :], w_down[...])
        gug_all[at, :FF] = (act_grad * u * sigma * (1.0 + g * (1.0 - sigma))).astype(BF)
        gug_all[at, FF:] = (act_grad * silu).astype(BF)
        dx_ref[s] = mm_nt(gug_all[at, :], w_in[...]).astype(BF)
        return carry

    lax.fori_loop(0, GROUP, per_slot, 0)
    for c in range(outer):
        part = mm_tn(x_all[:, c * GROUP * in_rows : (c + 1) * GROUP * in_rows], gug_all[...]).astype(BF)
        for r in range(GROUP):
            dw_ref[c, i ^ r, :in_rows, :] = part[r * in_rows : (r + 1) * in_rows]
        part = mm_tn(act_all[:, c * GROUP * down_rows : (c + 1) * GROUP * down_rows], g_all[...]).astype(BF)
        for r in range(GROUP):
            dw_ref[c, i ^ r, in_rows:, :] = part[r * down_rows : (r + 1) * down_rows]


def expert(idx, j, outer, in_rows, down_rows, xs, gs, own, lefts, rights):
    n_hops = outer - 1
    total = GROUP * CAP
    packed = in_rows + down_rows
    return call(
        functools.partial(expert_kernel, j, outer, in_rows, down_rows),
        "expert",
        [
            jax.ShapeDtypeStruct((GROUP, CAP, D), BF),
            jax.ShapeDtypeStruct((GROUP, CAP, D), BF),
            jax.ShapeDtypeStruct((outer, GROUP, packed, D), BF),
        ],
        [SMEM] + [ANY] * (2 * GROUP + 1 + 2 * n_hops),
        [VM] * 3,
        (idx, *xs, *gs, own, *lefts, *rights),
        scratch=[
            pltpu.VMEM((total, D), BF),
            pltpu.VMEM((total, D), BF),
            pltpu.VMEM((D, 2 * FF), BF),
            pltpu.VMEM((FF, D), BF),
            pltpu.VMEM((total, FF), BF),
            pltpu.VMEM((total, 2 * FF), BF),
            pltpu.SemaphoreType.DMA((GROUP,)),
            pltpu.SemaphoreType.DMA((GROUP,)),
            pltpu.SemaphoreType.DMA(((1 + 2 * n_hops) * GROUP,)),
            pltpu.SemaphoreType.DMA(((1 + 2 * n_hops) * GROUP,)),
        ],
        flops=18 * total * D * FF,
        moved=15 << 20,
    )


def pack_kernel(n_experts, in_rows, down_rows, idx_ref, in_ref, down_ref, *refs):
    outs, sems = refs[:-1], refs[-1]
    i = idx_ref[1]
    copies = []
    for j in range(n_experts):
        for m in range(GROUP):
            n = j * GROUP + m
            source = (i ^ m) * n_experts + j
            copies.append(
                pltpu.make_async_copy(in_ref.at[source], outs[m].at[j, pl.ds(0, in_rows)], sems.at[2 * n])
            )
            copies.append(
                pltpu.make_async_copy(
                    down_ref.at[source], outs[m].at[j, pl.ds(in_rows, down_rows)], sems.at[2 * n + 1]
                )
            )
    for c in copies:
        c.start()
    for c in copies:
        c.wait()


def pack_weights(idx, expert_in, expert_down):
    experts, in_rows, _ = expert_in.shape
    down_rows = expert_down.shape[1]
    n = experts // GROUP
    return call(
        functools.partial(pack_kernel, n, in_rows, down_rows),
        "pack_weights",
        [jax.ShapeDtypeStruct((n, in_rows + down_rows, D), BF)] * GROUP,
        [SMEM, ANY, ANY],
        [VM] * GROUP,
        (idx, expert_in, expert_down),
        scratch=[pltpu.SemaphoreType.DMA((2 * experts,))],
        moved=6 << 20,
    )


def place():
    d, t = lax.axis_index("dp"), lax.axis_index("tensor")
    return d, t, d // GROUP, d % GROUP


def flip(v, m):
    first, second = v % 2, (v // 2) % 2
    if m & 1:
        v = v + 1 - 2 * first
    if m & 2:
        v = v + 2 - 4 * second
    return v


def greet(outer, distances, tensor):
    d, t, o, _ = place()
    barrier = pltpu.get_barrier_semaphore()
    count = 0
    for m in distances:
        pl.semaphore_signal(barrier, inc=1, device_id=(flip(d, m), t), device_id_type=MESH)
        count += 1
    if tensor:
        pl.semaphore_signal(barrier, inc=1, device_id=(d, 1 - t), device_id_type=MESH)
        count += 1

    @pl.when(o > 0)
    def _():
        pl.semaphore_signal(barrier, inc=1, device_id=(d - GROUP, t), device_id_type=MESH)

    @pl.when(o < outer - 1)
    def _():
        pl.semaphore_signal(barrier, inc=1, device_id=(d + GROUP, t), device_id_type=MESH)

    neighbours = (o + outer - 1) // outer + (2 * outer - 2 - o) // outer
    pl.semaphore_wait(barrier, count + neighbours)


class Hops:
    def __init__(self, outer, steps, sent, came):
        d, t, o, _ = place()
        self.moves = []
        for n, (k, from_left, from_right, to_left, to_right) in enumerate(steps):
            back = outer - 1 - o
            right = pltpu.make_async_remote_copy(
                from_left, to_left, sent.at[2 * n], came.at[2 * n], device_id=(d + GROUP, t), device_id_type=MESH
            )
            left = pltpu.make_async_remote_copy(
                from_right,
                to_right,
                sent.at[2 * n + 1],
                came.at[2 * n + 1],
                device_id=(d - GROUP, t),
                device_id_type=MESH,
            )
            self.moves.append((right, (o >= k - 1) & (back >= 1), o >= k))
            self.moves.append((left, (back >= k - 1) & (o >= 1), back >= k))

    def start(self):
        for copy, sends, _ in self.moves:
            pl.when(sends)(copy.start)

    def wait(self):
        for copy, sends, receives in self.moves:
            pl.when(sends)(copy.wait_send)
            pl.when(receives)(copy.wait_recv)


def to_x(src, dst, sent, came):
    d, t, _, _ = place()
    return pltpu.make_async_remote_copy(src, dst, sent, came, device_id=(d, 1 - t), device_id_type=MESH)


def to_dp(m, src, dst, sent, came):
    d, t, _, _ = place()
    return pltpu.make_async_remote_copy(src, dst, sent, came, device_id=(flip(d, m), t), device_id_type=MESH)


def remote_call(kernel, name, collective_id, out_shape, in_specs, out_specs, args, scratch, flops):
    return pl.pallas_call(
        kernel,
        name=name,
        out_shape=out_shape,
        in_specs=in_specs,
        out_specs=out_specs,
        scratch_shapes=list(scratch),
        compiler_params=pltpu.CompilerParams(
            vmem_limit_bytes=VMEM_LIMIT, collective_id=collective_id, has_side_effects=True
        ),
        cost_estimate=pl.CostEstimate(flops=flops, bytes_accessed=8 << 20, transcendentals=0),
    )(*args)


def attention_kernel(outer, q_block, n_steps, len_ref, own_ref, other_ref, w_ref, cos_ref, sin_ref, x_ref, gain_ref, *refs):
    width = w_ref.shape[1] // 2
    heads = width // 2
    dy_refs, refs = refs[:2], refs[2:]
    sources, refs = refs[:n_steps], refs[n_steps:]
    qkv_ref, lse_ref, attn_ref, come_ref, hidden_ref, na_ref, nb_ref = refs[:7]
    refs = refs[7:]
    dy_outs, refs = refs[:4], refs[4:]
    to_left, refs = refs[:n_steps], refs[n_steps:]
    to_right, refs = refs[:n_steps], refs[n_steps:]
    send_ref, s_hop, r_hop, s_dy, r_dy, s_at, r_at = refs
    d, t, o, i = place()
    length = len_ref[0]
    rows = own_ref.shape[0]
    groups = width // (2 * LANES)
    greet(outer, (2,), True)
    hops = Hops(outer, [(1, s, s, l, r) for s, l, r in zip(sources, to_left, to_right, strict=True)], s_hop, r_hop)
    hops.start()
    ax, bx, ay, by = dy_outs
    dys = [
        to_x(dy_refs[0], ax, s_dy.at[0], r_dy.at[0]),
        to_dp(2, dy_refs[1], by, s_dy.at[1], r_dy.at[1]),
        to_x(dy_refs[1], bx, s_dy.at[2], r_dy.at[2]),
        to_dp(2, dy_refs[0], ay, s_dy.at[3], r_dy.at[3]),
    ]

    block = 256
    key_lanes = lax.broadcasted_iota(jnp.int32, (block, LANES), 1) < HD
    for part in range(2):
        for b in range(rows // block):
            at = pl.multiple_of((t if part == 0 else 1 - t) * rows + b * block, block)
            projected = mm((own_ref if part == 0 else other_ref)[b * block : (b + 1) * block], w_ref[:, :width])
            cosine, sine = cos_ref[pl.ds(at, block), :], sin_ref[pl.ds(at, block), :]
            for g in range(groups):
                q = projected[:, g * 2 * LANES : g * 2 * LANES + LANES]
                kv = projected[:, g * 2 * LANES + LANES : (g + 1) * 2 * LANES]
                q = q * cosine + swap_halves(q) * sine
                kv = jnp.where(key_lanes, kv * cosine + swap_halves(kv) * sine, kv)
                qkv_ref[pl.ds(at, block), g * 2 * LANES : g * 2 * LANES + LANES] = q.astype(BF)
                qkv_ref[pl.ds(at, block), g * 2 * LANES + LANES : (g + 1) * 2 * LANES] = kv.astype(BF)

    for copy in dys:
        copy.start()

    def exchange(g):
        lanes = pl.ds(pl.multiple_of(g * LANES, LANES), LANES)
        return to_x(send_ref.at[:, lanes], come_ref.at[:, lanes], s_at.at[g], r_at.at[g])

    def per_group(g, carry):
        q_lanes = pl.ds(pl.multiple_of(g * 2 * LANES, LANES), LANES)
        kv_lanes = pl.ds(pl.multiple_of(g * 2 * LANES + LANES, LANES), LANES)
        o_lanes = pl.ds(pl.multiple_of(g * LANES, LANES), LANES)
        keys, values = doubled(qkv_ref[:, kv_lanes])
        for b in range(2 * rows // q_block):
            start, n_keys = b * q_block, (b + 1) * q_block
            q = head_pair(qkv_ref[start : start + q_block, q_lanes])
            scores = mm_nt(keys[:n_keys], q) * (1.0 / math.sqrt(HD))
            scores = jnp.where(allowed(n_keys, q_block, start, length), scores, NEGATIVE)
            largest = jnp.max(scores, axis=0, keepdims=True)
            expon = jnp.exp(scores - largest)
            totals = jnp.sum(expon, axis=0, keepdims=True)
            probs = (expon * (1.0 / totals)).astype(BF)
            mixed = head_join(mm_tn(probs, values[:n_keys])).astype(BF)
            lse_ref[g, b : b + 1, :] = largest + jnp.log(totals)
            half, inner = start // rows, start % rows

            @pl.when(t == half)
            def _():
                attn_ref[inner : inner + q_block, o_lanes] = mixed

            @pl.when(t != half)
            def _():
                send_ref[inner : inner + q_block, o_lanes] = mixed

        exchange(g).start()
        return carry

    lax.fori_loop(0, groups, per_group, 0)

    def settle(g, carry):
        exchange(g).wait()
        return carry

    for p, normed_ref in enumerate((na_ref, nb_ref)):
        at = slice(p * rows // 2, (p + 1) * rows // 2)
        hidden_ref[at] = x_ref[at].astype(F32) + mm_nt(attn_ref[at], w_ref[:, width : width + heads])
    lax.fori_loop(0, groups, settle, 0)
    for p, normed_ref in enumerate((na_ref, nb_ref)):
        at = slice(p * rows // 2, (p + 1) * rows // 2)
        hidden = hidden_ref[at] + mm_nt(come_ref[at], w_ref[:, width + heads :])
        inverse = lax.rsqrt(jnp.mean(hidden * hidden, axis=-1, keepdims=True) + EPSILON)
        hidden_ref[at] = hidden
        normed_ref[...] = (hidden * inverse * gain_ref[...]).astype(BF)
    for copy in dys:
        copy.wait()
    hops.wait()


def attention(outer, q_block, length, own, other, weights_full, cosine, sine, x, gain, dys, sources):
    rows, groups = own.shape[0], weights_full.shape[1] // (4 * LANES)
    n = len(sources)
    piece = jax.ShapeDtypeStruct((rows // 2, D), BF)
    weights = [jax.ShapeDtypeStruct(s.shape, BF) for s in sources]
    out = remote_call(
        functools.partial(attention_kernel, outer, q_block, n),
        "attention",
        1,
        [
            jax.ShapeDtypeStruct((2 * rows, groups * 2 * LANES), BF),
            jax.ShapeDtypeStruct((groups, 2 * rows // q_block, 2 * q_block), F32),
            jax.ShapeDtypeStruct((rows, groups * LANES), BF),
            jax.ShapeDtypeStruct((rows, groups * LANES), BF),
            jax.ShapeDtypeStruct((rows, D), F32),
            piece,
            piece,
        ]
        + [piece] * 4
        + weights * 2,
        [SMEM] + [VM] * 7 + [ANY] * (2 + n),
        [VM] * 7 + [ANY] * (4 + 2 * n),
        (length, own, other, weights_full, cosine, sine, x, gain.reshape(1, D), *dys, *sources),
        [
            pltpu.VMEM((rows, groups * LANES), BF),
            pltpu.SemaphoreType.DMA((2 * n,)),
            pltpu.SemaphoreType.DMA((2 * n,)),
            pltpu.SemaphoreType.DMA((4,)),
            pltpu.SemaphoreType.DMA((4,)),
            pltpu.SemaphoreType.DMA((groups,)),
            pltpu.SemaphoreType.DMA((groups,)),
        ],
        30 << 30,
    )
    return out[:7], out[7:11], out[11 : 11 + n], out[11 + n :]


def one_hot_rows(pos, gate, j, n_rows):
    rank = lax.broadcasted_iota(jnp.int32, (CAP, n_rows), 0)
    chosen = rank == pos[j : j + 1, :]
    return jnp.where(chosen, 1.0 if gate is None else gate[j : j + 1, :], 0.0).astype(BF)


def spread_kernel(outer, steps, pos_ref, gate_ref, na_ref, nb_ref, *refs):
    n_steps = len(steps)
    dy_refs, refs = refs[:6], refs[6:]
    from_left, refs = refs[:n_steps], refs[n_steps:]
    from_right, refs = refs[:n_steps], refs[n_steps:]
    n_ref, dyx_ref, og_ref = refs[:3]
    refs = refs[3:]
    to_left, refs = refs[:n_steps], refs[n_steps:]
    to_right, refs = refs[:n_steps], refs[n_steps:]
    held, s_hop, r_hop, s_n, r_n, s_d, r_d, l_sem = refs
    height = na_ref.shape[0]
    n_experts = og_ref.shape[1]
    greet(outer, (1, 2), True)
    n_ax = to_x(na_ref, n_ref.at[0, 1], s_n.at[0], r_n.at[0])
    n_by = to_dp(2, nb_ref, n_ref.at[1, 2], s_n.at[1], r_n.at[1])
    n_bx = to_x(nb_ref, n_ref.at[0, 3], s_n.at[2], r_n.at[2])
    n_ay = to_dp(2, na_ref, n_ref.at[1, 0], s_n.at[3], r_n.at[3])
    n_axy = to_dp(2, n_ref.at[0, 1], n_ref.at[1, 1], s_n.at[4], r_n.at[4])
    n_bxy = to_x(n_ref.at[1, 2], n_ref.at[1, 3], s_n.at[5], r_n.at[5])
    core = {}
    for n, (s, p) in enumerate([(s, p) for s in range(2) for p in range(4)]):
        source = na_ref if (s, p) == (0, 0) else nb_ref if (s, p) == (0, 2) else n_ref.at[s, p]
        core[s, p] = to_dp(1, source, n_ref.at[2 + s, p], s_n.at[6 + n], r_n.at[6 + n])
    for copy in (n_ax, n_by, n_bx, n_ay):
        copy.start()
    d_a, d_b, d_ax, d_bx, d_ay, d_by = dy_refs
    d_axy = to_dp(2, d_ax, dyx_ref.at[0, 1], s_d.at[0], r_d.at[0])
    d_bxy = to_x(d_by, dyx_ref.at[0, 3], s_d.at[1], r_d.at[1])
    d_axy.start()
    d_bxy.start()
    d_near = [[d_a, d_ax, d_b, d_bx], [d_ay, dyx_ref.at[0, 1], d_by, dyx_ref.at[0, 3]]]
    d_core = {}
    for n, (s, p) in enumerate([(s, p) for s in range(2) for p in range(4)]):
        d_core[s, p] = to_dp(1, d_near[s][p], dyx_ref.at[1 + s, p], s_d.at[2 + n], r_d.at[2 + n])
    for key in ((0, 0), (0, 1), (0, 2), (0, 3), (1, 0), (1, 2)):
        d_core[key].start()
    core[0, 0].start()
    core[0, 2].start()
    hops = Hops(
        outer,
        [(k, a, b, l, r) for k, a, b, l, r in zip(steps, from_left, from_right, to_left, to_right, strict=True)],
        s_hop,
        r_hop,
    )
    hops.start()

    def load(s):
        pieces = d_near[s] if s < 2 else [dyx_ref.at[s - 1, p] for p in range(4)]
        return [
            pltpu.make_async_copy(piece, held.at[pl.ds(p * height, height)], l_sem.at[p])
            for p, piece in enumerate(pieces)
        ]

    def give(s):
        copies = load(s)
        for c in copies:
            c.start()
        for c in copies:
            c.wait()

        def one(j, carry):
            rank = lax.broadcasted_iota(jnp.int32, (CAP, 4 * height), 0)
            chosen = rank == pos_ref[s, pl.ds(j, 1), :]
            one_hot = jnp.where(chosen, gate_ref[s, pl.ds(j, 1), :], 0.0).astype(BF)
            og_ref[s, j] = mm(one_hot, held[...]).astype(BF)
            return carry

        lax.fori_loop(0, n_experts, one, 0)

    give(0)
    n_ax.wait()
    n_by.wait()
    n_axy.start()
    n_bxy.start()
    core[0, 1].start()
    core[1, 2].start()
    d_axy.wait()
    d_bxy.wait()
    d_core[1, 1].start()
    d_core[1, 3].start()
    give(1)
    n_bx.wait()
    n_ay.wait()
    core[0, 3].start()
    core[1, 0].start()
    for p in range(4):
        d_core[0, p].wait()
    give(2)
    n_axy.wait()
    n_bxy.wait()
    core[1, 1].start()
    core[1, 3].start()
    for p in range(4):
        d_core[1, p].wait()
    give(3)
    for key in core:
        core[key].wait()
    hops.wait()


def spread(outer, pos, gate, normed, dys, steps, from_left, from_right):
    height = normed[0].shape[0]
    n, n_experts = len(steps), pos.shape[1]
    weights = [jax.ShapeDtypeStruct(s.shape, BF) for s in from_left]
    out = remote_call(
        functools.partial(spread_kernel, outer, steps),
        "spread",
        2,
        [
            jax.ShapeDtypeStruct((GROUP, 4, height, D), BF),
            jax.ShapeDtypeStruct((3, 4, height, D), BF),
            jax.ShapeDtypeStruct((GROUP, n_experts, CAP, D), BF),
        ]
        + weights * 2,
        [VM] * 2 + [ANY] * (2 + 6 + 2 * n),
        [ANY, ANY, VM] + [ANY] * (2 * n),
        (pos, gate, *normed, *dys, *from_left, *from_right),
        [
            pltpu.VMEM((4 * height, D), BF),
            pltpu.SemaphoreType.DMA((2 * n,)),
            pltpu.SemaphoreType.DMA((2 * n,)),
            pltpu.SemaphoreType.DMA((14,)),
            pltpu.SemaphoreType.DMA((14,)),
            pltpu.SemaphoreType.DMA((10,)),
            pltpu.SemaphoreType.DMA((10,)),
            pltpu.SemaphoreType.DMA((4,)),
        ],
        12 << 30,
    )
    return out[0], out[2], out[3 : 3 + n], out[3 + n :]


def hand_out_kernel(outer, steps, pos_ref, na_ref, nb_ref, n_ref, *refs):
    n_steps = len(steps)
    from_left, refs = refs[:n_steps], refs[n_steps:]
    from_right, refs = refs[:n_steps], refs[n_steps:]
    x_ref, refs = refs[0], refs[1:]
    to_left, refs = refs[:n_steps], refs[n_steps:]
    to_right, refs = refs[:n_steps], refs[n_steps:]
    held, s_hop, r_hop, l_sem = refs
    height = na_ref.shape[0]
    n_experts = x_ref.shape[1]
    greet(outer, (), False)
    hops = Hops(
        outer,
        [(k, a, b, l, r) for k, a, b, l, r in zip(steps, from_left, from_right, to_left, to_right, strict=True)],
        s_hop,
        r_hop,
    )
    hops.start()

    def load(s):
        pieces = [na_ref, n_ref.at[0, 1], nb_ref, n_ref.at[0, 3]] if s == 0 else [n_ref.at[s, p] for p in range(4)]
        return [
            pltpu.make_async_copy(piece, held.at[s % 2, pl.ds(p * height, height)], l_sem.at[s % 2, p])
            for p, piece in enumerate(pieces)
        ]

    for c in load(0):
        c.start()
    for s in range(GROUP):
        if s + 1 < GROUP:
            for c in load(s + 1):
                c.start()
        for c in load(s):
            c.wait()

        def one(j, carry, s=s):
            rank = lax.broadcasted_iota(jnp.int32, (CAP, 4 * height), 0)
            one_hot = jnp.where(rank == pos_ref[s, pl.ds(j, 1), :], 1.0, 0.0).astype(BF)
            x_ref[s, j] = mm(one_hot, held[s % 2]).astype(BF)
            return carry

        lax.fori_loop(0, n_experts, one, 0)
    hops.wait()


def hand_out(outer, pos, normed, gathered, steps, from_left, from_right):
    height = normed[0].shape[0]
    n, n_experts = len(steps), pos.shape[1]
    weights = [jax.ShapeDtypeStruct(s.shape, BF) for s in from_left]
    out = remote_call(
        functools.partial(hand_out_kernel, outer, steps),
        "hand_out",
        3,
        [jax.ShapeDtypeStruct((GROUP, n_experts, CAP, D), BF)] + weights * 2,
        [VM] + [ANY] * (3 + 2 * n),
        [VM] + [ANY] * (2 * n),
        (pos, *normed, gathered, *from_left, *from_right),
        [
            pltpu.VMEM((2, 4 * height, D), BF),
            pltpu.SemaphoreType.DMA((2 * n,)),
            pltpu.SemaphoreType.DMA((2 * n,)),
            pltpu.SemaphoreType.DMA((2, 4)),
        ],
        12 << 30,
    )
    return out[0], out[1 : 1 + n], out[1 + n :]


def expert_step_kernel(j, outer, in_rows, down_rows, steps, x_ref, g_ref, own, *refs):
    n_hops, n_steps = outer - 1, len(steps)
    lefts, refs = refs[:n_hops], refs[n_hops:]
    rights, refs = refs[:n_hops], refs[n_hops:]
    from_left, refs = refs[:n_steps], refs[n_steps:]
    from_right, refs = refs[:n_steps], refs[n_steps:]
    y_ref, dx_ref, dw_ref = refs[:3]
    refs = refs[3:]
    to_left, refs = refs[:n_steps], refs[n_steps:]
    to_right, refs = refs[:n_steps], refs[n_steps:]
    x_all, g_all, w_in, w_down, act_all, gug_all, sem_x, sem_g, sem_w, sem_d, s_hop, r_hop = refs
    _, _, o, i = place()
    if n_steps:
        greet(outer, (), False)
        hops = Hops(
            outer,
            [(k, a, b, l, r) for k, a, b, l, r in zip(steps, from_left, from_right, to_left, to_right, strict=True)],
            s_hop,
            r_hop,
        )
        hops.start()

    def rows_of(source, held, sems):
        return [
            pltpu.make_async_copy(source.at[n, j], held.at[pl.ds(n * CAP, CAP)], sems.at[n]) for n in range(GROUP)
        ]

    def weight_copies(source, at, slot):
        made = []
        for m in range(GROUP):
            where = at * GROUP + flip(i, m)
            made.append(
                pltpu.make_async_copy(
                    source.at[m, pl.ds(0, in_rows)],
                    w_in.at[pl.ds(pl.multiple_of(where * in_rows, in_rows), in_rows)],
                    sem_w.at[slot * GROUP + m],
                )
            )
            made.append(
                pltpu.make_async_copy(
                    source.at[m, pl.ds(in_rows, down_rows)],
                    w_down.at[pl.ds(pl.multiple_of(where * down_rows, down_rows), down_rows)],
                    sem_d.at[slot * GROUP + m],
                )
            )
        return made

    def each_weight(act):
        act(weight_copies(own, o, 0))
        for k in range(1, outer):

            @pl.when(o >= k)
            def _():
                act(weight_copies(lefts[k - 1], o - k, k))

            @pl.when(o + k < outer)
            def _():
                act(weight_copies(rights[k - 1], o + k, n_hops + k))

    def start(made):
        for c in made:
            c.start()

    def wait(made):
        for c in made:
            c.wait()

    each_weight(start)
    copy_x, copy_g = rows_of(x_ref, x_all, sem_x), rows_of(g_ref, g_all, sem_g)
    start(copy_x)
    start(copy_g)
    each_weight(wait)
    wait(copy_x)
    wait(copy_g)

    def per_slot(s, carry):
        at = pl.ds(pl.multiple_of(s * CAP, CAP), CAP)
        gate_up = mm(x_all[at, :], w_in[...])
        g, u = gate_up[:, :FF], gate_up[:, FF:]
        sigma = 1.0 / (1.0 + jnp.exp(-g))
        silu = g * sigma
        act = (silu * u).astype(BF)
        act_all[at, :] = act
        y_ref[s] = mm(act, w_down[...]).astype(BF)
        act_grad = mm_nt(g_all[at, :], w_down[...])
        gug_all[at, :FF] = (act_grad * u * sigma * (1.0 + g * (1.0 - sigma))).astype(BF)
        gug_all[at, FF:] = (act_grad * silu).astype(BF)
        dx_ref[s] = mm_nt(gug_all[at, :], w_in[...]).astype(BF)
        return carry

    lax.fori_loop(0, GROUP, per_slot, 0)
    for c in range(outer):
        part = mm_tn(x_all[:, c * GROUP * in_rows : (c + 1) * GROUP * in_rows], gug_all[...]).astype(BF)
        for r in range(GROUP):
            dw_ref[c, flip(i, r), :in_rows, :] = part[r * in_rows : (r + 1) * in_rows]
        part = mm_tn(act_all[:, c * GROUP * down_rows : (c + 1) * GROUP * down_rows], g_all[...]).astype(BF)
        for r in range(GROUP):
            dw_ref[c, flip(i, r), in_rows:, :] = part[r * down_rows : (r + 1) * down_rows]
    if n_steps:
        hops.wait()


def expert_step(j, outer, in_rows, down_rows, x, g, own, lefts, rights, steps, from_left, from_right):
    n_hops, n = outer - 1, len(steps)
    total = GROUP * CAP
    packed = in_rows + down_rows
    weights = [jax.ShapeDtypeStruct(s.shape, BF) for s in from_left]
    shapes = [
        jax.ShapeDtypeStruct((GROUP, CAP, D), BF),
        jax.ShapeDtypeStruct((GROUP, CAP, D), BF),
        jax.ShapeDtypeStruct((outer, GROUP, packed, D), BF),
    ] + weights * 2
    in_specs = [ANY] * (3 + 2 * n_hops + 2 * n)
    out_specs = [VM] * 3 + [ANY] * (2 * n)
    args = (x, g, own, *lefts, *rights, *from_left, *from_right)
    scratch = [
        pltpu.VMEM((total, D), BF),
        pltpu.VMEM((total, D), BF),
        pltpu.VMEM((D, 2 * FF), BF),
        pltpu.VMEM((FF, D), BF),
        pltpu.VMEM((total, FF), BF),
        pltpu.VMEM((total, 2 * FF), BF),
        pltpu.SemaphoreType.DMA((GROUP,)),
        pltpu.SemaphoreType.DMA((GROUP,)),
        pltpu.SemaphoreType.DMA(((1 + 2 * n_hops) * GROUP,)),
        pltpu.SemaphoreType.DMA(((1 + 2 * n_hops) * GROUP,)),
        pltpu.SemaphoreType.DMA((max(1, 2 * n),)),
        pltpu.SemaphoreType.DMA((max(1, 2 * n),)),
    ]
    kernel = functools.partial(expert_step_kernel, j, outer, in_rows, down_rows, steps)
    flops = 18 * total * D * FF
    if n:
        out = remote_call(kernel, "expert_step", 4 + j, shapes, in_specs, out_specs, args, scratch, flops)
    else:
        out = call(kernel, "expert_last", shapes, in_specs, out_specs, args, scratch=scratch, flops=flops, moved=15 << 20)
    return out[:3], out[3 : 3 + n], out[3 + n :]


def layer(
    tokens,
    cotangent,
    lengths,
    expert_ids,
    gate_values,
    first_gain,
    qkv_weight,
    attn_out_weight,
    second_gain,
    expert_in_weight,
    expert_out_weight,
):
    rows = tokens.shape[0]
    n_tensor, n_dp = lax.axis_size("tensor"), lax.axis_size("dp")
    outer = n_dp // GROUP
    slot_rows = rows * n_tensor
    d, t = lax.axis_index("dp"), lax.axis_index("tensor")
    o, i = d // GROUP, d % GROUP
    length = lengths[0]
    idx = jnp.stack([o, i, t, length]).astype(jnp.int32)
    width = qkv_weight.shape[1] * qkv_weight.shape[2]
    experts_local, in_rows, _ = expert_in_weight.shape
    down_rows = expert_out_weight.shape[1]
    own_experts = experts_local // GROUP
    pair = n_tensor == 2
    q_block = 256
    half = rows // 2

    def across(v, m):
        return lax.ppermute(v, "dp", [(a, a ^ m) for a in range(n_dp)])

    def beside(v):
        return lax.ppermute(v, "tensor", [(0, 1), (1, 0)])

    def hop(pairs):
        up = [(a, a + GROUP) for a in range(n_dp - GROUP)]
        down = [(b, a) for a, b in up]
        return [(lax.ppermute(a, "dp", up), lax.ppermute(b, "dp", down)) for a, b in pairs]

    def gather_group(pieces):
        if pair:
            a, b = pieces
            ax, by, ay, bx = beside(a), across(b, 2), across(a, 2), beside(b)
            axy, bxy = across(ax, 2), beside(by)
            slots = [[a, ax, b, bx], [ay, axy, by, bxy]]
        else:
            slot = lax.all_gather(pieces[0], "tensor", axis=0, tiled=True)
            slots = [[slot], [across(slot, 2)]]
        return slots + [[across(p, 1) for p in s] for s in slots]

    positions = t * rows + jnp.arange(rows, dtype=jnp.int32)
    valid_rows = positions < length
    n_experts = experts_local * n_tensor
    chosen = expert_ids.T[None] == jnp.arange(n_experts, dtype=jnp.int32)[:, None, None]
    gates = jnp.sum(jnp.where(chosen, gate_values.T[None].astype(F32), 0.0), axis=1)
    gates = jnp.where(valid_rows[None, :], gates, 0.0).astype(BF)
    if pair:
        gates_x = beside(gates)
        slot_gates = jnp.concatenate(
            [gates[:, :half], gates_x[:, :half], gates[:, half:], gates_x[:, half:]], axis=1
        )
    else:
        slot_gates = lax.all_gather(gates, "tensor", axis=1, tiled=True)
    gates_y = across(slot_gates, 2)
    all_gates = jnp.stack([slot_gates, gates_y, across(slot_gates, 1), across(gates_y, 1)])
    own_gates = lax.dynamic_slice_in_dim(
        all_gates, t * experts_local + i * own_experts, own_experts, axis=1
    ).astype(F32)
    named = own_gates > 0
    before = (
        lax.broadcasted_iota(jnp.int32, (slot_rows, slot_rows), 0)
        < lax.broadcasted_iota(jnp.int32, (slot_rows, slot_rows), 1)
    ).astype(BF)
    ranks = jnp.dot(
        named.astype(BF).reshape(GROUP * own_experts, slot_rows), before, preferred_element_type=F32
    ).reshape(GROUP, own_experts, slot_rows)
    pos = jnp.where(named, ranks, -1.0).astype(jnp.int32)
    pos_columns, gate_columns = jnp.swapaxes(pos, 1, 2), jnp.swapaxes(own_gates, 1, 2)

    x = tokens.astype(F32)
    inverse_one = lax.rsqrt(jnp.mean(x * x, axis=-1, keepdims=True) + EPSILON)
    normed_one = (x * inverse_one * first_gain).astype(BF)
    cosine, sine = rope_tables(slot_rows)
    dy = jnp.where(valid_rows[:, None], cotangent, jnp.zeros_like(cotangent))
    expert_outs, row_grads, weight_grads = [], [], []
    if pair and outer == 4:
        other = beside(normed_one)
        out_shard = attn_out_weight.T
        shards = jnp.concatenate([qkv_weight.reshape(-1, width), out_shard, beside(out_shard)], axis=1)
        weights_full = lax.all_gather(shards, "dp", axis=0, tiled=True)
        by_distance = pack_weights(idx, expert_in_weight, expert_out_weight)
        by_distance = [by_distance[0]] + [across(by_distance[m], m) for m in range(1, GROUP)]
        own_weights = [jnp.stack([v[j] for v in by_distance]) for j in range(own_experts)]
        dys = [dy[:half], dy[half:]]
        main, dy_moved, one_l, one_r = attention(
            outer, q_block, lengths, normed_one, other, weights_full, cosine, sine, tokens, second_gain, dys, own_weights[:3]
        )
        qkv, lse, attn_own, attn_other, hidden, *normed_two = main
        attn_parts = [attn_own, attn_other]
        gathered, out_grads, moved_l, moved_r = spread(
            outer,
            pos,
            own_gates,
            normed_two,
            [*dys, *dy_moved],
            (1, 2, 2),
            [own_weights[3], one_l[0], one_l[1]],
            [own_weights[3], one_r[0], one_r[1]],
        )
        one_l, one_r = [*one_l, moved_l[0]], [*one_r, moved_r[0]]
        two_l, two_r = [*moved_l[1:]], [*moved_r[1:]]
        expert_rows, moved_l, moved_r = hand_out(
            outer, pos, normed_two, gathered, (3, 2), [two_l[0], one_l[2]], [two_r[0], one_r[2]]
        )
        three_l, three_r = [moved_l[0]], [moved_r[0]]
        two_l.append(moved_l[1])
        two_r.append(moved_r[1])
        plans = [
            ((3, 2), [two_l[1], one_l[3]], [two_r[1], one_r[3]]),
            ((3,), [two_l[2]], [two_r[2]]),
            None,
            ((), [], []),
        ]
        for j in range(own_experts):
            plan = plans[j] or ((3,), [two_l[3]], [two_r[3]])
            (y, dx, dw), moved_l, moved_r = expert_step(
                j,
                outer,
                in_rows,
                down_rows,
                expert_rows,
                out_grads,
                own_weights[j],
                [one_l[j], two_l[j], three_l[j]],
                [one_r[j], two_r[j], three_r[j]],
                *plan,
            )
            three_l.extend(moved_l[:1])
            three_r.extend(moved_r[:1])
            two_l.extend(moved_l[1:])
            two_r.extend(moved_r[1:])
            expert_outs.append(y)
            row_grads.append(dx)
            weight_grads.append(dw)
        qkv_full = weights_full[:, :width]
        out_parts = [weights_full[:, width : width + width // 2], weights_full[:, width + width // 2 :]]
    else:
        qkv_full = lax.all_gather(qkv_weight.reshape(qkv_weight.shape[0], width), "dp", axis=0, tiled=True)
        out_full = lax.all_gather(attn_out_weight.T, "dp", axis=0, tiled=True)
        by_distance = pack_weights(idx, expert_in_weight, expert_out_weight)
        by_distance = [by_distance[0]] + [across(by_distance[m], m) for m in range(1, GROUP)]
        own_weights = [jnp.stack([v[j] for v in by_distance]) for j in range(own_experts)]
        hops = [hop([(own, own) for own in own_weights])]
        if pair:
            out_parts = [out_full, beside(out_full)]
        else:
            gathered = lax.all_gather(out_full, "tensor", axis=0)
            out_parts = [gathered[k] for k in range(n_tensor)]

        if pair:
            other = beside(normed_one)
            normed_all = jnp.where(
                t == 0,
                jnp.concatenate([normed_one, other], axis=0),
                jnp.concatenate([other, normed_one], axis=0),
            )
        else:
            normed_all = lax.all_gather(normed_one, "tensor", axis=0, tiled=True)
        qkv = qkv_project(normed_all, qkv_full, cosine, sine)
        *attended, lse = attend(idx, qkv, 2 if pair else 1, q_block)
        if pair:
            attn_parts = [attended[0], beside(attended[1])]
        else:
            heads = attended[0].shape[1]
            exchanged = lax.all_to_all(attended[0].reshape(n_tensor, rows, heads), "tensor", 0, 0)
            attn_parts = [exchanged[k] for k in range(n_tensor)]
        attn_parts, hops[0] = lax.optimization_barrier((attn_parts, hops[0]))
        if outer > 2:
            hops.append(hop(hops[0]))
        hidden, *normed_two = project_out(tokens, second_gain, attn_parts, out_parts, 2 if pair else 1)

        dy_slots = gather_group([dy[:half], dy[half:]] if pair else [dy])
        out_grads = [dispatch(pos[s], own_gates[s], dy_slots[s], True) for s in range(GROUP)]
        normed_slots = gather_group(normed_two)
        normed_slots, out_grads, hops = lax.optimization_barrier((normed_slots, out_grads, hops))
        while len(hops) < outer - 1:
            hops.append(hop(hops[-1]))
        expert_rows = [dispatch(pos[s], own_gates[s], normed_slots[s], False) for s in range(GROUP)]

        for j in range(own_experts):
            if j:
                idx, expert_outs[-1] = lax.optimization_barrier((idx, expert_outs[-1]))
            y, dx, dw = expert(
                idx,
                j,
                outer,
                in_rows,
                down_rows,
                expert_rows,
                out_grads,
                own_weights[j],
                [h[j][0] for h in hops],
                [h[j][1] for h in hops],
            )
            expert_outs.append(y)
            row_grads.append(dx)
            weight_grads.append(dw)

    def sum_group(sources, scaled):
        def part(s, add, n_outs):
            return combine(pos_columns[s], gate_columns[s], sources, s, scaled, add, n_outs)

        far = [part(2, None, 1)[0], part(3, None, 1)[0]]
        near = [across(v, 1) for v in far]
        if pair:
            ay, axy, by, bxy = part(1, near[1], 4)
            a, ax, b, bx = part(0, near[0], 4)

            def add(p, q):
                return (p.astype(F32) + q.astype(F32)).astype(BF)

            a, ax = add(a, across(ay, 2)), add(ax, across(axy, 2))
            b, by = add(b, beside(bx)), add(by, beside(bxy))
            return [[a, beside(ax)], [b, across(by, 2)]]
        (y,) = part(1, near[1], 1)
        (v,) = part(0, near[0], 1)
        v = (v.astype(F32) + across(y, 2).astype(F32)).astype(BF)
        return [[lax.psum_scatter(v, "tensor", scatter_dimension=0, tiled=True)]]

    valid_column = valid_rows.astype(F32)[:, None]
    normed_two_grad = sum_group(row_grads, False)
    hidden_grad, branch_grad, second_gain_part, *attn_grads = hidden_back(
        valid_column, hidden, cotangent, second_gain, normed_two_grad, out_parts
    )
    if pair:
        attn_grads = [attn_grads[0], beside(attn_grads[1])]
    else:
        attn_grads = [
            lax.all_to_all(jnp.stack(attn_grads), "tensor", 0, 0).reshape(slot_rows, attn_grads[0].shape[1])
        ]
    projected_grads = attend_back(idx, qkv, lse, cosine, sine, attn_grads, q_block)

    def first_norm_part(v):
        return lax.dot_general(v, qkv_full, (((1,), (1,)), ((), ())), preferred_element_type=F32).astype(BF)

    if pair:
        theirs = beside(first_norm_part(projected_grads[1]))
        normed_one_grad = first_norm_part(projected_grads[0]).astype(F32) + theirs.astype(F32)
        qkv_part = mm_tn(normed_one, projected_grads[0]) + mm_tn(other, projected_grads[1])
    else:
        normed_one_grad = lax.psum_scatter(
            first_norm_part(projected_grads[0]), "tensor", scatter_dimension=0, tiled=True
        ).astype(F32)
        qkv_part = mm_tn(normed_all, projected_grads[0])
    first_gain_part = jnp.sum(normed_one_grad * (x * inverse_one), axis=0)
    scaled = normed_one_grad * first_gain
    tokens_grad = (
        hidden_grad
        + inverse_one * scaled
        - x * (inverse_one * inverse_one * inverse_one * jnp.mean(scaled * x, axis=-1, keepdims=True))
    )

    mixture = sum_group(expert_outs, True)
    mixture = jnp.concatenate([sum(v.astype(F32) for v in terms) for terms in mixture], axis=0)
    output = jnp.where(valid_rows[:, None], hidden + mixture, 0.0).astype(BF)

    outer_groups = [[a * GROUP + b for a in range(outer)] for b in range(GROUP)]
    received = [[] for _ in range(GROUP)]
    for dw in weight_grads:
        mine = lax.psum_scatter(dw, "dp", scatter_dimension=0, tiled=True, axis_index_groups=outer_groups)
        for m in range(GROUP):
            block = mine[0, m]
            received[m].append(block if m == 0 else across(block, m))
    by_distance = jnp.stack([jnp.stack(v) for v in received])
    by_source = jnp.take(by_distance, jnp.arange(GROUP) ^ i, axis=0).reshape(
        experts_local, in_rows + down_rows, D
    )
    expert_in_grad = by_source[:, :in_rows].astype(F32)
    expert_out_grad = by_source[:, in_rows:].astype(F32)

    attn_out_parts = [mm_tn(branch_grad, part).astype(BF) for part in attn_parts]
    if pair:
        attn_out_part = (attn_out_parts[0].astype(F32) + beside(attn_out_parts[1]).astype(F32)).astype(BF)
    else:
        attn_out_part = lax.psum_scatter(jnp.stack(attn_out_parts), "tensor", scatter_dimension=0, tiled=True)[0]
    qkv_grad = lax.psum_scatter(qkv_part.astype(BF), "dp", scatter_dimension=0, tiled=True).astype(F32)
    attn_out_grad = lax.psum_scatter(attn_out_part, "dp", scatter_dimension=0, tiled=True).astype(F32).T

    gains = jnp.stack([first_gain_part, second_gain_part[0]])
    if pair:
        gains = gains + beside(gains)
    else:
        gains = lax.psum(gains, "tensor")
    step = 1
    while step < n_dp:
        gains = gains + across(gains, step)
        step *= 2
    return (
        output,
        tokens_grad,
        gains[0],
        qkv_grad.reshape(qkv_weight.shape),
        attn_out_grad,
        gains[1],
        expert_in_grad,
        expert_out_grad,
    )


def solution(mesh):
    placed = (
        P(("dp", "tensor"), None),
        P(("dp", "tensor"), None),
        P("dp"),
        P(("dp", "tensor"), None),
        P(("dp", "tensor"), None),
        P(),
        P("dp", "tensor", None),
        P("tensor", "dp"),
        P(),
        P("tensor", "dp", None),
        P("tensor", "dp", None),
    )
    return jax.shard_map(
        layer,
        mesh=mesh,
        in_specs=placed,
        out_specs=(
            P(("dp", "tensor"), None),
            P(("dp", "tensor"), None),
            P(),
            P("dp", "tensor", None),
            P("tensor", "dp"),
            P(),
            P("tensor", "dp", None),
            P("tensor", "dp", None),
        ),
        check_vma=False,
    )
```

```python
import functools
import math

import jax
import jax.numpy as jnp
from jax import lax
from jax.experimental import pallas as pl
from jax.experimental.pallas import tpu as pltpu
from jax.sharding import PartitionSpec as P

D = 1024
HD = 64
FF = 512
G = 2
CAP = 288
GROUP = 4
LANES = 128

EPSILON = 1e-06
THETA = 10000.0
NEGATIVE = -1e30
BF = jnp.bfloat16
F32 = jnp.float32
VMEM_LIMIT = 60 * 1024 * 1024
MESH = pl.DeviceIdType.MESH

ANY = pl.BlockSpec(memory_space=pl.ANY)
SMEM = pl.BlockSpec(memory_space=pltpu.SMEM)
VM = pl.BlockSpec(memory_space=pltpu.VMEM)


def mm(a, b):
    return lax.dot_general(a, b, (((1,), (0,)), ((), ())), preferred_element_type=F32)


def mm_nt(a, b):
    return lax.dot_general(a, b, (((1,), (1,)), ((), ())), preferred_element_type=F32)


def mm_tn(a, b):
    return lax.dot_general(a, b, (((0,), (0,)), ((), ())), preferred_element_type=F32)


def call(kernel, name, out_shape, in_specs, out_specs, args, scratch=(), flops=0, moved=0, **more):
    return pl.pallas_call(
        kernel,
        name=name,
        out_shape=out_shape,
        in_specs=in_specs,
        out_specs=out_specs,
        scratch_shapes=list(scratch),
        compiler_params=pltpu.CompilerParams(vmem_limit_bytes=VMEM_LIMIT),
        cost_estimate=pl.CostEstimate(flops=flops, bytes_accessed=moved, transcendentals=0),
        **more,
    )(*args)


def rope_tables(total_rows):
    half = HD // 2
    positions = jnp.arange(total_rows).astype(F32)
    frequency = THETA ** (-(jnp.arange(half).astype(F32) * 2.0 / HD))
    angles = positions[:, None] * frequency[None, :]
    cosine, sine = jnp.cos(angles), jnp.sin(angles)
    return (
        jnp.concatenate([cosine] * 4, axis=1),
        jnp.concatenate([-sine, sine, -sine, sine], axis=1),
    )


def swap_halves(v):
    lane = lax.broadcasted_iota(jnp.int32, v.shape, 1)
    return jnp.where(lane % HD < HD // 2, pltpu.roll(v, LANES - HD // 2, 1), pltpu.roll(v, HD // 2, 1))


def qkv_kernel(n_ref, w_ref, cos_ref, sin_ref, out_ref):
    projected = mm(n_ref[...], w_ref[...])
    cosine, sine = cos_ref[...], sin_ref[...]
    key_lanes = lax.broadcasted_iota(jnp.int32, cosine.shape, 1) < HD
    for g in range(projected.shape[1] // (2 * LANES)):
        q = projected[:, g * 2 * LANES : g * 2 * LANES + LANES]
        kv = projected[:, g * 2 * LANES + LANES : (g + 1) * 2 * LANES]
        q = q * cosine + swap_halves(q) * sine
        kv = jnp.where(key_lanes, kv * cosine + swap_halves(kv) * sine, kv)
        out_ref[:, g * 2 * LANES : g * 2 * LANES + LANES] = q.astype(BF)
        out_ref[:, g * 2 * LANES + LANES : (g + 1) * 2 * LANES] = kv.astype(BF)


def qkv_project(normed, weight, cosine, sine):
    rows, width = normed.shape[0], weight.shape[1]
    block = 256
    return pl.pallas_call(
        qkv_kernel,
        name="qkv_rope",
        grid=(rows // block,),
        out_shape=jax.ShapeDtypeStruct((rows, width), BF),
        in_specs=[
            pl.BlockSpec((block, D), lambda b: (b, 0)),
            pl.BlockSpec((D, width), lambda b: (0, 0)),
            pl.BlockSpec((block, LANES), lambda b: (b, 0)),
            pl.BlockSpec((block, LANES), lambda b: (b, 0)),
        ],
        out_specs=pl.BlockSpec((block, width), lambda b: (b, 0)),
        compiler_params=pltpu.CompilerParams(vmem_limit_bytes=VMEM_LIMIT),
        cost_estimate=pl.CostEstimate(flops=2 * rows * D * width, bytes_accessed=6 << 20, transcendentals=0),
    )(normed, weight, cosine, sine)


def head_pair(v):
    first = lax.broadcasted_iota(jnp.int32, v.shape, 1) < HD
    zero = jnp.zeros_like(v)
    return jnp.concatenate([jnp.where(first, v, zero), jnp.where(first, zero, v)], axis=0)


def head_join(v):
    n = v.shape[0] // 2
    first = lax.broadcasted_iota(jnp.int32, (n, LANES), 1) < HD
    return jnp.where(first, v[:n], v[n:])


def doubled(kv):
    first = lax.broadcasted_iota(jnp.int32, kv.shape, 1) < HD
    other = pltpu.roll(kv.astype(F32), HD, 1).astype(BF)
    return jnp.where(first, kv, other), jnp.where(first, other, kv)


def allowed(n_keys, q_block, q_start, length):
    key = lax.broadcasted_iota(jnp.int32, (n_keys, 2 * q_block), 0)
    lane = lax.broadcasted_iota(jnp.int32, (n_keys, 2 * q_block), 1)
    query = q_start + jnp.where(lane < q_block, lane, lane - q_block)
    return (key <= query) & (key < length)


def attend_kernel(q_block, idx_ref, qkv_ref, *out_refs):
    outs, lse_ref = out_refs[:-1], out_refs[-1]
    rows = qkv_ref.shape[0]
    length = idx_ref[3]
    keys, values = doubled(qkv_ref[:, LANES:])
    for b in range(rows // q_block):
        start, n_keys = b * q_block, (b + 1) * q_block
        q = head_pair(qkv_ref[start : start + q_block, :LANES])
        scores = mm_nt(keys[:n_keys], q) * (1.0 / math.sqrt(HD))
        scores = jnp.where(allowed(n_keys, q_block, start, length), scores, NEGATIVE)
        largest = jnp.max(scores, axis=0, keepdims=True)
        expon = jnp.exp(scores - largest)
        totals = jnp.sum(expon, axis=0, keepdims=True)
        probs = (expon * (1.0 / totals)).astype(BF)
        mixed = head_join(mm_tn(probs, values[:n_keys])).astype(BF)
        lse_ref[0, b : b + 1, :] = largest + jnp.log(totals)
        if len(outs) == 1:
            outs[0][start : start + q_block] = mixed
        else:
            own_rows = rows // 2
            half, at = start // own_rows, start % own_rows
            mine = idx_ref[2] == half

            @pl.when(mine)
            def _():
                outs[0][at : at + q_block] = mixed

            @pl.when(jnp.logical_not(mine))
            def _():
                outs[1][at : at + q_block] = mixed


def attend(idx, qkv, parts, q_block):
    rows, groups = qkv.shape[0], qkv.shape[1] // (2 * LANES)
    out = jax.ShapeDtypeStruct((rows // parts, groups * LANES), BF)
    return pl.pallas_call(
        functools.partial(attend_kernel, q_block),
        name="attend",
        grid=(groups,),
        out_shape=[out] * parts + [jax.ShapeDtypeStruct((groups, rows // q_block, 2 * q_block), F32)],
        in_specs=[SMEM, pl.BlockSpec((rows, 2 * LANES), lambda g: (0, g))],
        out_specs=[pl.BlockSpec((rows // parts, LANES), lambda g: (0, g))] * parts
        + [pl.BlockSpec((1, rows // q_block, 2 * q_block), lambda g: (g, 0, 0))],
        compiler_params=pltpu.CompilerParams(vmem_limit_bytes=VMEM_LIMIT),
        cost_estimate=pl.CostEstimate(flops=14 << 30, bytes_accessed=4 << 20, transcendentals=0),
    )(idx, qkv)


def attend_back_kernel(q_block, n_grads, idx_ref, qkv_ref, lse_ref, cos_ref, sin_ref, *refs):
    grads, outs = refs[:n_grads], refs[n_grads : 2 * n_grads]
    do_ref, dq_ref, dk_ref, dv_ref = refs[2 * n_grads :]
    rows = qkv_ref.shape[0]
    own_rows = rows // n_grads
    length = idx_ref[3]
    for p in range(n_grads):
        at = pl.multiple_of((p ^ idx_ref[2] if n_grads == 2 else 0) * own_rows, own_rows)
        do_ref[pl.ds(at, own_rows), :] = grads[p][...]
    keys, values = doubled(qkv_ref[:, LANES:])
    dk_ref[...] = jnp.zeros_like(dk_ref)
    dv_ref[...] = jnp.zeros_like(dv_ref)
    scale = 1.0 / math.sqrt(HD)
    for b in range(rows // q_block):
        start, n_keys = b * q_block, (b + 1) * q_block
        q = head_pair(qkv_ref[start : start + q_block, :LANES])
        grad = head_pair(do_ref[start : start + q_block, :])
        scores = mm_nt(keys[:n_keys], q) * scale
        probs = jnp.where(
            allowed(n_keys, q_block, start, length), jnp.exp(scores - lse_ref[0, b : b + 1, :]), 0.0
        )
        prob_grad = mm_nt(values[:n_keys], grad)
        center = jnp.sum(probs * prob_grad, axis=0, keepdims=True)
        score_grad = (probs * (prob_grad - center)).astype(BF)
        dq_ref[start : start + q_block, :] = head_join(mm_tn(score_grad, keys[:n_keys])) * scale
        dk_ref[:n_keys, :] += mm(score_grad, q)
        dv_ref[:n_keys, :] += mm(probs.astype(BF), grad)
    cosine, sine = cos_ref[...], sin_ref[...]
    dq = dq_ref[...]
    dq = (dq * cosine - swap_halves(dq) * sine).astype(BF)
    dk, dv = dk_ref[...] * scale, dv_ref[...]
    dk = dk + pltpu.roll(dk, HD, 1)
    dv = dv + pltpu.roll(dv, HD, 1)
    dk = dk * cosine - swap_halves(dk) * sine
    first = lax.broadcasted_iota(jnp.int32, dk.shape, 1) < HD
    dkv = jnp.where(first, dk, dv).astype(BF)
    if n_grads == 1:
        outs[0][:, :LANES] = dq
        outs[0][:, LANES:] = dkv
    else:
        do_ref[...] = dq
        for p in range(2):
            at = pl.multiple_of((p ^ idx_ref[2]) * own_rows, own_rows)
            outs[p][:, :LANES] = do_ref[pl.ds(at, own_rows), :]
        do_ref[...] = dkv
        for p in range(2):
            at = pl.multiple_of((p ^ idx_ref[2]) * own_rows, own_rows)
            outs[p][:, LANES:] = do_ref[pl.ds(at, own_rows), :]


def attend_back(idx, qkv, lse, cosine, sine, grads, q_block):
    rows, groups, parts = qkv.shape[0], qkv.shape[1] // (2 * LANES), len(grads)
    return pl.pallas_call(
        functools.partial(attend_back_kernel, q_block, parts),
        name="attend_back",
        grid=(groups,),
        out_shape=[jax.ShapeDtypeStruct((rows // parts, groups * 2 * LANES), BF)] * parts,
        in_specs=[
            SMEM,
            pl.BlockSpec((rows, 2 * LANES), lambda g: (0, g)),
            pl.BlockSpec((1, rows // q_block, 2 * q_block), lambda g: (g, 0, 0)),
            pl.BlockSpec((rows, LANES), lambda g: (0, 0)),
            pl.BlockSpec((rows, LANES), lambda g: (0, 0)),
        ]
        + [pl.BlockSpec((rows // parts, LANES), lambda g: (0, g))] * parts,
        out_specs=[pl.BlockSpec((rows // parts, 2 * LANES), lambda g: (0, g))] * parts,
        scratch_shapes=[pltpu.VMEM((rows, LANES), BF)] + [pltpu.VMEM((rows, LANES), F32)] * 3,
        compiler_params=pltpu.CompilerParams(vmem_limit_bytes=VMEM_LIMIT),
        cost_estimate=pl.CostEstimate(flops=30 << 30, bytes_accessed=6 << 20, transcendentals=0),
    )(idx, qkv, lse, cosine, sine, *grads)


def project_out_kernel(n_parts, pieces, x_ref, gain_ref, *refs):
    attns, weights = refs[:n_parts], refs[n_parts : 2 * n_parts]
    hidden_ref, normed_refs = refs[2 * n_parts], refs[2 * n_parts + 1 :]
    rows = x_ref.shape[0] // pieces
    for p in range(pieces):
        at = slice(p * rows, (p + 1) * rows)
        hidden = x_ref[at].astype(F32)
        for a, w in zip(attns, weights, strict=True):
            hidden = hidden + mm_nt(a[at], w[...])
        inverse = lax.rsqrt(jnp.mean(hidden * hidden, axis=-1, keepdims=True) + EPSILON)
        hidden_ref[at] = hidden
        normed_refs[p][...] = (hidden * inverse * gain_ref[...]).astype(BF)


def project_out(x, gain, attns, weights, pieces):
    rows = x.shape[0]
    n = len(attns)
    return call(
        functools.partial(project_out_kernel, n, pieces),
        "project_out",
        [jax.ShapeDtypeStruct((rows, D), F32)] + [jax.ShapeDtypeStruct((rows // pieces, D), BF)] * pieces,
        [VM] * (2 + 2 * n),
        [VM] * (1 + pieces),
        (x, gain.reshape(1, D), *attns, *weights),
        flops=2 * rows * D * D,
        moved=7 << 20,
    )


def hidden_back_kernel(n_parts, pieces, n_sums, valid_ref, hidden_ref, cot_ref, gain_ref, *refs):
    sums, refs = refs[: pieces * n_sums], refs[pieces * n_sums :]
    weights, refs = refs[:n_parts], refs[n_parts:]
    grad_ref, low_ref, gain_grad_ref, attn_refs = refs[0], refs[1], refs[2], refs[3:]
    rows = hidden_ref.shape[0] // pieces
    gain = gain_ref[...]
    gain_grad = jnp.zeros((1, D), F32)
    for p in range(pieces):
        at = slice(p * rows, (p + 1) * rows)
        hidden = hidden_ref[at]
        normed_grad = sums[p * n_sums][...].astype(F32)
        for s in sums[p * n_sums + 1 : (p + 1) * n_sums]:
            normed_grad = normed_grad + s[...].astype(F32)
        inverse = lax.rsqrt(jnp.mean(hidden * hidden, axis=-1, keepdims=True) + EPSILON)
        gain_grad = gain_grad + jnp.sum(normed_grad * (hidden * inverse), axis=0, keepdims=True)
        scaled = normed_grad * gain
        back = inverse * scaled - hidden * (
            inverse * inverse * inverse * jnp.mean(scaled * hidden, axis=-1, keepdims=True)
        )
        dy = jnp.where(valid_ref[at] > 0, cot_ref[at].astype(F32), 0.0)
        total = dy + back
        grad_ref[at] = total
        low = total.astype(BF)
        low_ref[at] = low
        for a, w in zip(attn_refs, weights, strict=True):
            a[at] = mm(low, w[...]).astype(BF)
    gain_grad_ref[...] = gain_grad


def hidden_back(valid, hidden, cotangent, gain, sums, weights):
    rows, pieces, n_sums, n = hidden.shape[0], len(sums), len(sums[0]), len(weights)
    heads = weights[0].shape[1]
    return call(
        functools.partial(hidden_back_kernel, n, pieces, n_sums),
        "hidden_back",
        [
            jax.ShapeDtypeStruct((rows, D), F32),
            jax.ShapeDtypeStruct((rows, D), BF),
            jax.ShapeDtypeStruct((1, D), F32),
        ]
        + [jax.ShapeDtypeStruct((rows, heads), BF)] * n,
        [VM] * (4 + pieces * n_sums + n),
        [VM] * (3 + n),
        (valid, hidden, cotangent, gain.reshape(1, D), *[s for piece in sums for s in piece], *weights),
        flops=2 * rows * D * D,
        moved=10 << 20,
    )


def dispatch_kernel(n_pieces, scaled, pos_ref, gate_ref, *refs):
    pieces, out_ref, rows_ref, sems = refs[:n_pieces], refs[n_pieces], refs[n_pieces + 1], refs[n_pieces + 2]
    height = rows_ref.shape[0] // n_pieces
    copies = [
        pltpu.make_async_copy(piece, rows_ref.at[pl.ds(p * height, height)], sems.at[p])
        for p, piece in enumerate(pieces)
    ]
    for c in copies:
        c.start()
    rank = lax.broadcasted_iota(jnp.int32, (CAP, rows_ref.shape[0]), 0)
    for c in copies:
        c.wait()
    for j in range(out_ref.shape[0]):
        chosen = rank == pos_ref[j : j + 1, :]
        value = gate_ref[j : j + 1, :] if scaled else 1.0
        one_hot = jnp.where(chosen, value, 0.0).astype(BF)
        out_ref[j] = mm(one_hot, rows_ref[...]).astype(BF)


def dispatch(pos, gate, pieces, scaled):
    experts, rows = pos.shape
    return call(
        functools.partial(dispatch_kernel, len(pieces), scaled),
        "dispatch_scaled" if scaled else "dispatch",
        jax.ShapeDtypeStruct((experts, CAP, D), BF),
        [VM, VM] + [ANY] * len(pieces),
        VM,
        (pos, gate, *pieces),
        scratch=[pltpu.VMEM((rows, D), BF), pltpu.SemaphoreType.DMA((len(pieces),))],
        flops=2 * experts * CAP * rows * D,
        moved=5 << 20,
    )


def combine_kernel(n_experts, slot, scaled, n_adds, n_outs, pos_ref, gate_ref, *refs):
    sources, refs = refs[:n_experts], refs[n_experts:]
    adds, outs, (held, sems) = refs[:n_adds], refs[n_adds : n_adds + n_outs], refs[n_adds + n_outs :]
    copies = [
        pltpu.make_async_copy(source.at[slot], held.at[pl.ds(j * CAP, CAP)], sems.at[j])
        for j, source in enumerate(sources)
    ]
    for c in copies:
        c.start()
    for c in copies:
        c.wait()
    width = n_experts * CAP
    rows = pos_ref.shape[0]
    block = 256
    per_out = rows // n_outs
    for b in range(rows // block):
        at = slice(b * block, (b + 1) * block)
        tiles = []
        for first in range(0, width, LANES):
            size = min(LANES, width - first)
            lane = first + lax.broadcasted_iota(jnp.int32, (block, size), 1)
            tile = jnp.zeros((block, size), F32)
            for j in range(first // CAP, (first + size - 1) // CAP + 1):
                target = pos_ref[at, j : j + 1]
                target = jnp.where(target >= 0, target + j * CAP, -1)
                tile = jnp.where(lane == target, gate_ref[at, j : j + 1] if scaled else 1.0, tile)
            tiles.append(tile.astype(BF))
        total = mm(jnp.concatenate(tiles, axis=1), held[...])
        out, inner = outs[b * block // per_out], slice(b * block % per_out, b * block % per_out + block)
        if n_adds:
            total = total + adds[0][at].astype(F32)
        out[inner] = total.astype(BF)


def combine(pos, gate, sources, slot, scaled, add, n_outs):
    rows, n_experts = pos.shape
    adds = [] if add is None else [add]
    return call(
        functools.partial(combine_kernel, n_experts, slot, scaled, len(adds), n_outs),
        "combine_scaled" if scaled else "combine",
        [jax.ShapeDtypeStruct((rows // n_outs, D), BF)] * n_outs,
        [VM, VM] + [ANY] * n_experts + [VM] * len(adds),
        [VM] * n_outs,
        (pos, gate, *sources, *adds),
        scratch=[pltpu.VMEM((n_experts * CAP, D), BF), pltpu.SemaphoreType.DMA((n_experts,))],
        flops=2 * n_experts * CAP * rows * D,
        moved=5 << 20,
    )


def expert_kernel(j, outer, in_rows, down_rows, idx_ref, *refs):
    n_hops = outer - 1
    xs, refs = refs[:GROUP], refs[GROUP:]
    gs, refs = refs[:GROUP], refs[GROUP:]
    own, refs = refs[0], refs[1:]
    lefts, refs = refs[:n_hops], refs[n_hops:]
    rights, refs = refs[:n_hops], refs[n_hops:]
    y_ref, dx_ref, dw_ref = refs[:3]
    x_all, g_all, w_in, w_down, act_all, gug_all, sem_x, sem_g, sem_w, sem_d = refs[3:]
    o, i = idx_ref[0], idx_ref[1]

    def rows_of(sources, held, sems):
        return [
            pltpu.make_async_copy(s.at[j], held.at[pl.ds(n * CAP, CAP)], sems.at[n])
            for n, s in enumerate(sources)
        ]

    def weight_copies(source, at, slot):
        made = []
        for m in range(GROUP):
            place = at * GROUP + (i ^ m)
            made.append(
                pltpu.make_async_copy(
                    source.at[m, pl.ds(0, in_rows)],
                    w_in.at[pl.ds(pl.multiple_of(place * in_rows, in_rows), in_rows)],
                    sem_w.at[slot * GROUP + m],
                )
            )
            made.append(
                pltpu.make_async_copy(
                    source.at[m, pl.ds(in_rows, down_rows)],
                    w_down.at[pl.ds(pl.multiple_of(place * down_rows, down_rows), down_rows)],
                    sem_d.at[slot * GROUP + m],
                )
            )
        return made

    def each_weight(act):
        act(weight_copies(own, o, 0))
        for k in range(1, outer):

            @pl.when(o >= k)
            def _():
                act(weight_copies(lefts[k - 1], o - k, k))

            @pl.when(o + k < outer)
            def _():
                act(weight_copies(rights[k - 1], o + k, n_hops + k))

    def start(made):
        for c in made:
            c.start()

    def wait(made):
        for c in made:
            c.wait()

    each_weight(start)
    copy_x, copy_g = rows_of(xs, x_all, sem_x), rows_of(gs, g_all, sem_g)
    start(copy_x)
    start(copy_g)
    each_weight(wait)
    wait(copy_x)
    wait(copy_g)

    def per_slot(s, carry):
        at = pl.ds(pl.multiple_of(s * CAP, CAP), CAP)
        gate_up = mm(x_all[at, :], w_in[...])
        g, u = gate_up[:, :FF], gate_up[:, FF:]
        sigma = 1.0 / (1.0 + jnp.exp(-g))
        silu = g * sigma
        act = (silu * u).astype(BF)
        act_all[at, :] = act
        y_ref[s] = mm(act, w_down[...]).astype(BF)
        act_grad = mm_nt(g_all[at, :], w_down[...])
        gug_all[at, :FF] = (act_grad * u * sigma * (1.0 + g * (1.0 - sigma))).astype(BF)
        gug_all[at, FF:] = (act_grad * silu).astype(BF)
        dx_ref[s] = mm_nt(gug_all[at, :], w_in[...]).astype(BF)
        return carry

    lax.fori_loop(0, GROUP, per_slot, 0)
    for c in range(outer):
        part = mm_tn(x_all[:, c * GROUP * in_rows : (c + 1) * GROUP * in_rows], gug_all[...]).astype(BF)
        for r in range(GROUP):
            dw_ref[c, i ^ r, :in_rows, :] = part[r * in_rows : (r + 1) * in_rows]
        part = mm_tn(act_all[:, c * GROUP * down_rows : (c + 1) * GROUP * down_rows], g_all[...]).astype(BF)
        for r in range(GROUP):
            dw_ref[c, i ^ r, in_rows:, :] = part[r * down_rows : (r + 1) * down_rows]


def expert(idx, j, outer, in_rows, down_rows, xs, gs, own, lefts, rights):
    n_hops = outer - 1
    total = GROUP * CAP
    packed = in_rows + down_rows
    return call(
        functools.partial(expert_kernel, j, outer, in_rows, down_rows),
        "expert",
        [
            jax.ShapeDtypeStruct((GROUP, CAP, D), BF),
            jax.ShapeDtypeStruct((GROUP, CAP, D), BF),
            jax.ShapeDtypeStruct((outer, GROUP, packed, D), BF),
        ],
        [SMEM] + [ANY] * (2 * GROUP + 1 + 2 * n_hops),
        [VM] * 3,
        (idx, *xs, *gs, own, *lefts, *rights),
        scratch=[
            pltpu.VMEM((total, D), BF),
            pltpu.VMEM((total, D), BF),
            pltpu.VMEM((D, 2 * FF), BF),
            pltpu.VMEM((FF, D), BF),
            pltpu.VMEM((total, FF), BF),
            pltpu.VMEM((total, 2 * FF), BF),
            pltpu.SemaphoreType.DMA((GROUP,)),
            pltpu.SemaphoreType.DMA((GROUP,)),
            pltpu.SemaphoreType.DMA(((1 + 2 * n_hops) * GROUP,)),
            pltpu.SemaphoreType.DMA(((1 + 2 * n_hops) * GROUP,)),
        ],
        flops=18 * total * D * FF,
        moved=15 << 20,
    )


def pack_kernel(n_experts, in_rows, down_rows, idx_ref, in_ref, down_ref, *refs):
    outs, sems = refs[:-1], refs[-1]
    i = idx_ref[1]
    copies = []
    for j in range(n_experts):
        for m in range(GROUP):
            n = j * GROUP + m
            source = (i ^ m) * n_experts + j
            copies.append(
                pltpu.make_async_copy(in_ref.at[source], outs[m].at[j, pl.ds(0, in_rows)], sems.at[2 * n])
            )
            copies.append(
                pltpu.make_async_copy(
                    down_ref.at[source], outs[m].at[j, pl.ds(in_rows, down_rows)], sems.at[2 * n + 1]
                )
            )
    for c in copies:
        c.start()
    for c in copies:
        c.wait()


def pack_weights(idx, expert_in, expert_down):
    experts, in_rows, _ = expert_in.shape
    down_rows = expert_down.shape[1]
    n = experts // GROUP
    return call(
        functools.partial(pack_kernel, n, in_rows, down_rows),
        "pack_weights",
        [jax.ShapeDtypeStruct((n, in_rows + down_rows, D), BF)] * GROUP,
        [SMEM, ANY, ANY],
        [VM] * GROUP,
        (idx, expert_in, expert_down),
        scratch=[pltpu.SemaphoreType.DMA((2 * experts,))],
        moved=6 << 20,
    )


def place():
    d, t = lax.axis_index("dp"), lax.axis_index("tensor")
    return d, t, d // GROUP, d % GROUP


def flip(v, m):
    first, second = v % 2, (v // 2) % 2
    if m & 1:
        v = v + 1 - 2 * first
    if m & 2:
        v = v + 2 - 4 * second
    return v


def greet(outer, distances, tensor):
    d, t, o, _ = place()
    barrier = pltpu.get_barrier_semaphore()
    count = 0
    for m in distances:
        pl.semaphore_signal(barrier, inc=1, device_id=(flip(d, m), t), device_id_type=MESH)
        count += 1
    if tensor:
        pl.semaphore_signal(barrier, inc=1, device_id=(d, 1 - t), device_id_type=MESH)
        count += 1

    @pl.when(o > 0)
    def _():
        pl.semaphore_signal(barrier, inc=1, device_id=(d - GROUP, t), device_id_type=MESH)

    @pl.when(o < outer - 1)
    def _():
        pl.semaphore_signal(barrier, inc=1, device_id=(d + GROUP, t), device_id_type=MESH)

    neighbours = (o + outer - 1) // outer + (2 * outer - 2 - o) // outer
    pl.semaphore_wait(barrier, count + neighbours)


class Hops:
    def __init__(self, outer, steps, sent, came):
        d, t, o, _ = place()
        self.moves = []
        for n, (k, from_left, from_right, to_left, to_right) in enumerate(steps):
            back = outer - 1 - o
            right = pltpu.make_async_remote_copy(
                from_left, to_left, sent.at[2 * n], came.at[2 * n], device_id=(d + GROUP, t), device_id_type=MESH
            )
            left = pltpu.make_async_remote_copy(
                from_right,
                to_right,
                sent.at[2 * n + 1],
                came.at[2 * n + 1],
                device_id=(d - GROUP, t),
                device_id_type=MESH,
            )
            self.moves.append((right, (o >= k - 1) & (back >= 1), o >= k))
            self.moves.append((left, (back >= k - 1) & (o >= 1), back >= k))

    def start(self):
        for copy, sends, _ in self.moves:
            pl.when(sends)(copy.start)

    def wait(self):
        for copy, sends, receives in self.moves:
            pl.when(sends)(copy.wait_send)
            pl.when(receives)(copy.wait_recv)


def greet_all(outer):
    d, t, o, i = place()
    barrier = pltpu.get_barrier_semaphore()
    for m in range(1, GROUP):
        pl.semaphore_signal(barrier, inc=1, device_id=(flip(d, m), t), device_id_type=MESH)
    pl.semaphore_signal(barrier, inc=1, device_id=(d, 1 - t), device_id_type=MESH)
    for k in range(1, outer):
        pl.semaphore_signal(barrier, inc=1, device_id=((o + k) % outer * GROUP + i, t), device_id_type=MESH)
    pl.semaphore_wait(barrier, GROUP - 1 + outer)


def to_x(src, dst, sent, came):
    d, t, _, _ = place()
    return pltpu.make_async_remote_copy(src, dst, sent, came, device_id=(d, 1 - t), device_id_type=MESH)


def to_dp(m, src, dst, sent, came):
    d, t, _, _ = place()
    return pltpu.make_async_remote_copy(src, dst, sent, came, device_id=(flip(d, m), t), device_id_type=MESH)


def remote_call(kernel, name, collective_id, out_shape, in_specs, out_specs, args, scratch, flops):
    return pl.pallas_call(
        kernel,
        name=name,
        out_shape=out_shape,
        in_specs=in_specs,
        out_specs=out_specs,
        scratch_shapes=list(scratch),
        compiler_params=pltpu.CompilerParams(
            vmem_limit_bytes=VMEM_LIMIT, collective_id=collective_id, has_side_effects=True
        ),
        cost_estimate=pl.CostEstimate(flops=flops, bytes_accessed=8 << 20, transcendentals=0),
    )(*args)


def attention_kernel(outer, q_block, n_steps, len_ref, own_ref, other_ref, w_ref, cos_ref, sin_ref, x_ref, gain_ref, *refs):
    width = w_ref.shape[1] // 2
    heads = width // 2
    dy_refs, refs = refs[:2], refs[2:]
    sources, refs = refs[:n_steps], refs[n_steps:]
    qkv_ref, lse_ref, attn_ref, come_ref, hidden_ref, na_ref, nb_ref = refs[:7]
    refs = refs[7:]
    dy_outs, refs = refs[:4], refs[4:]
    to_left, refs = refs[:n_steps], refs[n_steps:]
    to_right, refs = refs[:n_steps], refs[n_steps:]
    send_ref, s_hop, r_hop, s_dy, r_dy, s_at, r_at = refs
    d, t, o, i = place()
    length = len_ref[0]
    rows = own_ref.shape[0]
    groups = width // (2 * LANES)
    greet(outer, (2,), True)
    hops = Hops(outer, [(1, s, s, l, r) for s, l, r in zip(sources, to_left, to_right, strict=True)], s_hop, r_hop)
    hops.start()
    ax, bx, ay, by = dy_outs
    dys = [
        to_x(dy_refs[0], ax, s_dy.at[0], r_dy.at[0]),
        to_dp(2, dy_refs[1], by, s_dy.at[1], r_dy.at[1]),
        to_x(dy_refs[1], bx, s_dy.at[2], r_dy.at[2]),
        to_dp(2, dy_refs[0], ay, s_dy.at[3], r_dy.at[3]),
    ]

    block = 256
    key_lanes = lax.broadcasted_iota(jnp.int32, (block, LANES), 1) < HD
    for part in range(2):
        for b in range(rows // block):
            at = pl.multiple_of((t if part == 0 else 1 - t) * rows + b * block, block)
            projected = mm((own_ref if part == 0 else other_ref)[b * block : (b + 1) * block], w_ref[:, :width])
            cosine, sine = cos_ref[pl.ds(at, block), :], sin_ref[pl.ds(at, block), :]
            for g in range(groups):
                q = projected[:, g * 2 * LANES : g * 2 * LANES + LANES]
                kv = projected[:, g * 2 * LANES + LANES : (g + 1) * 2 * LANES]
                q = q * cosine + swap_halves(q) * sine
                kv = jnp.where(key_lanes, kv * cosine + swap_halves(kv) * sine, kv)
                qkv_ref[pl.ds(at, block), g * 2 * LANES : g * 2 * LANES + LANES] = q.astype(BF)
                qkv_ref[pl.ds(at, block), g * 2 * LANES + LANES : (g + 1) * 2 * LANES] = kv.astype(BF)

    for copy in dys:
        copy.start()

    def exchange(g):
        lanes = pl.ds(pl.multiple_of(g * LANES, LANES), LANES)
        return to_x(send_ref.at[:, lanes], come_ref.at[:, lanes], s_at.at[g], r_at.at[g])

    def per_group(g, carry):
        q_lanes = pl.ds(pl.multiple_of(g * 2 * LANES, LANES), LANES)
        kv_lanes = pl.ds(pl.multiple_of(g * 2 * LANES + LANES, LANES), LANES)
        o_lanes = pl.ds(pl.multiple_of(g * LANES, LANES), LANES)
        keys, values = doubled(qkv_ref[:, kv_lanes])
        for b in range(2 * rows // q_block):
            start, n_keys = b * q_block, (b + 1) * q_block
            q = head_pair(qkv_ref[start : start + q_block, q_lanes])
            scores = mm_nt(keys[:n_keys], q) * (1.0 / math.sqrt(HD))
            scores = jnp.where(allowed(n_keys, q_block, start, length), scores, NEGATIVE)
            largest = jnp.max(scores, axis=0, keepdims=True)
            expon = jnp.exp(scores - largest)
            totals = jnp.sum(expon, axis=0, keepdims=True)
            probs = (expon * (1.0 / totals)).astype(BF)
            mixed = head_join(mm_tn(probs, values[:n_keys])).astype(BF)
            lse_ref[g, b : b + 1, :] = largest + jnp.log(totals)
            half, inner = start // rows, start % rows

            @pl.when(t == half)
            def _():
                attn_ref[inner : inner + q_block, o_lanes] = mixed

            @pl.when(t != half)
            def _():
                send_ref[inner : inner + q_block, o_lanes] = mixed

        exchange(g).start()
        return carry

    lax.fori_loop(0, groups, per_group, 0)

    def settle(g, carry):
        exchange(g).wait()
        return carry

    for p, normed_ref in enumerate((na_ref, nb_ref)):
        at = slice(p * rows // 2, (p + 1) * rows // 2)
        hidden_ref[at] = x_ref[at].astype(F32) + mm_nt(attn_ref[at], w_ref[:, width : width + heads])
    lax.fori_loop(0, groups, settle, 0)
    for p, normed_ref in enumerate((na_ref, nb_ref)):
        at = slice(p * rows // 2, (p + 1) * rows // 2)
        hidden = hidden_ref[at] + mm_nt(come_ref[at], w_ref[:, width + heads :])
        inverse = lax.rsqrt(jnp.mean(hidden * hidden, axis=-1, keepdims=True) + EPSILON)
        hidden_ref[at] = hidden
        normed_ref[...] = (hidden * inverse * gain_ref[...]).astype(BF)
    for copy in dys:
        copy.wait()
    hops.wait()


def attention(outer, q_block, length, own, other, weights_full, cosine, sine, x, gain, dys, sources):
    rows, groups = own.shape[0], weights_full.shape[1] // (4 * LANES)
    n = len(sources)
    piece = jax.ShapeDtypeStruct((rows // 2, D), BF)
    weights = [jax.ShapeDtypeStruct(s.shape, BF) for s in sources]
    out = remote_call(
        functools.partial(attention_kernel, outer, q_block, n),
        "attention",
        1,
        [
            jax.ShapeDtypeStruct((2 * rows, groups * 2 * LANES), BF),
            jax.ShapeDtypeStruct((groups, 2 * rows // q_block, 2 * q_block), F32),
            jax.ShapeDtypeStruct((rows, groups * LANES), BF),
            jax.ShapeDtypeStruct((rows, groups * LANES), BF),
            jax.ShapeDtypeStruct((rows, D), F32),
            piece,
            piece,
        ]
        + [piece] * 4
        + weights * 2,
        [SMEM] + [VM] * 7 + [ANY] * (2 + n),
        [VM] * 7 + [ANY] * (4 + 2 * n),
        (length, own, other, weights_full, cosine, sine, x, gain.reshape(1, D), *dys, *sources),
        [
            pltpu.VMEM((rows, groups * LANES), BF),
            pltpu.SemaphoreType.DMA((2 * n,)),
            pltpu.SemaphoreType.DMA((2 * n,)),
            pltpu.SemaphoreType.DMA((4,)),
            pltpu.SemaphoreType.DMA((4,)),
            pltpu.SemaphoreType.DMA((groups,)),
            pltpu.SemaphoreType.DMA((groups,)),
        ],
        30 << 30,
    )
    return out[:7], out[7:11], out[11 : 11 + n], out[11 + n :]


def one_hot_rows(pos, gate, j, n_rows):
    rank = lax.broadcasted_iota(jnp.int32, (CAP, n_rows), 0)
    chosen = rank == pos[j : j + 1, :]
    return jnp.where(chosen, 1.0 if gate is None else gate[j : j + 1, :], 0.0).astype(BF)


def spread_kernel(outer, steps, pos_ref, gate_ref, na_ref, nb_ref, *refs):
    n_steps = len(steps)
    dy_refs, refs = refs[:6], refs[6:]
    from_left, refs = refs[:n_steps], refs[n_steps:]
    from_right, refs = refs[:n_steps], refs[n_steps:]
    n_ref, dyx_ref, og_ref = refs[:3]
    refs = refs[3:]
    to_left, refs = refs[:n_steps], refs[n_steps:]
    to_right, refs = refs[:n_steps], refs[n_steps:]
    held, s_hop, r_hop, s_n, r_n, s_d, r_d, l_sem = refs
    height = na_ref.shape[0]
    n_experts = og_ref.shape[1]
    greet(outer, (1, 2), True)
    n_ax = to_x(na_ref, n_ref.at[0, 1], s_n.at[0], r_n.at[0])
    n_by = to_dp(2, nb_ref, n_ref.at[1, 2], s_n.at[1], r_n.at[1])
    n_bx = to_x(nb_ref, n_ref.at[0, 3], s_n.at[2], r_n.at[2])
    n_ay = to_dp(2, na_ref, n_ref.at[1, 0], s_n.at[3], r_n.at[3])
    n_axy = to_dp(2, n_ref.at[0, 1], n_ref.at[1, 1], s_n.at[4], r_n.at[4])
    n_bxy = to_x(n_ref.at[1, 2], n_ref.at[1, 3], s_n.at[5], r_n.at[5])
    core = {}
    for n, (s, p) in enumerate([(s, p) for s in range(2) for p in range(4)]):
        source = na_ref if (s, p) == (0, 0) else nb_ref if (s, p) == (0, 2) else n_ref.at[s, p]
        core[s, p] = to_dp(1, source, n_ref.at[2 + s, p], s_n.at[6 + n], r_n.at[6 + n])
    for copy in (n_ax, n_by, n_bx, n_ay):
        copy.start()
    d_a, d_b, d_ax, d_bx, d_ay, d_by = dy_refs
    d_axy = to_dp(2, d_ax, dyx_ref.at[0, 1], s_d.at[0], r_d.at[0])
    d_bxy = to_x(d_by, dyx_ref.at[0, 3], s_d.at[1], r_d.at[1])
    d_axy.start()
    d_bxy.start()
    d_near = [[d_a, d_ax, d_b, d_bx], [d_ay, dyx_ref.at[0, 1], d_by, dyx_ref.at[0, 3]]]
    d_core = {}
    for n, (s, p) in enumerate([(s, p) for s in range(2) for p in range(4)]):
        d_core[s, p] = to_dp(1, d_near[s][p], dyx_ref.at[1 + s, p], s_d.at[2 + n], r_d.at[2 + n])
    for key in ((0, 0), (0, 1), (0, 2), (0, 3), (1, 0), (1, 2)):
        d_core[key].start()
    core[0, 0].start()
    core[0, 2].start()
    hops = Hops(
        outer,
        [(k, a, b, l, r) for k, a, b, l, r in zip(steps, from_left, from_right, to_left, to_right, strict=True)],
        s_hop,
        r_hop,
    )
    hops.start()

    def load(s):
        pieces = d_near[s] if s < 2 else [dyx_ref.at[s - 1, p] for p in range(4)]
        return [
            pltpu.make_async_copy(piece, held.at[pl.ds(p * height, height)], l_sem.at[p])
            for p, piece in enumerate(pieces)
        ]

    def give(s):
        copies = load(s)
        for c in copies:
            c.start()
        for c in copies:
            c.wait()

        def one(j, carry):
            rank = lax.broadcasted_iota(jnp.int32, (CAP, 4 * height), 0)
            chosen = rank == pos_ref[s, pl.ds(j, 1), :]
            one_hot = jnp.where(chosen, gate_ref[s, pl.ds(j, 1), :], 0.0).astype(BF)
            og_ref[s, j] = mm(one_hot, held[...]).astype(BF)
            return carry

        lax.fori_loop(0, n_experts, one, 0)

    give(0)
    n_ax.wait()
    n_by.wait()
    n_axy.start()
    n_bxy.start()
    core[0, 1].start()
    core[1, 2].start()
    d_axy.wait()
    d_bxy.wait()
    d_core[1, 1].start()
    d_core[1, 3].start()
    give(1)
    n_bx.wait()
    n_ay.wait()
    core[0, 3].start()
    core[1, 0].start()
    for p in range(4):
        d_core[0, p].wait()
    give(2)
    n_axy.wait()
    n_bxy.wait()
    core[1, 1].start()
    core[1, 3].start()
    for p in range(4):
        d_core[1, p].wait()
    give(3)
    for key in core:
        core[key].wait()
    hops.wait()


def spread(outer, pos, gate, normed, dys, steps, from_left, from_right):
    height = normed[0].shape[0]
    n, n_experts = len(steps), pos.shape[1]
    weights = [jax.ShapeDtypeStruct(s.shape, BF) for s in from_left]
    out = remote_call(
        functools.partial(spread_kernel, outer, steps),
        "spread",
        2,
        [
            jax.ShapeDtypeStruct((GROUP, 4, height, D), BF),
            jax.ShapeDtypeStruct((3, 4, height, D), BF),
            jax.ShapeDtypeStruct((GROUP, n_experts, CAP, D), BF),
        ]
        + weights * 2,
        [VM] * 2 + [ANY] * (2 + 6 + 2 * n),
        [ANY, ANY, VM] + [ANY] * (2 * n),
        (pos, gate, *normed, *dys, *from_left, *from_right),
        [
            pltpu.VMEM((4 * height, D), BF),
            pltpu.SemaphoreType.DMA((2 * n,)),
            pltpu.SemaphoreType.DMA((2 * n,)),
            pltpu.SemaphoreType.DMA((14,)),
            pltpu.SemaphoreType.DMA((14,)),
            pltpu.SemaphoreType.DMA((10,)),
            pltpu.SemaphoreType.DMA((10,)),
            pltpu.SemaphoreType.DMA((4,)),
        ],
        12 << 30,
    )
    return out[0], out[2], out[3 : 3 + n], out[3 + n :]


def hand_out_kernel(outer, steps, pos_ref, na_ref, nb_ref, n_ref, *refs):
    n_steps = len(steps)
    from_left, refs = refs[:n_steps], refs[n_steps:]
    from_right, refs = refs[:n_steps], refs[n_steps:]
    x_ref, refs = refs[0], refs[1:]
    to_left, refs = refs[:n_steps], refs[n_steps:]
    to_right, refs = refs[:n_steps], refs[n_steps:]
    held, s_hop, r_hop, l_sem = refs
    height = na_ref.shape[0]
    n_experts = x_ref.shape[1]
    greet(outer, (), False)
    hops = Hops(
        outer,
        [(k, a, b, l, r) for k, a, b, l, r in zip(steps, from_left, from_right, to_left, to_right, strict=True)],
        s_hop,
        r_hop,
    )
    hops.start()

    def load(s):
        pieces = [na_ref, n_ref.at[0, 1], nb_ref, n_ref.at[0, 3]] if s == 0 else [n_ref.at[s, p] for p in range(4)]
        return [
            pltpu.make_async_copy(piece, held.at[s % 2, pl.ds(p * height, height)], l_sem.at[s % 2, p])
            for p, piece in enumerate(pieces)
        ]

    for c in load(0):
        c.start()
    for s in range(GROUP):
        if s + 1 < GROUP:
            for c in load(s + 1):
                c.start()
        for c in load(s):
            c.wait()

        def one(j, carry, s=s):
            rank = lax.broadcasted_iota(jnp.int32, (CAP, 4 * height), 0)
            one_hot = jnp.where(rank == pos_ref[s, pl.ds(j, 1), :], 1.0, 0.0).astype(BF)
            x_ref[s, j] = mm(one_hot, held[s % 2]).astype(BF)
            return carry

        lax.fori_loop(0, n_experts, one, 0)
    hops.wait()


def hand_out(outer, pos, normed, gathered, steps, from_left, from_right):
    height = normed[0].shape[0]
    n, n_experts = len(steps), pos.shape[1]
    weights = [jax.ShapeDtypeStruct(s.shape, BF) for s in from_left]
    out = remote_call(
        functools.partial(hand_out_kernel, outer, steps),
        "hand_out",
        3,
        [jax.ShapeDtypeStruct((GROUP, n_experts, CAP, D), BF)] + weights * 2,
        [VM] + [ANY] * (3 + 2 * n),
        [VM] + [ANY] * (2 * n),
        (pos, *normed, gathered, *from_left, *from_right),
        [
            pltpu.VMEM((2, 4 * height, D), BF),
            pltpu.SemaphoreType.DMA((2 * n,)),
            pltpu.SemaphoreType.DMA((2 * n,)),
            pltpu.SemaphoreType.DMA((2, 4)),
        ],
        12 << 30,
    )
    return out[0], out[1 : 1 + n], out[1 + n :]


def expert_step_kernel(j, outer, in_rows, down_rows, steps, sum_steps, x_ref, g_ref, own, *refs):
    n_hops, n_steps, n_sums = outer - 1, len(steps), len(sum_steps)
    lefts, refs = refs[:n_hops], refs[n_hops:]
    rights, refs = refs[:n_hops], refs[n_hops:]
    from_left, refs = refs[:n_steps], refs[n_steps:]
    from_right, refs = refs[:n_steps], refs[n_steps:]
    dws, refs = refs[:n_sums], refs[n_sums:]
    was_l, refs = refs[:n_sums], refs[n_sums:]
    was_r, refs = refs[:n_sums], refs[n_sums:]
    y_ref, dx_ref, dw_ref = refs[:3]
    refs = refs[3:]
    to_left, refs = refs[:n_steps], refs[n_steps:]
    to_right, refs = refs[:n_steps], refs[n_steps:]
    sum_left, refs = refs[:n_sums], refs[n_sums:]
    sum_right, refs = refs[:n_sums], refs[n_sums:]
    x_all, g_all, w_in, w_down, act_all, gug_all, sem_x, sem_g, sem_w, sem_d, s_hop, r_hop = refs[:12]
    _, _, o, i = place()
    greet(outer, (), False)
    sums = Sums(outer, sum_steps, dws, was_l, was_r, sum_left, sum_right, *refs[12:])
    if n_steps:
        hops = Hops(
            outer,
            [(k, a, b, l, r) for k, a, b, l, r in zip(steps, from_left, from_right, to_left, to_right, strict=True)],
            s_hop,
            r_hop,
        )
        hops.start()

    def rows_of(source, held, sems):
        return [
            pltpu.make_async_copy(source.at[n, j], held.at[pl.ds(n * CAP, CAP)], sems.at[n]) for n in range(GROUP)
        ]

    def weight_copies(source, at, slot):
        made = []
        for m in range(GROUP):
            where = at * GROUP + flip(i, m)
            made.append(
                pltpu.make_async_copy(
                    source.at[m, pl.ds(0, in_rows)],
                    w_in.at[pl.ds(pl.multiple_of(where * in_rows, in_rows), in_rows)],
                    sem_w.at[slot * GROUP + m],
                )
            )
            made.append(
                pltpu.make_async_copy(
                    source.at[m, pl.ds(in_rows, down_rows)],
                    w_down.at[pl.ds(pl.multiple_of(where * down_rows, down_rows), down_rows)],
                    sem_d.at[slot * GROUP + m],
                )
            )
        return made

    def each_weight(act):
        act(weight_copies(own, o, 0))
        for k in range(1, outer):

            @pl.when(o >= k)
            def _():
                act(weight_copies(lefts[k - 1], o - k, k))

            @pl.when(o + k < outer)
            def _():
                act(weight_copies(rights[k - 1], o + k, n_hops + k))

    def start(made):
        for c in made:
            c.start()

    def wait(made):
        for c in made:
            c.wait()

    sums.load()
    each_weight(start)
    copy_x, copy_g = rows_of(x_ref, x_all, sem_x), rows_of(g_ref, g_all, sem_g)
    start(copy_x)
    start(copy_g)
    sums.send()
    each_weight(wait)
    wait(copy_x)
    wait(copy_g)

    def per_slot(s, carry):
        at = pl.ds(pl.multiple_of(s * CAP, CAP), CAP)
        gate_up = mm(x_all[at, :], w_in[...])
        g, u = gate_up[:, :FF], gate_up[:, FF:]
        sigma = 1.0 / (1.0 + jnp.exp(-g))
        silu = g * sigma
        act = (silu * u).astype(BF)
        act_all[at, :] = act
        y_ref[s] = mm(act, w_down[...]).astype(BF)
        act_grad = mm_nt(g_all[at, :], w_down[...])
        gug_all[at, :FF] = (act_grad * u * sigma * (1.0 + g * (1.0 - sigma))).astype(BF)
        gug_all[at, FF:] = (act_grad * silu).astype(BF)
        dx_ref[s] = mm_nt(gug_all[at, :], w_in[...]).astype(BF)
        return carry

    lax.fori_loop(0, GROUP, per_slot, 0)
    for c in range(outer):
        part = mm_tn(x_all[:, c * GROUP * in_rows : (c + 1) * GROUP * in_rows], gug_all[...]).astype(BF)
        for r in range(GROUP):
            dw_ref[c, flip(i, r), :in_rows, :] = part[r * in_rows : (r + 1) * in_rows]
        part = mm_tn(act_all[:, c * GROUP * down_rows : (c + 1) * GROUP * down_rows], g_all[...]).astype(BF)
        for r in range(GROUP):
            dw_ref[c, flip(i, r), in_rows:, :] = part[r * down_rows : (r + 1) * down_rows]
    if n_steps:
        hops.wait()
    sums.wait()


def expert_step(j, outer, in_rows, down_rows, x, g, own, lefts, rights, hop_plan, sum_plan):
    (steps, from_left, from_right), (sum_steps, dws, was_l, was_r) = hop_plan, sum_plan
    n_hops, n, n_sums = outer - 1, len(steps), len(sum_steps)
    total = GROUP * CAP
    packed = in_rows + down_rows
    weights = [jax.ShapeDtypeStruct(s.shape, BF) for s in from_left]
    shapes = [
        jax.ShapeDtypeStruct((GROUP, CAP, D), BF),
        jax.ShapeDtypeStruct((GROUP, CAP, D), BF),
        jax.ShapeDtypeStruct((outer, GROUP, packed, D), BF),
    ] + weights * 2 + [jax.ShapeDtypeStruct((GROUP, packed, D), BF)] * (2 * n_sums)
    out = remote_call(
        functools.partial(expert_step_kernel, j, outer, in_rows, down_rows, steps, sum_steps),
        "expert_step",
        4 + j,
        shapes,
        [ANY] * (3 + 2 * n_hops + 2 * n + 3 * n_sums),
        [VM] * 3 + [ANY] * (2 * n + 2 * n_sums),
        (x, g, own, *lefts, *rights, *from_left, *from_right, *dws, *was_l, *was_r),
        [
            pltpu.VMEM((total, D), BF),
            pltpu.VMEM((total, D), BF),
            pltpu.VMEM((D, 2 * FF), BF),
            pltpu.VMEM((FF, D), BF),
            pltpu.VMEM((total, FF), BF),
            pltpu.VMEM((total, 2 * FF), BF),
            pltpu.SemaphoreType.DMA((GROUP,)),
            pltpu.SemaphoreType.DMA((GROUP,)),
            pltpu.SemaphoreType.DMA(((1 + 2 * n_hops) * GROUP,)),
            pltpu.SemaphoreType.DMA(((1 + 2 * n_hops) * GROUP,)),
            pltpu.SemaphoreType.DMA((max(1, 2 * n),)),
            pltpu.SemaphoreType.DMA((max(1, 2 * n),)),
            *sums_scratch(n_sums, packed),
        ],
        18 * total * D * FF,
    )
    out, rest = out[:3], out[3:]
    return out, rest[:n], rest[n : 2 * n], rest[2 * n : 2 * n + n_sums], rest[2 * n + n_sums :]


class Sums:
    def __init__(self, outer, steps, dws, was_left, was_right, to_left, to_right, message, term, loaded, added, sent, came):
        d, t, o, _ = place()
        back = outer - 1 - o
        self.moves = []
        for n, s in enumerate(steps):
            for side, near, target, was, to, peer in (
                (0, o, outer - s + o, was_left, to_left, d + GROUP),
                (1, back, s - 1 - back, was_right, to_right, d - GROUP),
            ):
                k = 2 * n + side
                own = pltpu.make_async_copy(dws[n].at[target], message.at[k], loaded.at[k])
                before = None if s == 1 else pltpu.make_async_copy(was[n], term.at[side], added.at[k])
                move = pltpu.make_async_remote_copy(
                    message.at[k], to[n], sent.at[k], came.at[k], device_id=(peer, t), device_id_type=MESH
                )
                sends, adds = near <= s - 1, (near <= s - 1) & (near >= 1)
                receives = (near >= 1) & (near <= s)
                self.moves.append((own, before, move, sends, adds, receives, message.at[k], term.at[side]))

    def load(self):
        for own, _, _, sends, *_ in self.moves:
            pl.when(sends)(own.start)

    def send(self):
        for n in range(0, len(self.moves), 2):
            pair = self.moves[n : n + 2]
            for _, before, _, _, adds, *_ in pair:
                if before is not None:
                    pl.when(adds)(before.start)
            for own, before, move, sends, adds, _, message, term in pair:
                pl.when(sends)(own.wait)
                if before is not None:

                    @pl.when(adds)
                    def _(before=before, message=message, term=term):
                        before.wait()

                        def one(m, carry):
                            message[m] = (message[m].astype(F32) + term[m].astype(F32)).astype(BF)
                            return carry

                        lax.fori_loop(0, GROUP, one, 0)

                pl.when(sends)(move.start)

    def wait(self):
        for _, _, move, sends, _, receives, *_ in self.moves:
            pl.when(sends)(move.wait_send)
            pl.when(receives)(move.wait_recv)


def sums_scratch(n, packed):
    n = max(1, n)
    return [
        pltpu.VMEM((2 * n, GROUP, packed, D), BF),
        pltpu.VMEM((2, GROUP, packed, D), BF),
        pltpu.SemaphoreType.DMA((2 * n,)),
        pltpu.SemaphoreType.DMA((2 * n,)),
        pltpu.SemaphoreType.DMA((2 * n,)),
        pltpu.SemaphoreType.DMA((2 * n,)),
    ]


def again(scratch):
    return [pltpu.SemaphoreType.DMA(s.shape) for s in scratch[2:]]


class Final:
    def __init__(self, outer, dw, left, right, mine, term, target, loaded, sent, came, kept):
        _, _, o, _ = place()
        self.from_left, self.from_right = o >= 1, o < outer - 1
        self.mine, self.term = mine, term
        self.own = pltpu.make_async_copy(dw.at[o], mine, loaded.at[0])
        self.left = pltpu.make_async_copy(left, term.at[0], loaded.at[1])
        self.right = pltpu.make_async_copy(right, term.at[1], loaded.at[2])
        self.moves = [to_dp(m, mine.at[m], target.at[m], sent.at[m - 1], came.at[m - 1]) for m in range(1, GROUP)]
        self.keep = pltpu.make_async_copy(mine.at[0], target.at[0], kept)

    def send(self):
        self.own.start()
        pl.when(self.from_left)(self.left.start)
        pl.when(self.from_right)(self.right.start)
        self.own.wait()

        def add(k):
            def one(m, carry):
                self.mine[m] = (self.mine[m].astype(F32) + self.term[k, m].astype(F32)).astype(BF)
                return carry

            lax.fori_loop(0, GROUP, one, 0)

        @pl.when(self.from_left)
        def _():
            self.left.wait()
            add(0)

        @pl.when(self.from_right)
        def _():
            self.right.wait()
            add(1)

        for move in self.moves:
            move.start()
        self.keep.start()

    def wait(self):
        for move in self.moves:
            move.wait()
        self.keep.wait()


def final_scratch(packed):
    return [
        pltpu.VMEM((GROUP, packed, D), BF),
        pltpu.SemaphoreType.DMA((3,)),
        pltpu.SemaphoreType.DMA((GROUP - 1,)),
        pltpu.SemaphoreType.DMA((GROUP - 1,)),
        pltpu.SemaphoreType.DMA,
    ]


class Mixer:
    def __init__(self, sources, pos_ref, gate_ref, held, sems):
        self.sources, self.pos, self.gate, self.held, self.sems = sources, pos_ref, gate_ref, held, sems

    def copies(self, slot, buffer):
        return [
            pltpu.make_async_copy(
                source.at[slot], self.held.at[buffer, pl.ds(j * CAP, CAP)], self.sems.at[buffer * len(self.sources) + j]
            )
            for j, source in enumerate(self.sources)
        ]

    def load(self, slot, buffer):
        for c in self.copies(slot, buffer):
            c.start()

    def mix(self, slot, buffer, out, add=None):
        for c in self.copies(slot, buffer):
            c.wait()
        n_experts = len(self.sources)
        width = n_experts * CAP
        block = 256

        def one(b, carry):
            at = pl.ds(pl.multiple_of(b * block, block), block)
            targets = []
            for j in range(n_experts):
                target = self.pos[slot, at, j : j + 1]
                targets.append(jnp.where(target >= 0, target + j * CAP, -1))
            tiles = []
            for first in range(0, width, LANES):
                size = min(LANES, width - first)
                lane = first + lax.broadcasted_iota(jnp.int32, (block, size), 1)
                tile = jnp.zeros((block, size), F32)
                for j in range(first // CAP, (first + size - 1) // CAP + 1):
                    value = 1.0 if self.gate is None else self.gate[slot, at, j : j + 1]
                    tile = jnp.where(lane == targets[j], value, tile)
                tiles.append(tile.astype(BF))
            total = mm(jnp.concatenate(tiles, axis=1), self.held[buffer])
            if add is not None:
                total = total + add[at, :].astype(F32)
            out[at, :] = total.astype(BF)
            return carry

        lax.fori_loop(0, out.shape[0] // block, one, 0)


class GroupSum:
    def __init__(self, far, come, near, come_ab, last_ab, sent, came):
        self.far, self.come, self.near, self.come_ab, self.last_ab = far, come, near, come_ab, last_ab
        q = near.shape[1] // 4
        self.q = q
        self.core = [to_dp(1, far.at[s], come.at[s], sent.at[s], came.at[s]) for s in range(2)]
        self.a = to_dp(2, near.at[1, pl.ds(0, 2 * q)], come_ab.at[0], sent.at[2], came.at[2])
        self.b = [
            to_x(near.at[s, pl.ds(3 * q, q)], come_ab.at[1, pl.ds(s * q, q)], sent.at[3 + s], came.at[3 + s])
            for s in range(2)
        ]
        self.last = [
            to_x(near.at[0, pl.ds(q, q)], last_ab.at[0], sent.at[5], came.at[5]),
            to_dp(2, near.at[1, pl.ds(2 * q, q)], last_ab.at[1], sent.at[6], came.at[6]),
        ]

    def second(self):
        q, near, come_ab = self.q, self.near, self.come_ab
        self.a.wait_recv()
        near[0, q : 2 * q] = (near[0, q : 2 * q].astype(F32) + come_ab[0, q : 2 * q].astype(F32)).astype(BF)
        self.last[0].start()
        self.b[1].wait_recv()
        near[1, 2 * q : 3 * q] = (near[1, 2 * q : 3 * q].astype(F32) + come_ab[1, q : 2 * q].astype(F32)).astype(BF)
        self.last[1].start()
        self.b[0].wait_recv()

    def terms(self, p):
        q = self.q
        self.last[p].wait_recv()
        return (
            self.near[0, 2 * p * q : 2 * p * q + q].astype(F32)
            + self.come_ab[p, :q].astype(F32)
            + self.last_ab[p].astype(F32)
        )

    def sent(self):
        for copy in (*self.core, self.a, *self.b, *self.last):
            copy.wait_send()


def group_scratch(rows, n_experts):
    return [
        pltpu.VMEM((2, n_experts * CAP, D), BF),
        pltpu.VMEM((2, rows, D), BF),
        pltpu.VMEM((2, rows, D), BF),
        pltpu.VMEM((2, rows, D), BF),
        pltpu.VMEM((2, rows // 2, D), BF),
        pltpu.VMEM((2, rows // 4, D), BF),
        pltpu.SemaphoreType.DMA((2 * n_experts,)),
        pltpu.SemaphoreType.DMA((7,)),
        pltpu.SemaphoreType.DMA((7,)),
    ]


def mix_and_sum(mixer, group):
    mixer.load(2, 0)
    mixer.load(3, 1)
    mixer.mix(2, 0, group.far.at[0])
    group.core[0].start()
    mixer.load(1, 0)
    mixer.mix(3, 1, group.far.at[1])
    group.core[1].start()
    mixer.load(0, 1)
    group.core[1].wait_recv()
    mixer.mix(1, 0, group.near.at[1], group.come.at[1])
    group.a.start()
    group.b[1].start()
    group.core[0].wait_recv()
    mixer.mix(0, 1, group.near.at[0], group.come.at[0])
    group.b[0].start()
    group.second()


def rows_back_kernel(outer, first, then, pos_ref, valid_ref, hidden_ref, cot_ref, gain_ref, w_ref, *refs):
    n_experts, n1, n2 = pos_ref.shape[2], len(first), len(then)
    sources, refs = refs[:n_experts], refs[n_experts:]
    dws, refs = refs[:n1], refs[n1:]
    was_l, refs = refs[:n1], refs[n1:]
    was_r, refs = refs[:n1], refs[n1:]
    grad_ref, low_ref, gain_grad_ref, own_ref, come_ref = refs[:5]
    refs = refs[5:]
    to_l, refs = refs[: n1 + n2], refs[n1 + n2 :]
    to_r, refs = refs[: n1 + n2], refs[n1 + n2 :]
    (held, far, come, near, come_ab, last_ab, l_sem, s_sem, r_sem), refs = refs[:9], refs[9:]
    sums_a, refs = refs[:6], refs[6:]
    sums_b, refs = (*sums_a[:2], *refs[:4]), refs[4:]
    send_ref, s_at, r_at = refs
    greet(outer, (1, 2), True)
    one = Sums(outer, first, dws, was_l, was_r, to_l[:n1], to_r[:n1], *sums_a)
    two = Sums(
        outer,
        [s for s, _ in then],
        [dws[k] for _, k in then],
        [to_l[k] for _, k in then],
        [to_r[k] for _, k in then],
        to_l[n1:],
        to_r[n1:],
        *sums_b,
    )
    group = GroupSum(far, come, near, come_ab, last_ab, s_sem, r_sem)
    mixer = Mixer(sources, pos_ref, None, held, l_sem)
    one.load()
    one.send()
    mix_and_sum(mixer, group)
    one.wait()
    two.load()
    two.send()
    rows = hidden_ref.shape[0] // 2
    width = w_ref.shape[1] // 2
    heads = width // 2
    gain = gain_ref[...]
    gain_grad = jnp.zeros((1, D), F32)
    for p in range(2):
        at = slice(p * rows, (p + 1) * rows)
        hidden = hidden_ref[at]
        normed_grad = group.terms(p)
        inverse = lax.rsqrt(jnp.mean(hidden * hidden, axis=-1, keepdims=True) + EPSILON)
        gain_grad = gain_grad + jnp.sum(normed_grad * (hidden * inverse), axis=0, keepdims=True)
        scaled = normed_grad * gain
        back = inverse * scaled - hidden * (
            inverse * inverse * inverse * jnp.mean(scaled * hidden, axis=-1, keepdims=True)
        )
        dy = jnp.where(valid_ref[at] > 0, cot_ref[at].astype(F32), 0.0)
        total = dy + back
        grad_ref[at] = total
        low = total.astype(BF)
        low_ref[at] = low
        send_ref[at] = mm(low, w_ref[:, width + heads :]).astype(BF)
    gain_grad_ref[...] = gain_grad
    away = to_x(send_ref, come_ref, s_at, r_at)
    away.start()
    own_ref[...] = mm(low_ref[...], w_ref[:, width : width + heads]).astype(BF)
    group.sent()
    away.wait()
    two.wait()


def rows_back(outer, pos, valid, hidden, cotangent, gain, weights_full, sources, first, then, dws, was_l, was_r):
    rows, heads = hidden.shape[0], weights_full.shape[1] // 4
    n = len(first) + len(then)
    packed = dws[0].shape[2]
    hop = [jax.ShapeDtypeStruct((GROUP, packed, D), BF)] * (2 * n)
    half = jax.ShapeDtypeStruct((rows, heads), BF)
    out = remote_call(
        functools.partial(rows_back_kernel, outer, first, then),
        "rows_back",
        10,
        [
            jax.ShapeDtypeStruct((rows, D), F32),
            jax.ShapeDtypeStruct((rows, D), BF),
            jax.ShapeDtypeStruct((1, D), F32),
            half,
            half,
        ]
        + hop,
        [VM] * 6 + [ANY] * (len(sources) + 3 * len(first)),
        [VM] * 5 + [ANY] * (2 * n),
        (pos, valid, hidden, cotangent, gain.reshape(1, D), weights_full, *sources, *dws, *was_l, *was_r),
        [
            *group_scratch(2 * rows, len(sources)),
            *sums_scratch(len(first), packed),
            *again(sums_scratch(len(first), packed)),
            pltpu.VMEM((rows, heads), BF),
            pltpu.SemaphoreType.DMA,
            pltpu.SemaphoreType.DMA,
        ],
        20 << 30,
    )
    return out[:5], out[5 : 5 + n], out[5 + n :]


def attention_back_kernel(outer, q_block, steps, len_ref, qkv_ref, lse_ref, cos_ref, sin_ref, own_ref, other_ref, *refs):
    n = len(steps)
    dws, refs = refs[:n], refs[n:]
    was_l, refs = refs[:n], refs[n:]
    was_r, refs = refs[:n], refs[n:]
    f_dw, f_left, f_right, refs = *refs[:3], refs[3:]
    outs, fin_ref, refs = refs[:2], refs[2], refs[3:]
    to_l, refs = refs[:n], refs[n:]
    to_r, refs = refs[:n], refs[n:]
    do_ref, dq_ref, dk_ref, dv_ref = refs[:4]
    sums_refs, final_refs = refs[4:10], refs[10:]
    _, t, _, _ = place()
    greet(outer, (1, 2, 3), False)
    sums = Sums(outer, steps, dws, was_l, was_r, to_l, to_r, *sums_refs)
    final = Final(outer, f_dw, f_left, f_right, final_refs[0], sums_refs[1], fin_ref, *final_refs[1:])
    sums.load()
    sums.send()
    final.send()
    length = len_ref[0]
    rows, own_rows = qkv_ref.shape[0], own_ref.shape[0]
    groups = own_ref.shape[1] // LANES
    scale = 1.0 / math.sqrt(HD)

    def per_group(g, carry):
        q_lanes = pl.ds(pl.multiple_of(g * 2 * LANES, LANES), LANES)
        kv_lanes = pl.ds(pl.multiple_of(g * 2 * LANES + LANES, LANES), LANES)
        o_lanes = pl.ds(pl.multiple_of(g * LANES, LANES), LANES)
        for half, grad_ref in ((t, own_ref), (1 - t, other_ref)):
            do_ref[pl.ds(pl.multiple_of(half * own_rows, own_rows), own_rows), :] = grad_ref[:, o_lanes]
        keys, values = doubled(qkv_ref[:, kv_lanes])
        dk_ref[...] = jnp.zeros_like(dk_ref)
        dv_ref[...] = jnp.zeros_like(dv_ref)
        for b in range(rows // q_block):
            start, n_keys = b * q_block, (b + 1) * q_block
            q = head_pair(qkv_ref[start : start + q_block, q_lanes])
            grad = head_pair(do_ref[start : start + q_block, :])
            scores = mm_nt(keys[:n_keys], q) * scale
            probs = jnp.where(
                allowed(n_keys, q_block, start, length), jnp.exp(scores - lse_ref[g, b : b + 1, :]), 0.0
            )
            prob_grad = mm_nt(values[:n_keys], grad)
            center = jnp.sum(probs * prob_grad, axis=0, keepdims=True)
            score_grad = (probs * (prob_grad - center)).astype(BF)
            dq_ref[start : start + q_block, :] = head_join(mm_tn(score_grad, keys[:n_keys])) * scale
            dk_ref[:n_keys, :] += mm(score_grad, q)
            dv_ref[:n_keys, :] += mm(probs.astype(BF), grad)
        for p, half in enumerate((t, 1 - t)):
            at = pl.ds(pl.multiple_of(half * own_rows, own_rows), own_rows)
            cosine, sine = cos_ref[at, :], sin_ref[at, :]
            dq = dq_ref[at, :]
            outs[p][:, q_lanes] = (dq * cosine - swap_halves(dq) * sine).astype(BF)
            dk, dv = dk_ref[at, :] * scale, dv_ref[at, :]
            dk = dk + pltpu.roll(dk, HD, 1)
            dv = dv + pltpu.roll(dv, HD, 1)
            dk = dk * cosine - swap_halves(dk) * sine
            first = lax.broadcasted_iota(jnp.int32, dk.shape, 1) < HD
            outs[p][:, kv_lanes] = jnp.where(first, dk, dv).astype(BF)
        return carry

    lax.fori_loop(0, groups, per_group, 0)
    final.wait()
    sums.wait()


def attention_back(outer, q_block, length, qkv, lse, cosine, sine, grads, steps, dws, was_l, was_r, final):
    rows, width = qkv.shape
    n = len(steps)
    packed = dws[0].shape[2]
    hop = jax.ShapeDtypeStruct((GROUP, packed, D), BF)
    out = remote_call(
        functools.partial(attention_back_kernel, outer, q_block, steps),
        "attention_back",
        12,
        [jax.ShapeDtypeStruct((rows // 2, width), BF)] * 2 + [hop] * (1 + 2 * n),
        [SMEM] + [VM] * 6 + [ANY] * (3 * n + 3),
        [VM] * 2 + [ANY] * (1 + 2 * n),
        (length, qkv, lse, cosine, sine, *grads, *dws, *was_l, *was_r, *final),
        [
            pltpu.VMEM((rows, LANES), BF),
            pltpu.VMEM((rows, LANES), F32),
            pltpu.VMEM((rows, LANES), F32),
            pltpu.VMEM((rows, LANES), F32),
            *sums_scratch(n, packed),
            *final_scratch(packed),
        ],
        30 << 30,
    )
    return out[:2], out[2], out[3 : 3 + n], out[3 + n :]


def finish_kernel(outer, in_rows, len_ref, pos_ref, gate_ref, valid_ref, hidden_ref, hgrad_ref, x_ref, gain_ref, w_any, *refs):
    (no_ref, nx_ref, po_ref, px_ref, ao_ref, sg_ref), refs = refs[:6], refs[6:]
    n_experts = pos_ref.shape[2]
    ys, refs = refs[:n_experts], refs[n_experts:]
    dws, refs = refs[:3], refs[3:]
    done, refs = refs[:2], refs[2:]
    was_l, refs = refs[:2], refs[2:]
    was_r, refs = refs[:2], refs[2:]
    out_ref, tgrad_ref, gains_ref, qkv_ref, outw_ref = refs[:5]
    fins, to_l, to_r, refs = refs[5:8], refs[8:11], refs[11:14], refs[14:]
    (held, far, come, near, come_ab, last_ab, l_sem, s_sem, r_sem), refs = refs[:9], refs[9:]
    sums_a, refs = refs[:6], refs[6:]
    sums_b, refs = (*sums_a[:2], *refs[:4]), refs[4:]
    final_refs, refs = [refs[5 * k : 5 * k + 5] for k in range(3)], refs[15:]
    part_ref, theirs_ref, p_send, p_recv = refs[:4]
    refs = refs[4:]
    qp, q_core, q_y, q_z, q_send, q_recv = refs[:6]
    g_buf, g_come, g_z, g_send, g_recv, w_ref, w_sem = refs[6:]
    d, t, o, i = place()
    y, c = i // 2, i % 2
    rows = hidden_ref.shape[0]
    width = w_ref.shape[1]
    w_copy = pltpu.make_async_copy(w_any.at[:, pl.ds(0, width)], w_ref, w_sem)
    w_copy.start()
    greet_all(outer)
    sums = Sums(outer, (2, 3), [dws[2], dws[1]], was_l, was_r, to_l[:2], to_r[:2], *sums_a)
    last = Sums(outer, (3,), [dws[2]], to_l[:1], to_r[:1], to_l[2:], to_r[2:], *sums_b)
    came = [done, (to_l[1], to_r[1]), (to_l[2], to_r[2])]
    finals = [
        Final(outer, dws[k], *came[k], final_refs[k][0], sums_a[1], fins[k], *final_refs[k][1:]) for k in range(3)
    ]
    group = GroupSum(far, come, near, come_ab, last_ab, s_sem, r_sem)
    mixer = Mixer(ys, pos_ref, gate_ref, held, l_sem)
    sums.load()
    sums.send()

    w_copy.wait()
    part_ref[...] = mm_nt(px_ref[...], w_ref[...]).astype(BF)
    exchange = to_x(part_ref, theirs_ref, p_send, p_recv)
    exchange.start()

    each = qkv_ref.shape[0]

    def weights_block(k, carry):
        lanes = pl.ds(pl.multiple_of(k * GROUP * each, GROUP * each), GROUP * each)
        total = (mm_tn(no_ref[:, lanes], po_ref[...]) + mm_tn(nx_ref[:, lanes], px_ref[...])).astype(BF)
        for r in range(GROUP):
            qp[k, r // 2, r % 2, :, :width] = total[r * each : (r + 1) * each]
            at = pl.ds(pl.multiple_of((k * GROUP + r) * each, each), each)
            qp[k, r // 2, r % 2, :, width:] = ao_ref[at, :]
        return carry

    lax.fori_loop(0, outer, weights_block, 0)
    to_core = to_dp(1, qp.at[:, :, 1 - c], q_core, q_send.at[0], q_recv.at[0])
    to_core.start()
    finals[0].send()

    mixer.load(2, 0)
    mixer.load(3, 1)
    mixer.mix(2, 0, group.far.at[0])
    group.core[0].start()
    mixer.load(1, 0)
    to_core.wait()

    def add_core(k, carry):
        for r in range(2):
            qp[k, r, c] = (qp[k, r, c].astype(F32) + q_core[k, r].astype(F32)).astype(BF)
        return carry

    lax.fori_loop(0, outer, add_core, 0)
    to_y = to_dp(2, qp.at[:, 1 - y, c], q_y, q_send.at[1], q_recv.at[1])
    to_y.start()
    mixer.mix(3, 1, group.far.at[1])
    group.core[1].start()
    mixer.load(0, 1)

    exchange.wait()
    gain_grad = jnp.zeros((1, D), F32)
    quarter = rows // 4
    for p in range(4):
        at = slice(p * quarter, (p + 1) * quarter)
        normed_grad = mm_nt(po_ref[at], w_ref[:, :width]).astype(BF).astype(F32) + theirs_ref[at].astype(F32)
        x = x_ref[at].astype(F32)
        inverse = lax.rsqrt(jnp.mean(x * x, axis=-1, keepdims=True) + EPSILON)
        gain_grad = gain_grad + jnp.sum(normed_grad * (x * inverse), axis=0, keepdims=True)
        scaled = normed_grad * gain_ref[...]
        tgrad_ref[at] = (
            hgrad_ref[at]
            + inverse * scaled
            - x * (inverse * inverse * inverse * jnp.mean(scaled * x, axis=-1, keepdims=True))
        )
    g_buf[0, 0:1, :] = gain_grad
    g_buf[0, 1:2, :] = sg_ref[...]
    g_buf[0, 2:8, :] = jnp.zeros((6, D), F32)
    g_moves = [
        to_x(g_buf.at[0], g_come.at[0], g_send.at[0], g_recv.at[0]),
        to_dp(1, g_buf.at[1], g_come.at[1], g_send.at[1], g_recv.at[1]),
        to_dp(2, g_buf.at[2], g_come.at[2], g_send.at[2], g_recv.at[2]),
    ]
    g_moves[0].start()
    g_moves[0].wait()
    g_buf[1] = g_buf[0] + g_come[0]
    g_moves[1].start()
    to_y.wait()

    def add_y(k, carry):
        qp[k, y, c] = (qp[k, y, c].astype(F32) + q_y[k].astype(F32)).astype(BF)
        return carry

    lax.fori_loop(0, outer, add_y, 0)
    z_moves = []
    for k in range(1, outer):
        peer = (o + k) % outer
        z_moves.append(
            pltpu.make_async_remote_copy(
                qp.at[peer, y, c],
                q_z.at[k - 1],
                q_send.at[1 + k],
                q_recv.at[1 + k],
                device_id=(peer * GROUP + i, t),
                device_id_type=MESH,
            )
        )
    for move in z_moves:
        move.start()
    group.core[1].wait_recv()
    mixer.mix(1, 0, group.near.at[1], group.come.at[1])
    group.a.start()
    group.b[1].start()
    sums.wait()
    last.load()
    last.send()
    g_moves[1].wait()
    g_buf[2] = g_buf[1] + g_come[1]
    g_moves[2].start()
    group.core[0].wait_recv()
    mixer.mix(0, 1, group.near.at[0], group.come.at[0])
    group.b[0].start()
    g_moves[2].wait()
    g_z[0] = g_buf[2] + g_come[2]
    gz_moves = []
    for k in range(1, outer):
        peer = (o + k) % outer
        gz_moves.append(
            pltpu.make_async_remote_copy(
                g_z.at[0],
                g_z.at[k],
                g_send.at[2 + k],
                g_recv.at[2 + k],
                device_id=(peer * GROUP + i, t),
                device_id_type=MESH,
            )
        )
    for move in gz_moves:
        move.start()
    group.second()
    finals[1].send()
    for move in z_moves:
        move.wait()
    total = qp[o, y, c].astype(F32)
    for k in range(1, outer):
        total = total + q_z[k - 1].astype(F32)
    qkv_ref[...] = total[:, :width]
    outw_ref[...] = total[:, width:]
    for move in gz_moves:
        move.wait()
    gains = g_z[(o + outer) % outer]
    for k in range(1, outer):
        gains = gains + g_z[(o - k + outer) % outer]
    gains_ref[...] = gains
    for p in range(2):
        at = slice(p * rows // 2, (p + 1) * rows // 2)
        out_ref[at] = jnp.where(valid_ref[at] > 0, hidden_ref[at] + group.terms(p), 0.0).astype(BF)
    last.wait()
    finals[2].send()
    group.sent()
    for final in finals:
        final.wait()


def finish(outer, in_rows, length, pos, gate, valid, hidden, hgrad, x, gain, weights_full, extra, ys, dws, done, was_l, was_r):
    rows = hidden.shape[0]
    n = len(ys)
    packed = dws[0].shape[2]
    width = weights_full.shape[1] // 2
    heads = width // 2
    each = D // (outer * GROUP)
    hop = jax.ShapeDtypeStruct((GROUP, packed, D), BF)
    columns = width + heads
    return remote_call(
        functools.partial(finish_kernel, outer, in_rows),
        "finish",
        11,
        [
            jax.ShapeDtypeStruct((rows, D), BF),
            jax.ShapeDtypeStruct((rows, D), F32),
            jax.ShapeDtypeStruct((8, D), F32),
            jax.ShapeDtypeStruct((each, width), F32),
            jax.ShapeDtypeStruct((each, heads), F32),
        ]
        + [hop] * 9,
        [SMEM] + [VM] * 7 + [ANY] + [VM] * 6 + [ANY] * (n + 9),
        [VM] * 5 + [ANY] * 9,
        (length, pos, gate, valid, hidden, hgrad, x, gain.reshape(1, D), weights_full, *extra, *ys, *dws, *done, *was_l, *was_r),
        [
            *group_scratch(2 * rows, n),
            *sums_scratch(2, packed),
            *again(sums_scratch(1, packed)),
            *final_scratch(packed) * 3,
            pltpu.VMEM((rows, D), BF),
            pltpu.VMEM((rows, D), BF),
            pltpu.SemaphoreType.DMA,
            pltpu.SemaphoreType.DMA,
            pltpu.VMEM((outer, 2, 2, each, columns), BF),
            pltpu.VMEM((outer, 2, each, columns), BF),
            pltpu.VMEM((outer, each, columns), BF),
            pltpu.VMEM((outer - 1, each, columns), BF),
            pltpu.SemaphoreType.DMA((1 + outer,)),
            pltpu.SemaphoreType.DMA((1 + outer,)),
            pltpu.VMEM((3, 8, D), F32),
            pltpu.VMEM((3, 8, D), F32),
            pltpu.VMEM((outer, 8, D), F32),
            pltpu.SemaphoreType.DMA((2 + outer,)),
            pltpu.SemaphoreType.DMA((2 + outer,)),
            pltpu.VMEM((D, width), BF),
            pltpu.SemaphoreType.DMA,
        ],
        30 << 30,
    )


def settle_kernel(n, in_rows, idx_ref, *refs):
    sources, (in_ref, down_ref) = refs[:n], refs[n:]
    j = pl.program_id(0)
    for k in range(n):

        @pl.when(j == k)
        def _(k=k):
            in_ref[0] = sources[k][0, :in_rows, :].astype(F32)
            down_ref[0] = sources[k][0, in_rows:, :].astype(F32)


def settle_experts(idx, fins, in_rows):
    n = len(fins)
    _, packed, _ = fins[0].shape
    experts = n * GROUP

    def source(k):
        return lambda j, m, idx_ref: (jnp.where(j == k, m, jnp.where(j < k, 0, GROUP - 1)), 0, 0)

    def target(j, m, idx_ref):
        return ((idx_ref[1] ^ m) * n + j, 0, 0)

    return pl.pallas_call(
        functools.partial(settle_kernel, n, in_rows),
        name="settle_experts",
        out_shape=[
            jax.ShapeDtypeStruct((experts, in_rows, D), F32),
            jax.ShapeDtypeStruct((experts, packed - in_rows, D), F32),
        ],
        grid_spec=pltpu.PrefetchScalarGridSpec(
            num_scalar_prefetch=1,
            grid=(n, GROUP),
            in_specs=[pl.BlockSpec((1, packed, D), source(k)) for k in range(n)],
            out_specs=[pl.BlockSpec((1, in_rows, D), target), pl.BlockSpec((1, packed - in_rows, D), target)],
        ),
        compiler_params=pltpu.CompilerParams(vmem_limit_bytes=VMEM_LIMIT),
        cost_estimate=pl.CostEstimate(flops=0, bytes_accessed=9 << 20, transcendentals=0),
    )(idx, *fins)


def layer(
    tokens,
    cotangent,
    lengths,
    expert_ids,
    gate_values,
    first_gain,
    qkv_weight,
    attn_out_weight,
    second_gain,
    expert_in_weight,
    expert_out_weight,
):
    rows = tokens.shape[0]
    n_tensor, n_dp = lax.axis_size("tensor"), lax.axis_size("dp")
    outer = n_dp // GROUP
    slot_rows = rows * n_tensor
    d, t = lax.axis_index("dp"), lax.axis_index("tensor")
    o, i = d // GROUP, d % GROUP
    length = lengths[0]
    idx = jnp.stack([o, i, t, length]).astype(jnp.int32)
    width = qkv_weight.shape[1] * qkv_weight.shape[2]
    experts_local, in_rows, _ = expert_in_weight.shape
    down_rows = expert_out_weight.shape[1]
    own_experts = experts_local // GROUP
    pair = n_tensor == 2
    q_block = 256
    half = rows // 2

    def across(v, m):
        return lax.ppermute(v, "dp", [(a, a ^ m) for a in range(n_dp)])

    def beside(v):
        return lax.ppermute(v, "tensor", [(0, 1), (1, 0)])

    def hop(pairs):
        up = [(a, a + GROUP) for a in range(n_dp - GROUP)]
        down = [(b, a) for a, b in up]
        return [(lax.ppermute(a, "dp", up), lax.ppermute(b, "dp", down)) for a, b in pairs]

    def gather_group(pieces):
        if pair:
            a, b = pieces
            ax, by, ay, bx = beside(a), across(b, 2), across(a, 2), beside(b)
            axy, bxy = across(ax, 2), beside(by)
            slots = [[a, ax, b, bx], [ay, axy, by, bxy]]
        else:
            slot = lax.all_gather(pieces[0], "tensor", axis=0, tiled=True)
            slots = [[slot], [across(slot, 2)]]
        return slots + [[across(p, 1) for p in s] for s in slots]

    positions = t * rows + jnp.arange(rows, dtype=jnp.int32)
    valid_rows = positions < length
    n_experts = experts_local * n_tensor
    chosen = expert_ids.T[None] == jnp.arange(n_experts, dtype=jnp.int32)[:, None, None]
    gates = jnp.sum(jnp.where(chosen, gate_values.T[None].astype(F32), 0.0), axis=1)
    gates = jnp.where(valid_rows[None, :], gates, 0.0).astype(BF)
    if pair:
        gates_x = beside(gates)
        slot_gates = jnp.concatenate(
            [gates[:, :half], gates_x[:, :half], gates[:, half:], gates_x[:, half:]], axis=1
        )
    else:
        slot_gates = lax.all_gather(gates, "tensor", axis=1, tiled=True)
    gates_y = across(slot_gates, 2)
    all_gates = jnp.stack([slot_gates, gates_y, across(slot_gates, 1), across(gates_y, 1)])
    own_gates = lax.dynamic_slice_in_dim(
        all_gates, t * experts_local + i * own_experts, own_experts, axis=1
    ).astype(F32)
    named = own_gates > 0
    before = (
        lax.broadcasted_iota(jnp.int32, (slot_rows, slot_rows), 0)
        < lax.broadcasted_iota(jnp.int32, (slot_rows, slot_rows), 1)
    ).astype(BF)
    ranks = jnp.dot(
        named.astype(BF).reshape(GROUP * own_experts, slot_rows), before, preferred_element_type=F32
    ).reshape(GROUP, own_experts, slot_rows)
    pos = jnp.where(named, ranks, -1.0).astype(jnp.int32)
    pos_columns, gate_columns = jnp.swapaxes(pos, 1, 2), jnp.swapaxes(own_gates, 1, 2)

    x = tokens.astype(F32)
    inverse_one = lax.rsqrt(jnp.mean(x * x, axis=-1, keepdims=True) + EPSILON)
    normed_one = (x * inverse_one * first_gain).astype(BF)
    cosine, sine = rope_tables(slot_rows)
    dy = jnp.where(valid_rows[:, None], cotangent, jnp.zeros_like(cotangent))
    expert_outs, row_grads, weight_grads = [], [], []
    if pair and outer == 4:
        other = beside(normed_one)
        out_shard = attn_out_weight.T
        shards = jnp.concatenate([qkv_weight.reshape(-1, width), out_shard, beside(out_shard)], axis=1)
        weights_full = lax.all_gather(shards, "dp", axis=0, tiled=True)
        by_distance = pack_weights(idx, expert_in_weight, expert_out_weight)
        by_distance = [by_distance[0]] + [across(by_distance[m], m) for m in range(1, GROUP)]
        own_weights = [jnp.stack([v[j] for v in by_distance]) for j in range(own_experts)]
        dys = [dy[:half], dy[half:]]
        main, dy_moved, one_l, one_r = attention(
            outer, q_block, lengths, normed_one, other, weights_full, cosine, sine, tokens, second_gain, dys, own_weights[:3]
        )
        qkv, lse, attn_own, attn_other, hidden, *normed_two = main
        attn_parts = [attn_own, attn_other]
        gathered, out_grads, moved_l, moved_r = spread(
            outer,
            pos,
            own_gates,
            normed_two,
            [*dys, *dy_moved],
            (1, 2, 2),
            [own_weights[3], one_l[0], one_l[1]],
            [own_weights[3], one_r[0], one_r[1]],
        )
        one_l, one_r = [*one_l, moved_l[0]], [*one_r, moved_r[0]]
        two_l, two_r = [*moved_l[1:]], [*moved_r[1:]]
        expert_rows, moved_l, moved_r = hand_out(
            outer, pos, normed_two, gathered, (3, 2), [two_l[0], one_l[2]], [two_r[0], one_r[2]]
        )
        three_l, three_r = [moved_l[0]], [moved_r[0]]
        two_l.append(moved_l[1])
        two_r.append(moved_r[1])
        hop_plans = [
            lambda: ((3, 2), [two_l[1], one_l[3]], [two_r[1], one_r[3]]),
            lambda: ((3,), [two_l[2]], [two_r[2]]),
            lambda: ((3,), [two_l[3]], [two_r[3]]),
            lambda: ((), [], []),
        ]
        sums_l, sums_r = [], []
        for j in range(own_experts):
            first_grad = weight_grads[:1]
            sum_plan = ((j,), first_grad, sums_l or first_grad, sums_r or first_grad) if j else ((), [], [], [])
            (y, dx, dw), moved_l, moved_r, sums_l, sums_r = expert_step(
                j,
                outer,
                in_rows,
                down_rows,
                expert_rows,
                out_grads,
                own_weights[j],
                [one_l[j], two_l[j], three_l[j]],
                [one_r[j], two_r[j], three_r[j]],
                hop_plans[j](),
                sum_plan,
            )
            three_l.extend(moved_l[:1])
            three_r.extend(moved_r[:1])
            two_l.extend(moved_l[1:])
            two_r.extend(moved_r[1:])
            expert_outs.append(y)
            row_grads.append(dx)
            weight_grads.append(dw)
        valid_column = valid_rows.astype(F32)[:, None]
        _, dw_b, dw_c, dw_d = weight_grads
        main, sum_l, sum_r = rows_back(
            outer,
            pos_columns,
            valid_column,
            hidden,
            cotangent,
            second_gain,
            weights_full,
            row_grads,
            (1, 1),
            ((2, 0), (2, 1)),
            [dw_b, dw_c],
            [dw_b, dw_c],
            [dw_b, dw_c],
        )
        hidden_grad, branch_grad, second_gain_part, attn_grad_own, attn_grad_other = main
        projected, fin_a, three_l, three_r = attention_back(
            outer,
            q_block,
            lengths,
            qkv,
            lse,
            cosine,
            sine,
            [attn_grad_own, attn_grad_other],
            (3, 1),
            [dw_b, dw_d],
            [sum_l[2], dw_d],
            [sum_r[2], dw_d],
            [weight_grads[0], sums_l[0], sums_r[0]],
        )
        out_own, out_other = (mm_tn(branch_grad, part).astype(BF) for part in attn_parts)
        attn_out_part = (out_own.astype(F32) + beside(out_other).astype(F32)).astype(BF)
        output, tokens_grad, gains, qkv_grad, attn_out_grad, *fins = finish(
            outer,
            in_rows,
            lengths,
            pos_columns,
            gate_columns,
            valid_column,
            hidden,
            hidden_grad,
            tokens,
            first_gain,
            weights_full,
            [normed_one, other, *projected, attn_out_part, second_gain_part],
            expert_outs,
            [dw_b, dw_c, dw_d],
            [three_l[0], three_r[0]],
            [three_l[1], sum_l[3]],
            [three_r[1], sum_r[3]],
        )
        expert_in_grad, expert_out_grad = settle_experts(idx, [fin_a, *fins[:3]], in_rows)
        return (
            output,
            tokens_grad,
            gains[0],
            qkv_grad.reshape(qkv_weight.shape),
            attn_out_grad.T,
            gains[1],
            expert_in_grad,
            expert_out_grad,
        )
    else:
        qkv_full = lax.all_gather(qkv_weight.reshape(qkv_weight.shape[0], width), "dp", axis=0, tiled=True)
        out_full = lax.all_gather(attn_out_weight.T, "dp", axis=0, tiled=True)
        by_distance = pack_weights(idx, expert_in_weight, expert_out_weight)
        by_distance = [by_distance[0]] + [across(by_distance[m], m) for m in range(1, GROUP)]
        own_weights = [jnp.stack([v[j] for v in by_distance]) for j in range(own_experts)]
        hops = [hop([(own, own) for own in own_weights])]
        if pair:
            out_parts = [out_full, beside(out_full)]
        else:
            gathered = lax.all_gather(out_full, "tensor", axis=0)
            out_parts = [gathered[k] for k in range(n_tensor)]

        if pair:
            other = beside(normed_one)
            normed_all = jnp.where(
                t == 0,
                jnp.concatenate([normed_one, other], axis=0),
                jnp.concatenate([other, normed_one], axis=0),
            )
        else:
            normed_all = lax.all_gather(normed_one, "tensor", axis=0, tiled=True)
        qkv = qkv_project(normed_all, qkv_full, cosine, sine)
        *attended, lse = attend(idx, qkv, 2 if pair else 1, q_block)
        if pair:
            attn_parts = [attended[0], beside(attended[1])]
        else:
            heads = attended[0].shape[1]
            exchanged = lax.all_to_all(attended[0].reshape(n_tensor, rows, heads), "tensor", 0, 0)
            attn_parts = [exchanged[k] for k in range(n_tensor)]
        attn_parts, hops[0] = lax.optimization_barrier((attn_parts, hops[0]))
        if outer > 2:
            hops.append(hop(hops[0]))
        hidden, *normed_two = project_out(tokens, second_gain, attn_parts, out_parts, 2 if pair else 1)

        dy_slots = gather_group([dy[:half], dy[half:]] if pair else [dy])
        out_grads = [dispatch(pos[s], own_gates[s], dy_slots[s], True) for s in range(GROUP)]
        normed_slots = gather_group(normed_two)
        normed_slots, out_grads, hops = lax.optimization_barrier((normed_slots, out_grads, hops))
        while len(hops) < outer - 1:
            hops.append(hop(hops[-1]))
        expert_rows = [dispatch(pos[s], own_gates[s], normed_slots[s], False) for s in range(GROUP)]

        for j in range(own_experts):
            if j:
                idx, expert_outs[-1] = lax.optimization_barrier((idx, expert_outs[-1]))
            y, dx, dw = expert(
                idx,
                j,
                outer,
                in_rows,
                down_rows,
                expert_rows,
                out_grads,
                own_weights[j],
                [h[j][0] for h in hops],
                [h[j][1] for h in hops],
            )
            expert_outs.append(y)
            row_grads.append(dx)
            weight_grads.append(dw)

    def sum_group(sources, scaled):
        def part(s, add, n_outs):
            return combine(pos_columns[s], gate_columns[s], sources, s, scaled, add, n_outs)

        far = [part(2, None, 1)[0], part(3, None, 1)[0]]
        near = [across(v, 1) for v in far]
        if pair:
            ay, axy, by, bxy = part(1, near[1], 4)
            a, ax, b, bx = part(0, near[0], 4)

            def add(p, q):
                return (p.astype(F32) + q.astype(F32)).astype(BF)

            a, ax = add(a, across(ay, 2)), add(ax, across(axy, 2))
            b, by = add(b, beside(bx)), add(by, beside(bxy))
            return [[a, beside(ax)], [b, across(by, 2)]]
        (y,) = part(1, near[1], 1)
        (v,) = part(0, near[0], 1)
        v = (v.astype(F32) + across(y, 2).astype(F32)).astype(BF)
        return [[lax.psum_scatter(v, "tensor", scatter_dimension=0, tiled=True)]]

    valid_column = valid_rows.astype(F32)[:, None]
    normed_two_grad = sum_group(row_grads, False)
    hidden_grad, branch_grad, second_gain_part, *attn_grads = hidden_back(
        valid_column, hidden, cotangent, second_gain, normed_two_grad, out_parts
    )
    if pair:
        attn_grads = [attn_grads[0], beside(attn_grads[1])]
    else:
        attn_grads = [
            lax.all_to_all(jnp.stack(attn_grads), "tensor", 0, 0).reshape(slot_rows, attn_grads[0].shape[1])
        ]
    projected_grads = attend_back(idx, qkv, lse, cosine, sine, attn_grads, q_block)

    def first_norm_part(v):
        return lax.dot_general(v, qkv_full, (((1,), (1,)), ((), ())), preferred_element_type=F32).astype(BF)

    if pair:
        theirs = beside(first_norm_part(projected_grads[1]))
        normed_one_grad = first_norm_part(projected_grads[0]).astype(F32) + theirs.astype(F32)
        qkv_part = mm_tn(normed_one, projected_grads[0]) + mm_tn(other, projected_grads[1])
    else:
        normed_one_grad = lax.psum_scatter(
            first_norm_part(projected_grads[0]), "tensor", scatter_dimension=0, tiled=True
        ).astype(F32)
        qkv_part = mm_tn(normed_all, projected_grads[0])
    first_gain_part = jnp.sum(normed_one_grad * (x * inverse_one), axis=0)
    scaled = normed_one_grad * first_gain
    tokens_grad = (
        hidden_grad
        + inverse_one * scaled
        - x * (inverse_one * inverse_one * inverse_one * jnp.mean(scaled * x, axis=-1, keepdims=True))
    )

    mixture = sum_group(expert_outs, True)
    mixture = jnp.concatenate([sum(v.astype(F32) for v in terms) for terms in mixture], axis=0)
    output = jnp.where(valid_rows[:, None], hidden + mixture, 0.0).astype(BF)

    outer_groups = [[a * GROUP + b for a in range(outer)] for b in range(GROUP)]
    received = [[] for _ in range(GROUP)]
    for dw in weight_grads:
        mine = lax.psum_scatter(dw, "dp", scatter_dimension=0, tiled=True, axis_index_groups=outer_groups)
        for m in range(GROUP):
            block = mine[0, m]
            received[m].append(block if m == 0 else across(block, m))
    by_distance = jnp.stack([jnp.stack(v) for v in received])
    by_source = jnp.take(by_distance, jnp.arange(GROUP) ^ i, axis=0).reshape(
        experts_local, in_rows + down_rows, D
    )
    expert_in_grad = by_source[:, :in_rows].astype(F32)
    expert_out_grad = by_source[:, in_rows:].astype(F32)

    attn_out_parts = [mm_tn(branch_grad, part).astype(BF) for part in attn_parts]
    if pair:
        attn_out_part = (attn_out_parts[0].astype(F32) + beside(attn_out_parts[1]).astype(F32)).astype(BF)
    else:
        attn_out_part = lax.psum_scatter(jnp.stack(attn_out_parts), "tensor", scatter_dimension=0, tiled=True)[0]
    qkv_grad = lax.psum_scatter(qkv_part.astype(BF), "dp", scatter_dimension=0, tiled=True).astype(F32)
    attn_out_grad = lax.psum_scatter(attn_out_part, "dp", scatter_dimension=0, tiled=True).astype(F32).T

    gains = jnp.stack([first_gain_part, second_gain_part[0]])
    if pair:
        gains = gains + beside(gains)
    else:
        gains = lax.psum(gains, "tensor")
    step = 1
    while step < n_dp:
        gains = gains + across(gains, step)
        step *= 2
    return (
        output,
        tokens_grad,
        gains[0],
        qkv_grad.reshape(qkv_weight.shape),
        attn_out_grad,
        gains[1],
        expert_in_grad,
        expert_out_grad,
    )


def solution(mesh):
    placed = (
        P(("dp", "tensor"), None),
        P(("dp", "tensor"), None),
        P("dp"),
        P(("dp", "tensor"), None),
        P(("dp", "tensor"), None),
        P(),
        P("dp", "tensor", None),
        P("tensor", "dp"),
        P(),
        P("tensor", "dp", None),
        P("tensor", "dp", None),
    )
    return jax.shard_map(
        layer,
        mesh=mesh,
        in_specs=placed,
        out_specs=(
            P(("dp", "tensor"), None),
            P(("dp", "tensor"), None),
            P(),
            P("dp", "tensor", None),
            P("tensor", "dp"),
            P(),
            P("tensor", "dp", None),
            P("tensor", "dp", None),
        ),
        check_vma=False,
    )
```

```python
import functools
import math

import jax
import jax.numpy as jnp
from jax import lax
from jax.experimental import pallas as pl
from jax.experimental.pallas import tpu as pltpu
from jax.sharding import PartitionSpec as P

D = 1024
HD = 64
FF = 512
G = 2
CAP = 288
GROUP = 4
LANES = 128

EPSILON = 1e-06
THETA = 10000.0
NEGATIVE = -1e30
BF = jnp.bfloat16
F32 = jnp.float32
VMEM_LIMIT = 60 * 1024 * 1024
MESH = pl.DeviceIdType.MESH

ANY = pl.BlockSpec(memory_space=pl.ANY)
SMEM = pl.BlockSpec(memory_space=pltpu.SMEM)
VM = pl.BlockSpec(memory_space=pltpu.VMEM)


def mm(a, b):
    return lax.dot_general(a, b, (((1,), (0,)), ((), ())), preferred_element_type=F32)


def mm_nt(a, b):
    return lax.dot_general(a, b, (((1,), (1,)), ((), ())), preferred_element_type=F32)


def mm_tn(a, b):
    return lax.dot_general(a, b, (((0,), (0,)), ((), ())), preferred_element_type=F32)


def call(kernel, name, out_shape, in_specs, out_specs, args, scratch=(), flops=0, moved=0, **more):
    return pl.pallas_call(
        kernel,
        name=name,
        out_shape=out_shape,
        in_specs=in_specs,
        out_specs=out_specs,
        scratch_shapes=list(scratch),
        compiler_params=pltpu.CompilerParams(vmem_limit_bytes=VMEM_LIMIT),
        cost_estimate=pl.CostEstimate(flops=flops, bytes_accessed=moved, transcendentals=0),
        **more,
    )(*args)


def rope_tables(total_rows):
    half = HD // 2
    positions = jnp.arange(total_rows).astype(F32)
    frequency = THETA ** (-(jnp.arange(half).astype(F32) * 2.0 / HD))
    angles = positions[:, None] * frequency[None, :]
    cosine, sine = jnp.cos(angles), jnp.sin(angles)
    return (
        jnp.concatenate([cosine] * 4, axis=1),
        jnp.concatenate([-sine, sine, -sine, sine], axis=1),
    )


def swap_halves(v):
    lane = lax.broadcasted_iota(jnp.int32, v.shape, 1)
    return jnp.where(lane % HD < HD // 2, pltpu.roll(v, LANES - HD // 2, 1), pltpu.roll(v, HD // 2, 1))


def qkv_kernel(n_ref, w_ref, cos_ref, sin_ref, out_ref):
    projected = mm(n_ref[...], w_ref[...])
    cosine, sine = cos_ref[...], sin_ref[...]
    key_lanes = lax.broadcasted_iota(jnp.int32, cosine.shape, 1) < HD
    for g in range(projected.shape[1] // (2 * LANES)):
        q = projected[:, g * 2 * LANES : g * 2 * LANES + LANES]
        kv = projected[:, g * 2 * LANES + LANES : (g + 1) * 2 * LANES]
        q = q * cosine + swap_halves(q) * sine
        kv = jnp.where(key_lanes, kv * cosine + swap_halves(kv) * sine, kv)
        out_ref[:, g * 2 * LANES : g * 2 * LANES + LANES] = q.astype(BF)
        out_ref[:, g * 2 * LANES + LANES : (g + 1) * 2 * LANES] = kv.astype(BF)


def qkv_project(normed, weight, cosine, sine):
    rows, width = normed.shape[0], weight.shape[1]
    block = 256
    return pl.pallas_call(
        qkv_kernel,
        name="qkv_rope",
        grid=(rows // block,),
        out_shape=jax.ShapeDtypeStruct((rows, width), BF),
        in_specs=[
            pl.BlockSpec((block, D), lambda b: (b, 0)),
            pl.BlockSpec((D, width), lambda b: (0, 0)),
            pl.BlockSpec((block, LANES), lambda b: (b, 0)),
            pl.BlockSpec((block, LANES), lambda b: (b, 0)),
        ],
        out_specs=pl.BlockSpec((block, width), lambda b: (b, 0)),
        compiler_params=pltpu.CompilerParams(vmem_limit_bytes=VMEM_LIMIT),
        cost_estimate=pl.CostEstimate(flops=2 * rows * D * width, bytes_accessed=6 << 20, transcendentals=0),
    )(normed, weight, cosine, sine)


def head_pair(v):
    first = lax.broadcasted_iota(jnp.int32, v.shape, 1) < HD
    zero = jnp.zeros_like(v)
    return jnp.concatenate([jnp.where(first, v, zero), jnp.where(first, zero, v)], axis=0)


def head_join(v):
    n = v.shape[0] // 2
    first = lax.broadcasted_iota(jnp.int32, (n, LANES), 1) < HD
    return jnp.where(first, v[:n], v[n:])


def doubled(kv):
    first = lax.broadcasted_iota(jnp.int32, kv.shape, 1) < HD
    other = pltpu.roll(kv.astype(F32), HD, 1).astype(BF)
    return jnp.where(first, kv, other), jnp.where(first, other, kv)


def allowed(n_keys, q_block, q_start, length):
    key = lax.broadcasted_iota(jnp.int32, (n_keys, 2 * q_block), 0)
    lane = lax.broadcasted_iota(jnp.int32, (n_keys, 2 * q_block), 1)
    query = q_start + jnp.where(lane < q_block, lane, lane - q_block)
    return (key <= query) & (key < length)


def attend_kernel(q_block, idx_ref, qkv_ref, *out_refs):
    outs, lse_ref = out_refs[:-1], out_refs[-1]
    rows = qkv_ref.shape[0]
    length = idx_ref[3]
    keys, values = doubled(qkv_ref[:, LANES:])
    for b in range(rows // q_block):
        start, n_keys = b * q_block, (b + 1) * q_block
        q = head_pair(qkv_ref[start : start + q_block, :LANES])
        scores = mm_nt(keys[:n_keys], q) * (1.0 / math.sqrt(HD))
        scores = jnp.where(allowed(n_keys, q_block, start, length), scores, NEGATIVE)
        largest = jnp.max(scores, axis=0, keepdims=True)
        expon = jnp.exp(scores - largest)
        totals = jnp.sum(expon, axis=0, keepdims=True)
        probs = (expon * (1.0 / totals)).astype(BF)
        mixed = head_join(mm_tn(probs, values[:n_keys])).astype(BF)
        lse_ref[0, b : b + 1, :] = largest + jnp.log(totals)
        if len(outs) == 1:
            outs[0][start : start + q_block] = mixed
        else:
            own_rows = rows // 2
            half, at = start // own_rows, start % own_rows
            mine = idx_ref[2] == half

            @pl.when(mine)
            def _():
                outs[0][at : at + q_block] = mixed

            @pl.when(jnp.logical_not(mine))
            def _():
                outs[1][at : at + q_block] = mixed


def attend(idx, qkv, parts, q_block):
    rows, groups = qkv.shape[0], qkv.shape[1] // (2 * LANES)
    out = jax.ShapeDtypeStruct((rows // parts, groups * LANES), BF)
    return pl.pallas_call(
        functools.partial(attend_kernel, q_block),
        name="attend",
        grid=(groups,),
        out_shape=[out] * parts + [jax.ShapeDtypeStruct((groups, rows // q_block, 2 * q_block), F32)],
        in_specs=[SMEM, pl.BlockSpec((rows, 2 * LANES), lambda g: (0, g))],
        out_specs=[pl.BlockSpec((rows // parts, LANES), lambda g: (0, g))] * parts
        + [pl.BlockSpec((1, rows // q_block, 2 * q_block), lambda g: (g, 0, 0))],
        compiler_params=pltpu.CompilerParams(vmem_limit_bytes=VMEM_LIMIT),
        cost_estimate=pl.CostEstimate(flops=14 << 30, bytes_accessed=4 << 20, transcendentals=0),
    )(idx, qkv)


def attend_back_kernel(q_block, n_grads, idx_ref, qkv_ref, lse_ref, cos_ref, sin_ref, *refs):
    grads, outs = refs[:n_grads], refs[n_grads : 2 * n_grads]
    do_ref, dq_ref, dk_ref, dv_ref = refs[2 * n_grads :]
    rows = qkv_ref.shape[0]
    own_rows = rows // n_grads
    length = idx_ref[3]
    for p in range(n_grads):
        at = pl.multiple_of((p ^ idx_ref[2] if n_grads == 2 else 0) * own_rows, own_rows)
        do_ref[pl.ds(at, own_rows), :] = grads[p][...]
    keys, values = doubled(qkv_ref[:, LANES:])
    dk_ref[...] = jnp.zeros_like(dk_ref)
    dv_ref[...] = jnp.zeros_like(dv_ref)
    scale = 1.0 / math.sqrt(HD)
    for b in range(rows // q_block):
        start, n_keys = b * q_block, (b + 1) * q_block
        q = head_pair(qkv_ref[start : start + q_block, :LANES])
        grad = head_pair(do_ref[start : start + q_block, :])
        scores = mm_nt(keys[:n_keys], q) * scale
        probs = jnp.where(
            allowed(n_keys, q_block, start, length), jnp.exp(scores - lse_ref[0, b : b + 1, :]), 0.0
        )
        prob_grad = mm_nt(values[:n_keys], grad)
        center = jnp.sum(probs * prob_grad, axis=0, keepdims=True)
        score_grad = (probs * (prob_grad - center)).astype(BF)
        dq_ref[start : start + q_block, :] = head_join(mm_tn(score_grad, keys[:n_keys])) * scale
        dk_ref[:n_keys, :] += mm(score_grad, q)
        dv_ref[:n_keys, :] += mm(probs.astype(BF), grad)
    cosine, sine = cos_ref[...], sin_ref[...]
    dq = dq_ref[...]
    dq = (dq * cosine - swap_halves(dq) * sine).astype(BF)
    dk, dv = dk_ref[...] * scale, dv_ref[...]
    dk = dk + pltpu.roll(dk, HD, 1)
    dv = dv + pltpu.roll(dv, HD, 1)
    dk = dk * cosine - swap_halves(dk) * sine
    first = lax.broadcasted_iota(jnp.int32, dk.shape, 1) < HD
    dkv = jnp.where(first, dk, dv).astype(BF)
    if n_grads == 1:
        outs[0][:, :LANES] = dq
        outs[0][:, LANES:] = dkv
    else:
        do_ref[...] = dq
        for p in range(2):
            at = pl.multiple_of((p ^ idx_ref[2]) * own_rows, own_rows)
            outs[p][:, :LANES] = do_ref[pl.ds(at, own_rows), :]
        do_ref[...] = dkv
        for p in range(2):
            at = pl.multiple_of((p ^ idx_ref[2]) * own_rows, own_rows)
            outs[p][:, LANES:] = do_ref[pl.ds(at, own_rows), :]


def attend_back(idx, qkv, lse, cosine, sine, grads, q_block):
    rows, groups, parts = qkv.shape[0], qkv.shape[1] // (2 * LANES), len(grads)
    return pl.pallas_call(
        functools.partial(attend_back_kernel, q_block, parts),
        name="attend_back",
        grid=(groups,),
        out_shape=[jax.ShapeDtypeStruct((rows // parts, groups * 2 * LANES), BF)] * parts,
        in_specs=[
            SMEM,
            pl.BlockSpec((rows, 2 * LANES), lambda g: (0, g)),
            pl.BlockSpec((1, rows // q_block, 2 * q_block), lambda g: (g, 0, 0)),
            pl.BlockSpec((rows, LANES), lambda g: (0, 0)),
            pl.BlockSpec((rows, LANES), lambda g: (0, 0)),
        ]
        + [pl.BlockSpec((rows // parts, LANES), lambda g: (0, g))] * parts,
        out_specs=[pl.BlockSpec((rows // parts, 2 * LANES), lambda g: (0, g))] * parts,
        scratch_shapes=[pltpu.VMEM((rows, LANES), BF)] + [pltpu.VMEM((rows, LANES), F32)] * 3,
        compiler_params=pltpu.CompilerParams(vmem_limit_bytes=VMEM_LIMIT),
        cost_estimate=pl.CostEstimate(flops=30 << 30, bytes_accessed=6 << 20, transcendentals=0),
    )(idx, qkv, lse, cosine, sine, *grads)


def project_out_kernel(n_parts, pieces, x_ref, gain_ref, *refs):
    attns, weights = refs[:n_parts], refs[n_parts : 2 * n_parts]
    hidden_ref, normed_refs = refs[2 * n_parts], refs[2 * n_parts + 1 :]
    rows = x_ref.shape[0] // pieces
    for p in range(pieces):
        at = slice(p * rows, (p + 1) * rows)
        hidden = x_ref[at].astype(F32)
        for a, w in zip(attns, weights, strict=True):
            hidden = hidden + mm_nt(a[at], w[...])
        inverse = lax.rsqrt(jnp.mean(hidden * hidden, axis=-1, keepdims=True) + EPSILON)
        hidden_ref[at] = hidden
        normed_refs[p][...] = (hidden * inverse * gain_ref[...]).astype(BF)


def project_out(x, gain, attns, weights, pieces):
    rows = x.shape[0]
    n = len(attns)
    return call(
        functools.partial(project_out_kernel, n, pieces),
        "project_out",
        [jax.ShapeDtypeStruct((rows, D), F32)] + [jax.ShapeDtypeStruct((rows // pieces, D), BF)] * pieces,
        [VM] * (2 + 2 * n),
        [VM] * (1 + pieces),
        (x, gain.reshape(1, D), *attns, *weights),
        flops=2 * rows * D * D,
        moved=7 << 20,
    )


def hidden_back_kernel(n_parts, pieces, n_sums, valid_ref, hidden_ref, cot_ref, gain_ref, *refs):
    sums, refs = refs[: pieces * n_sums], refs[pieces * n_sums :]
    weights, refs = refs[:n_parts], refs[n_parts:]
    grad_ref, low_ref, gain_grad_ref, attn_refs = refs[0], refs[1], refs[2], refs[3:]
    rows = hidden_ref.shape[0] // pieces
    gain = gain_ref[...]
    gain_grad = jnp.zeros((1, D), F32)
    for p in range(pieces):
        at = slice(p * rows, (p + 1) * rows)
        hidden = hidden_ref[at]
        normed_grad = sums[p * n_sums][...].astype(F32)
        for s in sums[p * n_sums + 1 : (p + 1) * n_sums]:
            normed_grad = normed_grad + s[...].astype(F32)
        inverse = lax.rsqrt(jnp.mean(hidden * hidden, axis=-1, keepdims=True) + EPSILON)
        gain_grad = gain_grad + jnp.sum(normed_grad * (hidden * inverse), axis=0, keepdims=True)
        scaled = normed_grad * gain
        back = inverse * scaled - hidden * (
            inverse * inverse * inverse * jnp.mean(scaled * hidden, axis=-1, keepdims=True)
        )
        dy = jnp.where(valid_ref[at] > 0, cot_ref[at].astype(F32), 0.0)
        total = dy + back
        grad_ref[at] = total
        low = total.astype(BF)
        low_ref[at] = low
        for a, w in zip(attn_refs, weights, strict=True):
            a[at] = mm(low, w[...]).astype(BF)
    gain_grad_ref[...] = gain_grad


def hidden_back(valid, hidden, cotangent, gain, sums, weights):
    rows, pieces, n_sums, n = hidden.shape[0], len(sums), len(sums[0]), len(weights)
    heads = weights[0].shape[1]
    return call(
        functools.partial(hidden_back_kernel, n, pieces, n_sums),
        "hidden_back",
        [
            jax.ShapeDtypeStruct((rows, D), F32),
            jax.ShapeDtypeStruct((rows, D), BF),
            jax.ShapeDtypeStruct((1, D), F32),
        ]
        + [jax.ShapeDtypeStruct((rows, heads), BF)] * n,
        [VM] * (4 + pieces * n_sums + n),
        [VM] * (3 + n),
        (valid, hidden, cotangent, gain.reshape(1, D), *[s for piece in sums for s in piece], *weights),
        flops=2 * rows * D * D,
        moved=10 << 20,
    )


def dispatch_kernel(n_pieces, scaled, pos_ref, gate_ref, *refs):
    pieces, out_ref, rows_ref, sems = refs[:n_pieces], refs[n_pieces], refs[n_pieces + 1], refs[n_pieces + 2]
    height = rows_ref.shape[0] // n_pieces
    copies = [
        pltpu.make_async_copy(piece, rows_ref.at[pl.ds(p * height, height)], sems.at[p])
        for p, piece in enumerate(pieces)
    ]
    for c in copies:
        c.start()
    rank = lax.broadcasted_iota(jnp.int32, (CAP, rows_ref.shape[0]), 0)
    for c in copies:
        c.wait()
    for j in range(out_ref.shape[0]):
        chosen = rank == pos_ref[j : j + 1, :]
        value = gate_ref[j : j + 1, :] if scaled else 1.0
        one_hot = jnp.where(chosen, value, 0.0).astype(BF)
        out_ref[j] = mm(one_hot, rows_ref[...]).astype(BF)


def dispatch(pos, gate, pieces, scaled):
    experts, rows = pos.shape
    return call(
        functools.partial(dispatch_kernel, len(pieces), scaled),
        "dispatch_scaled" if scaled else "dispatch",
        jax.ShapeDtypeStruct((experts, CAP, D), BF),
        [VM, VM] + [ANY] * len(pieces),
        VM,
        (pos, gate, *pieces),
        scratch=[pltpu.VMEM((rows, D), BF), pltpu.SemaphoreType.DMA((len(pieces),))],
        flops=2 * experts * CAP * rows * D,
        moved=5 << 20,
    )


def combine_kernel(n_experts, slot, scaled, n_adds, n_outs, pos_ref, gate_ref, *refs):
    sources, refs = refs[:n_experts], refs[n_experts:]
    adds, outs, (held, sems) = refs[:n_adds], refs[n_adds : n_adds + n_outs], refs[n_adds + n_outs :]
    copies = [
        pltpu.make_async_copy(source.at[slot], held.at[pl.ds(j * CAP, CAP)], sems.at[j])
        for j, source in enumerate(sources)
    ]
    for c in copies:
        c.start()
    for c in copies:
        c.wait()
    width = n_experts * CAP
    rows = pos_ref.shape[0]
    block = 256
    per_out = rows // n_outs
    for b in range(rows // block):
        at = slice(b * block, (b + 1) * block)
        tiles = []
        for first in range(0, width, LANES):
            size = min(LANES, width - first)
            lane = first + lax.broadcasted_iota(jnp.int32, (block, size), 1)
            tile = jnp.zeros((block, size), F32)
            for j in range(first // CAP, (first + size - 1) // CAP + 1):
                target = pos_ref[at, j : j + 1]
                target = jnp.where(target >= 0, target + j * CAP, -1)
                tile = jnp.where(lane == target, gate_ref[at, j : j + 1] if scaled else 1.0, tile)
            tiles.append(tile.astype(BF))
        total = mm(jnp.concatenate(tiles, axis=1), held[...])
        out, inner = outs[b * block // per_out], slice(b * block % per_out, b * block % per_out + block)
        if n_adds:
            total = total + adds[0][at].astype(F32)
        out[inner] = total.astype(BF)


def combine(pos, gate, sources, slot, scaled, add, n_outs):
    rows, n_experts = pos.shape
    adds = [] if add is None else [add]
    return call(
        functools.partial(combine_kernel, n_experts, slot, scaled, len(adds), n_outs),
        "combine_scaled" if scaled else "combine",
        [jax.ShapeDtypeStruct((rows // n_outs, D), BF)] * n_outs,
        [VM, VM] + [ANY] * n_experts + [VM] * len(adds),
        [VM] * n_outs,
        (pos, gate, *sources, *adds),
        scratch=[pltpu.VMEM((n_experts * CAP, D), BF), pltpu.SemaphoreType.DMA((n_experts,))],
        flops=2 * n_experts * CAP * rows * D,
        moved=5 << 20,
    )


def expert_kernel(j, outer, in_rows, down_rows, idx_ref, *refs):
    n_hops = outer - 1
    xs, refs = refs[:GROUP], refs[GROUP:]
    gs, refs = refs[:GROUP], refs[GROUP:]
    own, refs = refs[0], refs[1:]
    lefts, refs = refs[:n_hops], refs[n_hops:]
    rights, refs = refs[:n_hops], refs[n_hops:]
    y_ref, dx_ref, dw_ref = refs[:3]
    x_all, g_all, w_in, w_down, act_all, gug_all, sem_x, sem_g, sem_w, sem_d = refs[3:]
    o, i = idx_ref[0], idx_ref[1]

    def rows_of(sources, held, sems):
        return [
            pltpu.make_async_copy(s.at[j], held.at[pl.ds(n * CAP, CAP)], sems.at[n])
            for n, s in enumerate(sources)
        ]

    def weight_copies(source, at, slot):
        made = []
        for m in range(GROUP):
            place = at * GROUP + (i ^ m)
            made.append(
                pltpu.make_async_copy(
                    source.at[m, pl.ds(0, in_rows)],
                    w_in.at[pl.ds(pl.multiple_of(place * in_rows, in_rows), in_rows)],
                    sem_w.at[slot * GROUP + m],
                )
            )
            made.append(
                pltpu.make_async_copy(
                    source.at[m, pl.ds(in_rows, down_rows)],
                    w_down.at[pl.ds(pl.multiple_of(place * down_rows, down_rows), down_rows)],
                    sem_d.at[slot * GROUP + m],
                )
            )
        return made

    def each_weight(act):
        act(weight_copies(own, o, 0))
        for k in range(1, outer):

            @pl.when(o >= k)
            def _():
                act(weight_copies(lefts[k - 1], o - k, k))

            @pl.when(o + k < outer)
            def _():
                act(weight_copies(rights[k - 1], o + k, n_hops + k))

    def start(made):
        for c in made:
            c.start()

    def wait(made):
        for c in made:
            c.wait()

    each_weight(start)
    copy_x, copy_g = rows_of(xs, x_all, sem_x), rows_of(gs, g_all, sem_g)
    start(copy_x)
    start(copy_g)
    each_weight(wait)
    wait(copy_x)
    wait(copy_g)

    def per_slot(s, carry):
        at = pl.ds(pl.multiple_of(s * CAP, CAP), CAP)
        gate_up = mm(x_all[at, :], w_in[...])
        g, u = gate_up[:, :FF], gate_up[:, FF:]
        sigma = 1.0 / (1.0 + jnp.exp(-g))
        silu = g * sigma
        act = (silu * u).astype(BF)
        act_all[at, :] = act
        y_ref[s] = mm(act, w_down[...]).astype(BF)
        act_grad = mm_nt(g_all[at, :], w_down[...])
        gug_all[at, :FF] = (act_grad * u * sigma * (1.0 + g * (1.0 - sigma))).astype(BF)
        gug_all[at, FF:] = (act_grad * silu).astype(BF)
        dx_ref[s] = mm_nt(gug_all[at, :], w_in[...]).astype(BF)
        return carry

    lax.fori_loop(0, GROUP, per_slot, 0)
    for c in range(outer):
        part = mm_tn(x_all[:, c * GROUP * in_rows : (c + 1) * GROUP * in_rows], gug_all[...]).astype(BF)
        for r in range(GROUP):
            dw_ref[c, i ^ r, :in_rows, :] = part[r * in_rows : (r + 1) * in_rows]
        part = mm_tn(act_all[:, c * GROUP * down_rows : (c + 1) * GROUP * down_rows], g_all[...]).astype(BF)
        for r in range(GROUP):
            dw_ref[c, i ^ r, in_rows:, :] = part[r * down_rows : (r + 1) * down_rows]


def expert(idx, j, outer, in_rows, down_rows, xs, gs, own, lefts, rights):
    n_hops = outer - 1
    total = GROUP * CAP
    packed = in_rows + down_rows
    return call(
        functools.partial(expert_kernel, j, outer, in_rows, down_rows),
        "expert",
        [
            jax.ShapeDtypeStruct((GROUP, CAP, D), BF),
            jax.ShapeDtypeStruct((GROUP, CAP, D), BF),
            jax.ShapeDtypeStruct((outer, GROUP, packed, D), BF),
        ],
        [SMEM] + [ANY] * (2 * GROUP + 1 + 2 * n_hops),
        [VM] * 3,
        (idx, *xs, *gs, own, *lefts, *rights),
        scratch=[
            pltpu.VMEM((total, D), BF),
            pltpu.VMEM((total, D), BF),
            pltpu.VMEM((D, 2 * FF), BF),
            pltpu.VMEM((FF, D), BF),
            pltpu.VMEM((total, FF), BF),
            pltpu.VMEM((total, 2 * FF), BF),
            pltpu.SemaphoreType.DMA((GROUP,)),
            pltpu.SemaphoreType.DMA((GROUP,)),
            pltpu.SemaphoreType.DMA(((1 + 2 * n_hops) * GROUP,)),
            pltpu.SemaphoreType.DMA(((1 + 2 * n_hops) * GROUP,)),
        ],
        flops=18 * total * D * FF,
        moved=15 << 20,
    )


def pack_kernel(n_experts, in_rows, down_rows, idx_ref, in_ref, down_ref, *refs):
    outs, sems = refs[:-1], refs[-1]
    i = idx_ref[1]
    copies = []
    for j in range(n_experts):
        for m in range(GROUP):
            n = j * GROUP + m
            source = (i ^ m) * n_experts + j
            copies.append(
                pltpu.make_async_copy(in_ref.at[source], outs[m].at[j, pl.ds(0, in_rows)], sems.at[2 * n])
            )
            copies.append(
                pltpu.make_async_copy(
                    down_ref.at[source], outs[m].at[j, pl.ds(in_rows, down_rows)], sems.at[2 * n + 1]
                )
            )
    for c in copies:
        c.start()
    for c in copies:
        c.wait()


def pack_weights(idx, expert_in, expert_down):
    experts, in_rows, _ = expert_in.shape
    down_rows = expert_down.shape[1]
    n = experts // GROUP
    return call(
        functools.partial(pack_kernel, n, in_rows, down_rows),
        "pack_weights",
        [jax.ShapeDtypeStruct((n, in_rows + down_rows, D), BF)] * GROUP,
        [SMEM, ANY, ANY],
        [VM] * GROUP,
        (idx, expert_in, expert_down),
        scratch=[pltpu.SemaphoreType.DMA((2 * experts,))],
        moved=6 << 20,
    )


def place():
    d, t = lax.axis_index("dp"), lax.axis_index("tensor")
    return d, t, d // GROUP, d % GROUP


def flip(v, m):
    first, second = v % 2, (v // 2) % 2
    if m & 1:
        v = v + 1 - 2 * first
    if m & 2:
        v = v + 2 - 4 * second
    return v


def greet(outer, distances, tensor):
    d, t, o, _ = place()
    barrier = pltpu.get_barrier_semaphore()
    count = 0
    for m in distances:
        pl.semaphore_signal(barrier, inc=1, device_id=(flip(d, m), t), device_id_type=MESH)
        count += 1
    if tensor:
        pl.semaphore_signal(barrier, inc=1, device_id=(d, 1 - t), device_id_type=MESH)
        count += 1

    @pl.when(o > 0)
    def _():
        pl.semaphore_signal(barrier, inc=1, device_id=(d - GROUP, t), device_id_type=MESH)

    @pl.when(o < outer - 1)
    def _():
        pl.semaphore_signal(barrier, inc=1, device_id=(d + GROUP, t), device_id_type=MESH)

    neighbours = (o + outer - 1) // outer + (2 * outer - 2 - o) // outer
    pl.semaphore_wait(barrier, count + neighbours)


class Hops:
    def __init__(self, outer, steps, sent, came):
        d, t, o, _ = place()
        self.moves = []
        for n, (k, from_left, from_right, to_left, to_right) in enumerate(steps):
            back = outer - 1 - o
            right = pltpu.make_async_remote_copy(
                from_left, to_left, sent.at[2 * n], came.at[2 * n], device_id=(d + GROUP, t), device_id_type=MESH
            )
            left = pltpu.make_async_remote_copy(
                from_right,
                to_right,
                sent.at[2 * n + 1],
                came.at[2 * n + 1],
                device_id=(d - GROUP, t),
                device_id_type=MESH,
            )
            self.moves.append((right, (o >= k - 1) & (back >= 1), o >= k))
            self.moves.append((left, (back >= k - 1) & (o >= 1), back >= k))

    def start(self):
        for copy, sends, _ in self.moves:
            pl.when(sends)(copy.start)

    def wait(self):
        for copy, sends, receives in self.moves:
            pl.when(sends)(copy.wait_send)
            pl.when(receives)(copy.wait_recv)


def greet_all(outer):
    d, t, o, i = place()
    barrier = pltpu.get_barrier_semaphore()
    for m in range(1, GROUP):
        pl.semaphore_signal(barrier, inc=1, device_id=(flip(d, m), t), device_id_type=MESH)
    pl.semaphore_signal(barrier, inc=1, device_id=(d, 1 - t), device_id_type=MESH)
    for k in range(1, outer):
        pl.semaphore_signal(barrier, inc=1, device_id=((o + k) % outer * GROUP + i, t), device_id_type=MESH)
    pl.semaphore_wait(barrier, GROUP - 1 + outer)


def to_x(src, dst, sent, came):
    d, t, _, _ = place()
    return pltpu.make_async_remote_copy(src, dst, sent, came, device_id=(d, 1 - t), device_id_type=MESH)


def to_dp(m, src, dst, sent, came):
    d, t, _, _ = place()
    return pltpu.make_async_remote_copy(src, dst, sent, came, device_id=(flip(d, m), t), device_id_type=MESH)


def remote_call(kernel, name, collective_id, out_shape, in_specs, out_specs, args, scratch, flops):
    return pl.pallas_call(
        kernel,
        name=name,
        out_shape=out_shape,
        in_specs=in_specs,
        out_specs=out_specs,
        scratch_shapes=list(scratch),
        compiler_params=pltpu.CompilerParams(
            vmem_limit_bytes=VMEM_LIMIT, collective_id=collective_id, has_side_effects=True
        ),
        cost_estimate=pl.CostEstimate(flops=flops, bytes_accessed=8 << 20, transcendentals=0),
    )(*args)


def collect_kernel(outer, in_rows, down_rows, shard_ref, normed_ref, gates_ref, freq_ref, in_ref, down_ref, *refs):
    w_ref, other_ref, cos_ref, sin_ref, pos_ref, gate_ref, posc_ref, gatec_ref = refs[:8]
    own_refs, packed_refs, to_left, to_right = refs[8:10], refs[10:12], refs[12], refs[13]
    packed, gates_all, before, l_w, l_in, l_down, l_own = refs[14:21]
    s_z, r_z, s_y, r_y, s_c, r_c, s_x, r_x, s_g, r_g, s_a, r_a, s_hop, r_hop = refs[21:]
    d, t, o, i = place()
    each = shard_ref.shape[0]
    width = w_ref.shape[1] // 2
    own_width = shard_ref.shape[1]
    n_local = in_ref.shape[0]
    n = n_local // GROUP
    slot_rows = gates_all.shape[2]
    half = slot_rows // 4

    def block(which, index):
        return pl.ds(pl.multiple_of((which * GROUP + index) * each, each), each)

    def lanes(h):
        return pl.ds(h * width, width)

    local = pltpu.make_async_copy(shard_ref, w_ref.at[block(o, i), pl.ds(0, own_width)], l_w)
    local.start()
    packs = []
    for j in range(n):
        for m in range(GROUP):
            source, k = flip(i, m) * n + j, j * GROUP + m
            packs.append(
                (
                    pltpu.make_async_copy(in_ref.at[source], packed.at[j, m, pl.ds(0, in_rows)], l_in.at[k]),
                    pltpu.make_async_copy(down_ref.at[source], packed.at[j, m, pl.ds(in_rows, down_rows)], l_down.at[k]),
                )
            )
    for pair in packs:
        for c in pair:
            c.start()
    greet_all(outer)

    x_moves = [
        to_x(shard_ref.at[:, pl.ds(width, own_width - width)], w_ref.at[block(o, i), pl.ds(own_width, 2 * width - own_width)], s_x.at[0], r_x.at[0]),
        to_x(normed_ref, other_ref, s_x.at[1], r_x.at[1]),
    ]
    g_x = [
        to_x(
            gates_ref.at[:, pl.ds(p * half, half)],
            gates_all.at[0, :, pl.ds((2 * p + 1) * half, half)],
            s_g.at[p],
            r_g.at[p],
        )
        for p in range(2)
    ]
    g_y = to_dp(2, gates_all.at[0], gates_all.at[1], s_g.at[2], r_g.at[2])
    g_c = [to_dp(1, gates_all.at[s], gates_all.at[2 + s], s_g.at[3 + s], r_g.at[3 + s]) for s in range(2)]

    def z_move(k, h):
        peer = (o + k) % outer
        source = shard_ref.at[:, pl.ds(0, width)] if h == 0 else w_ref.at[block(o, i), lanes(1)]
        return pltpu.make_async_remote_copy(
            source,
            w_ref.at[block(o, i), lanes(h)],
            s_z.at[2 * k - 2 + h],
            r_z.at[2 * k - 2 + h],
            device_id=(peer * GROUP + i, t),
            device_id_type=MESH,
        )

    def near_source(b, h):
        if b == 0 and h == 0:
            return shard_ref.at[:, pl.ds(0, width)]
        return w_ref.at[block((o + outer - b) % outer, i), lanes(h)]

    def y_move(b, h):
        target = w_ref.at[block((o + outer - b) % outer, i), lanes(h)]
        return to_dp(2, near_source(b, h), target, s_y.at[2 * b + h], r_y.at[2 * b + h])

    def c_move(b, far, h):
        target = w_ref.at[block((o + outer - b) % outer, flip(i, 2) if far else i), lanes(h)]
        source = target if far else near_source(b, h)
        k = (2 * b + far) * 2 + h
        return to_dp(1, source, target, s_c.at[k], r_c.at[k])

    def weights_move(j, m):
        return to_dp(m, packed.at[j, m], own_refs[j].at[m], s_a.at[3 * j + m - 1], r_a.at[3 * j + m - 1])

    keeps = [pltpu.make_async_copy(packed.at[j, 0], own_refs[j].at[0], l_own.at[j]) for j in range(2)]
    stays = [pltpu.make_async_copy(packed.at[2 + j], packed_refs[j], l_own.at[2 + j]) for j in range(2)]
    hops = Hops(outer, [(1, own_refs[0], own_refs[0], to_left, to_right)], s_hop, r_hop)

    def packed_there(j):
        for pair in packs[j * GROUP : (j + 1) * GROUP]:
            for c in pair:
                c.wait()

    x_moves[0].start()
    for c in g_x:
        c.start()
    for k in range(1, outer):
        z_move(k, 0).start()
    y_move(0, 0).start()
    c_move(0, 0, 0).start()
    packed_there(0)
    for m in range(1, GROUP):
        weights_move(0, m).start()
    keeps[0].start()
    x_moves[1].start()
    local.wait()
    x_moves[0].wait()
    for k in range(1, outer):
        z_move(k, 1).start()
    packed_there(1)
    keeps[1].start()
    for j in range(2):
        packed_there(2 + j)
        stays[j].start()
    gates_all[0, :, 0:half] = gates_ref[:, 0:half]
    gates_all[0, :, 2 * half : 3 * half] = gates_ref[:, half:]
    angles = lax.broadcasted_iota(jnp.int32, (slot_rows, LANES), 0).astype(F32) * freq_ref[...]
    lane = lax.broadcasted_iota(jnp.int32, (slot_rows, LANES), 1)
    cos_ref[...] = jnp.cos(angles)
    sin_ref[...] = jnp.where(lane % HD < HD // 2, -jnp.sin(angles), jnp.sin(angles))
    for c in g_x:
        c.wait()
    g_y.start()
    g_c[0].start()
    for k in range(1, outer):
        z_move(k, 0).wait_recv()
        y_move(k, 0).start()
        c_move(k, 0, 0).start()
    for m in range(1, GROUP):
        weights_move(1, m).start()
    for b in range(1):
        y_move(b, 1).start()
        c_move(b, 0, 1).start()
    before[...] = (
        lax.broadcasted_iota(jnp.int32, before.shape, 0) < lax.broadcasted_iota(jnp.int32, before.shape, 1)
    ).astype(F32).astype(BF)
    keeps[0].wait()
    for m in range(1, GROUP):
        weights_move(0, m).wait_recv()
    hops.start()
    g_y.wait()
    g_c[1].start()
    for k in range(1, outer):
        z_move(k, 1).wait_recv()
        y_move(k, 1).start()
        c_move(k, 0, 1).start()
    for b in range(outer):
        y_move(b, 0).wait_recv()
        c_move(b, 1, 0).start()
    for c in g_c:
        c.wait()
    n_all = gates_all.shape[1]
    first = t * n_local + i * n
    pick = (
        lax.broadcasted_iota(jnp.int32, (8, n_all), 1) == lax.broadcasted_iota(jnp.int32, (8, n_all), 0) + first
    ).astype(F32).astype(BF)
    for s in range(GROUP):
        gate = mm(pick, gates_all[s])
        rank = mm((gate > 0).astype(F32).astype(BF), before[...])
        gate_ref[s] = gate[:n]
        pos_ref[s] = jnp.where(gate > 0, rank, -1.0).astype(jnp.int32)[:n]
        gate = lax.dot_general(gates_all[s], pick, (((0,), (1,)), ((), ())), preferred_element_type=F32)
        rank = mm_tn(before[...], (gate > 0).astype(F32).astype(BF))
        gatec_ref[s] = gate[:, :n]
        posc_ref[s] = jnp.where(gate > 0, rank, -1.0).astype(jnp.int32)[:, :n]
    for b in range(outer):
        y_move(b, 1).wait_recv()
        c_move(b, 1, 1).start()
    for k in range(1, outer):
        for h in range(2):
            z_move(k, h).wait_send()
    for b in range(outer):
        for h in range(2):
            y_move(b, h).wait_send()
            c_move(b, 0, h).wait()
            c_move(b, 1, h).wait()
    for m in range(1, GROUP):
        weights_move(0, m).wait_send()
        weights_move(1, m).wait()
    x_moves[1].wait()
    keeps[1].wait()
    for c in stays:
        c.wait()
    hops.wait()


def collect(outer, shard, normed, gates, frequency, expert_in, expert_down):
    each, own_width = shard.shape
    width = own_width * 2 // 3
    rows = normed.shape[0]
    experts, in_rows, _ = expert_in.shape
    down_rows = expert_down.shape[1]
    n = experts // GROUP
    packed = in_rows + down_rows
    hop = jax.ShapeDtypeStruct((GROUP, packed, D), BF)
    dma = pltpu.SemaphoreType.DMA
    out = remote_call(
        functools.partial(collect_kernel, outer, in_rows, down_rows),
        "collect",
        13,
        [
            jax.ShapeDtypeStruct((D, 2 * width), BF),
            jax.ShapeDtypeStruct((rows, D), BF),
            jax.ShapeDtypeStruct((2 * rows, LANES), F32),
            jax.ShapeDtypeStruct((2 * rows, LANES), F32),
            jax.ShapeDtypeStruct((GROUP, n, 2 * rows), jnp.int32),
            jax.ShapeDtypeStruct((GROUP, n, 2 * rows), F32),
            jax.ShapeDtypeStruct((GROUP, 2 * rows, n), jnp.int32),
            jax.ShapeDtypeStruct((GROUP, 2 * rows, n), F32),
        ]
        + [hop] * 6,
        [VM] * 4 + [ANY] * 2,
        [VM] * 8 + [ANY] * 6,
        (shard, normed, gates, frequency, expert_in, expert_down),
        [
            pltpu.VMEM((n, GROUP, packed, D), BF),
            pltpu.VMEM((GROUP, gates.shape[0], 2 * rows), BF),
            pltpu.VMEM((2 * rows, 2 * rows), BF),
            dma,
            dma((experts,)),
            dma((experts,)),
            dma((4,)),
            dma((2 * outer - 2,)),
            dma((2 * outer - 2,)),
            dma((2 * outer,)),
            dma((2 * outer,)),
            dma((4 * outer,)),
            dma((4 * outer,)),
            dma((2,)),
            dma((2,)),
            dma((5,)),
            dma((5,)),
            dma((6,)),
            dma((6,)),
            dma((2,)),
            dma((2,)),
        ],
        4 << 30,
    )
    return out[:8], out[8:10], out[10:12], out[12], out[13]


def attention_kernel(outer, q_block, n_steps, len_ref, own_ref, other_ref, w_ref, cos_ref, sin_ref, x_ref, gain_ref, *refs):
    width = w_ref.shape[1] // 2
    heads = width // 2
    cot_ref, ready, packed_refs, refs = refs[0], refs[1], refs[2:4], refs[4:]
    qkv_ref, lse_ref, attn_ref, come_ref, hidden_ref, na_ref, nb_ref = refs[:7]
    refs = refs[7:]
    dy_outs, own_refs, refs = refs[:4], refs[4:6], refs[6:]
    to_left, refs = refs[:n_steps], refs[n_steps:]
    to_right, refs = refs[:n_steps], refs[n_steps:]
    send_ref, s_hop, r_hop, s_later, r_later, s_dy, r_dy, s_at, r_at, s_a, r_a, l_own = refs
    d, t, o, i = place()
    length = len_ref[0]
    rows = own_ref.shape[0]
    groups = width // (2 * LANES)
    greet(outer, (1, 2, 3), True)
    hops = Hops(outer, [(1, ready, ready, to_left[0], to_right[0])], s_hop, r_hop)
    later = Hops(outer, [(1, own_refs[k], own_refs[k], to_left[1 + k], to_right[1 + k]) for k in range(2)], s_later, r_later)
    keeps = [pltpu.make_async_copy(packed_refs[k].at[0], own_refs[k].at[0], l_own.at[k]) for k in range(2)]
    weights = [
        to_dp(m, packed_refs[k].at[m], own_refs[k].at[m], s_a.at[3 * k + m - 1], r_a.at[3 * k + m - 1])
        for k in range(2)
        for m in range(1, GROUP)
    ]
    hops.start()
    for copy in (*weights, *keeps):
        copy.start()
    ax, bx, ay, by = dy_outs
    dy_a, dy_b = (cot_ref.at[pl.ds(p * rows // 2, rows // 2)] for p in range(2))
    dys = [
        to_x(dy_a, ax, s_dy.at[0], r_dy.at[0]),
        to_dp(2, dy_b, by, s_dy.at[1], r_dy.at[1]),
        to_x(dy_b, bx, s_dy.at[2], r_dy.at[2]),
        to_dp(2, dy_a, ay, s_dy.at[3], r_dy.at[3]),
    ]

    block = 256
    key_lanes = lax.broadcasted_iota(jnp.int32, (block, LANES), 1) < HD
    for part in range(2):
        for b in range(rows // block):
            at = pl.multiple_of((t if part == 0 else 1 - t) * rows + b * block, block)
            projected = mm((own_ref if part == 0 else other_ref)[b * block : (b + 1) * block], w_ref[:, :width])
            cosine, sine = cos_ref[pl.ds(at, block), :], sin_ref[pl.ds(at, block), :]
            for g in range(groups):
                q = projected[:, g * 2 * LANES : g * 2 * LANES + LANES]
                kv = projected[:, g * 2 * LANES + LANES : (g + 1) * 2 * LANES]
                q = q * cosine + swap_halves(q) * sine
                kv = jnp.where(key_lanes, kv * cosine + swap_halves(kv) * sine, kv)
                qkv_ref[pl.ds(at, block), g * 2 * LANES : g * 2 * LANES + LANES] = q.astype(BF)
                qkv_ref[pl.ds(at, block), g * 2 * LANES + LANES : (g + 1) * 2 * LANES] = kv.astype(BF)

    for copy in dys:
        copy.start()

    def exchange(g):
        lanes = pl.ds(pl.multiple_of(g * LANES, LANES), LANES)
        return to_x(send_ref.at[:, lanes], come_ref.at[:, lanes], s_at.at[g], r_at.at[g])

    def per_group(g, carry):
        q_lanes = pl.ds(pl.multiple_of(g * 2 * LANES, LANES), LANES)
        kv_lanes = pl.ds(pl.multiple_of(g * 2 * LANES + LANES, LANES), LANES)
        o_lanes = pl.ds(pl.multiple_of(g * LANES, LANES), LANES)
        keys, values = doubled(qkv_ref[:, kv_lanes])
        for b in range(2 * rows // q_block):
            start, n_keys = b * q_block, (b + 1) * q_block
            q = head_pair(qkv_ref[start : start + q_block, q_lanes])
            scores = mm_nt(keys[:n_keys], q) * (1.0 / math.sqrt(HD))
            scores = jnp.where(allowed(n_keys, q_block, start, length), scores, NEGATIVE)
            largest = jnp.max(scores, axis=0, keepdims=True)
            expon = jnp.exp(scores - largest)
            totals = jnp.sum(expon, axis=0, keepdims=True)
            probs = (expon * (1.0 / totals)).astype(BF)
            mixed = head_join(mm_tn(probs, values[:n_keys])).astype(BF)
            lse_ref[g, b : b + 1, :] = largest + jnp.log(totals)
            half, inner = start // rows, start % rows

            @pl.when(t == half)
            def _():
                attn_ref[inner : inner + q_block, o_lanes] = mixed

            @pl.when(t != half)
            def _():
                send_ref[inner : inner + q_block, o_lanes] = mixed

        exchange(g).start()

        @pl.when(g == groups // 2)
        def _():
            for copy in (*weights, *keeps):
                copy.wait()
            later.start()

        return carry

    lax.fori_loop(0, groups, per_group, 0)

    def settle(g, carry):
        exchange(g).wait()
        return carry

    for p, normed_ref in enumerate((na_ref, nb_ref)):
        at = slice(p * rows // 2, (p + 1) * rows // 2)
        hidden_ref[at] = x_ref[at].astype(F32) + mm_nt(attn_ref[at], w_ref[:, width : width + heads])
    lax.fori_loop(0, groups, settle, 0)
    for p, normed_ref in enumerate((na_ref, nb_ref)):
        at = slice(p * rows // 2, (p + 1) * rows // 2)
        hidden = hidden_ref[at] + mm_nt(come_ref[at], w_ref[:, width + heads :])
        inverse = lax.rsqrt(jnp.mean(hidden * hidden, axis=-1, keepdims=True) + EPSILON)
        hidden_ref[at] = hidden
        normed_ref[...] = (hidden * inverse * gain_ref[...]).astype(BF)
    for copy in dys:
        copy.wait()
    hops.wait()
    later.wait()


def attention(outer, q_block, length, own, other, weights_full, cosine, sine, x, gain, cotangent, ready, packed):
    rows, groups = own.shape[0], weights_full.shape[1] // (4 * LANES)
    n = 3
    piece = jax.ShapeDtypeStruct((rows // 2, D), BF)
    hop = jax.ShapeDtypeStruct(ready.shape, BF)
    out = remote_call(
        functools.partial(attention_kernel, outer, q_block, n),
        "attention",
        1,
        [
            jax.ShapeDtypeStruct((2 * rows, groups * 2 * LANES), BF),
            jax.ShapeDtypeStruct((groups, 2 * rows // q_block, 2 * q_block), F32),
            jax.ShapeDtypeStruct((rows, groups * LANES), BF),
            jax.ShapeDtypeStruct((rows, groups * LANES), BF),
            jax.ShapeDtypeStruct((rows, D), F32),
            piece,
            piece,
        ]
        + [piece] * 4
        + [hop] * (2 + 2 * n),
        [SMEM] + [VM] * 7 + [ANY] * 4,
        [VM] * 7 + [ANY] * (6 + 2 * n),
        (length, own, other, weights_full, cosine, sine, x, gain.reshape(1, D), cotangent, ready, *packed),
        [
            pltpu.VMEM((rows, groups * LANES), BF),
            pltpu.SemaphoreType.DMA((2,)),
            pltpu.SemaphoreType.DMA((2,)),
            pltpu.SemaphoreType.DMA((4,)),
            pltpu.SemaphoreType.DMA((4,)),
            pltpu.SemaphoreType.DMA((4,)),
            pltpu.SemaphoreType.DMA((4,)),
            pltpu.SemaphoreType.DMA((groups,)),
            pltpu.SemaphoreType.DMA((groups,)),
            pltpu.SemaphoreType.DMA((6,)),
            pltpu.SemaphoreType.DMA((6,)),
            pltpu.SemaphoreType.DMA((2,)),
        ],
        30 << 30,
    )
    return out[:7], out[7:11], out[11:13], out[13 : 13 + n], out[13 + n :]


def one_hot_rows(pos, gate, j, n_rows):
    rank = lax.broadcasted_iota(jnp.int32, (CAP, n_rows), 0)
    chosen = rank == pos[j : j + 1, :]
    return jnp.where(chosen, 1.0 if gate is None else gate[j : j + 1, :], 0.0).astype(BF)


def spread_kernel(outer, steps, pos_ref, gate_ref, na_ref, nb_ref, *refs):
    n_steps = len(steps)
    cot_ref, dy_refs, refs = refs[0], refs[1:5], refs[5:]
    from_left, refs = refs[:n_steps], refs[n_steps:]
    from_right, refs = refs[:n_steps], refs[n_steps:]
    n_ref, dyx_ref, og_ref = refs[:3]
    refs = refs[3:]
    to_left, refs = refs[:n_steps], refs[n_steps:]
    to_right, refs = refs[:n_steps], refs[n_steps:]
    held, s_hop, r_hop, s_n, r_n, s_d, r_d, l_sem = refs
    height = na_ref.shape[0]
    n_experts = og_ref.shape[1]
    greet(outer, (1, 2), True)
    n_ax = to_x(na_ref, n_ref.at[0, 1], s_n.at[0], r_n.at[0])
    n_by = to_dp(2, nb_ref, n_ref.at[1, 2], s_n.at[1], r_n.at[1])
    n_bx = to_x(nb_ref, n_ref.at[0, 3], s_n.at[2], r_n.at[2])
    n_ay = to_dp(2, na_ref, n_ref.at[1, 0], s_n.at[3], r_n.at[3])
    n_axy = to_dp(2, n_ref.at[0, 1], n_ref.at[1, 1], s_n.at[4], r_n.at[4])
    n_bxy = to_x(n_ref.at[1, 2], n_ref.at[1, 3], s_n.at[5], r_n.at[5])
    core = {}
    for n, (s, p) in enumerate([(s, p) for s in range(2) for p in range(4)]):
        source = na_ref if (s, p) == (0, 0) else nb_ref if (s, p) == (0, 2) else n_ref.at[s, p]
        core[s, p] = to_dp(1, source, n_ref.at[2 + s, p], s_n.at[6 + n], r_n.at[6 + n])
    for copy in (n_ax, n_by, n_bx, n_ay):
        copy.start()
    d_a, d_b = (cot_ref.at[pl.ds(p * height, height)] for p in range(2))
    d_ax, d_bx, d_ay, d_by = dy_refs
    d_axy = to_dp(2, d_ax, dyx_ref.at[0, 1], s_d.at[0], r_d.at[0])
    d_bxy = to_x(d_by, dyx_ref.at[0, 3], s_d.at[1], r_d.at[1])
    d_axy.start()
    d_bxy.start()
    d_near = [[d_a, d_ax, d_b, d_bx], [d_ay, dyx_ref.at[0, 1], d_by, dyx_ref.at[0, 3]]]
    d_core = {}
    for n, (s, p) in enumerate([(s, p) for s in range(2) for p in range(4)]):
        d_core[s, p] = to_dp(1, d_near[s][p], dyx_ref.at[1 + s, p], s_d.at[2 + n], r_d.at[2 + n])
    for key in ((0, 0), (0, 1), (0, 2), (0, 3), (1, 0), (1, 2)):
        d_core[key].start()
    core[0, 0].start()
    core[0, 2].start()
    hops = Hops(
        outer,
        [(k, a, b, l, r) for k, a, b, l, r in zip(steps, from_left, from_right, to_left, to_right, strict=True)],
        s_hop,
        r_hop,
    )
    hops.start()

    def load(s):
        pieces = d_near[s] if s < 2 else [dyx_ref.at[s - 1, p] for p in range(4)]
        return [
            pltpu.make_async_copy(piece, held.at[pl.ds(p * height, height)], l_sem.at[p])
            for p, piece in enumerate(pieces)
        ]

    def give(s):
        copies = load(s)
        for c in copies:
            c.start()
        for c in copies:
            c.wait()

        def one(j, carry):
            rank = lax.broadcasted_iota(jnp.int32, (CAP, 4 * height), 0)
            chosen = rank == pos_ref[s, pl.ds(j, 1), :]
            one_hot = jnp.where(chosen, gate_ref[s, pl.ds(j, 1), :], 0.0).astype(BF)
            og_ref[s, j] = mm(one_hot, held[...]).astype(BF)
            return carry

        lax.fori_loop(0, n_experts, one, 0)

    give(0)
    n_ax.wait()
    n_by.wait()
    n_axy.start()
    n_bxy.start()
    core[0, 1].start()
    core[1, 2].start()
    d_axy.wait()
    d_bxy.wait()
    d_core[1, 1].start()
    d_core[1, 3].start()
    give(1)
    n_bx.wait()
    n_ay.wait()
    core[0, 3].start()
    core[1, 0].start()
    for p in range(4):
        d_core[0, p].wait()
    give(2)
    n_axy.wait()
    n_bxy.wait()
    core[1, 1].start()
    core[1, 3].start()
    for p in range(4):
        d_core[1, p].wait()
    give(3)
    for key in core:
        core[key].wait()
    hops.wait()


def spread(outer, pos, gate, normed, dys, steps, from_left, from_right):
    height = normed[0].shape[0]
    n, n_experts = len(steps), pos.shape[1]
    weights = [jax.ShapeDtypeStruct(s.shape, BF) for s in from_left]
    out = remote_call(
        functools.partial(spread_kernel, outer, steps),
        "spread",
        2,
        [
            jax.ShapeDtypeStruct((GROUP, 4, height, D), BF),
            jax.ShapeDtypeStruct((3, 4, height, D), BF),
            jax.ShapeDtypeStruct((GROUP, n_experts, CAP, D), BF),
        ]
        + weights * 2,
        [VM] * 2 + [ANY] * (2 + 5 + 2 * n),
        [ANY, ANY, VM] + [ANY] * (2 * n),
        (pos, gate, *normed, *dys, *from_left, *from_right),
        [
            pltpu.VMEM((4 * height, D), BF),
            pltpu.SemaphoreType.DMA((2 * n,)),
            pltpu.SemaphoreType.DMA((2 * n,)),
            pltpu.SemaphoreType.DMA((14,)),
            pltpu.SemaphoreType.DMA((14,)),
            pltpu.SemaphoreType.DMA((10,)),
            pltpu.SemaphoreType.DMA((10,)),
            pltpu.SemaphoreType.DMA((4,)),
        ],
        12 << 30,
    )
    return out[0], out[2], out[3 : 3 + n], out[3 + n :]


def hand_out_kernel(outer, steps, pos_ref, na_ref, nb_ref, n_ref, *refs):
    n_steps = len(steps)
    from_left, refs = refs[:n_steps], refs[n_steps:]
    from_right, refs = refs[:n_steps], refs[n_steps:]
    x_ref, refs = refs[0], refs[1:]
    to_left, refs = refs[:n_steps], refs[n_steps:]
    to_right, refs = refs[:n_steps], refs[n_steps:]
    held, s_hop, r_hop, l_sem = refs
    height = na_ref.shape[0]
    n_experts = x_ref.shape[1]
    greet(outer, (), False)
    hops = Hops(
        outer,
        [(k, a, b, l, r) for k, a, b, l, r in zip(steps, from_left, from_right, to_left, to_right, strict=True)],
        s_hop,
        r_hop,
    )
    hops.start()

    def load(s):
        pieces = [na_ref, n_ref.at[0, 1], nb_ref, n_ref.at[0, 3]] if s == 0 else [n_ref.at[s, p] for p in range(4)]
        return [
            pltpu.make_async_copy(piece, held.at[s % 2, pl.ds(p * height, height)], l_sem.at[s % 2, p])
            for p, piece in enumerate(pieces)
        ]

    for c in load(0):
        c.start()
    for s in range(GROUP):
        if s + 1 < GROUP:
            for c in load(s + 1):
                c.start()
        for c in load(s):
            c.wait()

        def one(j, carry, s=s):
            rank = lax.broadcasted_iota(jnp.int32, (CAP, 4 * height), 0)
            one_hot = jnp.where(rank == pos_ref[s, pl.ds(j, 1), :], 1.0, 0.0).astype(BF)
            x_ref[s, j] = mm(one_hot, held[s % 2]).astype(BF)
            return carry

        lax.fori_loop(0, n_experts, one, 0)
    hops.wait()


def hand_out(outer, pos, normed, gathered, steps, from_left, from_right):
    height = normed[0].shape[0]
    n, n_experts = len(steps), pos.shape[1]
    weights = [jax.ShapeDtypeStruct(s.shape, BF) for s in from_left]
    out = remote_call(
        functools.partial(hand_out_kernel, outer, steps),
        "hand_out",
        3,
        [jax.ShapeDtypeStruct((GROUP, n_experts, CAP, D), BF)] + weights * 2,
        [VM] + [ANY] * (3 + 2 * n),
        [VM] + [ANY] * (2 * n),
        (pos, *normed, gathered, *from_left, *from_right),
        [
            pltpu.VMEM((2, 4 * height, D), BF),
            pltpu.SemaphoreType.DMA((2 * n,)),
            pltpu.SemaphoreType.DMA((2 * n,)),
            pltpu.SemaphoreType.DMA((2, 4)),
        ],
        12 << 30,
    )
    return out[0], out[1 : 1 + n], out[1 + n :]


def expert_step_kernel(j, outer, in_rows, down_rows, steps, sum_steps, x_ref, g_ref, own, *refs):
    n_hops, n_steps, n_sums = outer - 1, len(steps), len(sum_steps)
    lefts, refs = refs[:n_hops], refs[n_hops:]
    rights, refs = refs[:n_hops], refs[n_hops:]
    from_left, refs = refs[:n_steps], refs[n_steps:]
    from_right, refs = refs[:n_steps], refs[n_steps:]
    dws, refs = refs[:n_sums], refs[n_sums:]
    was_l, refs = refs[:n_sums], refs[n_sums:]
    was_r, refs = refs[:n_sums], refs[n_sums:]
    y_ref, dx_ref, dw_ref = refs[:3]
    refs = refs[3:]
    to_left, refs = refs[:n_steps], refs[n_steps:]
    to_right, refs = refs[:n_steps], refs[n_steps:]
    sum_left, refs = refs[:n_sums], refs[n_sums:]
    sum_right, refs = refs[:n_sums], refs[n_sums:]
    x_all, g_all, w_in, w_down, act_all, gug_all, sem_x, sem_g, sem_w, sem_d, s_hop, r_hop = refs[:12]
    _, _, o, i = place()
    greet(outer, (), False)
    sums = Sums(outer, sum_steps, dws, was_l, was_r, sum_left, sum_right, *refs[12:])
    if n_steps:
        hops = Hops(
            outer,
            [(k, a, b, l, r) for k, a, b, l, r in zip(steps, from_left, from_right, to_left, to_right, strict=True)],
            s_hop,
            r_hop,
        )
        hops.start()

    def rows_of(source, held, sems):
        return [
            pltpu.make_async_copy(source.at[n, j], held.at[pl.ds(n * CAP, CAP)], sems.at[n]) for n in range(GROUP)
        ]

    def weight_copies(source, at, slot):
        made = []
        for m in range(GROUP):
            where = at * GROUP + flip(i, m)
            made.append(
                pltpu.make_async_copy(
                    source.at[m, pl.ds(0, in_rows)],
                    w_in.at[pl.ds(pl.multiple_of(where * in_rows, in_rows), in_rows)],
                    sem_w.at[slot * GROUP + m],
                )
            )
            made.append(
                pltpu.make_async_copy(
                    source.at[m, pl.ds(in_rows, down_rows)],
                    w_down.at[pl.ds(pl.multiple_of(where * down_rows, down_rows), down_rows)],
                    sem_d.at[slot * GROUP + m],
                )
            )
        return made

    def each_weight(act):
        act(weight_copies(own, o, 0))
        for k in range(1, outer):

            @pl.when(o >= k)
            def _():
                act(weight_copies(lefts[k - 1], o - k, k))

            @pl.when(o + k < outer)
            def _():
                act(weight_copies(rights[k - 1], o + k, n_hops + k))

    def start(made):
        for c in made:
            c.start()

    def wait(made):
        for c in made:
            c.wait()

    sums.load()
    each_weight(start)
    copy_x, copy_g = rows_of(x_ref, x_all, sem_x), rows_of(g_ref, g_all, sem_g)
    start(copy_x)
    start(copy_g)
    sums.send()
    each_weight(wait)
    wait(copy_x)
    wait(copy_g)

    def per_slot(s, carry):
        at = pl.ds(pl.multiple_of(s * CAP, CAP), CAP)
        gate_up = mm(x_all[at, :], w_in[...])
        g, u = gate_up[:, :FF], gate_up[:, FF:]
        sigma = 1.0 / (1.0 + jnp.exp(-g))
        silu = g * sigma
        act = (silu * u).astype(BF)
        act_all[at, :] = act
        y_ref[s] = mm(act, w_down[...]).astype(BF)
        act_grad = mm_nt(g_all[at, :], w_down[...])
        gug_all[at, :FF] = (act_grad * u * sigma * (1.0 + g * (1.0 - sigma))).astype(BF)
        gug_all[at, FF:] = (act_grad * silu).astype(BF)
        dx_ref[s] = mm_nt(gug_all[at, :], w_in[...]).astype(BF)
        return carry

    lax.fori_loop(0, GROUP, per_slot, 0)
    for c in range(outer):
        part = mm_tn(x_all[:, c * GROUP * in_rows : (c + 1) * GROUP * in_rows], gug_all[...]).astype(BF)
        for r in range(GROUP):
            dw_ref[c, flip(i, r), :in_rows, :] = part[r * in_rows : (r + 1) * in_rows]
        part = mm_tn(act_all[:, c * GROUP * down_rows : (c + 1) * GROUP * down_rows], g_all[...]).astype(BF)
        for r in range(GROUP):
            dw_ref[c, flip(i, r), in_rows:, :] = part[r * down_rows : (r + 1) * down_rows]
    if n_steps:
        hops.wait()
    sums.wait()


def expert_step(j, outer, in_rows, down_rows, x, g, own, lefts, rights, hop_plan, sum_plan):
    (steps, from_left, from_right), (sum_steps, dws, was_l, was_r) = hop_plan, sum_plan
    n_hops, n, n_sums = outer - 1, len(steps), len(sum_steps)
    total = GROUP * CAP
    packed = in_rows + down_rows
    weights = [jax.ShapeDtypeStruct(s.shape, BF) for s in from_left]
    shapes = [
        jax.ShapeDtypeStruct((GROUP, CAP, D), BF),
        jax.ShapeDtypeStruct((GROUP, CAP, D), BF),
        jax.ShapeDtypeStruct((outer, GROUP, packed, D), BF),
    ] + weights * 2 + [jax.ShapeDtypeStruct((GROUP, packed, D), BF)] * (2 * n_sums)
    out = remote_call(
        functools.partial(expert_step_kernel, j, outer, in_rows, down_rows, steps, sum_steps),
        "expert_step",
        4 + j,
        shapes,
        [ANY] * (3 + 2 * n_hops + 2 * n + 3 * n_sums),
        [VM] * 3 + [ANY] * (2 * n + 2 * n_sums),
        (x, g, own, *lefts, *rights, *from_left, *from_right, *dws, *was_l, *was_r),
        [
            pltpu.VMEM((total, D), BF),
            pltpu.VMEM((total, D), BF),
            pltpu.VMEM((D, 2 * FF), BF),
            pltpu.VMEM((FF, D), BF),
            pltpu.VMEM((total, FF), BF),
            pltpu.VMEM((total, 2 * FF), BF),
            pltpu.SemaphoreType.DMA((GROUP,)),
            pltpu.SemaphoreType.DMA((GROUP,)),
            pltpu.SemaphoreType.DMA(((1 + 2 * n_hops) * GROUP,)),
            pltpu.SemaphoreType.DMA(((1 + 2 * n_hops) * GROUP,)),
            pltpu.SemaphoreType.DMA((max(1, 2 * n),)),
            pltpu.SemaphoreType.DMA((max(1, 2 * n),)),
            *sums_scratch(n_sums, packed),
        ],
        18 * total * D * FF,
    )
    out, rest = out[:3], out[3:]
    return out, rest[:n], rest[n : 2 * n], rest[2 * n : 2 * n + n_sums], rest[2 * n + n_sums :]


class Sums:
    def __init__(self, outer, steps, dws, was_left, was_right, to_left, to_right, message, term, loaded, added, sent, came):
        d, t, o, _ = place()
        back = outer - 1 - o
        self.moves = []
        for n, s in enumerate(steps):
            for side, near, target, was, to, peer in (
                (0, o, outer - s + o, was_left, to_left, d + GROUP),
                (1, back, s - 1 - back, was_right, to_right, d - GROUP),
            ):
                k = 2 * n + side
                own = pltpu.make_async_copy(dws[n].at[target], message.at[k], loaded.at[k])
                before = None if s == 1 else pltpu.make_async_copy(was[n], term.at[side], added.at[k])
                move = pltpu.make_async_remote_copy(
                    message.at[k], to[n], sent.at[k], came.at[k], device_id=(peer, t), device_id_type=MESH
                )
                sends, adds = near <= s - 1, (near <= s - 1) & (near >= 1)
                receives = (near >= 1) & (near <= s)
                self.moves.append((own, before, move, sends, adds, receives, message.at[k], term.at[side]))

    def load(self):
        for own, _, _, sends, *_ in self.moves:
            pl.when(sends)(own.start)

    def send(self):
        for n in range(0, len(self.moves), 2):
            pair = self.moves[n : n + 2]
            for _, before, _, _, adds, *_ in pair:
                if before is not None:
                    pl.when(adds)(before.start)
            for own, before, move, sends, adds, _, message, term in pair:
                pl.when(sends)(own.wait)
                if before is not None:

                    @pl.when(adds)
                    def _(before=before, message=message, term=term):
                        before.wait()

                        def one(m, carry):
                            message[m] = (message[m].astype(F32) + term[m].astype(F32)).astype(BF)
                            return carry

                        lax.fori_loop(0, GROUP, one, 0)

                pl.when(sends)(move.start)

    def wait(self):
        for _, _, move, sends, _, receives, *_ in self.moves:
            pl.when(sends)(move.wait_send)
            pl.when(receives)(move.wait_recv)


def sums_scratch(n, packed):
    n = max(1, n)
    return [
        pltpu.VMEM((2 * n, GROUP, packed, D), BF),
        pltpu.VMEM((2, GROUP, packed, D), BF),
        pltpu.SemaphoreType.DMA((2 * n,)),
        pltpu.SemaphoreType.DMA((2 * n,)),
        pltpu.SemaphoreType.DMA((2 * n,)),
        pltpu.SemaphoreType.DMA((2 * n,)),
    ]


def again(scratch):
    return [pltpu.SemaphoreType.DMA(s.shape) for s in scratch[2:]]


class Final:
    def __init__(self, outer, dw, left, right, mine, term, target, loaded, sent, came, kept):
        _, _, o, _ = place()
        self.from_left, self.from_right = o >= 1, o < outer - 1
        self.mine, self.term = mine, term
        self.own = pltpu.make_async_copy(dw.at[o], mine, loaded.at[0])
        self.left = pltpu.make_async_copy(left, term.at[0], loaded.at[1])
        self.right = pltpu.make_async_copy(right, term.at[1], loaded.at[2])
        self.moves = [to_dp(m, mine.at[m], target.at[m], sent.at[m - 1], came.at[m - 1]) for m in range(1, GROUP)]
        self.keep = pltpu.make_async_copy(mine.at[0], target.at[0], kept)

    def send(self):
        self.own.start()
        pl.when(self.from_left)(self.left.start)
        pl.when(self.from_right)(self.right.start)
        self.own.wait()

        def add(k):
            def one(m, carry):
                self.mine[m] = (self.mine[m].astype(F32) + self.term[k, m].astype(F32)).astype(BF)
                return carry

            lax.fori_loop(0, GROUP, one, 0)

        @pl.when(self.from_left)
        def _():
            self.left.wait()
            add(0)

        @pl.when(self.from_right)
        def _():
            self.right.wait()
            add(1)

        for move in self.moves:
            move.start()
        self.keep.start()

    def wait(self):
        for move in self.moves:
            move.wait()
        self.keep.wait()


def final_scratch(packed):
    return [
        pltpu.VMEM((GROUP, packed, D), BF),
        pltpu.SemaphoreType.DMA((3,)),
        pltpu.SemaphoreType.DMA((GROUP - 1,)),
        pltpu.SemaphoreType.DMA((GROUP - 1,)),
        pltpu.SemaphoreType.DMA,
    ]


class Mixer:
    def __init__(self, sources, pos_ref, gate_ref, held, sems):
        self.sources, self.pos, self.gate, self.held, self.sems = sources, pos_ref, gate_ref, held, sems

    def copies(self, slot, buffer):
        return [
            pltpu.make_async_copy(
                source.at[slot], self.held.at[buffer, pl.ds(j * CAP, CAP)], self.sems.at[buffer * len(self.sources) + j]
            )
            for j, source in enumerate(self.sources)
        ]

    def load(self, slot, buffer):
        for c in self.copies(slot, buffer):
            c.start()

    def mix(self, slot, buffer, out, add=None):
        for c in self.copies(slot, buffer):
            c.wait()
        n_experts = len(self.sources)
        width = n_experts * CAP
        block = 256

        def one(b, carry):
            at = pl.ds(pl.multiple_of(b * block, block), block)
            targets = []
            for j in range(n_experts):
                target = self.pos[slot, at, j : j + 1]
                targets.append(jnp.where(target >= 0, target + j * CAP, -1))
            tiles = []
            for first in range(0, width, LANES):
                size = min(LANES, width - first)
                lane = first + lax.broadcasted_iota(jnp.int32, (block, size), 1)
                tile = jnp.zeros((block, size), F32)
                for j in range(first // CAP, (first + size - 1) // CAP + 1):
                    value = 1.0 if self.gate is None else self.gate[slot, at, j : j + 1]
                    tile = jnp.where(lane == targets[j], value, tile)
                tiles.append(tile.astype(BF))
            total = mm(jnp.concatenate(tiles, axis=1), self.held[buffer])
            if add is not None:
                total = total + add[at, :].astype(F32)
            out[at, :] = total.astype(BF)
            return carry

        lax.fori_loop(0, out.shape[0] // block, one, 0)


class GroupSum:
    def __init__(self, far, come, near, come_ab, last_ab, sent, came):
        self.far, self.come, self.near, self.come_ab, self.last_ab = far, come, near, come_ab, last_ab
        q = near.shape[1] // 4
        self.q = q
        self.core = [to_dp(1, far.at[s], come.at[s], sent.at[s], came.at[s]) for s in range(2)]
        self.a = to_dp(2, near.at[1, pl.ds(0, 2 * q)], come_ab.at[0], sent.at[2], came.at[2])
        self.b = [
            to_x(near.at[s, pl.ds(3 * q, q)], come_ab.at[1, pl.ds(s * q, q)], sent.at[3 + s], came.at[3 + s])
            for s in range(2)
        ]
        self.last = [
            to_x(near.at[0, pl.ds(q, q)], last_ab.at[0], sent.at[5], came.at[5]),
            to_dp(2, near.at[1, pl.ds(2 * q, q)], last_ab.at[1], sent.at[6], came.at[6]),
        ]

    def second(self):
        q, near, come_ab = self.q, self.near, self.come_ab
        self.a.wait_recv()
        near[0, q : 2 * q] = (near[0, q : 2 * q].astype(F32) + come_ab[0, q : 2 * q].astype(F32)).astype(BF)
        self.last[0].start()
        self.b[1].wait_recv()
        near[1, 2 * q : 3 * q] = (near[1, 2 * q : 3 * q].astype(F32) + come_ab[1, q : 2 * q].astype(F32)).astype(BF)
        self.last[1].start()
        self.b[0].wait_recv()

    def terms(self, p):
        q = self.q
        self.last[p].wait_recv()
        return (
            self.near[0, 2 * p * q : 2 * p * q + q].astype(F32)
            + self.come_ab[p, :q].astype(F32)
            + self.last_ab[p].astype(F32)
        )

    def sent(self):
        for copy in (*self.core, self.a, *self.b, *self.last):
            copy.wait_send()


def group_scratch(rows, n_experts):
    return [
        pltpu.VMEM((2, n_experts * CAP, D), BF),
        pltpu.VMEM((2, rows, D), BF),
        pltpu.VMEM((2, rows, D), BF),
        pltpu.VMEM((2, rows, D), BF),
        pltpu.VMEM((2, rows // 2, D), BF),
        pltpu.VMEM((2, rows // 4, D), BF),
        pltpu.SemaphoreType.DMA((2 * n_experts,)),
        pltpu.SemaphoreType.DMA((7,)),
        pltpu.SemaphoreType.DMA((7,)),
    ]


def mix_and_sum(mixer, group):
    mixer.load(2, 0)
    mixer.load(3, 1)
    mixer.mix(2, 0, group.far.at[0])
    group.core[0].start()
    mixer.load(1, 0)
    mixer.mix(3, 1, group.far.at[1])
    group.core[1].start()
    mixer.load(0, 1)
    group.core[1].wait_recv()
    mixer.mix(1, 0, group.near.at[1], group.come.at[1])
    group.a.start()
    group.b[1].start()
    group.core[0].wait_recv()
    mixer.mix(0, 1, group.near.at[0], group.come.at[0])
    group.b[0].start()
    group.second()


def rows_back_kernel(outer, first, then, pos_ref, valid_ref, hidden_ref, cot_ref, gain_ref, w_ref, *refs):
    n_experts, n1, n2 = pos_ref.shape[2], len(first), len(then)
    sources, refs = refs[:n_experts], refs[n_experts:]
    dws, refs = refs[:n1], refs[n1:]
    was_l, refs = refs[:n1], refs[n1:]
    was_r, refs = refs[:n1], refs[n1:]
    grad_ref, low_ref, gain_grad_ref, own_ref, come_ref = refs[:5]
    refs = refs[5:]
    to_l, refs = refs[: n1 + n2], refs[n1 + n2 :]
    to_r, refs = refs[: n1 + n2], refs[n1 + n2 :]
    (held, far, come, near, come_ab, last_ab, l_sem, s_sem, r_sem), refs = refs[:9], refs[9:]
    sums_a, refs = refs[:6], refs[6:]
    sums_b, refs = (*sums_a[:2], *refs[:4]), refs[4:]
    send_ref, s_at, r_at = refs
    greet(outer, (1, 2), True)
    one = Sums(outer, first, dws, was_l, was_r, to_l[:n1], to_r[:n1], *sums_a)
    two = Sums(
        outer,
        [s for s, _ in then],
        [dws[k] for _, k in then],
        [to_l[k] for _, k in then],
        [to_r[k] for _, k in then],
        to_l[n1:],
        to_r[n1:],
        *sums_b,
    )
    group = GroupSum(far, come, near, come_ab, last_ab, s_sem, r_sem)
    mixer = Mixer(sources, pos_ref, None, held, l_sem)
    one.load()
    one.send()
    mix_and_sum(mixer, group)
    one.wait()
    two.load()
    two.send()
    rows = hidden_ref.shape[0] // 2
    width = w_ref.shape[1] // 2
    heads = width // 2
    gain = gain_ref[...]
    gain_grad = jnp.zeros((1, D), F32)
    for p in range(2):
        at = slice(p * rows, (p + 1) * rows)
        hidden = hidden_ref[at]
        normed_grad = group.terms(p)
        inverse = lax.rsqrt(jnp.mean(hidden * hidden, axis=-1, keepdims=True) + EPSILON)
        gain_grad = gain_grad + jnp.sum(normed_grad * (hidden * inverse), axis=0, keepdims=True)
        scaled = normed_grad * gain
        back = inverse * scaled - hidden * (
            inverse * inverse * inverse * jnp.mean(scaled * hidden, axis=-1, keepdims=True)
        )
        dy = jnp.where(valid_ref[at] > 0, cot_ref[at].astype(F32), 0.0)
        total = dy + back
        grad_ref[at] = total
        low = total.astype(BF)
        low_ref[at] = low
        send_ref[at] = mm(low, w_ref[:, width + heads :]).astype(BF)
    gain_grad_ref[...] = gain_grad
    away = to_x(send_ref, come_ref, s_at, r_at)
    away.start()
    own_ref[...] = mm(low_ref[...], w_ref[:, width : width + heads]).astype(BF)
    group.sent()
    away.wait()
    two.wait()


def rows_back(outer, pos, valid, hidden, cotangent, gain, weights_full, sources, first, then, dws, was_l, was_r):
    rows, heads = hidden.shape[0], weights_full.shape[1] // 4
    n = len(first) + len(then)
    packed = dws[0].shape[2]
    hop = [jax.ShapeDtypeStruct((GROUP, packed, D), BF)] * (2 * n)
    half = jax.ShapeDtypeStruct((rows, heads), BF)
    out = remote_call(
        functools.partial(rows_back_kernel, outer, first, then),
        "rows_back",
        10,
        [
            jax.ShapeDtypeStruct((rows, D), F32),
            jax.ShapeDtypeStruct((rows, D), BF),
            jax.ShapeDtypeStruct((1, D), F32),
            half,
            half,
        ]
        + hop,
        [VM] * 6 + [ANY] * (len(sources) + 3 * len(first)),
        [VM] * 5 + [ANY] * (2 * n),
        (pos, valid, hidden, cotangent, gain.reshape(1, D), weights_full, *sources, *dws, *was_l, *was_r),
        [
            *group_scratch(2 * rows, len(sources)),
            *sums_scratch(len(first), packed),
            *again(sums_scratch(len(first), packed)),
            pltpu.VMEM((rows, heads), BF),
            pltpu.SemaphoreType.DMA,
            pltpu.SemaphoreType.DMA,
        ],
        20 << 30,
    )
    return out[:5], out[5 : 5 + n], out[5 + n :]


def attention_back_kernel(outer, q_block, steps, len_ref, qkv_ref, lse_ref, cos_ref, sin_ref, own_ref, other_ref, *refs):
    n = len(steps)
    dws, refs = refs[:n], refs[n:]
    was_l, refs = refs[:n], refs[n:]
    was_r, refs = refs[:n], refs[n:]
    f_dw, f_left, f_right, refs = *refs[:3], refs[3:]
    outs, fin_ref, refs = refs[:2], refs[2], refs[3:]
    to_l, refs = refs[:n], refs[n:]
    to_r, refs = refs[:n], refs[n:]
    do_ref, dq_ref, dk_ref, dv_ref = refs[:4]
    sums_refs, final_refs = refs[4:10], refs[10:]
    _, t, _, _ = place()
    greet(outer, (1, 2, 3), False)
    sums = Sums(outer, steps, dws, was_l, was_r, to_l, to_r, *sums_refs)
    final = Final(outer, f_dw, f_left, f_right, final_refs[0], sums_refs[1], fin_ref, *final_refs[1:])
    sums.load()
    sums.send()
    final.send()
    length = len_ref[0]
    rows, own_rows = qkv_ref.shape[0], own_ref.shape[0]
    groups = own_ref.shape[1] // LANES
    scale = 1.0 / math.sqrt(HD)

    def per_group(g, carry):
        q_lanes = pl.ds(pl.multiple_of(g * 2 * LANES, LANES), LANES)
        kv_lanes = pl.ds(pl.multiple_of(g * 2 * LANES + LANES, LANES), LANES)
        o_lanes = pl.ds(pl.multiple_of(g * LANES, LANES), LANES)
        for half, grad_ref in ((t, own_ref), (1 - t, other_ref)):
            do_ref[pl.ds(pl.multiple_of(half * own_rows, own_rows), own_rows), :] = grad_ref[:, o_lanes]
        keys, values = doubled(qkv_ref[:, kv_lanes])
        dk_ref[...] = jnp.zeros_like(dk_ref)
        dv_ref[...] = jnp.zeros_like(dv_ref)
        for b in range(rows // q_block):
            start, n_keys = b * q_block, (b + 1) * q_block
            q = head_pair(qkv_ref[start : start + q_block, q_lanes])
            grad = head_pair(do_ref[start : start + q_block, :])
            scores = mm_nt(keys[:n_keys], q) * scale
            probs = jnp.where(
                allowed(n_keys, q_block, start, length), jnp.exp(scores - lse_ref[g, b : b + 1, :]), 0.0
            )
            prob_grad = mm_nt(values[:n_keys], grad)
            center = jnp.sum(probs * prob_grad, axis=0, keepdims=True)
            score_grad = (probs * (prob_grad - center)).astype(BF)
            dq_ref[start : start + q_block, :] = head_join(mm_tn(score_grad, keys[:n_keys])) * scale
            dk_ref[:n_keys, :] += mm(score_grad, q)
            dv_ref[:n_keys, :] += mm(probs.astype(BF), grad)
        for p, half in enumerate((t, 1 - t)):
            at = pl.ds(pl.multiple_of(half * own_rows, own_rows), own_rows)
            cosine, sine = cos_ref[at, :], sin_ref[at, :]
            dq = dq_ref[at, :]
            outs[p][:, q_lanes] = (dq * cosine - swap_halves(dq) * sine).astype(BF)
            dk, dv = dk_ref[at, :] * scale, dv_ref[at, :]
            dk = dk + pltpu.roll(dk, HD, 1)
            dv = dv + pltpu.roll(dv, HD, 1)
            dk = dk * cosine - swap_halves(dk) * sine
            first = lax.broadcasted_iota(jnp.int32, dk.shape, 1) < HD
            outs[p][:, kv_lanes] = jnp.where(first, dk, dv).astype(BF)
        return carry

    lax.fori_loop(0, groups, per_group, 0)
    final.wait()
    sums.wait()


def attention_back(outer, q_block, length, qkv, lse, cosine, sine, grads, steps, dws, was_l, was_r, final):
    rows, width = qkv.shape
    n = len(steps)
    packed = dws[0].shape[2]
    hop = jax.ShapeDtypeStruct((GROUP, packed, D), BF)
    out = remote_call(
        functools.partial(attention_back_kernel, outer, q_block, steps),
        "attention_back",
        12,
        [jax.ShapeDtypeStruct((rows // 2, width), BF)] * 2 + [hop] * (1 + 2 * n),
        [SMEM] + [VM] * 6 + [ANY] * (3 * n + 3),
        [VM] * 2 + [ANY] * (1 + 2 * n),
        (length, qkv, lse, cosine, sine, *grads, *dws, *was_l, *was_r, *final),
        [
            pltpu.VMEM((rows, LANES), BF),
            pltpu.VMEM((rows, LANES), F32),
            pltpu.VMEM((rows, LANES), F32),
            pltpu.VMEM((rows, LANES), F32),
            *sums_scratch(n, packed),
            *final_scratch(packed),
        ],
        30 << 30,
    )
    return out[:2], out[2], out[3 : 3 + n], out[3 + n :]


def finish_kernel(outer, in_rows, len_ref, pos_ref, gate_ref, valid_ref, hidden_ref, hgrad_ref, x_ref, gain_ref, w_any, *refs):
    (no_ref, nx_ref, po_ref, px_ref, ao_ref, sg_ref), refs = refs[:6], refs[6:]
    n_experts = pos_ref.shape[2]
    ys, refs = refs[:n_experts], refs[n_experts:]
    dws, refs = refs[:3], refs[3:]
    done, refs = refs[:2], refs[2:]
    was_l, refs = refs[:2], refs[2:]
    was_r, refs = refs[:2], refs[2:]
    out_ref, tgrad_ref, gains_ref, qkv_ref, outw_ref = refs[:5]
    fins, to_l, to_r, refs = refs[5:8], refs[8:11], refs[11:14], refs[14:]
    (held, far, come, near, come_ab, last_ab, l_sem, s_sem, r_sem), refs = refs[:9], refs[9:]
    sums_a, refs = refs[:6], refs[6:]
    sums_b, refs = (*sums_a[:2], *refs[:4]), refs[4:]
    final_refs, refs = [refs[5 * k : 5 * k + 5] for k in range(3)], refs[15:]
    part_ref, theirs_ref, p_send, p_recv = refs[:4]
    refs = refs[4:]
    qp, q_core, q_y, q_z, q_send, q_recv = refs[:6]
    g_buf, g_come, g_z, g_send, g_recv, w_ref, w_sem = refs[6:]
    d, t, o, i = place()
    y, c = i // 2, i % 2
    rows = hidden_ref.shape[0]
    width = w_ref.shape[1]
    w_copy = pltpu.make_async_copy(w_any.at[:, pl.ds(0, width)], w_ref, w_sem)
    w_copy.start()
    greet_all(outer)
    sums = Sums(outer, (2, 3), [dws[2], dws[1]], was_l, was_r, to_l[:2], to_r[:2], *sums_a)
    last = Sums(outer, (3,), [dws[2]], to_l[:1], to_r[:1], to_l[2:], to_r[2:], *sums_b)
    came = [done, (to_l[1], to_r[1]), (to_l[2], to_r[2])]
    finals = [
        Final(outer, dws[k], *came[k], final_refs[k][0], sums_a[1], fins[k], *final_refs[k][1:]) for k in range(3)
    ]
    group = GroupSum(far, come, near, come_ab, last_ab, s_sem, r_sem)
    mixer = Mixer(ys, pos_ref, gate_ref, held, l_sem)
    sums.load()
    sums.send()

    w_copy.wait()
    part_ref[...] = mm_nt(px_ref[...], w_ref[...]).astype(BF)
    exchange = to_x(part_ref, theirs_ref, p_send, p_recv)
    exchange.start()

    each = qkv_ref.shape[0]

    def weights_block(k, carry):
        lanes = pl.ds(pl.multiple_of(k * GROUP * each, GROUP * each), GROUP * each)
        total = (mm_tn(no_ref[:, lanes], po_ref[...]) + mm_tn(nx_ref[:, lanes], px_ref[...])).astype(BF)
        for r in range(GROUP):
            qp[k, r // 2, r % 2, :, :width] = total[r * each : (r + 1) * each]
            at = pl.ds(pl.multiple_of((k * GROUP + r) * each, each), each)
            qp[k, r // 2, r % 2, :, width:] = ao_ref[at, :]
        return carry

    lax.fori_loop(0, outer, weights_block, 0)
    to_core = to_dp(1, qp.at[:, :, 1 - c], q_core, q_send.at[0], q_recv.at[0])
    to_core.start()
    finals[0].send()

    mixer.load(2, 0)
    mixer.load(3, 1)
    mixer.mix(2, 0, group.far.at[0])
    group.core[0].start()
    mixer.load(1, 0)
    to_core.wait()

    def add_core(k, carry):
        for r in range(2):
            qp[k, r, c] = (qp[k, r, c].astype(F32) + q_core[k, r].astype(F32)).astype(BF)
        return carry

    lax.fori_loop(0, outer, add_core, 0)
    to_y = to_dp(2, qp.at[:, 1 - y, c], q_y, q_send.at[1], q_recv.at[1])
    to_y.start()
    mixer.mix(3, 1, group.far.at[1])
    group.core[1].start()
    mixer.load(0, 1)

    exchange.wait()
    gain_grad = jnp.zeros((1, D), F32)
    quarter = rows // 4
    for p in range(4):
        at = slice(p * quarter, (p + 1) * quarter)
        normed_grad = mm_nt(po_ref[at], w_ref[:, :width]).astype(BF).astype(F32) + theirs_ref[at].astype(F32)
        x = x_ref[at].astype(F32)
        inverse = lax.rsqrt(jnp.mean(x * x, axis=-1, keepdims=True) + EPSILON)
        gain_grad = gain_grad + jnp.sum(normed_grad * (x * inverse), axis=0, keepdims=True)
        scaled = normed_grad * gain_ref[...]
        tgrad_ref[at] = (
            hgrad_ref[at]
            + inverse * scaled
            - x * (inverse * inverse * inverse * jnp.mean(scaled * x, axis=-1, keepdims=True))
        )
    g_buf[0, 0:1, :] = gain_grad
    g_buf[0, 1:2, :] = sg_ref[...]
    g_buf[0, 2:8, :] = jnp.zeros((6, D), F32)
    g_moves = [
        to_x(g_buf.at[0], g_come.at[0], g_send.at[0], g_recv.at[0]),
        to_dp(1, g_buf.at[1], g_come.at[1], g_send.at[1], g_recv.at[1]),
        to_dp(2, g_buf.at[2], g_come.at[2], g_send.at[2], g_recv.at[2]),
    ]
    g_moves[0].start()
    g_moves[0].wait()
    g_buf[1] = g_buf[0] + g_come[0]
    g_moves[1].start()
    to_y.wait()

    def add_y(k, carry):
        qp[k, y, c] = (qp[k, y, c].astype(F32) + q_y[k].astype(F32)).astype(BF)
        return carry

    lax.fori_loop(0, outer, add_y, 0)
    z_moves = []
    for k in range(1, outer):
        peer = (o + k) % outer
        z_moves.append(
            pltpu.make_async_remote_copy(
                qp.at[peer, y, c],
                q_z.at[k - 1],
                q_send.at[1 + k],
                q_recv.at[1 + k],
                device_id=(peer * GROUP + i, t),
                device_id_type=MESH,
            )
        )
    for move in z_moves:
        move.start()
    group.core[1].wait_recv()
    mixer.mix(1, 0, group.near.at[1], group.come.at[1])
    group.a.start()
    group.b[1].start()
    sums.wait()
    last.load()
    last.send()
    g_moves[1].wait()
    g_buf[2] = g_buf[1] + g_come[1]
    g_moves[2].start()
    group.core[0].wait_recv()
    mixer.mix(0, 1, group.near.at[0], group.come.at[0])
    group.b[0].start()
    g_moves[2].wait()
    g_z[0] = g_buf[2] + g_come[2]
    gz_moves = []
    for k in range(1, outer):
        peer = (o + k) % outer
        gz_moves.append(
            pltpu.make_async_remote_copy(
                g_z.at[0],
                g_z.at[k],
                g_send.at[2 + k],
                g_recv.at[2 + k],
                device_id=(peer * GROUP + i, t),
                device_id_type=MESH,
            )
        )
    for move in gz_moves:
        move.start()
    group.second()
    finals[1].send()
    for move in z_moves:
        move.wait()
    total = qp[o, y, c].astype(F32)
    for k in range(1, outer):
        total = total + q_z[k - 1].astype(F32)
    qkv_ref[...] = total[:, :width]
    outw_ref[...] = total[:, width:]
    for move in gz_moves:
        move.wait()
    gains = g_z[(o + outer) % outer]
    for k in range(1, outer):
        gains = gains + g_z[(o - k + outer) % outer]
    gains_ref[...] = gains
    for p in range(2):
        at = slice(p * rows // 2, (p + 1) * rows // 2)
        out_ref[at] = jnp.where(valid_ref[at] > 0, hidden_ref[at] + group.terms(p), 0.0).astype(BF)
    last.wait()
    finals[2].send()
    group.sent()
    for final in finals:
        final.wait()


def finish(outer, in_rows, length, pos, gate, valid, hidden, hgrad, x, gain, weights_full, extra, ys, dws, done, was_l, was_r):
    rows = hidden.shape[0]
    n = len(ys)
    packed = dws[0].shape[2]
    width = weights_full.shape[1] // 2
    heads = width // 2
    each = D // (outer * GROUP)
    hop = jax.ShapeDtypeStruct((GROUP, packed, D), BF)
    columns = width + heads
    return remote_call(
        functools.partial(finish_kernel, outer, in_rows),
        "finish",
        11,
        [
            jax.ShapeDtypeStruct((rows, D), BF),
            jax.ShapeDtypeStruct((rows, D), F32),
            jax.ShapeDtypeStruct((8, D), F32),
            jax.ShapeDtypeStruct((each, width), F32),
            jax.ShapeDtypeStruct((each, heads), F32),
        ]
        + [hop] * 9,
        [SMEM] + [VM] * 7 + [ANY] + [VM] * 6 + [ANY] * (n + 9),
        [VM] * 5 + [ANY] * 9,
        (length, pos, gate, valid, hidden, hgrad, x, gain.reshape(1, D), weights_full, *extra, *ys, *dws, *done, *was_l, *was_r),
        [
            *group_scratch(2 * rows, n),
            *sums_scratch(2, packed),
            *again(sums_scratch(1, packed)),
            *final_scratch(packed) * 3,
            pltpu.VMEM((rows, D), BF),
            pltpu.VMEM((rows, D), BF),
            pltpu.SemaphoreType.DMA,
            pltpu.SemaphoreType.DMA,
            pltpu.VMEM((outer, 2, 2, each, columns), BF),
            pltpu.VMEM((outer, 2, each, columns), BF),
            pltpu.VMEM((outer, each, columns), BF),
            pltpu.VMEM((outer - 1, each, columns), BF),
            pltpu.SemaphoreType.DMA((1 + outer,)),
            pltpu.SemaphoreType.DMA((1 + outer,)),
            pltpu.VMEM((3, 8, D), F32),
            pltpu.VMEM((3, 8, D), F32),
            pltpu.VMEM((outer, 8, D), F32),
            pltpu.SemaphoreType.DMA((2 + outer,)),
            pltpu.SemaphoreType.DMA((2 + outer,)),
            pltpu.VMEM((D, width), BF),
            pltpu.SemaphoreType.DMA,
        ],
        30 << 30,
    )


def settle_kernel(n, in_rows, idx_ref, *refs):
    sources, (in_ref, down_ref) = refs[:n], refs[n:]
    j = pl.program_id(0)
    for k in range(n):

        @pl.when(j == k)
        def _(k=k):
            in_ref[0] = sources[k][0, :in_rows, :].astype(F32)
            down_ref[0] = sources[k][0, in_rows:, :].astype(F32)


def settle_experts(idx, fins, in_rows):
    n = len(fins)
    _, packed, _ = fins[0].shape
    experts = n * GROUP

    def source(k):
        return lambda j, m, idx_ref: (jnp.where(j == k, m, jnp.where(j < k, 0, GROUP - 1)), 0, 0)

    def target(j, m, idx_ref):
        return ((idx_ref[1] ^ m) * n + j, 0, 0)

    return pl.pallas_call(
        functools.partial(settle_kernel, n, in_rows),
        name="settle_experts",
        out_shape=[
            jax.ShapeDtypeStruct((experts, in_rows, D), F32),
            jax.ShapeDtypeStruct((experts, packed - in_rows, D), F32),
        ],
        grid_spec=pltpu.PrefetchScalarGridSpec(
            num_scalar_prefetch=1,
            grid=(n, GROUP),
            in_specs=[pl.BlockSpec((1, packed, D), source(k)) for k in range(n)],
            out_specs=[pl.BlockSpec((1, in_rows, D), target), pl.BlockSpec((1, packed - in_rows, D), target)],
        ),
        compiler_params=pltpu.CompilerParams(vmem_limit_bytes=VMEM_LIMIT),
        cost_estimate=pl.CostEstimate(flops=0, bytes_accessed=9 << 20, transcendentals=0),
    )(idx, *fins)


def layer(
    tokens,
    cotangent,
    lengths,
    expert_ids,
    gate_values,
    first_gain,
    qkv_weight,
    attn_out_weight,
    second_gain,
    expert_in_weight,
    expert_out_weight,
):
    rows = tokens.shape[0]
    n_tensor, n_dp = lax.axis_size("tensor"), lax.axis_size("dp")
    outer = n_dp // GROUP
    slot_rows = rows * n_tensor
    d, t = lax.axis_index("dp"), lax.axis_index("tensor")
    o, i = d // GROUP, d % GROUP
    length = lengths[0]
    idx = jnp.stack([o, i, t, length]).astype(jnp.int32)
    width = qkv_weight.shape[1] * qkv_weight.shape[2]
    experts_local, in_rows, _ = expert_in_weight.shape
    down_rows = expert_out_weight.shape[1]
    own_experts = experts_local // GROUP
    pair = n_tensor == 2
    q_block = 256
    half = rows // 2

    def across(v, m):
        return lax.ppermute(v, "dp", [(a, a ^ m) for a in range(n_dp)])

    def beside(v):
        return lax.ppermute(v, "tensor", [(0, 1), (1, 0)])

    def hop(pairs):
        up = [(a, a + GROUP) for a in range(n_dp - GROUP)]
        down = [(b, a) for a, b in up]
        return [(lax.ppermute(a, "dp", up), lax.ppermute(b, "dp", down)) for a, b in pairs]

    def gather_group(pieces):
        if pair:
            a, b = pieces
            ax, by, ay, bx = beside(a), across(b, 2), across(a, 2), beside(b)
            axy, bxy = across(ax, 2), beside(by)
            slots = [[a, ax, b, bx], [ay, axy, by, bxy]]
        else:
            slot = lax.all_gather(pieces[0], "tensor", axis=0, tiled=True)
            slots = [[slot], [across(slot, 2)]]
        return slots + [[across(p, 1) for p in s] for s in slots]

    positions = t * rows + jnp.arange(rows, dtype=jnp.int32)
    valid_rows = positions < length
    n_experts = experts_local * n_tensor
    chosen = expert_ids.T[None] == jnp.arange(n_experts, dtype=jnp.int32)[:, None, None]
    gates = jnp.sum(jnp.where(chosen, gate_values.T[None].astype(F32), 0.0), axis=1)
    gates = jnp.where(valid_rows[None, :], gates, 0.0).astype(BF)
    x = tokens.astype(F32)
    inverse_one = lax.rsqrt(jnp.mean(x * x, axis=-1, keepdims=True) + EPSILON)
    normed_one = (x * inverse_one * first_gain).astype(BF)
    expert_outs, row_grads, weight_grads = [], [], []
    if pair and outer == 4:
        frequency = THETA ** (-(jnp.arange(HD // 2).astype(F32) * 2.0 / HD))
        shard = jnp.concatenate([qkv_weight.reshape(-1, width), attn_out_weight.T], axis=1)
        main, ready, packed, first_l, first_r = collect(
            outer, shard, normed_one, gates, jnp.tile(frequency, 4)[None, :], expert_in_weight, expert_out_weight
        )
        weights_full, other, cosine, sine, pos, own_gates, pos_columns, gate_columns = main
        main, dy_moved, later, one_l, one_r = attention(
            outer,
            q_block,
            lengths,
            normed_one,
            other,
            weights_full,
            cosine,
            sine,
            tokens,
            second_gain,
            cotangent,
            ready[1],
            packed,
        )
        own_weights = [*ready, *later]
        one_l, one_r = [first_l, *one_l], [first_r, *one_r]
        qkv, lse, attn_own, attn_other, hidden, *normed_two = main
        attn_parts = [attn_own, attn_other]
        gathered, out_grads, moved_l, moved_r = spread(
            outer,
            pos,
            own_gates,
            normed_two,
            [cotangent, *dy_moved],
            (2, 2, 2),
            one_l[:3],
            one_r[:3],
        )
        two_l, two_r = [*moved_l], [*moved_r]
        expert_rows, moved_l, moved_r = hand_out(
            outer, pos, normed_two, gathered, (3, 2), [two_l[0], one_l[3]], [two_r[0], one_r[3]]
        )
        three_l, three_r = [moved_l[0]], [moved_r[0]]
        two_l.append(moved_l[1])
        two_r.append(moved_r[1])
        hop_plans = [
            lambda: ((3,), [two_l[1]], [two_r[1]]),
            lambda: ((3,), [two_l[2]], [two_r[2]]),
            lambda: ((3,), [two_l[3]], [two_r[3]]),
            lambda: ((), [], []),
        ]
        sums_l, sums_r = [], []
        for j in range(own_experts):
            first_grad = weight_grads[:1]
            sum_plan = ((j,), first_grad, sums_l or first_grad, sums_r or first_grad) if j else ((), [], [], [])
            (y, dx, dw), moved_l, moved_r, sums_l, sums_r = expert_step(
                j,
                outer,
                in_rows,
                down_rows,
                expert_rows,
                out_grads,
                own_weights[j],
                [one_l[j], two_l[j], three_l[j]],
                [one_r[j], two_r[j], three_r[j]],
                hop_plans[j](),
                sum_plan,
            )
            three_l.extend(moved_l[:1])
            three_r.extend(moved_r[:1])
            expert_outs.append(y)
            row_grads.append(dx)
            weight_grads.append(dw)
        valid_column = valid_rows.astype(F32)[:, None]
        _, dw_b, dw_c, dw_d = weight_grads
        main, sum_l, sum_r = rows_back(
            outer,
            pos_columns,
            valid_column,
            hidden,
            cotangent,
            second_gain,
            weights_full,
            row_grads,
            (1, 1),
            ((2, 0), (2, 1)),
            [dw_b, dw_c],
            [dw_b, dw_c],
            [dw_b, dw_c],
        )
        hidden_grad, branch_grad, second_gain_part, attn_grad_own, attn_grad_other = main
        projected, fin_a, three_l, three_r = attention_back(
            outer,
            q_block,
            lengths,
            qkv,
            lse,
            cosine,
            sine,
            [attn_grad_own, attn_grad_other],
            (3, 1),
            [dw_b, dw_d],
            [sum_l[2], dw_d],
            [sum_r[2], dw_d],
            [weight_grads[0], sums_l[0], sums_r[0]],
        )
        out_own, out_other = (mm_tn(branch_grad, part).astype(BF) for part in attn_parts)
        attn_out_part = (out_own.astype(F32) + beside(out_other).astype(F32)).astype(BF)
        output, tokens_grad, gains, qkv_grad, attn_out_grad, *fins = finish(
            outer,
            in_rows,
            lengths,
            pos_columns,
            gate_columns,
            valid_column,
            hidden,
            hidden_grad,
            tokens,
            first_gain,
            weights_full,
            [normed_one, other, *projected, attn_out_part, second_gain_part],
            expert_outs,
            [dw_b, dw_c, dw_d],
            [three_l[0], three_r[0]],
            [three_l[1], sum_l[3]],
            [three_r[1], sum_r[3]],
        )
        expert_in_grad, expert_out_grad = settle_experts(idx, [fin_a, *fins[:3]], in_rows)
        return (
            output,
            tokens_grad,
            gains[0],
            qkv_grad.reshape(qkv_weight.shape),
            attn_out_grad.T,
            gains[1],
            expert_in_grad,
            expert_out_grad,
        )
    else:
        if pair:
            gates_x = beside(gates)
            slot_gates = jnp.concatenate(
                [gates[:, :half], gates_x[:, :half], gates[:, half:], gates_x[:, half:]], axis=1
            )
        else:
            slot_gates = lax.all_gather(gates, "tensor", axis=1, tiled=True)
        gates_y = across(slot_gates, 2)
        all_gates = jnp.stack([slot_gates, gates_y, across(slot_gates, 1), across(gates_y, 1)])
        own_gates = lax.dynamic_slice_in_dim(
            all_gates, t * experts_local + i * own_experts, own_experts, axis=1
        ).astype(F32)
        named = own_gates > 0
        before = (
            lax.broadcasted_iota(jnp.int32, (slot_rows, slot_rows), 0)
            < lax.broadcasted_iota(jnp.int32, (slot_rows, slot_rows), 1)
        ).astype(BF)
        ranks = jnp.dot(
            named.astype(BF).reshape(GROUP * own_experts, slot_rows), before, preferred_element_type=F32
        ).reshape(GROUP, own_experts, slot_rows)
        pos = jnp.where(named, ranks, -1.0).astype(jnp.int32)
        pos_columns, gate_columns = jnp.swapaxes(pos, 1, 2), jnp.swapaxes(own_gates, 1, 2)

        cosine, sine = rope_tables(slot_rows)
        dy = jnp.where(valid_rows[:, None], cotangent, jnp.zeros_like(cotangent))
        qkv_full = lax.all_gather(qkv_weight.reshape(qkv_weight.shape[0], width), "dp", axis=0, tiled=True)
        out_full = lax.all_gather(attn_out_weight.T, "dp", axis=0, tiled=True)
        by_distance = pack_weights(idx, expert_in_weight, expert_out_weight)
        by_distance = [by_distance[0]] + [across(by_distance[m], m) for m in range(1, GROUP)]
        own_weights = [jnp.stack([v[j] for v in by_distance]) for j in range(own_experts)]
        hops = [hop([(own, own) for own in own_weights])]
        if pair:
            out_parts = [out_full, beside(out_full)]
        else:
            gathered = lax.all_gather(out_full, "tensor", axis=0)
            out_parts = [gathered[k] for k in range(n_tensor)]

        if pair:
            other = beside(normed_one)
            normed_all = jnp.where(
                t == 0,
                jnp.concatenate([normed_one, other], axis=0),
                jnp.concatenate([other, normed_one], axis=0),
            )
        else:
            normed_all = lax.all_gather(normed_one, "tensor", axis=0, tiled=True)
        qkv = qkv_project(normed_all, qkv_full, cosine, sine)
        *attended, lse = attend(idx, qkv, 2 if pair else 1, q_block)
        if pair:
            attn_parts = [attended[0], beside(attended[1])]
        else:
            heads = attended[0].shape[1]
            exchanged = lax.all_to_all(attended[0].reshape(n_tensor, rows, heads), "tensor", 0, 0)
            attn_parts = [exchanged[k] for k in range(n_tensor)]
        attn_parts, hops[0] = lax.optimization_barrier((attn_parts, hops[0]))
        if outer > 2:
            hops.append(hop(hops[0]))
        hidden, *normed_two = project_out(tokens, second_gain, attn_parts, out_parts, 2 if pair else 1)

        dy_slots = gather_group([dy[:half], dy[half:]] if pair else [dy])
        out_grads = [dispatch(pos[s], own_gates[s], dy_slots[s], True) for s in range(GROUP)]
        normed_slots = gather_group(normed_two)
        normed_slots, out_grads, hops = lax.optimization_barrier((normed_slots, out_grads, hops))
        while len(hops) < outer - 1:
            hops.append(hop(hops[-1]))
        expert_rows = [dispatch(pos[s], own_gates[s], normed_slots[s], False) for s in range(GROUP)]

        for j in range(own_experts):
            if j:
                idx, expert_outs[-1] = lax.optimization_barrier((idx, expert_outs[-1]))
            y, dx, dw = expert(
                idx,
                j,
                outer,
                in_rows,
                down_rows,
                expert_rows,
                out_grads,
                own_weights[j],
                [h[j][0] for h in hops],
                [h[j][1] for h in hops],
            )
            expert_outs.append(y)
            row_grads.append(dx)
            weight_grads.append(dw)

    def sum_group(sources, scaled):
        def part(s, add, n_outs):
            return combine(pos_columns[s], gate_columns[s], sources, s, scaled, add, n_outs)

        far = [part(2, None, 1)[0], part(3, None, 1)[0]]
        near = [across(v, 1) for v in far]
        if pair:
            ay, axy, by, bxy = part(1, near[1], 4)
            a, ax, b, bx = part(0, near[0], 4)

            def add(p, q):
                return (p.astype(F32) + q.astype(F32)).astype(BF)

            a, ax = add(a, across(ay, 2)), add(ax, across(axy, 2))
            b, by = add(b, beside(bx)), add(by, beside(bxy))
            return [[a, beside(ax)], [b, across(by, 2)]]
        (y,) = part(1, near[1], 1)
        (v,) = part(0, near[0], 1)
        v = (v.astype(F32) + across(y, 2).astype(F32)).astype(BF)
        return [[lax.psum_scatter(v, "tensor", scatter_dimension=0, tiled=True)]]

    valid_column = valid_rows.astype(F32)[:, None]
    normed_two_grad = sum_group(row_grads, False)
    hidden_grad, branch_grad, second_gain_part, *attn_grads = hidden_back(
        valid_column, hidden, cotangent, second_gain, normed_two_grad, out_parts
    )
    if pair:
        attn_grads = [attn_grads[0], beside(attn_grads[1])]
    else:
        attn_grads = [
            lax.all_to_all(jnp.stack(attn_grads), "tensor", 0, 0).reshape(slot_rows, attn_grads[0].shape[1])
        ]
    projected_grads = attend_back(idx, qkv, lse, cosine, sine, attn_grads, q_block)

    def first_norm_part(v):
        return lax.dot_general(v, qkv_full, (((1,), (1,)), ((), ())), preferred_element_type=F32).astype(BF)

    if pair:
        theirs = beside(first_norm_part(projected_grads[1]))
        normed_one_grad = first_norm_part(projected_grads[0]).astype(F32) + theirs.astype(F32)
        qkv_part = mm_tn(normed_one, projected_grads[0]) + mm_tn(other, projected_grads[1])
    else:
        normed_one_grad = lax.psum_scatter(
            first_norm_part(projected_grads[0]), "tensor", scatter_dimension=0, tiled=True
        ).astype(F32)
        qkv_part = mm_tn(normed_all, projected_grads[0])
    first_gain_part = jnp.sum(normed_one_grad * (x * inverse_one), axis=0)
    scaled = normed_one_grad * first_gain
    tokens_grad = (
        hidden_grad
        + inverse_one * scaled
        - x * (inverse_one * inverse_one * inverse_one * jnp.mean(scaled * x, axis=-1, keepdims=True))
    )

    mixture = sum_group(expert_outs, True)
    mixture = jnp.concatenate([sum(v.astype(F32) for v in terms) for terms in mixture], axis=0)
    output = jnp.where(valid_rows[:, None], hidden + mixture, 0.0).astype(BF)

    outer_groups = [[a * GROUP + b for a in range(outer)] for b in range(GROUP)]
    received = [[] for _ in range(GROUP)]
    for dw in weight_grads:
        mine = lax.psum_scatter(dw, "dp", scatter_dimension=0, tiled=True, axis_index_groups=outer_groups)
        for m in range(GROUP):
            block = mine[0, m]
            received[m].append(block if m == 0 else across(block, m))
    by_distance = jnp.stack([jnp.stack(v) for v in received])
    by_source = jnp.take(by_distance, jnp.arange(GROUP) ^ i, axis=0).reshape(
        experts_local, in_rows + down_rows, D
    )
    expert_in_grad = by_source[:, :in_rows].astype(F32)
    expert_out_grad = by_source[:, in_rows:].astype(F32)

    attn_out_parts = [mm_tn(branch_grad, part).astype(BF) for part in attn_parts]
    if pair:
        attn_out_part = (attn_out_parts[0].astype(F32) + beside(attn_out_parts[1]).astype(F32)).astype(BF)
    else:
        attn_out_part = lax.psum_scatter(jnp.stack(attn_out_parts), "tensor", scatter_dimension=0, tiled=True)[0]
    qkv_grad = lax.psum_scatter(qkv_part.astype(BF), "dp", scatter_dimension=0, tiled=True).astype(F32)
    attn_out_grad = lax.psum_scatter(attn_out_part, "dp", scatter_dimension=0, tiled=True).astype(F32).T

    gains = jnp.stack([first_gain_part, second_gain_part[0]])
    if pair:
        gains = gains + beside(gains)
    else:
        gains = lax.psum(gains, "tensor")
    step = 1
    while step < n_dp:
        gains = gains + across(gains, step)
        step *= 2
    return (
        output,
        tokens_grad,
        gains[0],
        qkv_grad.reshape(qkv_weight.shape),
        attn_out_grad,
        gains[1],
        expert_in_grad,
        expert_out_grad,
    )


def solution(mesh):
    placed = (
        P(("dp", "tensor"), None),
        P(("dp", "tensor"), None),
        P("dp"),
        P(("dp", "tensor"), None),
        P(("dp", "tensor"), None),
        P(),
        P("dp", "tensor", None),
        P("tensor", "dp"),
        P(),
        P("tensor", "dp", None),
        P("tensor", "dp", None),
    )
    return jax.shard_map(
        layer,
        mesh=mesh,
        in_specs=placed,
        out_specs=(
            P(("dp", "tensor"), None),
            P(("dp", "tensor"), None),
            P(),
            P("dp", "tensor", None),
            P("tensor", "dp"),
            P(),
            P("tensor", "dp", None),
            P("tensor", "dp", None),
        ),
        check_vma=False,
    )
```

```python
import functools
import math

import jax
import jax.numpy as jnp
from jax import lax
from jax.experimental import pallas as pl
from jax.experimental.pallas import tpu as pltpu
from jax.sharding import PartitionSpec as P

D = 1024
HD = 64
FF = 512
G = 2
CAP = 288
GROUP = 4
LANES = 128

EPSILON = 1e-06
THETA = 10000.0
NEGATIVE = -1e30
BF = jnp.bfloat16
F32 = jnp.float32
VMEM_LIMIT = 60 * 1024 * 1024
MESH = pl.DeviceIdType.MESH

ANY = pl.BlockSpec(memory_space=pl.ANY)
SMEM = pl.BlockSpec(memory_space=pltpu.SMEM)
VM = pl.BlockSpec(memory_space=pltpu.VMEM)


def mm(a, b):
    return lax.dot_general(a, b, (((1,), (0,)), ((), ())), preferred_element_type=F32)


def mm_nt(a, b):
    return lax.dot_general(a, b, (((1,), (1,)), ((), ())), preferred_element_type=F32)


def mm_tn(a, b):
    return lax.dot_general(a, b, (((0,), (0,)), ((), ())), preferred_element_type=F32)


def call(kernel, name, out_shape, in_specs, out_specs, args, scratch=(), flops=0, moved=0, **more):
    return pl.pallas_call(
        kernel,
        name=name,
        out_shape=out_shape,
        in_specs=in_specs,
        out_specs=out_specs,
        scratch_shapes=list(scratch),
        compiler_params=pltpu.CompilerParams(vmem_limit_bytes=VMEM_LIMIT),
        cost_estimate=pl.CostEstimate(flops=flops, bytes_accessed=moved, transcendentals=0),
        **more,
    )(*args)


def rope_tables(total_rows):
    half = HD // 2
    positions = jnp.arange(total_rows).astype(F32)
    frequency = THETA ** (-(jnp.arange(half).astype(F32) * 2.0 / HD))
    angles = positions[:, None] * frequency[None, :]
    cosine, sine = jnp.cos(angles), jnp.sin(angles)
    return (
        jnp.concatenate([cosine] * 4, axis=1),
        jnp.concatenate([-sine, sine, -sine, sine], axis=1),
    )


def swap_halves(v):
    lane = lax.broadcasted_iota(jnp.int32, v.shape, 1)
    return jnp.where(lane % HD < HD // 2, pltpu.roll(v, LANES - HD // 2, 1), pltpu.roll(v, HD // 2, 1))


def qkv_kernel(n_ref, w_ref, cos_ref, sin_ref, out_ref):
    projected = mm(n_ref[...], w_ref[...])
    cosine, sine = cos_ref[...], sin_ref[...]
    key_lanes = lax.broadcasted_iota(jnp.int32, cosine.shape, 1) < HD
    for g in range(projected.shape[1] // (2 * LANES)):
        q = projected[:, g * 2 * LANES : g * 2 * LANES + LANES]
        kv = projected[:, g * 2 * LANES + LANES : (g + 1) * 2 * LANES]
        q = q * cosine + swap_halves(q) * sine
        kv = jnp.where(key_lanes, kv * cosine + swap_halves(kv) * sine, kv)
        out_ref[:, g * 2 * LANES : g * 2 * LANES + LANES] = q.astype(BF)
        out_ref[:, g * 2 * LANES + LANES : (g + 1) * 2 * LANES] = kv.astype(BF)


def qkv_project(normed, weight, cosine, sine):
    rows, width = normed.shape[0], weight.shape[1]
    block = 256
    return pl.pallas_call(
        qkv_kernel,
        name="qkv_rope",
        grid=(rows // block,),
        out_shape=jax.ShapeDtypeStruct((rows, width), BF),
        in_specs=[
            pl.BlockSpec((block, D), lambda b: (b, 0)),
            pl.BlockSpec((D, width), lambda b: (0, 0)),
            pl.BlockSpec((block, LANES), lambda b: (b, 0)),
            pl.BlockSpec((block, LANES), lambda b: (b, 0)),
        ],
        out_specs=pl.BlockSpec((block, width), lambda b: (b, 0)),
        compiler_params=pltpu.CompilerParams(vmem_limit_bytes=VMEM_LIMIT),
        cost_estimate=pl.CostEstimate(flops=2 * rows * D * width, bytes_accessed=6 << 20, transcendentals=0),
    )(normed, weight, cosine, sine)


def head_pair(v):
    first = lax.broadcasted_iota(jnp.int32, v.shape, 1) < HD
    zero = jnp.zeros_like(v)
    return jnp.concatenate([jnp.where(first, v, zero), jnp.where(first, zero, v)], axis=0)


def head_join(v):
    n = v.shape[0] // 2
    first = lax.broadcasted_iota(jnp.int32, (n, LANES), 1) < HD
    return jnp.where(first, v[:n], v[n:])


def doubled(kv):
    first = lax.broadcasted_iota(jnp.int32, kv.shape, 1) < HD
    other = pltpu.roll(kv.astype(F32), HD, 1).astype(BF)
    return jnp.where(first, kv, other), jnp.where(first, other, kv)


def allowed(n_keys, q_block, q_start, length):
    key = lax.broadcasted_iota(jnp.int32, (n_keys, 2 * q_block), 0)
    lane = lax.broadcasted_iota(jnp.int32, (n_keys, 2 * q_block), 1)
    query = q_start + jnp.where(lane < q_block, lane, lane - q_block)
    return (key <= query) & (key < length)


def attend_kernel(q_block, idx_ref, qkv_ref, *out_refs):
    outs, lse_ref = out_refs[:-1], out_refs[-1]
    rows = qkv_ref.shape[0]
    length = idx_ref[3]
    keys, values = doubled(qkv_ref[:, LANES:])
    for b in range(rows // q_block):
        start, n_keys = b * q_block, (b + 1) * q_block
        q = head_pair(qkv_ref[start : start + q_block, :LANES])
        scores = mm_nt(keys[:n_keys], q) * (1.0 / math.sqrt(HD))
        scores = jnp.where(allowed(n_keys, q_block, start, length), scores, NEGATIVE)
        largest = jnp.max(scores, axis=0, keepdims=True)
        expon = jnp.exp(scores - largest)
        totals = jnp.sum(expon, axis=0, keepdims=True)
        probs = (expon * (1.0 / totals)).astype(BF)
        mixed = head_join(mm_tn(probs, values[:n_keys])).astype(BF)
        lse_ref[0, b : b + 1, :] = largest + jnp.log(totals)
        if len(outs) == 1:
            outs[0][start : start + q_block] = mixed
        else:
            own_rows = rows // 2
            half, at = start // own_rows, start % own_rows
            mine = idx_ref[2] == half

            @pl.when(mine)
            def _():
                outs[0][at : at + q_block] = mixed

            @pl.when(jnp.logical_not(mine))
            def _():
                outs[1][at : at + q_block] = mixed


def attend(idx, qkv, parts, q_block):
    rows, groups = qkv.shape[0], qkv.shape[1] // (2 * LANES)
    out = jax.ShapeDtypeStruct((rows // parts, groups * LANES), BF)
    return pl.pallas_call(
        functools.partial(attend_kernel, q_block),
        name="attend",
        grid=(groups,),
        out_shape=[out] * parts + [jax.ShapeDtypeStruct((groups, rows // q_block, 2 * q_block), F32)],
        in_specs=[SMEM, pl.BlockSpec((rows, 2 * LANES), lambda g: (0, g))],
        out_specs=[pl.BlockSpec((rows // parts, LANES), lambda g: (0, g))] * parts
        + [pl.BlockSpec((1, rows // q_block, 2 * q_block), lambda g: (g, 0, 0))],
        compiler_params=pltpu.CompilerParams(vmem_limit_bytes=VMEM_LIMIT),
        cost_estimate=pl.CostEstimate(flops=14 << 30, bytes_accessed=4 << 20, transcendentals=0),
    )(idx, qkv)


def attend_back_kernel(q_block, n_grads, idx_ref, qkv_ref, lse_ref, cos_ref, sin_ref, *refs):
    grads, outs = refs[:n_grads], refs[n_grads : 2 * n_grads]
    do_ref, dq_ref, dk_ref, dv_ref = refs[2 * n_grads :]
    rows = qkv_ref.shape[0]
    own_rows = rows // n_grads
    length = idx_ref[3]
    for p in range(n_grads):
        at = pl.multiple_of((p ^ idx_ref[2] if n_grads == 2 else 0) * own_rows, own_rows)
        do_ref[pl.ds(at, own_rows), :] = grads[p][...]
    keys, values = doubled(qkv_ref[:, LANES:])
    dk_ref[...] = jnp.zeros_like(dk_ref)
    dv_ref[...] = jnp.zeros_like(dv_ref)
    scale = 1.0 / math.sqrt(HD)
    for b in range(rows // q_block):
        start, n_keys = b * q_block, (b + 1) * q_block
        q = head_pair(qkv_ref[start : start + q_block, :LANES])
        grad = head_pair(do_ref[start : start + q_block, :])
        scores = mm_nt(keys[:n_keys], q) * scale
        probs = jnp.where(
            allowed(n_keys, q_block, start, length), jnp.exp(scores - lse_ref[0, b : b + 1, :]), 0.0
        )
        prob_grad = mm_nt(values[:n_keys], grad)
        center = jnp.sum(probs * prob_grad, axis=0, keepdims=True)
        score_grad = (probs * (prob_grad - center)).astype(BF)
        dq_ref[start : start + q_block, :] = head_join(mm_tn(score_grad, keys[:n_keys])) * scale
        dk_ref[:n_keys, :] += mm(score_grad, q)
        dv_ref[:n_keys, :] += mm(probs.astype(BF), grad)
    cosine, sine = cos_ref[...], sin_ref[...]
    dq = dq_ref[...]
    dq = (dq * cosine - swap_halves(dq) * sine).astype(BF)
    dk, dv = dk_ref[...] * scale, dv_ref[...]
    dk = dk + pltpu.roll(dk, HD, 1)
    dv = dv + pltpu.roll(dv, HD, 1)
    dk = dk * cosine - swap_halves(dk) * sine
    first = lax.broadcasted_iota(jnp.int32, dk.shape, 1) < HD
    dkv = jnp.where(first, dk, dv).astype(BF)
    if n_grads == 1:
        outs[0][:, :LANES] = dq
        outs[0][:, LANES:] = dkv
    else:
        do_ref[...] = dq
        for p in range(2):
            at = pl.multiple_of((p ^ idx_ref[2]) * own_rows, own_rows)
            outs[p][:, :LANES] = do_ref[pl.ds(at, own_rows), :]
        do_ref[...] = dkv
        for p in range(2):
            at = pl.multiple_of((p ^ idx_ref[2]) * own_rows, own_rows)
            outs[p][:, LANES:] = do_ref[pl.ds(at, own_rows), :]


def attend_back(idx, qkv, lse, cosine, sine, grads, q_block):
    rows, groups, parts = qkv.shape[0], qkv.shape[1] // (2 * LANES), len(grads)
    return pl.pallas_call(
        functools.partial(attend_back_kernel, q_block, parts),
        name="attend_back",
        grid=(groups,),
        out_shape=[jax.ShapeDtypeStruct((rows // parts, groups * 2 * LANES), BF)] * parts,
        in_specs=[
            SMEM,
            pl.BlockSpec((rows, 2 * LANES), lambda g: (0, g)),
            pl.BlockSpec((1, rows // q_block, 2 * q_block), lambda g: (g, 0, 0)),
            pl.BlockSpec((rows, LANES), lambda g: (0, 0)),
            pl.BlockSpec((rows, LANES), lambda g: (0, 0)),
        ]
        + [pl.BlockSpec((rows // parts, LANES), lambda g: (0, g))] * parts,
        out_specs=[pl.BlockSpec((rows // parts, 2 * LANES), lambda g: (0, g))] * parts,
        scratch_shapes=[pltpu.VMEM((rows, LANES), BF)] + [pltpu.VMEM((rows, LANES), F32)] * 3,
        compiler_params=pltpu.CompilerParams(vmem_limit_bytes=VMEM_LIMIT),
        cost_estimate=pl.CostEstimate(flops=30 << 30, bytes_accessed=6 << 20, transcendentals=0),
    )(idx, qkv, lse, cosine, sine, *grads)


def project_out_kernel(n_parts, pieces, x_ref, gain_ref, *refs):
    attns, weights = refs[:n_parts], refs[n_parts : 2 * n_parts]
    hidden_ref, normed_refs = refs[2 * n_parts], refs[2 * n_parts + 1 :]
    rows = x_ref.shape[0] // pieces
    for p in range(pieces):
        at = slice(p * rows, (p + 1) * rows)
        hidden = x_ref[at].astype(F32)
        for a, w in zip(attns, weights, strict=True):
            hidden = hidden + mm_nt(a[at], w[...])
        inverse = lax.rsqrt(jnp.mean(hidden * hidden, axis=-1, keepdims=True) + EPSILON)
        hidden_ref[at] = hidden
        normed_refs[p][...] = (hidden * inverse * gain_ref[...]).astype(BF)


def project_out(x, gain, attns, weights, pieces):
    rows = x.shape[0]
    n = len(attns)
    return call(
        functools.partial(project_out_kernel, n, pieces),
        "project_out",
        [jax.ShapeDtypeStruct((rows, D), F32)] + [jax.ShapeDtypeStruct((rows // pieces, D), BF)] * pieces,
        [VM] * (2 + 2 * n),
        [VM] * (1 + pieces),
        (x, gain.reshape(1, D), *attns, *weights),
        flops=2 * rows * D * D,
        moved=7 << 20,
    )


def hidden_back_kernel(n_parts, pieces, n_sums, valid_ref, hidden_ref, cot_ref, gain_ref, *refs):
    sums, refs = refs[: pieces * n_sums], refs[pieces * n_sums :]
    weights, refs = refs[:n_parts], refs[n_parts:]
    grad_ref, low_ref, gain_grad_ref, attn_refs = refs[0], refs[1], refs[2], refs[3:]
    rows = hidden_ref.shape[0] // pieces
    gain = gain_ref[...]
    gain_grad = jnp.zeros((1, D), F32)
    for p in range(pieces):
        at = slice(p * rows, (p + 1) * rows)
        hidden = hidden_ref[at]
        normed_grad = sums[p * n_sums][...].astype(F32)
        for s in sums[p * n_sums + 1 : (p + 1) * n_sums]:
            normed_grad = normed_grad + s[...].astype(F32)
        inverse = lax.rsqrt(jnp.mean(hidden * hidden, axis=-1, keepdims=True) + EPSILON)
        gain_grad = gain_grad + jnp.sum(normed_grad * (hidden * inverse), axis=0, keepdims=True)
        scaled = normed_grad * gain
        back = inverse * scaled - hidden * (
            inverse * inverse * inverse * jnp.mean(scaled * hidden, axis=-1, keepdims=True)
        )
        dy = jnp.where(valid_ref[at] > 0, cot_ref[at].astype(F32), 0.0)
        total = dy + back
        grad_ref[at] = total
        low = total.astype(BF)
        low_ref[at] = low
        for a, w in zip(attn_refs, weights, strict=True):
            a[at] = mm(low, w[...]).astype(BF)
    gain_grad_ref[...] = gain_grad


def hidden_back(valid, hidden, cotangent, gain, sums, weights):
    rows, pieces, n_sums, n = hidden.shape[0], len(sums), len(sums[0]), len(weights)
    heads = weights[0].shape[1]
    return call(
        functools.partial(hidden_back_kernel, n, pieces, n_sums),
        "hidden_back",
        [
            jax.ShapeDtypeStruct((rows, D), F32),
            jax.ShapeDtypeStruct((rows, D), BF),
            jax.ShapeDtypeStruct((1, D), F32),
        ]
        + [jax.ShapeDtypeStruct((rows, heads), BF)] * n,
        [VM] * (4 + pieces * n_sums + n),
        [VM] * (3 + n),
        (valid, hidden, cotangent, gain.reshape(1, D), *[s for piece in sums for s in piece], *weights),
        flops=2 * rows * D * D,
        moved=10 << 20,
    )


def dispatch_kernel(n_pieces, scaled, pos_ref, gate_ref, *refs):
    pieces, out_ref, rows_ref, sems = refs[:n_pieces], refs[n_pieces], refs[n_pieces + 1], refs[n_pieces + 2]
    height = rows_ref.shape[0] // n_pieces
    copies = [
        pltpu.make_async_copy(piece, rows_ref.at[pl.ds(p * height, height)], sems.at[p])
        for p, piece in enumerate(pieces)
    ]
    for c in copies:
        c.start()
    rank = lax.broadcasted_iota(jnp.int32, (CAP, rows_ref.shape[0]), 0)
    for c in copies:
        c.wait()
    for j in range(out_ref.shape[0]):
        chosen = rank == pos_ref[j : j + 1, :]
        value = gate_ref[j : j + 1, :] if scaled else 1.0
        one_hot = jnp.where(chosen, value, 0.0).astype(BF)
        out_ref[j] = mm(one_hot, rows_ref[...]).astype(BF)


def dispatch(pos, gate, pieces, scaled):
    experts, rows = pos.shape
    return call(
        functools.partial(dispatch_kernel, len(pieces), scaled),
        "dispatch_scaled" if scaled else "dispatch",
        jax.ShapeDtypeStruct((experts, CAP, D), BF),
        [VM, VM] + [ANY] * len(pieces),
        VM,
        (pos, gate, *pieces),
        scratch=[pltpu.VMEM((rows, D), BF), pltpu.SemaphoreType.DMA((len(pieces),))],
        flops=2 * experts * CAP * rows * D,
        moved=5 << 20,
    )


def combine_kernel(n_experts, slot, scaled, n_adds, n_outs, pos_ref, gate_ref, *refs):
    sources, refs = refs[:n_experts], refs[n_experts:]
    adds, outs, (held, sems) = refs[:n_adds], refs[n_adds : n_adds + n_outs], refs[n_adds + n_outs :]
    copies = [
        pltpu.make_async_copy(source.at[slot], held.at[pl.ds(j * CAP, CAP)], sems.at[j])
        for j, source in enumerate(sources)
    ]
    for c in copies:
        c.start()
    for c in copies:
        c.wait()
    width = n_experts * CAP
    rows = pos_ref.shape[0]
    block = 256
    per_out = rows // n_outs
    for b in range(rows // block):
        at = slice(b * block, (b + 1) * block)
        tiles = []
        for first in range(0, width, LANES):
            size = min(LANES, width - first)
            lane = first + lax.broadcasted_iota(jnp.int32, (block, size), 1)
            tile = jnp.zeros((block, size), F32)
            for j in range(first // CAP, (first + size - 1) // CAP + 1):
                target = pos_ref[at, j : j + 1]
                target = jnp.where(target >= 0, target + j * CAP, -1)
                tile = jnp.where(lane == target, gate_ref[at, j : j + 1] if scaled else 1.0, tile)
            tiles.append(tile.astype(BF))
        total = mm(jnp.concatenate(tiles, axis=1), held[...])
        out, inner = outs[b * block // per_out], slice(b * block % per_out, b * block % per_out + block)
        if n_adds:
            total = total + adds[0][at].astype(F32)
        out[inner] = total.astype(BF)


def combine(pos, gate, sources, slot, scaled, add, n_outs):
    rows, n_experts = pos.shape
    adds = [] if add is None else [add]
    return call(
        functools.partial(combine_kernel, n_experts, slot, scaled, len(adds), n_outs),
        "combine_scaled" if scaled else "combine",
        [jax.ShapeDtypeStruct((rows // n_outs, D), BF)] * n_outs,
        [VM, VM] + [ANY] * n_experts + [VM] * len(adds),
        [VM] * n_outs,
        (pos, gate, *sources, *adds),
        scratch=[pltpu.VMEM((n_experts * CAP, D), BF), pltpu.SemaphoreType.DMA((n_experts,))],
        flops=2 * n_experts * CAP * rows * D,
        moved=5 << 20,
    )


def expert_kernel(j, outer, in_rows, down_rows, idx_ref, *refs):
    n_hops = outer - 1
    xs, refs = refs[:GROUP], refs[GROUP:]
    gs, refs = refs[:GROUP], refs[GROUP:]
    own, refs = refs[0], refs[1:]
    lefts, refs = refs[:n_hops], refs[n_hops:]
    rights, refs = refs[:n_hops], refs[n_hops:]
    y_ref, dx_ref, dw_ref = refs[:3]
    x_all, g_all, w_in, w_down, act_all, gug_all, sem_x, sem_g, sem_w, sem_d = refs[3:]
    o, i = idx_ref[0], idx_ref[1]

    def rows_of(sources, held, sems):
        return [
            pltpu.make_async_copy(s.at[j], held.at[pl.ds(n * CAP, CAP)], sems.at[n])
            for n, s in enumerate(sources)
        ]

    def weight_copies(source, at, slot):
        made = []
        for m in range(GROUP):
            place = at * GROUP + (i ^ m)
            made.append(
                pltpu.make_async_copy(
                    source.at[m, pl.ds(0, in_rows)],
                    w_in.at[pl.ds(pl.multiple_of(place * in_rows, in_rows), in_rows)],
                    sem_w.at[slot * GROUP + m],
                )
            )
            made.append(
                pltpu.make_async_copy(
                    source.at[m, pl.ds(in_rows, down_rows)],
                    w_down.at[pl.ds(pl.multiple_of(place * down_rows, down_rows), down_rows)],
                    sem_d.at[slot * GROUP + m],
                )
            )
        return made

    def each_weight(act):
        act(weight_copies(own, o, 0))
        for k in range(1, outer):

            @pl.when(o >= k)
            def _():
                act(weight_copies(lefts[k - 1], o - k, k))

            @pl.when(o + k < outer)
            def _():
                act(weight_copies(rights[k - 1], o + k, n_hops + k))

    def start(made):
        for c in made:
            c.start()

    def wait(made):
        for c in made:
            c.wait()

    each_weight(start)
    copy_x, copy_g = rows_of(xs, x_all, sem_x), rows_of(gs, g_all, sem_g)
    start(copy_x)
    start(copy_g)
    each_weight(wait)
    wait(copy_x)
    wait(copy_g)

    def per_slot(s, carry):
        at = pl.ds(pl.multiple_of(s * CAP, CAP), CAP)
        gate_up = mm(x_all[at, :], w_in[...])
        g, u = gate_up[:, :FF], gate_up[:, FF:]
        sigma = 1.0 / (1.0 + jnp.exp(-g))
        silu = g * sigma
        act = (silu * u).astype(BF)
        act_all[at, :] = act
        y_ref[s] = mm(act, w_down[...]).astype(BF)
        act_grad = mm_nt(g_all[at, :], w_down[...])
        gug_all[at, :FF] = (act_grad * u * sigma * (1.0 + g * (1.0 - sigma))).astype(BF)
        gug_all[at, FF:] = (act_grad * silu).astype(BF)
        dx_ref[s] = mm_nt(gug_all[at, :], w_in[...]).astype(BF)
        return carry

    lax.fori_loop(0, GROUP, per_slot, 0)
    for c in range(outer):
        part = mm_tn(x_all[:, c * GROUP * in_rows : (c + 1) * GROUP * in_rows], gug_all[...]).astype(BF)
        for r in range(GROUP):
            dw_ref[c, i ^ r, :in_rows, :] = part[r * in_rows : (r + 1) * in_rows]
        part = mm_tn(act_all[:, c * GROUP * down_rows : (c + 1) * GROUP * down_rows], g_all[...]).astype(BF)
        for r in range(GROUP):
            dw_ref[c, i ^ r, in_rows:, :] = part[r * down_rows : (r + 1) * down_rows]


def expert(idx, j, outer, in_rows, down_rows, xs, gs, own, lefts, rights):
    n_hops = outer - 1
    total = GROUP * CAP
    packed = in_rows + down_rows
    return call(
        functools.partial(expert_kernel, j, outer, in_rows, down_rows),
        "expert",
        [
            jax.ShapeDtypeStruct((GROUP, CAP, D), BF),
            jax.ShapeDtypeStruct((GROUP, CAP, D), BF),
            jax.ShapeDtypeStruct((outer, GROUP, packed, D), BF),
        ],
        [SMEM] + [ANY] * (2 * GROUP + 1 + 2 * n_hops),
        [VM] * 3,
        (idx, *xs, *gs, own, *lefts, *rights),
        scratch=[
            pltpu.VMEM((total, D), BF),
            pltpu.VMEM((total, D), BF),
            pltpu.VMEM((D, 2 * FF), BF),
            pltpu.VMEM((FF, D), BF),
            pltpu.VMEM((total, FF), BF),
            pltpu.VMEM((total, 2 * FF), BF),
            pltpu.SemaphoreType.DMA((GROUP,)),
            pltpu.SemaphoreType.DMA((GROUP,)),
            pltpu.SemaphoreType.DMA(((1 + 2 * n_hops) * GROUP,)),
            pltpu.SemaphoreType.DMA(((1 + 2 * n_hops) * GROUP,)),
        ],
        flops=18 * total * D * FF,
        moved=15 << 20,
    )


def pack_kernel(n_experts, in_rows, down_rows, idx_ref, in_ref, down_ref, *refs):
    outs, sems = refs[:-1], refs[-1]
    i = idx_ref[1]
    copies = []
    for j in range(n_experts):
        for m in range(GROUP):
            n = j * GROUP + m
            source = (i ^ m) * n_experts + j
            copies.append(
                pltpu.make_async_copy(in_ref.at[source], outs[m].at[j, pl.ds(0, in_rows)], sems.at[2 * n])
            )
            copies.append(
                pltpu.make_async_copy(
                    down_ref.at[source], outs[m].at[j, pl.ds(in_rows, down_rows)], sems.at[2 * n + 1]
                )
            )
    for c in copies:
        c.start()
    for c in copies:
        c.wait()


def pack_weights(idx, expert_in, expert_down):
    experts, in_rows, _ = expert_in.shape
    down_rows = expert_down.shape[1]
    n = experts // GROUP
    return call(
        functools.partial(pack_kernel, n, in_rows, down_rows),
        "pack_weights",
        [jax.ShapeDtypeStruct((n, in_rows + down_rows, D), BF)] * GROUP,
        [SMEM, ANY, ANY],
        [VM] * GROUP,
        (idx, expert_in, expert_down),
        scratch=[pltpu.SemaphoreType.DMA((2 * experts,))],
        moved=6 << 20,
    )


def place():
    d, t = lax.axis_index("dp"), lax.axis_index("tensor")
    return d, t, d // GROUP, d % GROUP


def flip(v, m):
    first, second = v % 2, (v // 2) % 2
    if m & 1:
        v = v + 1 - 2 * first
    if m & 2:
        v = v + 2 - 4 * second
    return v


def greet(outer, distances, tensor):
    d, t, o, _ = place()
    barrier = pltpu.get_barrier_semaphore()
    count = 0
    for m in distances:
        pl.semaphore_signal(barrier, inc=1, device_id=(flip(d, m), t), device_id_type=MESH)
        count += 1
    if tensor:
        pl.semaphore_signal(barrier, inc=1, device_id=(d, 1 - t), device_id_type=MESH)
        count += 1

    @pl.when(o > 0)
    def _():
        pl.semaphore_signal(barrier, inc=1, device_id=(d - GROUP, t), device_id_type=MESH)

    @pl.when(o < outer - 1)
    def _():
        pl.semaphore_signal(barrier, inc=1, device_id=(d + GROUP, t), device_id_type=MESH)

    neighbours = (o + outer - 1) // outer + (2 * outer - 2 - o) // outer
    pl.semaphore_wait(barrier, count + neighbours)


class Hops:
    def __init__(self, outer, steps, sent, came):
        d, t, o, _ = place()
        self.moves = []
        for n, (k, from_left, from_right, to_left, to_right) in enumerate(steps):
            back = outer - 1 - o
            right = pltpu.make_async_remote_copy(
                from_left, to_left, sent.at[2 * n], came.at[2 * n], device_id=(d + GROUP, t), device_id_type=MESH
            )
            left = pltpu.make_async_remote_copy(
                from_right,
                to_right,
                sent.at[2 * n + 1],
                came.at[2 * n + 1],
                device_id=(d - GROUP, t),
                device_id_type=MESH,
            )
            self.moves.append((right, (o >= k - 1) & (back >= 1), o >= k))
            self.moves.append((left, (back >= k - 1) & (o >= 1), back >= k))

    def start(self):
        for copy, sends, _ in self.moves:
            pl.when(sends)(copy.start)

    def wait(self):
        for copy, sends, receives in self.moves:
            pl.when(sends)(copy.wait_send)
            pl.when(receives)(copy.wait_recv)


def greet_all(outer):
    d, t, o, i = place()
    barrier = pltpu.get_barrier_semaphore()
    for m in range(1, GROUP):
        pl.semaphore_signal(barrier, inc=1, device_id=(flip(d, m), t), device_id_type=MESH)
    pl.semaphore_signal(barrier, inc=1, device_id=(d, 1 - t), device_id_type=MESH)
    for k in range(1, outer):
        pl.semaphore_signal(barrier, inc=1, device_id=((o + k) % outer * GROUP + i, t), device_id_type=MESH)
    pl.semaphore_wait(barrier, GROUP - 1 + outer)


def to_x(src, dst, sent, came):
    d, t, _, _ = place()
    return pltpu.make_async_remote_copy(src, dst, sent, came, device_id=(d, 1 - t), device_id_type=MESH)


def to_dp(m, src, dst, sent, came):
    d, t, _, _ = place()
    return pltpu.make_async_remote_copy(src, dst, sent, came, device_id=(flip(d, m), t), device_id_type=MESH)


def remote_call(kernel, name, collective_id, out_shape, in_specs, out_specs, args, scratch, flops):
    return pl.pallas_call(
        kernel,
        name=name,
        out_shape=out_shape,
        in_specs=in_specs,
        out_specs=out_specs,
        scratch_shapes=list(scratch),
        compiler_params=pltpu.CompilerParams(
            vmem_limit_bytes=VMEM_LIMIT, collective_id=collective_id, has_side_effects=True
        ),
        cost_estimate=pl.CostEstimate(flops=flops, bytes_accessed=8 << 20, transcendentals=0),
    )(*args)


def collect_kernel(outer, in_rows, down_rows, shard_ref, normed_ref, gates_ref, freq_ref, in_ref, down_ref, *refs):
    w_ref, other_ref, cos_ref, sin_ref, pos_ref, gate_ref, posc_ref, gatec_ref = refs[:8]
    own_refs, packed_refs, to_left, to_right = refs[8:10], refs[10:12], refs[12], refs[13]
    packed, gates_all, before, l_w, l_in, l_down, l_own = refs[14:21]
    s_z, r_z, s_y, r_y, s_c, r_c, s_x, r_x, s_g, r_g, s_a, r_a, s_hop, r_hop = refs[21:]
    d, t, o, i = place()
    each = shard_ref.shape[0]
    width = w_ref.shape[1] // 2
    own_width = shard_ref.shape[1]
    n_local = in_ref.shape[0]
    n = n_local // GROUP
    slot_rows = gates_all.shape[2]
    half = slot_rows // 4

    def block(which, index):
        return pl.ds(pl.multiple_of((which * GROUP + index) * each, each), each)

    def lanes(h):
        return pl.ds(h * width, width)

    local = pltpu.make_async_copy(shard_ref, w_ref.at[block(o, i), pl.ds(0, own_width)], l_w)
    local.start()
    packs = []
    for j in range(n):
        for m in range(GROUP):
            source, k = flip(i, m) * n + j, j * GROUP + m
            packs.append(
                (
                    pltpu.make_async_copy(in_ref.at[source], packed.at[j, m, pl.ds(0, in_rows)], l_in.at[k]),
                    pltpu.make_async_copy(down_ref.at[source], packed.at[j, m, pl.ds(in_rows, down_rows)], l_down.at[k]),
                )
            )
    for pair in packs:
        for c in pair:
            c.start()
    greet_all(outer)

    x_moves = [
        to_x(shard_ref.at[:, pl.ds(width, own_width - width)], w_ref.at[block(o, i), pl.ds(own_width, 2 * width - own_width)], s_x.at[0], r_x.at[0]),
        to_x(normed_ref, other_ref, s_x.at[1], r_x.at[1]),
    ]
    g_x = [
        to_x(
            gates_ref.at[:, pl.ds(p * half, half)],
            gates_all.at[0, :, pl.ds((2 * p + 1) * half, half)],
            s_g.at[p],
            r_g.at[p],
        )
        for p in range(2)
    ]
    g_y = to_dp(2, gates_all.at[0], gates_all.at[1], s_g.at[2], r_g.at[2])
    g_c = [to_dp(1, gates_all.at[s], gates_all.at[2 + s], s_g.at[3 + s], r_g.at[3 + s]) for s in range(2)]

    def z_move(k, h):
        peer = (o + k) % outer
        source = shard_ref.at[:, pl.ds(0, width)] if h == 0 else w_ref.at[block(o, i), lanes(1)]
        return pltpu.make_async_remote_copy(
            source,
            w_ref.at[block(o, i), lanes(h)],
            s_z.at[2 * k - 2 + h],
            r_z.at[2 * k - 2 + h],
            device_id=(peer * GROUP + i, t),
            device_id_type=MESH,
        )

    def near_source(b, h):
        if b == 0 and h == 0:
            return shard_ref.at[:, pl.ds(0, width)]
        return w_ref.at[block((o + outer - b) % outer, i), lanes(h)]

    def y_move(b, h):
        target = w_ref.at[block((o + outer - b) % outer, i), lanes(h)]
        return to_dp(2, near_source(b, h), target, s_y.at[2 * b + h], r_y.at[2 * b + h])

    def c_move(b, far, h):
        target = w_ref.at[block((o + outer - b) % outer, flip(i, 2) if far else i), lanes(h)]
        source = target if far else near_source(b, h)
        k = (2 * b + far) * 2 + h
        return to_dp(1, source, target, s_c.at[k], r_c.at[k])

    def weights_move(j, m):
        return to_dp(m, packed.at[j, m], own_refs[j].at[m], s_a.at[3 * j + m - 1], r_a.at[3 * j + m - 1])

    keeps = [pltpu.make_async_copy(packed.at[j, 0], own_refs[j].at[0], l_own.at[j]) for j in range(2)]
    stays = [pltpu.make_async_copy(packed.at[2 + j], packed_refs[j], l_own.at[2 + j]) for j in range(2)]
    hops = Hops(outer, [(1, own_refs[0], own_refs[0], to_left, to_right)], s_hop, r_hop)

    def packed_there(j):
        for pair in packs[j * GROUP : (j + 1) * GROUP]:
            for c in pair:
                c.wait()

    x_moves[0].start()
    for c in g_x:
        c.start()
    for k in range(1, outer):
        z_move(k, 0).start()
    y_move(0, 0).start()
    c_move(0, 0, 0).start()
    packed_there(0)
    for m in range(1, GROUP):
        weights_move(0, m).start()
    keeps[0].start()
    x_moves[1].start()
    local.wait()
    x_moves[0].wait()
    for k in range(1, outer):
        z_move(k, 1).start()
    packed_there(1)
    keeps[1].start()
    for j in range(2):
        packed_there(2 + j)
        stays[j].start()
    gates_all[0, :, 0:half] = gates_ref[:, 0:half]
    gates_all[0, :, 2 * half : 3 * half] = gates_ref[:, half:]
    angles = lax.broadcasted_iota(jnp.int32, (slot_rows, LANES), 0).astype(F32) * freq_ref[...]
    lane = lax.broadcasted_iota(jnp.int32, (slot_rows, LANES), 1)
    cos_ref[...] = jnp.cos(angles)
    sin_ref[...] = jnp.where(lane % HD < HD // 2, -jnp.sin(angles), jnp.sin(angles))
    for c in g_x:
        c.wait()
    g_y.start()
    g_c[0].start()
    for k in range(1, outer):
        z_move(k, 0).wait_recv()
        y_move(k, 0).start()
        c_move(k, 0, 0).start()
    for m in range(1, GROUP):
        weights_move(1, m).start()
    for b in range(1):
        y_move(b, 1).start()
        c_move(b, 0, 1).start()
    before[...] = (
        lax.broadcasted_iota(jnp.int32, before.shape, 0) < lax.broadcasted_iota(jnp.int32, before.shape, 1)
    ).astype(F32).astype(BF)
    keeps[0].wait()
    for m in range(1, GROUP):
        weights_move(0, m).wait_recv()
    hops.start()
    g_y.wait()
    g_c[1].start()
    for k in range(1, outer):
        z_move(k, 1).wait_recv()
        y_move(k, 1).start()
        c_move(k, 0, 1).start()
    for b in range(outer):
        y_move(b, 0).wait_recv()
        c_move(b, 1, 0).start()
    for c in g_c:
        c.wait()
    n_all = gates_all.shape[1]
    first = t * n_local + i * n
    pick = (
        lax.broadcasted_iota(jnp.int32, (8, n_all), 1) == lax.broadcasted_iota(jnp.int32, (8, n_all), 0) + first
    ).astype(F32).astype(BF)
    for s in range(GROUP):
        gate = mm(pick, gates_all[s])
        rank = mm((gate > 0).astype(F32).astype(BF), before[...])
        gate_ref[s] = gate[:n]
        pos_ref[s] = jnp.where(gate > 0, rank, -1.0).astype(jnp.int32)[:n]
        gate = lax.dot_general(gates_all[s], pick, (((0,), (1,)), ((), ())), preferred_element_type=F32)
        rank = mm_tn(before[...], (gate > 0).astype(F32).astype(BF))
        gatec_ref[s] = gate[:, :n]
        posc_ref[s] = jnp.where(gate > 0, rank, -1.0).astype(jnp.int32)[:, :n]
    for b in range(outer):
        y_move(b, 1).wait_recv()
        c_move(b, 1, 1).start()
    for k in range(1, outer):
        for h in range(2):
            z_move(k, h).wait_send()
    for b in range(outer):
        for h in range(2):
            y_move(b, h).wait_send()
            c_move(b, 0, h).wait()
            c_move(b, 1, h).wait()
    for m in range(1, GROUP):
        weights_move(0, m).wait_send()
        weights_move(1, m).wait()
    x_moves[1].wait()
    keeps[1].wait()
    for c in stays:
        c.wait()
    hops.wait()


def collect(outer, shard, normed, gates, frequency, expert_in, expert_down):
    each, own_width = shard.shape
    width = own_width * 2 // 3
    rows = normed.shape[0]
    experts, in_rows, _ = expert_in.shape
    down_rows = expert_down.shape[1]
    n = experts // GROUP
    packed = in_rows + down_rows
    hop = jax.ShapeDtypeStruct((GROUP, packed, D), BF)
    dma = pltpu.SemaphoreType.DMA
    out = remote_call(
        functools.partial(collect_kernel, outer, in_rows, down_rows),
        "collect",
        13,
        [
            jax.ShapeDtypeStruct((D, 2 * width), BF),
            jax.ShapeDtypeStruct((rows, D), BF),
            jax.ShapeDtypeStruct((2 * rows, LANES), F32),
            jax.ShapeDtypeStruct((2 * rows, LANES), F32),
            jax.ShapeDtypeStruct((GROUP, n, 2 * rows), jnp.int32),
            jax.ShapeDtypeStruct((GROUP, n, 2 * rows), F32),
            jax.ShapeDtypeStruct((GROUP, 2 * rows, n), jnp.int32),
            jax.ShapeDtypeStruct((GROUP, 2 * rows, n), F32),
        ]
        + [hop] * 6,
        [VM] * 4 + [ANY] * 2,
        [VM] * 8 + [ANY] * 6,
        (shard, normed, gates, frequency, expert_in, expert_down),
        [
            pltpu.VMEM((n, GROUP, packed, D), BF),
            pltpu.VMEM((GROUP, gates.shape[0], 2 * rows), BF),
            pltpu.VMEM((2 * rows, 2 * rows), BF),
            dma,
            dma((experts,)),
            dma((experts,)),
            dma((4,)),
            dma((2 * outer - 2,)),
            dma((2 * outer - 2,)),
            dma((2 * outer,)),
            dma((2 * outer,)),
            dma((4 * outer,)),
            dma((4 * outer,)),
            dma((2,)),
            dma((2,)),
            dma((5,)),
            dma((5,)),
            dma((6,)),
            dma((6,)),
            dma((2,)),
            dma((2,)),
        ],
        4 << 30,
    )
    return out[:8], out[8:10], out[10:12], out[12], out[13]


def attention_kernel(outer, q_block, n_steps, len_ref, own_ref, other_ref, w_ref, cos_ref, sin_ref, x_ref, gain_ref, *refs):
    width = w_ref.shape[1] // 2
    heads = width // 2
    cot_ref, ready, packed_refs, refs = refs[0], refs[1], refs[2:4], refs[4:]
    qkv_ref, lse_ref, attn_ref, come_ref, hidden_ref, na_ref, nb_ref = refs[:7]
    refs = refs[7:]
    dy_outs, own_refs, refs = refs[:4], refs[4:6], refs[6:]
    to_left, refs = refs[:n_steps], refs[n_steps:]
    to_right, refs = refs[:n_steps], refs[n_steps:]
    send_ref, s_hop, r_hop, s_later, r_later, s_dy, r_dy, s_at, r_at, s_a, r_a, l_own = refs
    d, t, o, i = place()
    length = len_ref[0]
    rows = own_ref.shape[0]
    groups = width // (2 * LANES)
    greet(outer, (1, 2, 3), True)
    hops = Hops(outer, [(1, ready, ready, to_left[0], to_right[0])], s_hop, r_hop)
    later = Hops(outer, [(1, own_refs[k], own_refs[k], to_left[1 + k], to_right[1 + k]) for k in range(2)], s_later, r_later)
    keeps = [pltpu.make_async_copy(packed_refs[k].at[0], own_refs[k].at[0], l_own.at[k]) for k in range(2)]
    weights = [
        to_dp(m, packed_refs[k].at[m], own_refs[k].at[m], s_a.at[3 * k + m - 1], r_a.at[3 * k + m - 1])
        for k in range(2)
        for m in range(1, GROUP)
    ]
    hops.start()
    for copy in (*weights, *keeps):
        copy.start()
    ax, bx, ay, by = dy_outs
    dy_a, dy_b = (cot_ref.at[pl.ds(p * rows // 2, rows // 2)] for p in range(2))
    dys = [
        to_x(dy_a, ax, s_dy.at[0], r_dy.at[0]),
        to_dp(2, dy_b, by, s_dy.at[1], r_dy.at[1]),
        to_x(dy_b, bx, s_dy.at[2], r_dy.at[2]),
        to_dp(2, dy_a, ay, s_dy.at[3], r_dy.at[3]),
    ]

    block = 256
    key_lanes = lax.broadcasted_iota(jnp.int32, (block, LANES), 1) < HD
    for part in range(2):
        for b in range(rows // block):
            at = pl.multiple_of((t if part == 0 else 1 - t) * rows + b * block, block)
            projected = mm((own_ref if part == 0 else other_ref)[b * block : (b + 1) * block], w_ref[:, :width])
            cosine, sine = cos_ref[pl.ds(at, block), :], sin_ref[pl.ds(at, block), :]
            for g in range(groups):
                q = projected[:, g * 2 * LANES : g * 2 * LANES + LANES]
                kv = projected[:, g * 2 * LANES + LANES : (g + 1) * 2 * LANES]
                q = q * cosine + swap_halves(q) * sine
                kv = jnp.where(key_lanes, kv * cosine + swap_halves(kv) * sine, kv)
                qkv_ref[pl.ds(at, block), g * 2 * LANES : g * 2 * LANES + LANES] = q.astype(BF)
                qkv_ref[pl.ds(at, block), g * 2 * LANES + LANES : (g + 1) * 2 * LANES] = kv.astype(BF)

    for copy in dys:
        copy.start()

    def exchange(g):
        lanes = pl.ds(pl.multiple_of(g * LANES, LANES), LANES)
        return to_x(send_ref.at[:, lanes], come_ref.at[:, lanes], s_at.at[g], r_at.at[g])

    def per_group(g, carry):
        q_lanes = pl.ds(pl.multiple_of(g * 2 * LANES, LANES), LANES)
        kv_lanes = pl.ds(pl.multiple_of(g * 2 * LANES + LANES, LANES), LANES)
        o_lanes = pl.ds(pl.multiple_of(g * LANES, LANES), LANES)
        keys, values = doubled(qkv_ref[:, kv_lanes])
        for b in range(2 * rows // q_block):
            start, n_keys = b * q_block, (b + 1) * q_block
            q = head_pair(qkv_ref[start : start + q_block, q_lanes])
            scores = mm_nt(keys[:n_keys], q) * (1.0 / math.sqrt(HD))
            scores = jnp.where(allowed(n_keys, q_block, start, length), scores, NEGATIVE)
            largest = jnp.max(scores, axis=0, keepdims=True)
            expon = jnp.exp(scores - largest)
            totals = jnp.sum(expon, axis=0, keepdims=True)
            probs = (expon * (1.0 / totals)).astype(BF)
            mixed = head_join(mm_tn(probs, values[:n_keys])).astype(BF)
            lse_ref[g, b : b + 1, :] = largest + jnp.log(totals)
            half, inner = start // rows, start % rows

            @pl.when(t == half)
            def _():
                attn_ref[inner : inner + q_block, o_lanes] = mixed

            @pl.when(t != half)
            def _():
                send_ref[inner : inner + q_block, o_lanes] = mixed

        exchange(g).start()

        @pl.when(g == groups // 2)
        def _():
            for copy in (*weights, *keeps):
                copy.wait()
            later.start()

        return carry

    lax.fori_loop(0, groups, per_group, 0)

    def settle(g, carry):
        exchange(g).wait()
        return carry

    for p, normed_ref in enumerate((na_ref, nb_ref)):
        at = slice(p * rows // 2, (p + 1) * rows // 2)
        hidden_ref[at] = x_ref[at].astype(F32) + mm_nt(attn_ref[at], w_ref[:, width : width + heads])
    lax.fori_loop(0, groups, settle, 0)
    for p, normed_ref in enumerate((na_ref, nb_ref)):
        at = slice(p * rows // 2, (p + 1) * rows // 2)
        hidden = hidden_ref[at] + mm_nt(come_ref[at], w_ref[:, width + heads :])
        inverse = lax.rsqrt(jnp.mean(hidden * hidden, axis=-1, keepdims=True) + EPSILON)
        hidden_ref[at] = hidden
        normed_ref[...] = (hidden * inverse * gain_ref[...]).astype(BF)
    for copy in dys:
        copy.wait()
    hops.wait()
    later.wait()


def attention(outer, q_block, length, own, other, weights_full, cosine, sine, x, gain, cotangent, ready, packed):
    rows, groups = own.shape[0], weights_full.shape[1] // (4 * LANES)
    n = 3
    piece = jax.ShapeDtypeStruct((rows // 2, D), BF)
    hop = jax.ShapeDtypeStruct(ready.shape, BF)
    out = remote_call(
        functools.partial(attention_kernel, outer, q_block, n),
        "attention",
        1,
        [
            jax.ShapeDtypeStruct((2 * rows, groups * 2 * LANES), BF),
            jax.ShapeDtypeStruct((groups, 2 * rows // q_block, 2 * q_block), F32),
            jax.ShapeDtypeStruct((rows, groups * LANES), BF),
            jax.ShapeDtypeStruct((rows, groups * LANES), BF),
            jax.ShapeDtypeStruct((rows, D), F32),
            piece,
            piece,
        ]
        + [piece] * 4
        + [hop] * (2 + 2 * n),
        [SMEM] + [VM] * 7 + [ANY] * 4,
        [VM] * 7 + [ANY] * (6 + 2 * n),
        (length, own, other, weights_full, cosine, sine, x, gain.reshape(1, D), cotangent, ready, *packed),
        [
            pltpu.VMEM((rows, groups * LANES), BF),
            pltpu.SemaphoreType.DMA((2,)),
            pltpu.SemaphoreType.DMA((2,)),
            pltpu.SemaphoreType.DMA((4,)),
            pltpu.SemaphoreType.DMA((4,)),
            pltpu.SemaphoreType.DMA((4,)),
            pltpu.SemaphoreType.DMA((4,)),
            pltpu.SemaphoreType.DMA((groups,)),
            pltpu.SemaphoreType.DMA((groups,)),
            pltpu.SemaphoreType.DMA((6,)),
            pltpu.SemaphoreType.DMA((6,)),
            pltpu.SemaphoreType.DMA((2,)),
        ],
        30 << 30,
    )
    return out[:7], out[7:11], out[11:13], out[13 : 13 + n], out[13 + n :]


def one_hot_rows(pos, gate, j, n_rows):
    rank = lax.broadcasted_iota(jnp.int32, (CAP, n_rows), 0)
    chosen = rank == pos[j : j + 1, :]
    return jnp.where(chosen, 1.0 if gate is None else gate[j : j + 1, :], 0.0).astype(BF)


def spread_kernel(outer, steps, pos_ref, gate_ref, na_ref, nb_ref, *refs):
    n_steps = len(steps)
    cot_ref, dy_refs, refs = refs[0], refs[1:5], refs[5:]
    from_left, refs = refs[:n_steps], refs[n_steps:]
    from_right, refs = refs[:n_steps], refs[n_steps:]
    n_ref, dyx_ref, og_ref = refs[:3]
    refs = refs[3:]
    to_left, refs = refs[:n_steps], refs[n_steps:]
    to_right, refs = refs[:n_steps], refs[n_steps:]
    held, s_hop, r_hop, s_n, r_n, s_d, r_d, l_sem = refs
    height = na_ref.shape[0]
    n_experts = og_ref.shape[1]
    greet(outer, (1, 2), True)
    n_ax = to_x(na_ref, n_ref.at[0, 1], s_n.at[0], r_n.at[0])
    n_by = to_dp(2, nb_ref, n_ref.at[1, 2], s_n.at[1], r_n.at[1])
    n_bx = to_x(nb_ref, n_ref.at[0, 3], s_n.at[2], r_n.at[2])
    n_ay = to_dp(2, na_ref, n_ref.at[1, 0], s_n.at[3], r_n.at[3])
    n_axy = to_dp(2, n_ref.at[0, 1], n_ref.at[1, 1], s_n.at[4], r_n.at[4])
    n_bxy = to_x(n_ref.at[1, 2], n_ref.at[1, 3], s_n.at[5], r_n.at[5])
    core = {}
    for n, (s, p) in enumerate([(s, p) for s in range(2) for p in range(4)]):
        source = na_ref if (s, p) == (0, 0) else nb_ref if (s, p) == (0, 2) else n_ref.at[s, p]
        core[s, p] = to_dp(1, source, n_ref.at[2 + s, p], s_n.at[6 + n], r_n.at[6 + n])
    for copy in (n_ax, n_by, n_bx, n_ay):
        copy.start()
    d_a, d_b = (cot_ref.at[pl.ds(p * height, height)] for p in range(2))
    d_ax, d_bx, d_ay, d_by = dy_refs
    d_axy = to_dp(2, d_ax, dyx_ref.at[0, 1], s_d.at[0], r_d.at[0])
    d_bxy = to_x(d_by, dyx_ref.at[0, 3], s_d.at[1], r_d.at[1])
    d_axy.start()
    d_bxy.start()
    d_near = [[d_a, d_ax, d_b, d_bx], [d_ay, dyx_ref.at[0, 1], d_by, dyx_ref.at[0, 3]]]
    d_core = {}
    for n, (s, p) in enumerate([(s, p) for s in range(2) for p in range(4)]):
        d_core[s, p] = to_dp(1, d_near[s][p], dyx_ref.at[1 + s, p], s_d.at[2 + n], r_d.at[2 + n])
    for key in ((0, 0), (0, 1), (0, 2), (0, 3), (1, 0), (1, 2)):
        d_core[key].start()
    core[0, 0].start()
    core[0, 2].start()
    hops = Hops(
        outer,
        [(k, a, b, l, r) for k, a, b, l, r in zip(steps, from_left, from_right, to_left, to_right, strict=True)],
        s_hop,
        r_hop,
    )
    hops.start()

    def load(s):
        pieces = d_near[s] if s < 2 else [dyx_ref.at[s - 1, p] for p in range(4)]
        return [
            pltpu.make_async_copy(piece, held.at[pl.ds(p * height, height)], l_sem.at[p])
            for p, piece in enumerate(pieces)
        ]

    def give(s):
        copies = load(s)
        for c in copies:
            c.start()
        for c in copies:
            c.wait()

        def one(j, carry):
            rank = lax.broadcasted_iota(jnp.int32, (CAP, 4 * height), 0)
            chosen = rank == pos_ref[s, pl.ds(j, 1), :]
            one_hot = jnp.where(chosen, gate_ref[s, pl.ds(j, 1), :], 0.0).astype(BF)
            og_ref[s, j] = mm(one_hot, held[...]).astype(BF)
            return carry

        lax.fori_loop(0, n_experts, one, 0)

    give(0)
    n_ax.wait()
    n_by.wait()
    n_axy.start()
    n_bxy.start()
    core[0, 1].start()
    core[1, 2].start()
    d_axy.wait()
    d_bxy.wait()
    d_core[1, 1].start()
    d_core[1, 3].start()
    give(1)
    n_bx.wait()
    n_ay.wait()
    core[0, 3].start()
    core[1, 0].start()
    for p in range(4):
        d_core[0, p].wait()
    give(2)
    n_axy.wait()
    n_bxy.wait()
    core[1, 1].start()
    core[1, 3].start()
    for p in range(4):
        d_core[1, p].wait()
    give(3)
    for key in core:
        core[key].wait()
    hops.wait()


def spread(outer, pos, gate, normed, dys, steps, from_left, from_right):
    height = normed[0].shape[0]
    n, n_experts = len(steps), pos.shape[1]
    weights = [jax.ShapeDtypeStruct(s.shape, BF) for s in from_left]
    out = remote_call(
        functools.partial(spread_kernel, outer, steps),
        "spread",
        2,
        [
            jax.ShapeDtypeStruct((GROUP, 4, height, D), BF),
            jax.ShapeDtypeStruct((3, 4, height, D), BF),
            jax.ShapeDtypeStruct((GROUP, n_experts, CAP, D), BF),
        ]
        + weights * 2,
        [VM] * 2 + [ANY] * (2 + 5 + 2 * n),
        [ANY, ANY, VM] + [ANY] * (2 * n),
        (pos, gate, *normed, *dys, *from_left, *from_right),
        [
            pltpu.VMEM((4 * height, D), BF),
            pltpu.SemaphoreType.DMA((2 * n,)),
            pltpu.SemaphoreType.DMA((2 * n,)),
            pltpu.SemaphoreType.DMA((14,)),
            pltpu.SemaphoreType.DMA((14,)),
            pltpu.SemaphoreType.DMA((10,)),
            pltpu.SemaphoreType.DMA((10,)),
            pltpu.SemaphoreType.DMA((4,)),
        ],
        12 << 30,
    )
    return out[0], out[2], out[3 : 3 + n], out[3 + n :]


def hand_out_kernel(outer, steps, pos_ref, na_ref, nb_ref, n_ref, *refs):
    n_steps = len(steps)
    from_left, refs = refs[:n_steps], refs[n_steps:]
    from_right, refs = refs[:n_steps], refs[n_steps:]
    x_ref, refs = refs[0], refs[1:]
    to_left, refs = refs[:n_steps], refs[n_steps:]
    to_right, refs = refs[:n_steps], refs[n_steps:]
    held, s_hop, r_hop, l_sem = refs
    height = na_ref.shape[0]
    n_experts = x_ref.shape[1]
    greet(outer, (), False)
    hops = Hops(
        outer,
        [(k, a, b, l, r) for k, a, b, l, r in zip(steps, from_left, from_right, to_left, to_right, strict=True)],
        s_hop,
        r_hop,
    )
    hops.start()

    def load(s):
        pieces = [na_ref, n_ref.at[0, 1], nb_ref, n_ref.at[0, 3]] if s == 0 else [n_ref.at[s, p] for p in range(4)]
        return [
            pltpu.make_async_copy(piece, held.at[s % 2, pl.ds(p * height, height)], l_sem.at[s % 2, p])
            for p, piece in enumerate(pieces)
        ]

    for c in load(0):
        c.start()
    for s in range(GROUP):
        if s + 1 < GROUP:
            for c in load(s + 1):
                c.start()
        for c in load(s):
            c.wait()

        def one(j, carry, s=s):
            rank = lax.broadcasted_iota(jnp.int32, (CAP, 4 * height), 0)
            one_hot = jnp.where(rank == pos_ref[s, pl.ds(j, 1), :], 1.0, 0.0).astype(BF)
            x_ref[s, j] = mm(one_hot, held[s % 2]).astype(BF)
            return carry

        lax.fori_loop(0, n_experts, one, 0)
    hops.wait()


def hand_out(outer, pos, normed, gathered, steps, from_left, from_right):
    height = normed[0].shape[0]
    n, n_experts = len(steps), pos.shape[1]
    weights = [jax.ShapeDtypeStruct(s.shape, BF) for s in from_left]
    out = remote_call(
        functools.partial(hand_out_kernel, outer, steps),
        "hand_out",
        3,
        [jax.ShapeDtypeStruct((GROUP, n_experts, CAP, D), BF)] + weights * 2,
        [VM] + [ANY] * (3 + 2 * n),
        [VM] + [ANY] * (2 * n),
        (pos, *normed, gathered, *from_left, *from_right),
        [
            pltpu.VMEM((2, 4 * height, D), BF),
            pltpu.SemaphoreType.DMA((2 * n,)),
            pltpu.SemaphoreType.DMA((2 * n,)),
            pltpu.SemaphoreType.DMA((2, 4)),
        ],
        12 << 30,
    )
    return out[0], out[1 : 1 + n], out[1 + n :]


def expert_step_kernel(j, outer, in_rows, down_rows, steps, sum_steps, x_ref, g_ref, own, *refs):
    n_hops, n_steps, n_sums = outer - 1, len(steps), len(sum_steps)
    lefts, refs = refs[:n_hops], refs[n_hops:]
    rights, refs = refs[:n_hops], refs[n_hops:]
    from_left, refs = refs[:n_steps], refs[n_steps:]
    from_right, refs = refs[:n_steps], refs[n_steps:]
    dws, refs = refs[:n_sums], refs[n_sums:]
    was_l, refs = refs[:n_sums], refs[n_sums:]
    was_r, refs = refs[:n_sums], refs[n_sums:]
    y_ref, dx_ref, dw_ref = refs[:3]
    refs = refs[3:]
    to_left, refs = refs[:n_steps], refs[n_steps:]
    to_right, refs = refs[:n_steps], refs[n_steps:]
    sum_left, refs = refs[:n_sums], refs[n_sums:]
    sum_right, refs = refs[:n_sums], refs[n_sums:]
    x_all, g_all, w_in, w_down, act_all, gug_all, sem_x, sem_g, sem_w, sem_d, s_hop, r_hop = refs[:12]
    _, _, o, i = place()
    greet(outer, (), False)
    sums = Sums(outer, sum_steps, dws, was_l, was_r, sum_left, sum_right, *refs[12:])
    if n_steps:
        hops = Hops(
            outer,
            [(k, a, b, l, r) for k, a, b, l, r in zip(steps, from_left, from_right, to_left, to_right, strict=True)],
            s_hop,
            r_hop,
        )
        hops.start()

    def rows_of(source, held, sems):
        return [
            pltpu.make_async_copy(source.at[n, j], held.at[pl.ds(n * CAP, CAP)], sems.at[n]) for n in range(GROUP)
        ]

    def weight_copies(source, at, slot):
        made = []
        for m in range(GROUP):
            where = at * GROUP + flip(i, m)
            made.append(
                pltpu.make_async_copy(
                    source.at[m, pl.ds(0, in_rows)],
                    w_in.at[pl.ds(pl.multiple_of(where * in_rows, in_rows), in_rows)],
                    sem_w.at[slot * GROUP + m],
                )
            )
            made.append(
                pltpu.make_async_copy(
                    source.at[m, pl.ds(in_rows, down_rows)],
                    w_down.at[pl.ds(pl.multiple_of(where * down_rows, down_rows), down_rows)],
                    sem_d.at[slot * GROUP + m],
                )
            )
        return made

    def each_weight(act):
        act(weight_copies(own, o, 0))
        for k in range(1, outer):

            @pl.when(o >= k)
            def _():
                act(weight_copies(lefts[k - 1], o - k, k))

            @pl.when(o + k < outer)
            def _():
                act(weight_copies(rights[k - 1], o + k, n_hops + k))

    def start(made):
        for c in made:
            c.start()

    def wait(made):
        for c in made:
            c.wait()

    sums.load()
    each_weight(start)
    copy_x, copy_g = rows_of(x_ref, x_all, sem_x), rows_of(g_ref, g_all, sem_g)
    start(copy_x)
    start(copy_g)
    sums.send()
    each_weight(wait)
    wait(copy_x)
    wait(copy_g)

    def per_slot(s, carry):
        at = pl.ds(pl.multiple_of(s * CAP, CAP), CAP)
        gate_up = mm(x_all[at, :], w_in[...])
        g, u = gate_up[:, :FF], gate_up[:, FF:]
        sigma = 1.0 / (1.0 + jnp.exp(-g))
        silu = g * sigma
        act = (silu * u).astype(BF)
        act_all[at, :] = act
        y_ref[s] = mm(act, w_down[...]).astype(BF)
        act_grad = mm_nt(g_all[at, :], w_down[...])
        gug_all[at, :FF] = (act_grad * u * sigma * (1.0 + g * (1.0 - sigma))).astype(BF)
        gug_all[at, FF:] = (act_grad * silu).astype(BF)
        dx_ref[s] = mm_nt(gug_all[at, :], w_in[...]).astype(BF)
        return carry

    lax.fori_loop(0, GROUP, per_slot, 0)
    in_block, down_block = GROUP * in_rows, GROUP * down_rows

    def per_owner(c, carry):
        lanes = pl.ds(pl.multiple_of(c * in_block, in_block), in_block)
        part = mm_tn(x_all[:, lanes], gug_all[...]).astype(BF)
        for r in range(GROUP):
            dw_ref[c, flip(i, r), :in_rows, :] = part[r * in_rows : (r + 1) * in_rows]
        lanes = pl.ds(pl.multiple_of(c * down_block, down_block), down_block)
        part = mm_tn(act_all[:, lanes], g_all[...]).astype(BF)
        for r in range(GROUP):
            dw_ref[c, flip(i, r), in_rows:, :] = part[r * down_rows : (r + 1) * down_rows]
        return carry

    lax.fori_loop(0, outer, per_owner, 0)
    if n_steps:
        hops.wait()
    sums.wait()


def expert_step(j, outer, in_rows, down_rows, x, g, own, lefts, rights, hop_plan, sum_plan):
    (steps, from_left, from_right), (sum_steps, dws, was_l, was_r) = hop_plan, sum_plan
    n_hops, n, n_sums = outer - 1, len(steps), len(sum_steps)
    total = GROUP * CAP
    packed = in_rows + down_rows
    weights = [jax.ShapeDtypeStruct(s.shape, BF) for s in from_left]
    shapes = [
        jax.ShapeDtypeStruct((GROUP, CAP, D), BF),
        jax.ShapeDtypeStruct((GROUP, CAP, D), BF),
        jax.ShapeDtypeStruct((outer, GROUP, packed, D), BF),
    ] + weights * 2 + [jax.ShapeDtypeStruct((GROUP, packed, D), BF)] * (2 * n_sums)
    out = remote_call(
        functools.partial(expert_step_kernel, j, outer, in_rows, down_rows, steps, sum_steps),
        "expert_step",
        4 + j,
        shapes,
        [ANY] * (3 + 2 * n_hops + 2 * n + 3 * n_sums),
        [VM] * 3 + [ANY] * (2 * n + 2 * n_sums),
        (x, g, own, *lefts, *rights, *from_left, *from_right, *dws, *was_l, *was_r),
        [
            pltpu.VMEM((total, D), BF),
            pltpu.VMEM((total, D), BF),
            pltpu.VMEM((D, 2 * FF), BF),
            pltpu.VMEM((FF, D), BF),
            pltpu.VMEM((total, FF), BF),
            pltpu.VMEM((total, 2 * FF), BF),
            pltpu.SemaphoreType.DMA((GROUP,)),
            pltpu.SemaphoreType.DMA((GROUP,)),
            pltpu.SemaphoreType.DMA(((1 + 2 * n_hops) * GROUP,)),
            pltpu.SemaphoreType.DMA(((1 + 2 * n_hops) * GROUP,)),
            pltpu.SemaphoreType.DMA((max(1, 2 * n),)),
            pltpu.SemaphoreType.DMA((max(1, 2 * n),)),
            *sums_scratch(n_sums, packed),
        ],
        18 * total * D * FF,
    )
    out, rest = out[:3], out[3:]
    return out, rest[:n], rest[n : 2 * n], rest[2 * n : 2 * n + n_sums], rest[2 * n + n_sums :]


class Sums:
    def __init__(self, outer, steps, dws, was_left, was_right, to_left, to_right, message, term, loaded, added, sent, came):
        d, t, o, _ = place()
        back = outer - 1 - o
        self.moves = []
        for n, s in enumerate(steps):
            for side, near, target, was, to, peer in (
                (0, o, outer - s + o, was_left, to_left, d + GROUP),
                (1, back, s - 1 - back, was_right, to_right, d - GROUP),
            ):
                k = 2 * n + side
                own = pltpu.make_async_copy(dws[n].at[target], message.at[k], loaded.at[k])
                before = None if s == 1 else pltpu.make_async_copy(was[n], term.at[side], added.at[k])
                move = pltpu.make_async_remote_copy(
                    message.at[k], to[n], sent.at[k], came.at[k], device_id=(peer, t), device_id_type=MESH
                )
                sends, adds = near <= s - 1, (near <= s - 1) & (near >= 1)
                receives = (near >= 1) & (near <= s)
                self.moves.append((own, before, move, sends, adds, receives, message.at[k], term.at[side]))

    def load(self):
        for own, _, _, sends, *_ in self.moves:
            pl.when(sends)(own.start)

    def send(self):
        for n in range(0, len(self.moves), 2):
            pair = self.moves[n : n + 2]
            for _, before, _, _, adds, *_ in pair:
                if before is not None:
                    pl.when(adds)(before.start)
            for own, before, move, sends, adds, _, message, term in pair:
                pl.when(sends)(own.wait)
                if before is not None:

                    @pl.when(adds)
                    def _(before=before, message=message, term=term):
                        before.wait()

                        def one(m, carry):
                            message[m] = (message[m].astype(F32) + term[m].astype(F32)).astype(BF)
                            return carry

                        lax.fori_loop(0, GROUP, one, 0)

                pl.when(sends)(move.start)

    def wait(self):
        for _, _, move, sends, _, receives, *_ in self.moves:
            pl.when(sends)(move.wait_send)
            pl.when(receives)(move.wait_recv)


def sums_scratch(n, packed):
    n = max(1, n)
    return [
        pltpu.VMEM((2 * n, GROUP, packed, D), BF),
        pltpu.VMEM((2, GROUP, packed, D), BF),
        pltpu.SemaphoreType.DMA((2 * n,)),
        pltpu.SemaphoreType.DMA((2 * n,)),
        pltpu.SemaphoreType.DMA((2 * n,)),
        pltpu.SemaphoreType.DMA((2 * n,)),
    ]


def again(scratch):
    return [pltpu.SemaphoreType.DMA(s.shape) for s in scratch[2:]]


class Final:
    def __init__(self, outer, dw, left, right, mine, term, target, loaded, sent, came, kept):
        _, _, o, _ = place()
        self.from_left, self.from_right = o >= 1, o < outer - 1
        self.mine, self.term = mine, term
        self.own = pltpu.make_async_copy(dw.at[o], mine, loaded.at[0])
        self.left = pltpu.make_async_copy(left, term.at[0], loaded.at[1])
        self.right = pltpu.make_async_copy(right, term.at[1], loaded.at[2])
        self.moves = [to_dp(m, mine.at[m], target.at[m], sent.at[m - 1], came.at[m - 1]) for m in range(1, GROUP)]
        self.keep = pltpu.make_async_copy(mine.at[0], target.at[0], kept)

    def send(self):
        self.own.start()
        pl.when(self.from_left)(self.left.start)
        pl.when(self.from_right)(self.right.start)
        self.own.wait()

        def add(k):
            def one(m, carry):
                self.mine[m] = (self.mine[m].astype(F32) + self.term[k, m].astype(F32)).astype(BF)
                return carry

            lax.fori_loop(0, GROUP, one, 0)

        @pl.when(self.from_left)
        def _():
            self.left.wait()
            add(0)

        @pl.when(self.from_right)
        def _():
            self.right.wait()
            add(1)

        for move in self.moves:
            move.start()
        self.keep.start()

    def wait(self):
        for move in self.moves:
            move.wait()
        self.keep.wait()


def final_scratch(packed):
    return [
        pltpu.VMEM((GROUP, packed, D), BF),
        pltpu.SemaphoreType.DMA((3,)),
        pltpu.SemaphoreType.DMA((GROUP - 1,)),
        pltpu.SemaphoreType.DMA((GROUP - 1,)),
        pltpu.SemaphoreType.DMA,
    ]


class Mixer:
    def __init__(self, sources, pos_ref, gate_ref, held, sems):
        self.sources, self.pos, self.gate, self.held, self.sems = sources, pos_ref, gate_ref, held, sems

    def copies(self, slot, buffer):
        return [
            pltpu.make_async_copy(
                source.at[slot], self.held.at[buffer, pl.ds(j * CAP, CAP)], self.sems.at[buffer * len(self.sources) + j]
            )
            for j, source in enumerate(self.sources)
        ]

    def load(self, slot, buffer):
        for c in self.copies(slot, buffer):
            c.start()

    def mix(self, slot, buffer, out, add=None):
        for c in self.copies(slot, buffer):
            c.wait()
        n_experts = len(self.sources)
        width = n_experts * CAP
        block = 256

        def one(b, carry):
            at = pl.ds(pl.multiple_of(b * block, block), block)
            targets = []
            for j in range(n_experts):
                target = self.pos[slot, at, j : j + 1]
                targets.append(jnp.where(target >= 0, target + j * CAP, -1))
            tiles = []
            for first in range(0, width, LANES):
                size = min(LANES, width - first)
                lane = first + lax.broadcasted_iota(jnp.int32, (block, size), 1)
                tile = jnp.zeros((block, size), F32)
                for j in range(first // CAP, (first + size - 1) // CAP + 1):
                    value = 1.0 if self.gate is None else self.gate[slot, at, j : j + 1]
                    tile = jnp.where(lane == targets[j], value, tile)
                tiles.append(tile.astype(BF))
            total = mm(jnp.concatenate(tiles, axis=1), self.held[buffer])
            if add is not None:
                total = total + add[at, :].astype(F32)
            out[at, :] = total.astype(BF)
            return carry

        lax.fori_loop(0, out.shape[0] // block, one, 0)


class GroupSum:
    def __init__(self, near, q, middle, mine, come_ab, last_ab, sent, came):
        self.middle, self.mine, self.come_ab, self.last_ab, self.q = middle, mine, come_ab, last_ab, q
        self.a = [
            to_dp(2, near.at[1, pl.ds(s * q, q)], come_ab.at[0, pl.ds(s * q, q)], sent.at[s], came.at[s]) for s in range(2)
        ]
        self.b = [
            to_x(near.at[s, pl.ds(3 * q, q)], come_ab.at[1, pl.ds(s * q, q)], sent.at[2 + s], came.at[2 + s])
            for s in range(2)
        ]
        self.last = [
            to_x(middle[0], last_ab.at[0], sent.at[4], came.at[4]),
            to_dp(2, middle[1], last_ab.at[1], sent.at[5], came.at[5]),
        ]

    def second(self):
        q = self.q
        for p, first in enumerate((self.a[1], self.b[1])):
            first.wait_recv()
            self.middle[p][...] = (
                self.middle[p][...].astype(F32) + self.come_ab[p, q : 2 * q].astype(F32)
            ).astype(BF)
            self.last[p].start()

    def terms(self, p):
        (self.a, self.b)[p][0].wait_recv()
        self.last[p].wait_recv()
        return (
            self.mine[p][...].astype(F32) + self.come_ab[p, : self.q].astype(F32) + self.last_ab[p].astype(F32)
        )

    def sent(self):
        for copy in (*self.a, *self.b, *self.last):
            copy.wait_send()


def group_scratch(rows):
    return [
        pltpu.VMEM((2, rows // 2, D), BF),
        pltpu.VMEM((2, rows // 4, D), BF),
        pltpu.SemaphoreType.DMA((6,)),
        pltpu.SemaphoreType.DMA((6,)),
    ]


def rows_back_kernel(outer, first, then, pos_ref, gate_ref, valid_ref, hidden_ref, cot_ref, gain_ref, w_any, *refs):
    n_experts, n1, n2 = pos_ref.shape[2], len(first), len(then)
    sources, refs = refs[:n_experts], refs[n_experts:]
    ys, refs = refs[:n_experts], refs[n_experts:]
    dws, refs = refs[: n1 + 1], refs[n1 + 1 :]
    was_l, refs = refs[:n1], refs[n1:]
    was_r, refs = refs[:n1], refs[n1:]
    f_dw, f_left, f_right, refs = *refs[:3], refs[3:]
    grad_ref, low_ref, gain_grad_ref, own_ref, come_ref, mixed, fin_ref = refs[:7]
    refs = refs[7:]
    to_l, refs = refs[: n1 + n2], refs[n1 + n2 :]
    to_r, refs = refs[: n1 + n2], refs[n1 + n2 :]
    (held, far, come, mixed_come, near, l_sem, s_core, r_core), refs = refs[:8], refs[8:]
    (come_ab, last_ab, s_sem, r_sem), refs = refs[:4], refs[4:]
    sums_a, refs = refs[:6], refs[6:]
    sums_b, refs = (*sums_a[:2], *refs[:4]), refs[4:]
    send_ref, s_at, r_at, w_ref, w_sem = refs[:5]
    final_refs = refs[5:]
    heads = w_ref.shape[1] // 2
    w_copy = pltpu.make_async_copy(w_any.at[:, pl.ds(2 * heads, 2 * heads)], w_ref, w_sem)
    w_copy.start()
    mixer = Mixer(sources, pos_ref, None, held, l_sem)
    mixer.load(3, 0)
    mixer.load(2, 1)
    greet(outer, (1, 2, 3), True)
    one = Sums(outer, first, dws[:n1], was_l, was_r, to_l[:n1], to_r[:n1], *sums_a)
    final = Final(outer, f_dw, f_left, f_right, final_refs[0], sums_a[1], fin_ref, *final_refs[1:])
    two = Sums(
        outer,
        [s for s, _ in then],
        [dws[k] for _, k in then],
        [None if s == 1 else to_l[k] for s, k in then],
        [None if s == 1 else to_r[k] for s, k in then],
        to_l[n1:],
        to_r[n1:],
        *sums_b,
    )
    q = near.shape[1] // 4
    group = GroupSum(
        near,
        q,
        [near.at[0, pl.ds(q, q)], near.at[1, pl.ds(2 * q, q)]],
        [near.at[0, pl.ds(0, q)], near.at[0, pl.ds(2 * q, q)]],
        come_ab,
        last_ab,
        s_sem,
        r_sem,
    )
    core = [to_dp(1, far.at[s], come.at[s], s_core.at[s], r_core.at[s]) for s in range(2)]
    mixed_core = [to_dp(1, far.at[s], mixed_come.at[s], s_core.at[2 + s], r_core.at[2 + s]) for s in range(2)]
    one.load()
    one.send()
    final.send()
    mixer.mix(3, 0, far.at[1])
    core[1].start()
    mixer.load(1, 0)
    mixer.mix(2, 1, far.at[0])
    core[0].start()
    mixer.load(0, 1)
    core[1].wait_recv()
    mixer.mix(1, 0, near.at[1], come.at[1])
    group.a[1].start()
    group.b[1].start()
    group.a[0].start()
    outputs = Mixer(ys, pos_ref, gate_ref, held, l_sem)
    outputs.load(3, 0)
    core[0].wait_recv()
    mixer.mix(0, 1, near.at[0], come.at[0])
    group.b[0].start()
    outputs.load(2, 1)
    core[1].wait_send()
    outputs.mix(3, 0, far.at[1])
    mixed_core[1].start()
    outputs.load(1, 0)
    group.second()
    core[0].wait_send()
    outputs.mix(2, 1, far.at[0])
    mixed_core[0].start()
    outputs.load(0, 1)
    one.wait()
    two.load()
    two.send()
    mixed_core[1].wait_recv()
    outputs.mix(1, 0, mixed.at[1], mixed_come.at[1])
    w_copy.wait()
    rows = hidden_ref.shape[0] // 2
    gain = gain_ref[...]
    gain_grad = jnp.zeros((1, D), F32)
    aways = []
    for p in range(2):
        at = slice(p * rows, (p + 1) * rows)
        hidden = hidden_ref[at]
        normed_grad = group.terms(p)
        inverse = lax.rsqrt(jnp.mean(hidden * hidden, axis=-1, keepdims=True) + EPSILON)
        gain_grad = gain_grad + jnp.sum(normed_grad * (hidden * inverse), axis=0, keepdims=True)
        scaled = normed_grad * gain
        back = inverse * scaled - hidden * (
            inverse * inverse * inverse * jnp.mean(scaled * hidden, axis=-1, keepdims=True)
        )
        dy = jnp.where(valid_ref[at] > 0, cot_ref[at].astype(F32), 0.0)
        total = dy + back
        grad_ref[at] = total
        low = total.astype(BF)
        low_ref[at] = low
        send_ref[at] = mm(low, w_ref[:, heads:]).astype(BF)
        part = pl.ds(p * rows, rows)
        aways.append(to_x(send_ref.at[part], come_ref.at[part], s_at.at[p], r_at.at[p]))
        aways[p].start()
    gain_grad_ref[...] = gain_grad
    mixed_core[0].wait_recv()
    outputs.mix(0, 1, mixed.at[0], mixed_come.at[0])
    own_ref[...] = mm(low_ref[...], w_ref[:, :heads]).astype(BF)
    group.sent()
    for copy in mixed_core:
        copy.wait_send()
    for away in aways:
        away.wait()
    final.wait()
    two.wait()


def rows_back(
    outer, pos, gate, valid, hidden, cotangent, gain, weights_full, sources, ys, first, then, dws, was_l, was_r, final
):
    rows, heads = hidden.shape[0], weights_full.shape[1] // 4
    n, n_experts = len(first) + len(then), len(sources)
    packed = dws[0].shape[2]
    hop = [jax.ShapeDtypeStruct((GROUP, packed, D), BF)] * (2 * n)
    half = jax.ShapeDtypeStruct((rows, heads), BF)
    most = max(len(first), len(then))
    slots = pltpu.VMEM((2, 2 * rows, D), BF)
    out = remote_call(
        functools.partial(rows_back_kernel, outer, first, then),
        "rows_back",
        10,
        [
            jax.ShapeDtypeStruct((rows, D), F32),
            jax.ShapeDtypeStruct((rows, D), BF),
            jax.ShapeDtypeStruct((1, D), F32),
            half,
            half,
            jax.ShapeDtypeStruct((2, 2 * rows, D), BF),
        ]
        + hop[:1]
        + hop,
        [VM] * 6 + [ANY] * (4 + 2 * n_experts + len(dws) + 2 * len(first)),
        [VM] * 6 + [ANY] * (1 + 2 * n),
        (pos, gate, valid, hidden, cotangent, gain.reshape(1, D), weights_full, *sources, *ys, *dws, *was_l, *was_r, *final),
        [
            pltpu.VMEM((2, n_experts * CAP, D), BF),
            slots,
            slots,
            slots,
            slots,
            pltpu.SemaphoreType.DMA((2 * n_experts,)),
            pltpu.SemaphoreType.DMA((4,)),
            pltpu.SemaphoreType.DMA((4,)),
            *group_scratch(2 * rows),
            *sums_scratch(most, packed),
            *again(sums_scratch(most, packed)),
            pltpu.VMEM((rows, heads), BF),
            pltpu.SemaphoreType.DMA((2,)),
            pltpu.SemaphoreType.DMA((2,)),
            pltpu.VMEM((D, 2 * heads), BF),
            pltpu.SemaphoreType.DMA,
            *final_scratch(packed),
        ],
        30 << 30,
    )
    return out[:6], out[6], out[7 : 7 + n], out[7 + n :]


def attention_back_kernel(
    outer, q_block, steps, len_ref, qkv_ref, lse_ref, cos_ref, sin_ref, own_ref, other_ref, hidden_ref, valid_ref, *refs
):
    n = len(steps)
    mixed, refs = refs[0], refs[1:]
    dws, refs = refs[:n], refs[n:]
    was_l, refs = refs[:n], refs[n:]
    was_r, refs = refs[:n], refs[n:]
    outs, out_ref, refs = refs[:2], refs[2], refs[3:]
    to_l, refs = refs[:n], refs[n:]
    to_r, refs = refs[:n], refs[n:]
    do_ref, dq_ref, dk_ref, dv_ref = refs[:4]
    sums_refs, refs = refs[4:10], refs[10:]
    middle, mine, l_sem, come_ab, last_ab, s_sem, r_sem = refs
    _, t, _, _ = place()
    q = middle.shape[1]
    loads = [
        pltpu.make_async_copy(mixed.at[0, pl.ds(q, q)], middle.at[0], l_sem.at[0]),
        pltpu.make_async_copy(mixed.at[1, pl.ds(2 * q, q)], middle.at[1], l_sem.at[1]),
        pltpu.make_async_copy(mixed.at[0, pl.ds(0, q)], mine.at[0], l_sem.at[2]),
        pltpu.make_async_copy(mixed.at[0, pl.ds(2 * q, q)], mine.at[1], l_sem.at[3]),
    ]
    for c in loads:
        c.start()
    greet(outer, (2,), True)
    group = GroupSum(
        mixed, q, [middle.at[0], middle.at[1]], [mine.at[0], mine.at[1]], come_ab, last_ab, s_sem, r_sem
    )
    for copy in (group.a[1], group.b[1], group.a[0], group.b[0]):
        copy.start()
    sums = Sums(outer, steps, dws, was_l, was_r, to_l, to_r, *sums_refs)
    sums.load()
    sums.send()
    length = len_ref[0]
    rows, own_rows = qkv_ref.shape[0], own_ref.shape[0]
    groups = own_ref.shape[1] // LANES
    scale = 1.0 / math.sqrt(HD)

    def per_group(g, carry):
        q_lanes = pl.ds(pl.multiple_of(g * 2 * LANES, LANES), LANES)
        kv_lanes = pl.ds(pl.multiple_of(g * 2 * LANES + LANES, LANES), LANES)
        o_lanes = pl.ds(pl.multiple_of(g * LANES, LANES), LANES)
        for half, grad_ref in ((t, own_ref), (1 - t, other_ref)):
            do_ref[pl.ds(pl.multiple_of(half * own_rows, own_rows), own_rows), :] = grad_ref[:, o_lanes]
        keys, values = doubled(qkv_ref[:, kv_lanes])
        dk_ref[...] = jnp.zeros_like(dk_ref)
        dv_ref[...] = jnp.zeros_like(dv_ref)
        for b in range(rows // q_block):
            start, n_keys = b * q_block, (b + 1) * q_block
            q = head_pair(qkv_ref[start : start + q_block, q_lanes])
            grad = head_pair(do_ref[start : start + q_block, :])
            scores = mm_nt(keys[:n_keys], q) * scale
            probs = jnp.where(
                allowed(n_keys, q_block, start, length), jnp.exp(scores - lse_ref[g, b : b + 1, :]), 0.0
            )
            prob_grad = mm_nt(values[:n_keys], grad)
            center = jnp.sum(probs * prob_grad, axis=0, keepdims=True)
            score_grad = (probs * (prob_grad - center)).astype(BF)
            dq_ref[start : start + q_block, :] = head_join(mm_tn(score_grad, keys[:n_keys])) * scale
            dk_ref[:n_keys, :] += mm(score_grad, q)
            dv_ref[:n_keys, :] += mm(probs.astype(BF), grad)
        for p, half in enumerate((t, 1 - t)):
            at = pl.ds(pl.multiple_of(half * own_rows, own_rows), own_rows)
            cosine, sine = cos_ref[at, :], sin_ref[at, :]
            dq = dq_ref[at, :]
            outs[p][:, q_lanes] = (dq * cosine - swap_halves(dq) * sine).astype(BF)
            dk, dv = dk_ref[at, :] * scale, dv_ref[at, :]
            dk = dk + pltpu.roll(dk, HD, 1)
            dv = dv + pltpu.roll(dv, HD, 1)
            dk = dk * cosine - swap_halves(dk) * sine
            first = lax.broadcasted_iota(jnp.int32, dk.shape, 1) < HD
            outs[p][:, kv_lanes] = jnp.where(first, dk, dv).astype(BF)

        @pl.when(g == groups // 2)
        def _():
            for c in loads:
                c.wait()
            group.second()

        return carry

    lax.fori_loop(0, groups, per_group, 0)
    for p in range(2):
        at = slice(p * q, (p + 1) * q)
        out_ref[at] = jnp.where(valid_ref[at] > 0, hidden_ref[at] + group.terms(p), 0.0).astype(BF)
    group.sent()
    sums.wait()


def attention_back(
    outer, q_block, length, qkv, lse, cosine, sine, grads, hidden, valid, mixed, steps, dws, was_l, was_r
):
    rows, width = qkv.shape
    n = len(steps)
    packed = dws[0].shape[2]
    hop = jax.ShapeDtypeStruct((GROUP, packed, D), BF)
    out = remote_call(
        functools.partial(attention_back_kernel, outer, q_block, steps),
        "attention_back",
        12,
        [jax.ShapeDtypeStruct((rows // 2, width), BF)] * 2
        + [jax.ShapeDtypeStruct((rows // 2, D), BF)]
        + [hop] * (2 * n),
        [SMEM] + [VM] * 8 + [ANY] * (3 * n + 1),
        [VM] * 3 + [ANY] * (2 * n),
        (length, qkv, lse, cosine, sine, *grads, hidden, valid, mixed, *dws, *was_l, *was_r),
        [
            pltpu.VMEM((rows, LANES), BF),
            pltpu.VMEM((rows, LANES), F32),
            pltpu.VMEM((rows, LANES), F32),
            pltpu.VMEM((rows, LANES), F32),
            *sums_scratch(n, packed),
            pltpu.VMEM((2, rows // 4, D), BF),
            pltpu.VMEM((2, rows // 4, D), BF),
            pltpu.SemaphoreType.DMA((4,)),
            *group_scratch(rows),
        ],
        30 << 30,
    )
    return out[:3], out[3 : 3 + n], out[3 + n :]


def over_outer(outer, source, target, sent, came, base):
    _, t, o, i = place()
    return [
        pltpu.make_async_remote_copy(
            source((o + k) % outer),
            target(k),
            sent.at[base + k],
            came.at[base + k],
            device_id=((o + k) % outer * GROUP + i, t),
            device_id_type=MESH,
        )
        for k in range(1, outer)
    ]


class Spread:
    def __init__(self, outer, terms, come_core, come_y, come_z, sent, came):
        _, _, self.o, i = place()
        self.outer, self.terms, self.come_core, self.come_y, self.come_z = outer, terms, come_core, come_y, come_z
        y, c = i // 2, i % 2
        self.y, self.c = y, c
        self.core = to_dp(1, terms.at[:, :, 1 - c], come_core, sent.at[0], came.at[0])
        self.side = to_dp(2, terms.at[:, 1 - y, c], come_y, sent.at[1], came.at[1])
        self.moves = over_outer(outer, lambda peer: terms.at[peer, y, c], lambda k: come_z.at[k - 1], sent, came, 1)

    def over_core(self):
        self.core.start()

    def over_y(self):
        self.core.wait()

        def add(k, carry):
            for r in range(2):
                self.terms[k, r, self.c] = (
                    self.terms[k, r, self.c].astype(F32) + self.come_core[k, r].astype(F32)
                ).astype(BF)
            return carry

        lax.fori_loop(0, self.outer, add, 0)
        self.side.start()

    def over_z(self):
        self.side.wait()

        def add(k, carry):
            self.terms[k, self.y, self.c] = (
                self.terms[k, self.y, self.c].astype(F32) + self.come_y[k].astype(F32)
            ).astype(BF)
            return carry

        lax.fori_loop(0, self.outer, add, 0)
        for move in self.moves:
            move.start()

    def total(self):
        for move in self.moves:
            move.wait()
        total = self.terms[self.o, self.y, self.c].astype(F32)
        for k in range(1, self.outer):
            total = total + self.come_z[k - 1].astype(F32)
        return total


def spread_scratch(outer, each, columns):
    return [
        pltpu.VMEM((outer, 2, 2, each, columns), BF),
        pltpu.VMEM((outer, 2, each, columns), BF),
        pltpu.VMEM((outer, each, columns), BF),
        pltpu.VMEM((outer - 1, each, columns), BF),
        pltpu.SemaphoreType.DMA((1 + outer,)),
        pltpu.SemaphoreType.DMA((1 + outer,)),
    ]


def finish_kernel(outer, hgrad_ref, x_ref, gain_ref, w_any, *refs):
    (no_ref, nx_ref, po_ref, px_ref, oo_ref, ox_ref, sg_ref), refs = refs[:7], refs[7:]
    dws, refs = refs[:3], refs[3:]
    done, refs = refs[:2], refs[2:]
    was_l, refs = refs[:2], refs[2:]
    was_r, refs = refs[:2], refs[2:]
    tgrad_ref, gains_ref, qkv_ref, outw_ref = refs[:4]
    fins, to_l, to_r, refs = refs[4:7], refs[7:9], refs[9:11], refs[11:]
    sums_refs, refs = [refs[:6], refs[6:12]], refs[12:]
    final_refs, refs = [refs[5 * k : 5 * k + 5] for k in range(3)], refs[15:]
    part_ref, theirs_ref, p_send, p_recv, out_ref, come_ref, c_send, c_recv = refs[:8]
    q_refs, o_refs, refs = refs[8:14], refs[14:20], refs[20:]
    g_buf, g_come, g_z, g_send, g_recv, w_ref, w_sem = refs
    d, t, o, i = place()
    rows = hgrad_ref.shape[0]
    width = w_ref.shape[1]
    w_copy = pltpu.make_async_copy(w_any.at[:, pl.ds(0, width)], w_ref, w_sem)
    w_copy.start()
    greet_all(outer)
    sums = [
        Sums(outer, (3,), [dws[1 + k]], [was_l[k]], [was_r[k]], [to_l[k]], [to_r[k]], *sums_refs[k]) for k in range(2)
    ]
    came = [done, (to_l[0], to_r[0]), (to_l[1], to_r[1])]
    finals = [
        Final(outer, dws[k], *came[k], final_refs[k][0], sums_refs[0][1], fins[k], *final_refs[k][1:]) for k in range(3)
    ]
    for one in sums:
        one.load()
    for one in sums:
        one.send()
    whole, part = Spread(outer, *q_refs), Spread(outer, *o_refs)
    each, heads = outw_ref.shape

    def out_block(k, carry):
        for r in range(GROUP):
            at = pl.ds(pl.multiple_of((k * GROUP + r) * each, each), each)
            part.terms[k, r // 2, r % 2, :, :heads] = oo_ref[at, :]
            part.terms[k, r // 2, r % 2, :, heads:] = ox_ref[at, :]
        return carry

    lax.fori_loop(0, outer, out_block, 0)
    part.over_core()

    w_copy.wait()
    part_ref[...] = mm_nt(px_ref[...], w_ref[...]).astype(BF)
    exchange = to_x(part_ref, theirs_ref, p_send, p_recv)
    exchange.start()

    def weights_block(k, carry):
        lanes = pl.ds(pl.multiple_of(k * GROUP * each, GROUP * each), GROUP * each)
        total = (mm_tn(no_ref[:, lanes], po_ref[...]) + mm_tn(nx_ref[:, lanes], px_ref[...])).astype(BF)
        for r in range(GROUP):
            whole.terms[k, r // 2, r % 2] = total[r * each : (r + 1) * each]
        return carry

    part.over_y()
    lax.fori_loop(0, outer, weights_block, 0)
    whole.over_core()
    finals[0].send()
    whole.over_y()
    part.over_z()
    sums[0].wait()
    finals[1].send()

    exchange.wait()
    quarter = rows // 4

    def norm_rows(p, gain_grad):
        at = pl.ds(pl.multiple_of(p * quarter, quarter), quarter)
        normed_grad = mm_nt(po_ref[at, :], w_ref[...]).astype(BF).astype(F32) + theirs_ref[at, :].astype(F32)
        x = x_ref[at, :].astype(F32)
        inverse = lax.rsqrt(jnp.mean(x * x, axis=-1, keepdims=True) + EPSILON)
        scaled = normed_grad * gain_ref[...]
        tgrad_ref[at, :] = (
            hgrad_ref[at, :]
            + inverse * scaled
            - x * (inverse * inverse * inverse * jnp.mean(scaled * x, axis=-1, keepdims=True))
        )
        return gain_grad + jnp.sum(normed_grad * (x * inverse), axis=0, keepdims=True)

    g_buf[0, 0:1, :] = lax.fori_loop(0, 4, norm_rows, jnp.zeros((1, D), F32))
    g_buf[0, 1:2, :] = sg_ref[...]
    g_buf[0, 2:8, :] = jnp.zeros((6, D), F32)
    g_moves = [
        to_dp(1, g_buf.at[0], g_come.at[0], g_send.at[0], g_recv.at[0]),
        to_dp(2, g_buf.at[1], g_come.at[1], g_send.at[1], g_recv.at[1]),
        to_x(g_buf.at[2], g_come.at[2], g_send.at[2], g_recv.at[2]),
    ]
    g_moves[0].start()
    whole.over_z()
    g_moves[0].wait()
    g_buf[1] = g_buf[0] + g_come[0]
    g_moves[1].start()
    sums[1].wait()
    finals[2].send()
    g_moves[1].wait()
    g_buf[2] = g_buf[1] + g_come[1]
    g_moves[2].start()
    out = part.total()
    outw_ref[...] = out[:, :heads]
    out_ref[...] = out[:, heads:].astype(BF)
    to_other = to_x(out_ref, come_ref, c_send, c_recv)
    to_other.start()
    g_moves[2].wait()
    g_z[0] = g_buf[2] + g_come[2]
    gz_moves = over_outer(outer, lambda peer: g_z.at[0], lambda k: g_z.at[k], g_send, g_recv, 2)
    for move in gz_moves:
        move.start()
    qkv_ref[...] = whole.total()
    to_other.wait()
    outw_ref[...] = outw_ref[...] + come_ref[...].astype(F32)
    for move in gz_moves:
        move.wait()
    gains = g_z[(o + outer) % outer]
    for k in range(1, outer):
        gains = gains + g_z[(o - k + outer) % outer]
    gains_ref[...] = gains
    for final in finals:
        final.wait()


def finish(outer, hgrad, x, gain, weights_full, extra, dws, done, was_l, was_r):
    rows = hgrad.shape[0]
    packed = dws[0].shape[2]
    width = weights_full.shape[1] // 2
    heads = width // 2
    each = D // (outer * GROUP)
    hop = jax.ShapeDtypeStruct((GROUP, packed, D), BF)
    return remote_call(
        functools.partial(finish_kernel, outer),
        "finish",
        11,
        [
            jax.ShapeDtypeStruct((rows, D), F32),
            jax.ShapeDtypeStruct((8, D), F32),
            jax.ShapeDtypeStruct((each, width), F32),
            jax.ShapeDtypeStruct((each, heads), F32),
        ]
        + [hop] * 7,
        [VM] * 3 + [ANY] + [VM] * 7 + [ANY] * 9,
        [VM] * 4 + [ANY] * 7,
        (hgrad, x, gain.reshape(1, D), weights_full, *extra, *dws, *done, *was_l, *was_r),
        [
            *sums_scratch(1, packed) * 2,
            *final_scratch(packed) * 3,
            pltpu.VMEM((rows, D), BF),
            pltpu.VMEM((rows, D), BF),
            pltpu.SemaphoreType.DMA,
            pltpu.SemaphoreType.DMA,
            pltpu.VMEM((each, heads), BF),
            pltpu.VMEM((each, heads), BF),
            pltpu.SemaphoreType.DMA,
            pltpu.SemaphoreType.DMA,
            *spread_scratch(outer, each, width),
            *spread_scratch(outer, each, 2 * heads),
            pltpu.VMEM((3, 8, D), F32),
            pltpu.VMEM((3, 8, D), F32),
            pltpu.VMEM((outer, 8, D), F32),
            pltpu.SemaphoreType.DMA((2 + outer,)),
            pltpu.SemaphoreType.DMA((2 + outer,)),
            pltpu.VMEM((D, width), BF),
            pltpu.SemaphoreType.DMA,
        ],
        30 << 30,
    )


def settle_kernel(in_rows, idx_ref, *refs):
    n = len(refs) - 7
    sources, (in_ref, down_ref, held, wide_in, wide_down, l_sem, s_sem) = refs[:n], refs[n:]
    loads = [pltpu.make_async_copy(source, held.at[j], l_sem.at[j]) for j, source in enumerate(sources)]
    for c in loads:
        c.start()
    stores = []
    for j in range(n):
        loads[j].wait()
        for m in range(GROUP):
            k = j * GROUP + m
            at = (idx_ref[1] ^ m) * n + j
            wide_in[k] = held[j, m, :in_rows, :].astype(F32)
            wide_down[k] = held[j, m, in_rows:, :].astype(F32)
            stores.append(pltpu.make_async_copy(wide_in.at[k], in_ref.at[at], s_sem.at[2 * k]))
            stores.append(pltpu.make_async_copy(wide_down.at[k], down_ref.at[at], s_sem.at[2 * k + 1]))
            for c in stores[-2:]:
                c.start()
    for c in stores:
        c.wait()


def settle_experts(idx, fins, in_rows):
    n = len(fins)
    _, packed, _ = fins[0].shape
    experts, down_rows = n * GROUP, packed - in_rows
    return call(
        functools.partial(settle_kernel, in_rows),
        "settle_experts",
        [jax.ShapeDtypeStruct((experts, in_rows, D), F32), jax.ShapeDtypeStruct((experts, down_rows, D), F32)],
        [SMEM] + [ANY] * n,
        [ANY] * 2,
        (idx, *fins),
        scratch=[
            pltpu.VMEM((n, GROUP, packed, D), BF),
            pltpu.VMEM((experts, in_rows, D), F32),
            pltpu.VMEM((experts, down_rows, D), F32),
            pltpu.SemaphoreType.DMA((n,)),
            pltpu.SemaphoreType.DMA((2 * experts,)),
        ],
        moved=9 << 20,
    )


def layer(
    tokens,
    cotangent,
    lengths,
    expert_ids,
    gate_values,
    first_gain,
    qkv_weight,
    attn_out_weight,
    second_gain,
    expert_in_weight,
    expert_out_weight,
):
    rows = tokens.shape[0]
    n_tensor, n_dp = lax.axis_size("tensor"), lax.axis_size("dp")
    outer = n_dp // GROUP
    slot_rows = rows * n_tensor
    d, t = lax.axis_index("dp"), lax.axis_index("tensor")
    o, i = d // GROUP, d % GROUP
    length = lengths[0]
    idx = jnp.stack([o, i, t, length]).astype(jnp.int32)
    width = qkv_weight.shape[1] * qkv_weight.shape[2]
    experts_local, in_rows, _ = expert_in_weight.shape
    down_rows = expert_out_weight.shape[1]
    own_experts = experts_local // GROUP
    pair = n_tensor == 2
    q_block = 256
    half = rows // 2

    def across(v, m):
        return lax.ppermute(v, "dp", [(a, a ^ m) for a in range(n_dp)])

    def beside(v):
        return lax.ppermute(v, "tensor", [(0, 1), (1, 0)])

    def hop(pairs):
        up = [(a, a + GROUP) for a in range(n_dp - GROUP)]
        down = [(b, a) for a, b in up]
        return [(lax.ppermute(a, "dp", up), lax.ppermute(b, "dp", down)) for a, b in pairs]

    def gather_group(pieces):
        if pair:
            a, b = pieces
            ax, by, ay, bx = beside(a), across(b, 2), across(a, 2), beside(b)
            axy, bxy = across(ax, 2), beside(by)
            slots = [[a, ax, b, bx], [ay, axy, by, bxy]]
        else:
            slot = lax.all_gather(pieces[0], "tensor", axis=0, tiled=True)
            slots = [[slot], [across(slot, 2)]]
        return slots + [[across(p, 1) for p in s] for s in slots]

    positions = t * rows + jnp.arange(rows, dtype=jnp.int32)
    valid_rows = positions < length
    n_experts = experts_local * n_tensor
    chosen = expert_ids.T[None] == jnp.arange(n_experts, dtype=jnp.int32)[:, None, None]
    gates = jnp.sum(jnp.where(chosen, gate_values.T[None].astype(F32), 0.0), axis=1)
    gates = jnp.where(valid_rows[None, :], gates, 0.0).astype(BF)
    x = tokens.astype(F32)
    inverse_one = lax.rsqrt(jnp.mean(x * x, axis=-1, keepdims=True) + EPSILON)
    normed_one = (x * inverse_one * first_gain).astype(BF)
    expert_outs, row_grads, weight_grads = [], [], []
    if pair and outer == 4:
        frequency = THETA ** (-(jnp.arange(HD // 2).astype(F32) * 2.0 / HD))
        shard = jnp.concatenate([qkv_weight.reshape(-1, width), attn_out_weight.T], axis=1)
        main, ready, packed, first_l, first_r = collect(
            outer, shard, normed_one, gates, jnp.tile(frequency, 4)[None, :], expert_in_weight, expert_out_weight
        )
        weights_full, other, cosine, sine, pos, own_gates, pos_columns, gate_columns = main
        main, dy_moved, later, one_l, one_r = attention(
            outer,
            q_block,
            lengths,
            normed_one,
            other,
            weights_full,
            cosine,
            sine,
            tokens,
            second_gain,
            cotangent,
            ready[1],
            packed,
        )
        own_weights = [*ready, *later]
        one_l, one_r = [first_l, *one_l], [first_r, *one_r]
        qkv, lse, attn_own, attn_other, hidden, *normed_two = main
        attn_parts = [attn_own, attn_other]
        gathered, out_grads, moved_l, moved_r = spread(
            outer,
            pos,
            own_gates,
            normed_two,
            [cotangent, *dy_moved],
            (2, 2, 2),
            one_l[:3],
            one_r[:3],
        )
        two_l, two_r = [*moved_l], [*moved_r]
        expert_rows, moved_l, moved_r = hand_out(
            outer, pos, normed_two, gathered, (3, 2), [two_l[0], one_l[3]], [two_r[0], one_r[3]]
        )
        three_l, three_r = [moved_l[0]], [moved_r[0]]
        two_l.append(moved_l[1])
        two_r.append(moved_r[1])
        hop_plans = [
            lambda: ((3,), [two_l[1]], [two_r[1]]),
            lambda: ((3,), [two_l[2]], [two_r[2]]),
            lambda: ((3,), [two_l[3]], [two_r[3]]),
            lambda: ((), [], []),
        ]
        sums_l, sums_r = [], []
        for j in range(own_experts):
            first_grad = weight_grads[:1]
            sum_plan = ((j,), first_grad, sums_l or first_grad, sums_r or first_grad) if j else ((), [], [], [])
            if j == own_experts - 1:
                second_grad = weight_grads[1]
                sum_plan = ((j, 1), weight_grads[:2], [*sums_l, second_grad], [*sums_r, second_grad])
            (y, dx, dw), moved_l, moved_r, sums_l, sums_r = expert_step(
                j,
                outer,
                in_rows,
                down_rows,
                expert_rows,
                out_grads,
                own_weights[j],
                [one_l[j], two_l[j], three_l[j]],
                [one_r[j], two_r[j], three_r[j]],
                hop_plans[j](),
                sum_plan,
            )
            three_l.extend(moved_l[:1])
            three_r.extend(moved_r[:1])
            expert_outs.append(y)
            row_grads.append(dx)
            weight_grads.append(dw)
        valid_column = valid_rows.astype(F32)[:, None]
        _, dw_b, dw_c, dw_d = weight_grads
        main, fin_a, sum_l, sum_r = rows_back(
            outer,
            pos_columns,
            gate_columns,
            valid_column,
            hidden,
            cotangent,
            second_gain,
            weights_full,
            row_grads,
            expert_outs,
            (2, 1),
            ((2, 1), (1, 2)),
            [dw_b, dw_c, dw_d],
            [sums_l[1], dw_c],
            [sums_r[1], dw_c],
            [weight_grads[0], sums_l[0], sums_r[0]],
        )
        hidden_grad, branch_grad, second_gain_part, attn_grad_own, attn_grad_other, mixed = main
        (projected_own, projected_other, output), three_l, three_r = attention_back(
            outer,
            q_block,
            lengths,
            qkv,
            lse,
            cosine,
            sine,
            [attn_grad_own, attn_grad_other],
            hidden,
            valid_column,
            mixed,
            (3, 2),
            [dw_b, dw_d],
            [sum_l[0], sum_l[3]],
            [sum_r[0], sum_r[3]],
        )
        out_own, out_other = (mm_tn(branch_grad, part).astype(BF) for part in attn_parts)
        tokens_grad, gains, qkv_grad, attn_out_grad, *fins = finish(
            outer,
            hidden_grad,
            tokens,
            first_gain,
            weights_full,
            [normed_one, other, projected_own, projected_other, out_own, out_other, second_gain_part],
            [dw_b, dw_c, dw_d],
            [three_l[0], three_r[0]],
            [sum_l[2], three_l[1]],
            [sum_r[2], three_r[1]],
        )
        expert_in_grad, expert_out_grad = settle_experts(idx, [fin_a, *fins[:3]], in_rows)
        return (
            output,
            tokens_grad,
            gains[0],
            qkv_grad.reshape(qkv_weight.shape),
            attn_out_grad.T,
            gains[1],
            expert_in_grad,
            expert_out_grad,
        )
    else:
        if pair:
            gates_x = beside(gates)
            slot_gates = jnp.concatenate(
                [gates[:, :half], gates_x[:, :half], gates[:, half:], gates_x[:, half:]], axis=1
            )
        else:
            slot_gates = lax.all_gather(gates, "tensor", axis=1, tiled=True)
        gates_y = across(slot_gates, 2)
        all_gates = jnp.stack([slot_gates, gates_y, across(slot_gates, 1), across(gates_y, 1)])
        own_gates = lax.dynamic_slice_in_dim(
            all_gates, t * experts_local + i * own_experts, own_experts, axis=1
        ).astype(F32)
        named = own_gates > 0
        before = (
            lax.broadcasted_iota(jnp.int32, (slot_rows, slot_rows), 0)
            < lax.broadcasted_iota(jnp.int32, (slot_rows, slot_rows), 1)
        ).astype(BF)
        ranks = jnp.dot(
            named.astype(BF).reshape(GROUP * own_experts, slot_rows), before, preferred_element_type=F32
        ).reshape(GROUP, own_experts, slot_rows)
        pos = jnp.where(named, ranks, -1.0).astype(jnp.int32)
        pos_columns, gate_columns = jnp.swapaxes(pos, 1, 2), jnp.swapaxes(own_gates, 1, 2)

        cosine, sine = rope_tables(slot_rows)
        dy = jnp.where(valid_rows[:, None], cotangent, jnp.zeros_like(cotangent))
        qkv_full = lax.all_gather(qkv_weight.reshape(qkv_weight.shape[0], width), "dp", axis=0, tiled=True)
        out_full = lax.all_gather(attn_out_weight.T, "dp", axis=0, tiled=True)
        by_distance = pack_weights(idx, expert_in_weight, expert_out_weight)
        by_distance = [by_distance[0]] + [across(by_distance[m], m) for m in range(1, GROUP)]
        own_weights = [jnp.stack([v[j] for v in by_distance]) for j in range(own_experts)]
        hops = [hop([(own, own) for own in own_weights])]
        if pair:
            out_parts = [out_full, beside(out_full)]
        else:
            gathered = lax.all_gather(out_full, "tensor", axis=0)
            out_parts = [gathered[k] for k in range(n_tensor)]

        if pair:
            other = beside(normed_one)
            normed_all = jnp.where(
                t == 0,
                jnp.concatenate([normed_one, other], axis=0),
                jnp.concatenate([other, normed_one], axis=0),
            )
        else:
            normed_all = lax.all_gather(normed_one, "tensor", axis=0, tiled=True)
        qkv = qkv_project(normed_all, qkv_full, cosine, sine)
        *attended, lse = attend(idx, qkv, 2 if pair else 1, q_block)
        if pair:
            attn_parts = [attended[0], beside(attended[1])]
        else:
            heads = attended[0].shape[1]
            exchanged = lax.all_to_all(attended[0].reshape(n_tensor, rows, heads), "tensor", 0, 0)
            attn_parts = [exchanged[k] for k in range(n_tensor)]
        attn_parts, hops[0] = lax.optimization_barrier((attn_parts, hops[0]))
        if outer > 2:
            hops.append(hop(hops[0]))
        hidden, *normed_two = project_out(tokens, second_gain, attn_parts, out_parts, 2 if pair else 1)

        dy_slots = gather_group([dy[:half], dy[half:]] if pair else [dy])
        out_grads = [dispatch(pos[s], own_gates[s], dy_slots[s], True) for s in range(GROUP)]
        normed_slots = gather_group(normed_two)
        normed_slots, out_grads, hops = lax.optimization_barrier((normed_slots, out_grads, hops))
        while len(hops) < outer - 1:
            hops.append(hop(hops[-1]))
        expert_rows = [dispatch(pos[s], own_gates[s], normed_slots[s], False) for s in range(GROUP)]

        for j in range(own_experts):
            if j:
                idx, expert_outs[-1] = lax.optimization_barrier((idx, expert_outs[-1]))
            y, dx, dw = expert(
                idx,
                j,
                outer,
                in_rows,
                down_rows,
                expert_rows,
                out_grads,
                own_weights[j],
                [h[j][0] for h in hops],
                [h[j][1] for h in hops],
            )
            expert_outs.append(y)
            row_grads.append(dx)
            weight_grads.append(dw)

    def sum_group(sources, scaled):
        def part(s, add, n_outs):
            return combine(pos_columns[s], gate_columns[s], sources, s, scaled, add, n_outs)

        far = [part(2, None, 1)[0], part(3, None, 1)[0]]
        near = [across(v, 1) for v in far]
        if pair:
            ay, axy, by, bxy = part(1, near[1], 4)
            a, ax, b, bx = part(0, near[0], 4)

            def add(p, q):
                return (p.astype(F32) + q.astype(F32)).astype(BF)

            a, ax = add(a, across(ay, 2)), add(ax, across(axy, 2))
            b, by = add(b, beside(bx)), add(by, beside(bxy))
            return [[a, beside(ax)], [b, across(by, 2)]]
        (y,) = part(1, near[1], 1)
        (v,) = part(0, near[0], 1)
        v = (v.astype(F32) + across(y, 2).astype(F32)).astype(BF)
        return [[lax.psum_scatter(v, "tensor", scatter_dimension=0, tiled=True)]]

    valid_column = valid_rows.astype(F32)[:, None]
    normed_two_grad = sum_group(row_grads, False)
    hidden_grad, branch_grad, second_gain_part, *attn_grads = hidden_back(
        valid_column, hidden, cotangent, second_gain, normed_two_grad, out_parts
    )
    if pair:
        attn_grads = [attn_grads[0], beside(attn_grads[1])]
    else:
        attn_grads = [
            lax.all_to_all(jnp.stack(attn_grads), "tensor", 0, 0).reshape(slot_rows, attn_grads[0].shape[1])
        ]
    projected_grads = attend_back(idx, qkv, lse, cosine, sine, attn_grads, q_block)

    def first_norm_part(v):
        return lax.dot_general(v, qkv_full, (((1,), (1,)), ((), ())), preferred_element_type=F32).astype(BF)

    if pair:
        theirs = beside(first_norm_part(projected_grads[1]))
        normed_one_grad = first_norm_part(projected_grads[0]).astype(F32) + theirs.astype(F32)
        qkv_part = mm_tn(normed_one, projected_grads[0]) + mm_tn(other, projected_grads[1])
    else:
        normed_one_grad = lax.psum_scatter(
            first_norm_part(projected_grads[0]), "tensor", scatter_dimension=0, tiled=True
        ).astype(F32)
        qkv_part = mm_tn(normed_all, projected_grads[0])
    first_gain_part = jnp.sum(normed_one_grad * (x * inverse_one), axis=0)
    scaled = normed_one_grad * first_gain
    tokens_grad = (
        hidden_grad
        + inverse_one * scaled
        - x * (inverse_one * inverse_one * inverse_one * jnp.mean(scaled * x, axis=-1, keepdims=True))
    )

    mixture = sum_group(expert_outs, True)
    mixture = jnp.concatenate([sum(v.astype(F32) for v in terms) for terms in mixture], axis=0)
    output = jnp.where(valid_rows[:, None], hidden + mixture, 0.0).astype(BF)

    outer_groups = [[a * GROUP + b for a in range(outer)] for b in range(GROUP)]
    received = [[] for _ in range(GROUP)]
    for dw in weight_grads:
        mine = lax.psum_scatter(dw, "dp", scatter_dimension=0, tiled=True, axis_index_groups=outer_groups)
        for m in range(GROUP):
            block = mine[0, m]
            received[m].append(block if m == 0 else across(block, m))
    by_distance = jnp.stack([jnp.stack(v) for v in received])
    by_source = jnp.take(by_distance, jnp.arange(GROUP) ^ i, axis=0).reshape(
        experts_local, in_rows + down_rows, D
    )
    expert_in_grad = by_source[:, :in_rows].astype(F32)
    expert_out_grad = by_source[:, in_rows:].astype(F32)

    attn_out_parts = [mm_tn(branch_grad, part).astype(BF) for part in attn_parts]
    if pair:
        attn_out_part = (attn_out_parts[0].astype(F32) + beside(attn_out_parts[1]).astype(F32)).astype(BF)
    else:
        attn_out_part = lax.psum_scatter(jnp.stack(attn_out_parts), "tensor", scatter_dimension=0, tiled=True)[0]
    qkv_grad = lax.psum_scatter(qkv_part.astype(BF), "dp", scatter_dimension=0, tiled=True).astype(F32)
    attn_out_grad = lax.psum_scatter(attn_out_part, "dp", scatter_dimension=0, tiled=True).astype(F32).T

    gains = jnp.stack([first_gain_part, second_gain_part[0]])
    if pair:
        gains = gains + beside(gains)
    else:
        gains = lax.psum(gains, "tensor")
    step = 1
    while step < n_dp:
        gains = gains + across(gains, step)
        step *= 2
    return (
        output,
        tokens_grad,
        gains[0],
        qkv_grad.reshape(qkv_weight.shape),
        attn_out_grad,
        gains[1],
        expert_in_grad,
        expert_out_grad,
    )


def solution(mesh):
    placed = (
        P(("dp", "tensor"), None),
        P(("dp", "tensor"), None),
        P("dp"),
        P(("dp", "tensor"), None),
        P(("dp", "tensor"), None),
        P(),
        P("dp", "tensor", None),
        P("tensor", "dp"),
        P(),
        P("tensor", "dp", None),
        P("tensor", "dp", None),
    )
    return jax.shard_map(
        layer,
        mesh=mesh,
        in_specs=placed,
        out_specs=(
            P(("dp", "tensor"), None),
            P(("dp", "tensor"), None),
            P(),
            P("dp", "tensor", None),
            P("tensor", "dp"),
            P(),
            P("tensor", "dp", None),
            P("tensor", "dp", None),
        ),
        check_vma=False,
    )
```

```python
import functools
import math

import jax
import jax.numpy as jnp
from jax import lax
from jax.experimental import pallas as pl
from jax.experimental.pallas import tpu as pltpu
from jax.sharding import PartitionSpec as P

D = 1024
HD = 64
FF = 512
G = 2
CAP = 288
GROUP = 4
LANES = 128

EPSILON = 1e-06
THETA = 10000.0
NEGATIVE = -1e30
BF = jnp.bfloat16
F32 = jnp.float32
VMEM_LIMIT = 60 * 1024 * 1024
MESH = pl.DeviceIdType.MESH

ANY = pl.BlockSpec(memory_space=pl.ANY)
SMEM = pl.BlockSpec(memory_space=pltpu.SMEM)
VM = pl.BlockSpec(memory_space=pltpu.VMEM)


def mm(a, b):
    return lax.dot_general(a, b, (((1,), (0,)), ((), ())), preferred_element_type=F32)


def mm_nt(a, b):
    return lax.dot_general(a, b, (((1,), (1,)), ((), ())), preferred_element_type=F32)


def mm_tn(a, b):
    return lax.dot_general(a, b, (((0,), (0,)), ((), ())), preferred_element_type=F32)


def call(kernel, name, out_shape, in_specs, out_specs, args, scratch=(), flops=0, moved=0, **more):
    return pl.pallas_call(
        kernel,
        name=name,
        out_shape=out_shape,
        in_specs=in_specs,
        out_specs=out_specs,
        scratch_shapes=list(scratch),
        compiler_params=pltpu.CompilerParams(vmem_limit_bytes=VMEM_LIMIT),
        cost_estimate=pl.CostEstimate(flops=flops, bytes_accessed=moved, transcendentals=0),
        **more,
    )(*args)


def rope_tables(total_rows):
    half = HD // 2
    positions = jnp.arange(total_rows).astype(F32)
    frequency = THETA ** (-(jnp.arange(half).astype(F32) * 2.0 / HD))
    angles = positions[:, None] * frequency[None, :]
    cosine, sine = jnp.cos(angles), jnp.sin(angles)
    return (
        jnp.concatenate([cosine] * 4, axis=1),
        jnp.concatenate([-sine, sine, -sine, sine], axis=1),
    )


def swap_halves(v):
    lane = lax.broadcasted_iota(jnp.int32, v.shape, 1)
    return jnp.where(lane % HD < HD // 2, pltpu.roll(v, LANES - HD // 2, 1), pltpu.roll(v, HD // 2, 1))


def qkv_kernel(n_ref, w_ref, cos_ref, sin_ref, out_ref):
    projected = mm(n_ref[...], w_ref[...])
    cosine, sine = cos_ref[...], sin_ref[...]
    key_lanes = lax.broadcasted_iota(jnp.int32, cosine.shape, 1) < HD
    for g in range(projected.shape[1] // (2 * LANES)):
        q = projected[:, g * 2 * LANES : g * 2 * LANES + LANES]
        kv = projected[:, g * 2 * LANES + LANES : (g + 1) * 2 * LANES]
        q = q * cosine + swap_halves(q) * sine
        kv = jnp.where(key_lanes, kv * cosine + swap_halves(kv) * sine, kv)
        out_ref[:, g * 2 * LANES : g * 2 * LANES + LANES] = q.astype(BF)
        out_ref[:, g * 2 * LANES + LANES : (g + 1) * 2 * LANES] = kv.astype(BF)


def qkv_project(normed, weight, cosine, sine):
    rows, width = normed.shape[0], weight.shape[1]
    block = 256
    return pl.pallas_call(
        qkv_kernel,
        name="qkv_rope",
        grid=(rows // block,),
        out_shape=jax.ShapeDtypeStruct((rows, width), BF),
        in_specs=[
            pl.BlockSpec((block, D), lambda b: (b, 0)),
            pl.BlockSpec((D, width), lambda b: (0, 0)),
            pl.BlockSpec((block, LANES), lambda b: (b, 0)),
            pl.BlockSpec((block, LANES), lambda b: (b, 0)),
        ],
        out_specs=pl.BlockSpec((block, width), lambda b: (b, 0)),
        compiler_params=pltpu.CompilerParams(vmem_limit_bytes=VMEM_LIMIT),
        cost_estimate=pl.CostEstimate(flops=2 * rows * D * width, bytes_accessed=6 << 20, transcendentals=0),
    )(normed, weight, cosine, sine)


def head_pair(v):
    first = lax.broadcasted_iota(jnp.int32, v.shape, 1) < HD
    zero = jnp.zeros_like(v)
    return jnp.concatenate([jnp.where(first, v, zero), jnp.where(first, zero, v)], axis=0)


def head_join(v):
    n = v.shape[0] // 2
    first = lax.broadcasted_iota(jnp.int32, (n, LANES), 1) < HD
    return jnp.where(first, v[:n], v[n:])


def doubled(kv):
    first = lax.broadcasted_iota(jnp.int32, kv.shape, 1) < HD
    other = pltpu.roll(kv.astype(F32), HD, 1).astype(BF)
    return jnp.where(first, kv, other), jnp.where(first, other, kv)


def allowed(n_keys, q_block, q_start, length):
    key = lax.broadcasted_iota(jnp.int32, (n_keys, 2 * q_block), 0)
    lane = lax.broadcasted_iota(jnp.int32, (n_keys, 2 * q_block), 1)
    query = q_start + jnp.where(lane < q_block, lane, lane - q_block)
    return (key <= query) & (key < length)


def attend_kernel(q_block, idx_ref, qkv_ref, *out_refs):
    outs, lse_ref = out_refs[:-1], out_refs[-1]
    rows = qkv_ref.shape[0]
    length = idx_ref[3]
    keys, values = doubled(qkv_ref[:, LANES:])
    for b in range(rows // q_block):
        start, n_keys = b * q_block, (b + 1) * q_block
        q = head_pair(qkv_ref[start : start + q_block, :LANES])
        scores = mm_nt(keys[:n_keys], q) * (1.0 / math.sqrt(HD))
        scores = jnp.where(allowed(n_keys, q_block, start, length), scores, NEGATIVE)
        largest = jnp.max(scores, axis=0, keepdims=True)
        expon = jnp.exp(scores - largest)
        totals = jnp.sum(expon, axis=0, keepdims=True)
        probs = (expon * (1.0 / totals)).astype(BF)
        mixed = head_join(mm_tn(probs, values[:n_keys])).astype(BF)
        lse_ref[0, b : b + 1, :] = largest + jnp.log(totals)
        if len(outs) == 1:
            outs[0][start : start + q_block] = mixed
        else:
            own_rows = rows // 2
            half, at = start // own_rows, start % own_rows
            mine = idx_ref[2] == half

            @pl.when(mine)
            def _():
                outs[0][at : at + q_block] = mixed

            @pl.when(jnp.logical_not(mine))
            def _():
                outs[1][at : at + q_block] = mixed


def attend(idx, qkv, parts, q_block):
    rows, groups = qkv.shape[0], qkv.shape[1] // (2 * LANES)
    out = jax.ShapeDtypeStruct((rows // parts, groups * LANES), BF)
    return pl.pallas_call(
        functools.partial(attend_kernel, q_block),
        name="attend",
        grid=(groups,),
        out_shape=[out] * parts + [jax.ShapeDtypeStruct((groups, rows // q_block, 2 * q_block), F32)],
        in_specs=[SMEM, pl.BlockSpec((rows, 2 * LANES), lambda g: (0, g))],
        out_specs=[pl.BlockSpec((rows // parts, LANES), lambda g: (0, g))] * parts
        + [pl.BlockSpec((1, rows // q_block, 2 * q_block), lambda g: (g, 0, 0))],
        compiler_params=pltpu.CompilerParams(vmem_limit_bytes=VMEM_LIMIT),
        cost_estimate=pl.CostEstimate(flops=14 << 30, bytes_accessed=4 << 20, transcendentals=0),
    )(idx, qkv)


def attend_back_kernel(q_block, n_grads, idx_ref, qkv_ref, lse_ref, cos_ref, sin_ref, *refs):
    grads, outs = refs[:n_grads], refs[n_grads : 2 * n_grads]
    do_ref, dq_ref, dk_ref, dv_ref = refs[2 * n_grads :]
    rows = qkv_ref.shape[0]
    own_rows = rows // n_grads
    length = idx_ref[3]
    for p in range(n_grads):
        at = pl.multiple_of((p ^ idx_ref[2] if n_grads == 2 else 0) * own_rows, own_rows)
        do_ref[pl.ds(at, own_rows), :] = grads[p][...]
    keys, values = doubled(qkv_ref[:, LANES:])
    dk_ref[...] = jnp.zeros_like(dk_ref)
    dv_ref[...] = jnp.zeros_like(dv_ref)
    scale = 1.0 / math.sqrt(HD)
    for b in range(rows // q_block):
        start, n_keys = b * q_block, (b + 1) * q_block
        q = head_pair(qkv_ref[start : start + q_block, :LANES])
        grad = head_pair(do_ref[start : start + q_block, :])
        scores = mm_nt(keys[:n_keys], q) * scale
        probs = jnp.where(
            allowed(n_keys, q_block, start, length), jnp.exp(scores - lse_ref[0, b : b + 1, :]), 0.0
        )
        prob_grad = mm_nt(values[:n_keys], grad)
        center = jnp.sum(probs * prob_grad, axis=0, keepdims=True)
        score_grad = (probs * (prob_grad - center)).astype(BF)
        dq_ref[start : start + q_block, :] = head_join(mm_tn(score_grad, keys[:n_keys])) * scale
        dk_ref[:n_keys, :] += mm(score_grad, q)
        dv_ref[:n_keys, :] += mm(probs.astype(BF), grad)
    cosine, sine = cos_ref[...], sin_ref[...]
    dq = dq_ref[...]
    dq = (dq * cosine - swap_halves(dq) * sine).astype(BF)
    dk, dv = dk_ref[...] * scale, dv_ref[...]
    dk = dk + pltpu.roll(dk, HD, 1)
    dv = dv + pltpu.roll(dv, HD, 1)
    dk = dk * cosine - swap_halves(dk) * sine
    first = lax.broadcasted_iota(jnp.int32, dk.shape, 1) < HD
    dkv = jnp.where(first, dk, dv).astype(BF)
    if n_grads == 1:
        outs[0][:, :LANES] = dq
        outs[0][:, LANES:] = dkv
    else:
        do_ref[...] = dq
        for p in range(2):
            at = pl.multiple_of((p ^ idx_ref[2]) * own_rows, own_rows)
            outs[p][:, :LANES] = do_ref[pl.ds(at, own_rows), :]
        do_ref[...] = dkv
        for p in range(2):
            at = pl.multiple_of((p ^ idx_ref[2]) * own_rows, own_rows)
            outs[p][:, LANES:] = do_ref[pl.ds(at, own_rows), :]


def attend_back(idx, qkv, lse, cosine, sine, grads, q_block):
    rows, groups, parts = qkv.shape[0], qkv.shape[1] // (2 * LANES), len(grads)
    return pl.pallas_call(
        functools.partial(attend_back_kernel, q_block, parts),
        name="attend_back",
        grid=(groups,),
        out_shape=[jax.ShapeDtypeStruct((rows // parts, groups * 2 * LANES), BF)] * parts,
        in_specs=[
            SMEM,
            pl.BlockSpec((rows, 2 * LANES), lambda g: (0, g)),
            pl.BlockSpec((1, rows // q_block, 2 * q_block), lambda g: (g, 0, 0)),
            pl.BlockSpec((rows, LANES), lambda g: (0, 0)),
            pl.BlockSpec((rows, LANES), lambda g: (0, 0)),
        ]
        + [pl.BlockSpec((rows // parts, LANES), lambda g: (0, g))] * parts,
        out_specs=[pl.BlockSpec((rows // parts, 2 * LANES), lambda g: (0, g))] * parts,
        scratch_shapes=[pltpu.VMEM((rows, LANES), BF)] + [pltpu.VMEM((rows, LANES), F32)] * 3,
        compiler_params=pltpu.CompilerParams(vmem_limit_bytes=VMEM_LIMIT),
        cost_estimate=pl.CostEstimate(flops=30 << 30, bytes_accessed=6 << 20, transcendentals=0),
    )(idx, qkv, lse, cosine, sine, *grads)


def project_out_kernel(n_parts, pieces, x_ref, gain_ref, *refs):
    attns, weights = refs[:n_parts], refs[n_parts : 2 * n_parts]
    hidden_ref, normed_refs = refs[2 * n_parts], refs[2 * n_parts + 1 :]
    rows = x_ref.shape[0] // pieces
    for p in range(pieces):
        at = slice(p * rows, (p + 1) * rows)
        hidden = x_ref[at].astype(F32)
        for a, w in zip(attns, weights, strict=True):
            hidden = hidden + mm_nt(a[at], w[...])
        inverse = lax.rsqrt(jnp.mean(hidden * hidden, axis=-1, keepdims=True) + EPSILON)
        hidden_ref[at] = hidden
        normed_refs[p][...] = (hidden * inverse * gain_ref[...]).astype(BF)


def project_out(x, gain, attns, weights, pieces):
    rows = x.shape[0]
    n = len(attns)
    return call(
        functools.partial(project_out_kernel, n, pieces),
        "project_out",
        [jax.ShapeDtypeStruct((rows, D), F32)] + [jax.ShapeDtypeStruct((rows // pieces, D), BF)] * pieces,
        [VM] * (2 + 2 * n),
        [VM] * (1 + pieces),
        (x, gain.reshape(1, D), *attns, *weights),
        flops=2 * rows * D * D,
        moved=7 << 20,
    )


def hidden_back_kernel(n_parts, pieces, n_sums, valid_ref, hidden_ref, cot_ref, gain_ref, *refs):
    sums, refs = refs[: pieces * n_sums], refs[pieces * n_sums :]
    weights, refs = refs[:n_parts], refs[n_parts:]
    grad_ref, low_ref, gain_grad_ref, attn_refs = refs[0], refs[1], refs[2], refs[3:]
    rows = hidden_ref.shape[0] // pieces
    gain = gain_ref[...]
    gain_grad = jnp.zeros((1, D), F32)
    for p in range(pieces):
        at = slice(p * rows, (p + 1) * rows)
        hidden = hidden_ref[at]
        normed_grad = sums[p * n_sums][...].astype(F32)
        for s in sums[p * n_sums + 1 : (p + 1) * n_sums]:
            normed_grad = normed_grad + s[...].astype(F32)
        inverse = lax.rsqrt(jnp.mean(hidden * hidden, axis=-1, keepdims=True) + EPSILON)
        gain_grad = gain_grad + jnp.sum(normed_grad * (hidden * inverse), axis=0, keepdims=True)
        scaled = normed_grad * gain
        back = inverse * scaled - hidden * (
            inverse * inverse * inverse * jnp.mean(scaled * hidden, axis=-1, keepdims=True)
        )
        dy = jnp.where(valid_ref[at] > 0, cot_ref[at].astype(F32), 0.0)
        total = dy + back
        grad_ref[at] = total
        low = total.astype(BF)
        low_ref[at] = low
        for a, w in zip(attn_refs, weights, strict=True):
            a[at] = mm(low, w[...]).astype(BF)
    gain_grad_ref[...] = gain_grad


def hidden_back(valid, hidden, cotangent, gain, sums, weights):
    rows, pieces, n_sums, n = hidden.shape[0], len(sums), len(sums[0]), len(weights)
    heads = weights[0].shape[1]
    return call(
        functools.partial(hidden_back_kernel, n, pieces, n_sums),
        "hidden_back",
        [
            jax.ShapeDtypeStruct((rows, D), F32),
            jax.ShapeDtypeStruct((rows, D), BF),
            jax.ShapeDtypeStruct((1, D), F32),
        ]
        + [jax.ShapeDtypeStruct((rows, heads), BF)] * n,
        [VM] * (4 + pieces * n_sums + n),
        [VM] * (3 + n),
        (valid, hidden, cotangent, gain.reshape(1, D), *[s for piece in sums for s in piece], *weights),
        flops=2 * rows * D * D,
        moved=10 << 20,
    )


def dispatch_kernel(n_pieces, scaled, pos_ref, gate_ref, *refs):
    pieces, out_ref, rows_ref, sems = refs[:n_pieces], refs[n_pieces], refs[n_pieces + 1], refs[n_pieces + 2]
    height = rows_ref.shape[0] // n_pieces
    copies = [
        pltpu.make_async_copy(piece, rows_ref.at[pl.ds(p * height, height)], sems.at[p])
        for p, piece in enumerate(pieces)
    ]
    for c in copies:
        c.start()
    rank = lax.broadcasted_iota(jnp.int32, (CAP, rows_ref.shape[0]), 0)
    for c in copies:
        c.wait()
    for j in range(out_ref.shape[0]):
        chosen = rank == pos_ref[j : j + 1, :]
        value = gate_ref[j : j + 1, :] if scaled else 1.0
        one_hot = jnp.where(chosen, value, 0.0).astype(BF)
        out_ref[j] = mm(one_hot, rows_ref[...]).astype(BF)


def dispatch(pos, gate, pieces, scaled):
    experts, rows = pos.shape
    return call(
        functools.partial(dispatch_kernel, len(pieces), scaled),
        "dispatch_scaled" if scaled else "dispatch",
        jax.ShapeDtypeStruct((experts, CAP, D), BF),
        [VM, VM] + [ANY] * len(pieces),
        VM,
        (pos, gate, *pieces),
        scratch=[pltpu.VMEM((rows, D), BF), pltpu.SemaphoreType.DMA((len(pieces),))],
        flops=2 * experts * CAP * rows * D,
        moved=5 << 20,
    )


def combine_kernel(n_experts, slot, scaled, n_adds, n_outs, pos_ref, gate_ref, *refs):
    sources, refs = refs[:n_experts], refs[n_experts:]
    adds, outs, (held, sems) = refs[:n_adds], refs[n_adds : n_adds + n_outs], refs[n_adds + n_outs :]
    copies = [
        pltpu.make_async_copy(source.at[slot], held.at[pl.ds(j * CAP, CAP)], sems.at[j])
        for j, source in enumerate(sources)
    ]
    for c in copies:
        c.start()
    for c in copies:
        c.wait()
    width = n_experts * CAP
    rows = pos_ref.shape[0]
    block = 256
    per_out = rows // n_outs
    for b in range(rows // block):
        at = slice(b * block, (b + 1) * block)
        tiles = []
        for first in range(0, width, LANES):
            size = min(LANES, width - first)
            lane = first + lax.broadcasted_iota(jnp.int32, (block, size), 1)
            tile = jnp.zeros((block, size), F32)
            for j in range(first // CAP, (first + size - 1) // CAP + 1):
                target = pos_ref[at, j : j + 1]
                target = jnp.where(target >= 0, target + j * CAP, -1)
                tile = jnp.where(lane == target, gate_ref[at, j : j + 1] if scaled else 1.0, tile)
            tiles.append(tile.astype(BF))
        total = mm(jnp.concatenate(tiles, axis=1), held[...])
        out, inner = outs[b * block // per_out], slice(b * block % per_out, b * block % per_out + block)
        if n_adds:
            total = total + adds[0][at].astype(F32)
        out[inner] = total.astype(BF)


def combine(pos, gate, sources, slot, scaled, add, n_outs):
    rows, n_experts = pos.shape
    adds = [] if add is None else [add]
    return call(
        functools.partial(combine_kernel, n_experts, slot, scaled, len(adds), n_outs),
        "combine_scaled" if scaled else "combine",
        [jax.ShapeDtypeStruct((rows // n_outs, D), BF)] * n_outs,
        [VM, VM] + [ANY] * n_experts + [VM] * len(adds),
        [VM] * n_outs,
        (pos, gate, *sources, *adds),
        scratch=[pltpu.VMEM((n_experts * CAP, D), BF), pltpu.SemaphoreType.DMA((n_experts,))],
        flops=2 * n_experts * CAP * rows * D,
        moved=5 << 20,
    )


def expert_kernel(j, outer, in_rows, down_rows, idx_ref, *refs):
    n_hops = outer - 1
    xs, refs = refs[:GROUP], refs[GROUP:]
    gs, refs = refs[:GROUP], refs[GROUP:]
    own, refs = refs[0], refs[1:]
    lefts, refs = refs[:n_hops], refs[n_hops:]
    rights, refs = refs[:n_hops], refs[n_hops:]
    y_ref, dx_ref, dw_ref = refs[:3]
    x_all, g_all, w_in, w_down, act_all, gug_all, sem_x, sem_g, sem_w, sem_d = refs[3:]
    o, i = idx_ref[0], idx_ref[1]

    def rows_of(sources, held, sems):
        return [
            pltpu.make_async_copy(s.at[j], held.at[pl.ds(n * CAP, CAP)], sems.at[n])
            for n, s in enumerate(sources)
        ]

    def weight_copies(source, at, slot):
        made = []
        for m in range(GROUP):
            place = at * GROUP + (i ^ m)
            made.append(
                pltpu.make_async_copy(
                    source.at[m, pl.ds(0, in_rows)],
                    w_in.at[pl.ds(pl.multiple_of(place * in_rows, in_rows), in_rows)],
                    sem_w.at[slot * GROUP + m],
                )
            )
            made.append(
                pltpu.make_async_copy(
                    source.at[m, pl.ds(in_rows, down_rows)],
                    w_down.at[pl.ds(pl.multiple_of(place * down_rows, down_rows), down_rows)],
                    sem_d.at[slot * GROUP + m],
                )
            )
        return made

    def each_weight(act):
        act(weight_copies(own, o, 0))
        for k in range(1, outer):

            @pl.when(o >= k)
            def _():
                act(weight_copies(lefts[k - 1], o - k, k))

            @pl.when(o + k < outer)
            def _():
                act(weight_copies(rights[k - 1], o + k, n_hops + k))

    def start(made):
        for c in made:
            c.start()

    def wait(made):
        for c in made:
            c.wait()

    each_weight(start)
    copy_x, copy_g = rows_of(xs, x_all, sem_x), rows_of(gs, g_all, sem_g)
    start(copy_x)
    start(copy_g)
    each_weight(wait)
    wait(copy_x)
    wait(copy_g)

    def per_slot(s, carry):
        at = pl.ds(pl.multiple_of(s * CAP, CAP), CAP)
        gate_up = mm(x_all[at, :], w_in[...])
        g, u = gate_up[:, :FF], gate_up[:, FF:]
        sigma = 1.0 / (1.0 + jnp.exp(-g))
        silu = g * sigma
        act = (silu * u).astype(BF)
        act_all[at, :] = act
        y_ref[s] = mm(act, w_down[...]).astype(BF)
        act_grad = mm_nt(g_all[at, :], w_down[...])
        gug_all[at, :FF] = (act_grad * u * sigma * (1.0 + g * (1.0 - sigma))).astype(BF)
        gug_all[at, FF:] = (act_grad * silu).astype(BF)
        dx_ref[s] = mm_nt(gug_all[at, :], w_in[...]).astype(BF)
        return carry

    lax.fori_loop(0, GROUP, per_slot, 0)
    for c in range(outer):
        part = mm_tn(x_all[:, c * GROUP * in_rows : (c + 1) * GROUP * in_rows], gug_all[...]).astype(BF)
        for r in range(GROUP):
            dw_ref[c, i ^ r, :in_rows, :] = part[r * in_rows : (r + 1) * in_rows]
        part = mm_tn(act_all[:, c * GROUP * down_rows : (c + 1) * GROUP * down_rows], g_all[...]).astype(BF)
        for r in range(GROUP):
            dw_ref[c, i ^ r, in_rows:, :] = part[r * down_rows : (r + 1) * down_rows]


def expert(idx, j, outer, in_rows, down_rows, xs, gs, own, lefts, rights):
    n_hops = outer - 1
    total = GROUP * CAP
    packed = in_rows + down_rows
    return call(
        functools.partial(expert_kernel, j, outer, in_rows, down_rows),
        "expert",
        [
            jax.ShapeDtypeStruct((GROUP, CAP, D), BF),
            jax.ShapeDtypeStruct((GROUP, CAP, D), BF),
            jax.ShapeDtypeStruct((outer, GROUP, packed, D), BF),
        ],
        [SMEM] + [ANY] * (2 * GROUP + 1 + 2 * n_hops),
        [VM] * 3,
        (idx, *xs, *gs, own, *lefts, *rights),
        scratch=[
            pltpu.VMEM((total, D), BF),
            pltpu.VMEM((total, D), BF),
            pltpu.VMEM((D, 2 * FF), BF),
            pltpu.VMEM((FF, D), BF),
            pltpu.VMEM((total, FF), BF),
            pltpu.VMEM((total, 2 * FF), BF),
            pltpu.SemaphoreType.DMA((GROUP,)),
            pltpu.SemaphoreType.DMA((GROUP,)),
            pltpu.SemaphoreType.DMA(((1 + 2 * n_hops) * GROUP,)),
            pltpu.SemaphoreType.DMA(((1 + 2 * n_hops) * GROUP,)),
        ],
        flops=18 * total * D * FF,
        moved=15 << 20,
    )


def pack_kernel(n_experts, in_rows, down_rows, idx_ref, in_ref, down_ref, *refs):
    outs, sems = refs[:-1], refs[-1]
    i = idx_ref[1]
    copies = []
    for j in range(n_experts):
        for m in range(GROUP):
            n = j * GROUP + m
            source = (i ^ m) * n_experts + j
            copies.append(
                pltpu.make_async_copy(in_ref.at[source], outs[m].at[j, pl.ds(0, in_rows)], sems.at[2 * n])
            )
            copies.append(
                pltpu.make_async_copy(
                    down_ref.at[source], outs[m].at[j, pl.ds(in_rows, down_rows)], sems.at[2 * n + 1]
                )
            )
    for c in copies:
        c.start()
    for c in copies:
        c.wait()


def pack_weights(idx, expert_in, expert_down):
    experts, in_rows, _ = expert_in.shape
    down_rows = expert_down.shape[1]
    n = experts // GROUP
    return call(
        functools.partial(pack_kernel, n, in_rows, down_rows),
        "pack_weights",
        [jax.ShapeDtypeStruct((n, in_rows + down_rows, D), BF)] * GROUP,
        [SMEM, ANY, ANY],
        [VM] * GROUP,
        (idx, expert_in, expert_down),
        scratch=[pltpu.SemaphoreType.DMA((2 * experts,))],
        moved=6 << 20,
    )


def place():
    d, t = lax.axis_index("dp"), lax.axis_index("tensor")
    return d, t, d // GROUP, d % GROUP


def flip(v, m):
    first, second = v % 2, (v // 2) % 2
    if m & 1:
        v = v + 1 - 2 * first
    if m & 2:
        v = v + 2 - 4 * second
    return v


def greet(outer, distances, tensor):
    d, t, o, _ = place()
    barrier = pltpu.get_barrier_semaphore()
    count = 0
    for m in distances:
        pl.semaphore_signal(barrier, inc=1, device_id=(flip(d, m), t), device_id_type=MESH)
        count += 1
    if tensor:
        pl.semaphore_signal(barrier, inc=1, device_id=(d, 1 - t), device_id_type=MESH)
        count += 1

    @pl.when(o > 0)
    def _():
        pl.semaphore_signal(barrier, inc=1, device_id=(d - GROUP, t), device_id_type=MESH)

    @pl.when(o < outer - 1)
    def _():
        pl.semaphore_signal(barrier, inc=1, device_id=(d + GROUP, t), device_id_type=MESH)

    neighbours = (o + outer - 1) // outer + (2 * outer - 2 - o) // outer
    pl.semaphore_wait(barrier, count + neighbours)


class Hops:
    def __init__(self, outer, steps, sent, came):
        d, t, o, _ = place()
        self.moves = []
        for n, (k, from_left, from_right, to_left, to_right) in enumerate(steps):
            back = outer - 1 - o
            right = pltpu.make_async_remote_copy(
                from_left, to_left, sent.at[2 * n], came.at[2 * n], device_id=(d + GROUP, t), device_id_type=MESH
            )
            left = pltpu.make_async_remote_copy(
                from_right,
                to_right,
                sent.at[2 * n + 1],
                came.at[2 * n + 1],
                device_id=(d - GROUP, t),
                device_id_type=MESH,
            )
            self.moves.append((right, (o >= k - 1) & (back >= 1), o >= k))
            self.moves.append((left, (back >= k - 1) & (o >= 1), back >= k))

    def start(self):
        for copy, sends, _ in self.moves:
            pl.when(sends)(copy.start)

    def wait(self):
        for copy, sends, receives in self.moves:
            pl.when(sends)(copy.wait_send)
            pl.when(receives)(copy.wait_recv)


def greet_all(outer):
    d, t, o, i = place()
    barrier = pltpu.get_barrier_semaphore()
    for m in range(1, GROUP):
        pl.semaphore_signal(barrier, inc=1, device_id=(flip(d, m), t), device_id_type=MESH)
    pl.semaphore_signal(barrier, inc=1, device_id=(d, 1 - t), device_id_type=MESH)
    for k in range(1, outer):
        pl.semaphore_signal(barrier, inc=1, device_id=((o + k) % outer * GROUP + i, t), device_id_type=MESH)
    pl.semaphore_wait(barrier, GROUP - 1 + outer)


def to_x(src, dst, sent, came):
    d, t, _, _ = place()
    return pltpu.make_async_remote_copy(src, dst, sent, came, device_id=(d, 1 - t), device_id_type=MESH)


def to_dp(m, src, dst, sent, came):
    d, t, _, _ = place()
    return pltpu.make_async_remote_copy(src, dst, sent, came, device_id=(flip(d, m), t), device_id_type=MESH)


def remote_call(kernel, name, collective_id, out_shape, in_specs, out_specs, args, scratch, flops):
    return pl.pallas_call(
        kernel,
        name=name,
        out_shape=out_shape,
        in_specs=in_specs,
        out_specs=out_specs,
        scratch_shapes=list(scratch),
        compiler_params=pltpu.CompilerParams(
            vmem_limit_bytes=VMEM_LIMIT, collective_id=collective_id, has_side_effects=True
        ),
        cost_estimate=pl.CostEstimate(flops=flops, bytes_accessed=8 << 20, transcendentals=0),
    )(*args)


def collect_kernel(outer, in_rows, down_rows, shard_ref, normed_ref, gates_ref, freq_ref, in_ref, down_ref, *refs):
    w_ref, other_ref, cos_ref, sin_ref, pos_ref, gate_ref, posc_ref, gatec_ref = refs[:8]
    own_refs, packed_refs, to_left, to_right = refs[8:10], refs[10:12], refs[12], refs[13]
    packed, gates_all, before, l_w, l_in, l_down, l_own = refs[14:21]
    s_z, r_z, s_y, r_y, s_c, r_c, s_x, r_x, s_g, r_g, s_a, r_a, s_hop, r_hop = refs[21:]
    d, t, o, i = place()
    each = shard_ref.shape[0]
    width = w_ref.shape[1] // 2
    own_width = shard_ref.shape[1]
    n_local = in_ref.shape[0]
    n = n_local // GROUP
    slot_rows = gates_all.shape[2]
    half = slot_rows // 4

    def block(which, index):
        return pl.ds(pl.multiple_of((which * GROUP + index) * each, each), each)

    def lanes(h):
        return pl.ds(h * width, width)

    local = pltpu.make_async_copy(shard_ref, w_ref.at[block(o, i), pl.ds(0, own_width)], l_w)
    local.start()
    packs = []
    for j in range(n):
        for m in range(GROUP):
            source, k = flip(i, m) * n + j, j * GROUP + m
            packs.append(
                (
                    pltpu.make_async_copy(in_ref.at[source], packed.at[j, m, pl.ds(0, in_rows)], l_in.at[k]),
                    pltpu.make_async_copy(down_ref.at[source], packed.at[j, m, pl.ds(in_rows, down_rows)], l_down.at[k]),
                )
            )
    for pair in packs:
        for c in pair:
            c.start()
    greet_all(outer)

    x_moves = [
        to_x(shard_ref.at[:, pl.ds(width, own_width - width)], w_ref.at[block(o, i), pl.ds(own_width, 2 * width - own_width)], s_x.at[0], r_x.at[0]),
        to_x(normed_ref, other_ref, s_x.at[1], r_x.at[1]),
    ]
    g_x = [
        to_x(
            gates_ref.at[:, pl.ds(p * half, half)],
            gates_all.at[0, :, pl.ds((2 * p + 1) * half, half)],
            s_g.at[p],
            r_g.at[p],
        )
        for p in range(2)
    ]
    g_y = to_dp(2, gates_all.at[0], gates_all.at[1], s_g.at[2], r_g.at[2])
    g_c = [to_dp(1, gates_all.at[s], gates_all.at[2 + s], s_g.at[3 + s], r_g.at[3 + s]) for s in range(2)]

    def z_move(k, h):
        peer = (o + k) % outer
        source = shard_ref.at[:, pl.ds(0, width)] if h == 0 else w_ref.at[block(o, i), lanes(1)]
        return pltpu.make_async_remote_copy(
            source,
            w_ref.at[block(o, i), lanes(h)],
            s_z.at[2 * k - 2 + h],
            r_z.at[2 * k - 2 + h],
            device_id=(peer * GROUP + i, t),
            device_id_type=MESH,
        )

    def near_source(b, h):
        if b == 0 and h == 0:
            return shard_ref.at[:, pl.ds(0, width)]
        return w_ref.at[block((o + outer - b) % outer, i), lanes(h)]

    def y_move(b, h):
        target = w_ref.at[block((o + outer - b) % outer, i), lanes(h)]
        return to_dp(2, near_source(b, h), target, s_y.at[2 * b + h], r_y.at[2 * b + h])

    def c_move(b, far, h):
        target = w_ref.at[block((o + outer - b) % outer, flip(i, 2) if far else i), lanes(h)]
        source = target if far else near_source(b, h)
        k = (2 * b + far) * 2 + h
        return to_dp(1, source, target, s_c.at[k], r_c.at[k])

    def weights_move(j, m):
        return to_dp(m, packed.at[j, m], own_refs[j].at[m], s_a.at[3 * j + m - 1], r_a.at[3 * j + m - 1])

    keeps = [pltpu.make_async_copy(packed.at[j, 0], own_refs[j].at[0], l_own.at[j]) for j in range(2)]
    stays = [pltpu.make_async_copy(packed.at[2 + j], packed_refs[j], l_own.at[2 + j]) for j in range(2)]
    hops = Hops(outer, [(1, own_refs[0], own_refs[0], to_left, to_right)], s_hop, r_hop)

    def packed_there(j):
        for pair in packs[j * GROUP : (j + 1) * GROUP]:
            for c in pair:
                c.wait()

    x_moves[0].start()
    for c in g_x:
        c.start()
    for k in range(1, outer):
        z_move(k, 0).start()
    y_move(0, 0).start()
    c_move(0, 0, 0).start()
    packed_there(0)
    for m in range(1, GROUP):
        weights_move(0, m).start()
    keeps[0].start()
    x_moves[1].start()
    local.wait()
    x_moves[0].wait()
    for k in range(1, outer):
        z_move(k, 1).start()
    packed_there(1)
    keeps[1].start()
    for j in range(2):
        packed_there(2 + j)
        stays[j].start()
    gates_all[0, :, 0:half] = gates_ref[:, 0:half]
    gates_all[0, :, 2 * half : 3 * half] = gates_ref[:, half:]
    block_rows = 128

    def table(b, carry):
        at = pl.ds(pl.multiple_of(b * block_rows, block_rows), block_rows)
        row = b * block_rows + lax.broadcasted_iota(jnp.int32, (block_rows, LANES), 0)
        angles = row.astype(F32) * freq_ref[...]
        lane = lax.broadcasted_iota(jnp.int32, (block_rows, LANES), 1)
        sine = jnp.sin(angles)
        cos_ref[at, :] = jnp.cos(angles)
        sin_ref[at, :] = jnp.where(lane % HD < HD // 2, -sine, sine)
        return carry

    lax.fori_loop(0, slot_rows // block_rows, table, 0)
    for c in g_x:
        c.wait()
    g_y.start()
    g_c[0].start()
    for k in range(1, outer):
        z_move(k, 0).wait_recv()
        y_move(k, 0).start()
        c_move(k, 0, 0).start()
    for m in range(1, GROUP):
        weights_move(1, m).start()
    for b in range(1):
        y_move(b, 1).start()
        c_move(b, 0, 1).start()
    before[...] = (
        lax.broadcasted_iota(jnp.int32, before.shape, 0) < lax.broadcasted_iota(jnp.int32, before.shape, 1)
    ).astype(F32).astype(BF)
    keeps[0].wait()
    for m in range(1, GROUP):
        weights_move(0, m).wait_recv()
    hops.start()
    g_y.wait()
    g_c[1].start()
    for k in range(1, outer):
        z_move(k, 1).wait_recv()
        y_move(k, 1).start()
        c_move(k, 0, 1).start()
    for b in range(outer):
        y_move(b, 0).wait_recv()
        c_move(b, 1, 0).start()
    for c in g_c:
        c.wait()
    n_all = gates_all.shape[1]
    first = t * n_local + i * n
    pick = (
        lax.broadcasted_iota(jnp.int32, (8, n_all), 1) == lax.broadcasted_iota(jnp.int32, (8, n_all), 0) + first
    ).astype(F32).astype(BF)
    for s in range(GROUP):
        gate = mm(pick, gates_all[s])
        rank = mm((gate > 0).astype(F32).astype(BF), before[...])
        gate_ref[s] = gate[:n]
        pos_ref[s] = jnp.where(gate > 0, rank, -1.0).astype(jnp.int32)[:n]
        gate = lax.dot_general(gates_all[s], pick, (((0,), (1,)), ((), ())), preferred_element_type=F32)
        rank = mm_tn(before[...], (gate > 0).astype(F32).astype(BF))
        gatec_ref[s] = gate[:, :n]
        posc_ref[s] = jnp.where(gate > 0, rank, -1.0).astype(jnp.int32)[:, :n]
    for b in range(outer):
        y_move(b, 1).wait_recv()
        c_move(b, 1, 1).start()
    for k in range(1, outer):
        for h in range(2):
            z_move(k, h).wait_send()
    for b in range(outer):
        for h in range(2):
            y_move(b, h).wait_send()
            c_move(b, 0, h).wait()
            c_move(b, 1, h).wait()
    for m in range(1, GROUP):
        weights_move(0, m).wait_send()
        weights_move(1, m).wait()
    x_moves[1].wait()
    keeps[1].wait()
    for c in stays:
        c.wait()
    hops.wait()


def collect(outer, shard, normed, gates, frequency, expert_in, expert_down):
    each, own_width = shard.shape
    width = own_width * 2 // 3
    rows = normed.shape[0]
    experts, in_rows, _ = expert_in.shape
    down_rows = expert_down.shape[1]
    n = experts // GROUP
    packed = in_rows + down_rows
    hop = jax.ShapeDtypeStruct((GROUP, packed, D), BF)
    dma = pltpu.SemaphoreType.DMA
    out = remote_call(
        functools.partial(collect_kernel, outer, in_rows, down_rows),
        "collect",
        13,
        [
            jax.ShapeDtypeStruct((D, 2 * width), BF),
            jax.ShapeDtypeStruct((rows, D), BF),
            jax.ShapeDtypeStruct((2 * rows, LANES), F32),
            jax.ShapeDtypeStruct((2 * rows, LANES), F32),
            jax.ShapeDtypeStruct((GROUP, n, 2 * rows), jnp.int32),
            jax.ShapeDtypeStruct((GROUP, n, 2 * rows), F32),
            jax.ShapeDtypeStruct((GROUP, 2 * rows, n), jnp.int32),
            jax.ShapeDtypeStruct((GROUP, 2 * rows, n), F32),
        ]
        + [hop] * 6,
        [VM] * 4 + [ANY] * 2,
        [VM] * 8 + [ANY] * 6,
        (shard, normed, gates, frequency, expert_in, expert_down),
        [
            pltpu.VMEM((n, GROUP, packed, D), BF),
            pltpu.VMEM((GROUP, gates.shape[0], 2 * rows), BF),
            pltpu.VMEM((2 * rows, 2 * rows), BF),
            dma,
            dma((experts,)),
            dma((experts,)),
            dma((4,)),
            dma((2 * outer - 2,)),
            dma((2 * outer - 2,)),
            dma((2 * outer,)),
            dma((2 * outer,)),
            dma((4 * outer,)),
            dma((4 * outer,)),
            dma((2,)),
            dma((2,)),
            dma((5,)),
            dma((5,)),
            dma((6,)),
            dma((6,)),
            dma((2,)),
            dma((2,)),
        ],
        4 << 30,
    )
    return out[:8], out[8:10], out[10:12], out[12], out[13]


def attention_kernel(outer, q_block, n_steps, len_ref, own_ref, other_ref, w_ref, cos_ref, sin_ref, x_ref, gain_ref, *refs):
    width = w_ref.shape[1] // 2
    heads = width // 2
    cot_ref, ready, packed_refs, refs = refs[0], refs[1], refs[2:4], refs[4:]
    qkv_ref, lse_ref, attn_ref, come_ref, hidden_ref, na_ref, nb_ref = refs[:7]
    refs = refs[7:]
    dy_outs, own_refs, refs = refs[:4], refs[4:6], refs[6:]
    to_left, refs = refs[:n_steps], refs[n_steps:]
    to_right, refs = refs[:n_steps], refs[n_steps:]
    send_ref, s_hop, r_hop, s_later, r_later, s_dy, r_dy, s_at, r_at, s_a, r_a, l_own = refs
    d, t, o, i = place()
    length = len_ref[0]
    rows = own_ref.shape[0]
    groups = width // (2 * LANES)
    greet(outer, (1, 2, 3), True)
    hops = Hops(outer, [(1, ready, ready, to_left[0], to_right[0])], s_hop, r_hop)
    later = Hops(outer, [(1, own_refs[k], own_refs[k], to_left[1 + k], to_right[1 + k]) for k in range(2)], s_later, r_later)
    keeps = [pltpu.make_async_copy(packed_refs[k].at[0], own_refs[k].at[0], l_own.at[k]) for k in range(2)]
    weights = [
        to_dp(m, packed_refs[k].at[m], own_refs[k].at[m], s_a.at[3 * k + m - 1], r_a.at[3 * k + m - 1])
        for k in range(2)
        for m in range(1, GROUP)
    ]
    hops.start()
    for copy in (*weights, *keeps):
        copy.start()
    ax, bx, ay, by = dy_outs
    dy_a, dy_b = (cot_ref.at[pl.ds(p * rows // 2, rows // 2)] for p in range(2))
    dys = [
        to_x(dy_a, ax, s_dy.at[0], r_dy.at[0]),
        to_dp(2, dy_b, by, s_dy.at[1], r_dy.at[1]),
        to_x(dy_b, bx, s_dy.at[2], r_dy.at[2]),
        to_dp(2, dy_a, ay, s_dy.at[3], r_dy.at[3]),
    ]

    block = 256
    key_lanes = lax.broadcasted_iota(jnp.int32, (block, LANES), 1) < HD
    for part, source in enumerate((own_ref, other_ref)):

        def project(b, carry, part=part, source=source):
            here = pl.ds(pl.multiple_of(b * block, block), block)
            at = pl.multiple_of((t if part == 0 else 1 - t) * rows + b * block, block)
            projected = mm(source[here, :], w_ref[:, :width])
            cosine, sine = cos_ref[pl.ds(at, block), :], sin_ref[pl.ds(at, block), :]
            for g in range(groups):
                q = projected[:, g * 2 * LANES : g * 2 * LANES + LANES]
                kv = projected[:, g * 2 * LANES + LANES : (g + 1) * 2 * LANES]
                q = q * cosine + swap_halves(q) * sine
                kv = jnp.where(key_lanes, kv * cosine + swap_halves(kv) * sine, kv)
                qkv_ref[pl.ds(at, block), g * 2 * LANES : g * 2 * LANES + LANES] = q.astype(BF)
                qkv_ref[pl.ds(at, block), g * 2 * LANES + LANES : (g + 1) * 2 * LANES] = kv.astype(BF)
            return carry

        lax.fori_loop(0, rows // block, project, 0)

    for copy in dys:
        copy.start()

    def exchange(g):
        lanes = pl.ds(pl.multiple_of(g * LANES, LANES), LANES)
        return to_x(send_ref.at[:, lanes], come_ref.at[:, lanes], s_at.at[g], r_at.at[g])

    def per_group(g, carry):
        q_lanes = pl.ds(pl.multiple_of(g * 2 * LANES, LANES), LANES)
        kv_lanes = pl.ds(pl.multiple_of(g * 2 * LANES + LANES, LANES), LANES)
        o_lanes = pl.ds(pl.multiple_of(g * LANES, LANES), LANES)
        keys, values = doubled(qkv_ref[:, kv_lanes])
        for b in range(2 * rows // q_block):
            start, n_keys = b * q_block, (b + 1) * q_block
            q = head_pair(qkv_ref[start : start + q_block, q_lanes])
            scores = mm_nt(keys[:n_keys], q) * (1.0 / math.sqrt(HD))
            scores = jnp.where(allowed(n_keys, q_block, start, length), scores, NEGATIVE)
            largest = jnp.max(scores, axis=0, keepdims=True)
            expon = jnp.exp(scores - largest)
            totals = jnp.sum(expon, axis=0, keepdims=True)
            probs = (expon * (1.0 / totals)).astype(BF)
            mixed = head_join(mm_tn(probs, values[:n_keys])).astype(BF)
            lse_ref[g, b : b + 1, :] = largest + jnp.log(totals)
            half, inner = start // rows, start % rows

            @pl.when(t == half)
            def _():
                attn_ref[inner : inner + q_block, o_lanes] = mixed

            @pl.when(t != half)
            def _():
                send_ref[inner : inner + q_block, o_lanes] = mixed

        exchange(g).start()

        @pl.when(g == groups // 2)
        def _():
            for copy in (*weights, *keeps):
                copy.wait()
            later.start()

        return carry

    lax.fori_loop(0, groups, per_group, 0)

    def settle(g, carry):
        exchange(g).wait()
        return carry

    for p, normed_ref in enumerate((na_ref, nb_ref)):
        at = slice(p * rows // 2, (p + 1) * rows // 2)
        hidden_ref[at] = x_ref[at].astype(F32) + mm_nt(attn_ref[at], w_ref[:, width : width + heads])
    lax.fori_loop(0, groups, settle, 0)
    for p, normed_ref in enumerate((na_ref, nb_ref)):
        at = slice(p * rows // 2, (p + 1) * rows // 2)
        hidden = hidden_ref[at] + mm_nt(come_ref[at], w_ref[:, width + heads :])
        inverse = lax.rsqrt(jnp.mean(hidden * hidden, axis=-1, keepdims=True) + EPSILON)
        hidden_ref[at] = hidden
        normed_ref[...] = (hidden * inverse * gain_ref[...]).astype(BF)
    for copy in dys:
        copy.wait()
    hops.wait()
    later.wait()


def attention(outer, q_block, length, own, other, weights_full, cosine, sine, x, gain, cotangent, ready, packed):
    rows, groups = own.shape[0], weights_full.shape[1] // (4 * LANES)
    n = 3
    piece = jax.ShapeDtypeStruct((rows // 2, D), BF)
    hop = jax.ShapeDtypeStruct(ready.shape, BF)
    out = remote_call(
        functools.partial(attention_kernel, outer, q_block, n),
        "attention",
        1,
        [
            jax.ShapeDtypeStruct((2 * rows, groups * 2 * LANES), BF),
            jax.ShapeDtypeStruct((groups, 2 * rows // q_block, 2 * q_block), F32),
            jax.ShapeDtypeStruct((rows, groups * LANES), BF),
            jax.ShapeDtypeStruct((rows, groups * LANES), BF),
            jax.ShapeDtypeStruct((rows, D), F32),
            piece,
            piece,
        ]
        + [piece] * 4
        + [hop] * (2 + 2 * n),
        [SMEM] + [VM] * 7 + [ANY] * 4,
        [VM] * 7 + [ANY] * (6 + 2 * n),
        (length, own, other, weights_full, cosine, sine, x, gain.reshape(1, D), cotangent, ready, *packed),
        [
            pltpu.VMEM((rows, groups * LANES), BF),
            pltpu.SemaphoreType.DMA((2,)),
            pltpu.SemaphoreType.DMA((2,)),
            pltpu.SemaphoreType.DMA((4,)),
            pltpu.SemaphoreType.DMA((4,)),
            pltpu.SemaphoreType.DMA((4,)),
            pltpu.SemaphoreType.DMA((4,)),
            pltpu.SemaphoreType.DMA((groups,)),
            pltpu.SemaphoreType.DMA((groups,)),
            pltpu.SemaphoreType.DMA((6,)),
            pltpu.SemaphoreType.DMA((6,)),
            pltpu.SemaphoreType.DMA((2,)),
        ],
        30 << 30,
    )
    return out[:7], out[7:11], out[11:13], out[13 : 13 + n], out[13 + n :]


def one_hot_rows(pos, gate, j, n_rows):
    rank = lax.broadcasted_iota(jnp.int32, (CAP, n_rows), 0)
    chosen = rank == pos[j : j + 1, :]
    return jnp.where(chosen, 1.0 if gate is None else gate[j : j + 1, :], 0.0).astype(BF)


def spread_kernel(outer, steps, pos_ref, gate_ref, na_ref, nb_ref, *refs):
    n_steps = len(steps)
    cot_ref, dy_refs, refs = refs[0], refs[1:5], refs[5:]
    from_left, refs = refs[:n_steps], refs[n_steps:]
    from_right, refs = refs[:n_steps], refs[n_steps:]
    n_ref, dyx_ref, og_out = refs[:3]
    refs = refs[3:]
    to_left, refs = refs[:n_steps], refs[n_steps:]
    to_right, refs = refs[:n_steps], refs[n_steps:]
    held, s_hop, r_hop, s_n, r_n, s_d, r_d, l_sem, og_ref, o_sem = refs
    height = na_ref.shape[0]
    n_experts = og_ref.shape[1]
    leave = [pltpu.make_async_copy(og_ref.at[s % 2], og_out.at[s], o_sem.at[s]) for s in range(GROUP)]
    greet(outer, (1, 2), True)
    n_ax = to_x(na_ref, n_ref.at[0, 1], s_n.at[0], r_n.at[0])
    n_by = to_dp(2, nb_ref, n_ref.at[1, 2], s_n.at[1], r_n.at[1])
    n_bx = to_x(nb_ref, n_ref.at[0, 3], s_n.at[2], r_n.at[2])
    n_ay = to_dp(2, na_ref, n_ref.at[1, 0], s_n.at[3], r_n.at[3])
    n_axy = to_dp(2, n_ref.at[0, 1], n_ref.at[1, 1], s_n.at[4], r_n.at[4])
    n_bxy = to_x(n_ref.at[1, 2], n_ref.at[1, 3], s_n.at[5], r_n.at[5])
    core = {}
    for n, (s, p) in enumerate([(s, p) for s in range(2) for p in range(4)]):
        source = na_ref if (s, p) == (0, 0) else nb_ref if (s, p) == (0, 2) else n_ref.at[s, p]
        core[s, p] = to_dp(1, source, n_ref.at[2 + s, p], s_n.at[6 + n], r_n.at[6 + n])
    for copy in (n_ax, n_by, n_bx, n_ay):
        copy.start()
    d_a, d_b = (cot_ref.at[pl.ds(p * height, height)] for p in range(2))
    d_ax, d_bx, d_ay, d_by = dy_refs
    d_axy = to_dp(2, d_ax, dyx_ref.at[0, 1], s_d.at[0], r_d.at[0])
    d_bxy = to_x(d_by, dyx_ref.at[0, 3], s_d.at[1], r_d.at[1])
    d_axy.start()
    d_bxy.start()
    d_near = [[d_a, d_ax, d_b, d_bx], [d_ay, dyx_ref.at[0, 1], d_by, dyx_ref.at[0, 3]]]
    d_core = {}
    for n, (s, p) in enumerate([(s, p) for s in range(2) for p in range(4)]):
        d_core[s, p] = to_dp(1, d_near[s][p], dyx_ref.at[1 + s, p], s_d.at[2 + n], r_d.at[2 + n])
    for key in ((0, 0), (0, 1), (0, 2), (0, 3), (1, 0), (1, 2)):
        d_core[key].start()
    core[0, 0].start()
    core[0, 2].start()
    hops = Hops(
        outer,
        [(k, a, b, l, r) for k, a, b, l, r in zip(steps, from_left, from_right, to_left, to_right, strict=True)],
        s_hop,
        r_hop,
    )
    hops.start()

    def load(s):
        pieces = d_near[s] if s < 2 else [dyx_ref.at[s - 1, p] for p in range(4)]
        return [
            pltpu.make_async_copy(piece, held.at[pl.ds(p * height, height)], l_sem.at[p])
            for p, piece in enumerate(pieces)
        ]

    def give(s):
        copies = load(s)
        for c in copies:
            c.start()
        for c in copies:
            c.wait()
        if s >= 2:
            leave[s - 2].wait()

        def one(j, carry):
            rank = lax.broadcasted_iota(jnp.int32, (CAP, 4 * height), 0)
            chosen = rank == pos_ref[s, pl.ds(j, 1), :]
            one_hot = jnp.where(chosen, gate_ref[s, pl.ds(j, 1), :], 0.0).astype(BF)
            og_ref[s % 2, j] = mm(one_hot, held[...]).astype(BF)
            return carry

        lax.fori_loop(0, n_experts, one, 0)
        leave[s].start()

    give(0)
    n_ax.wait()
    n_by.wait()
    n_axy.start()
    n_bxy.start()
    core[0, 1].start()
    core[1, 2].start()
    d_axy.wait()
    d_bxy.wait()
    d_core[1, 1].start()
    d_core[1, 3].start()
    give(1)
    n_bx.wait()
    n_ay.wait()
    core[0, 3].start()
    core[1, 0].start()
    for p in range(4):
        d_core[0, p].wait()
    give(2)
    n_axy.wait()
    n_bxy.wait()
    core[1, 1].start()
    core[1, 3].start()
    for p in range(4):
        d_core[1, p].wait()
    give(3)
    for key in core:
        core[key].wait()
    for s in range(2, GROUP):
        leave[s].wait()
    hops.wait()


def spread(outer, pos, gate, normed, dys, steps, from_left, from_right):
    height = normed[0].shape[0]
    n, n_experts = len(steps), pos.shape[1]
    weights = [jax.ShapeDtypeStruct(s.shape, BF) for s in from_left]
    out = remote_call(
        functools.partial(spread_kernel, outer, steps),
        "spread",
        2,
        [
            jax.ShapeDtypeStruct((GROUP, 4, height, D), BF),
            jax.ShapeDtypeStruct((3, 4, height, D), BF),
            jax.ShapeDtypeStruct((GROUP, n_experts, CAP, D), BF),
        ]
        + weights * 2,
        [VM] * 2 + [ANY] * (2 + 5 + 2 * n),
        [ANY] * (3 + 2 * n),
        (pos, gate, *normed, *dys, *from_left, *from_right),
        [
            pltpu.VMEM((4 * height, D), BF),
            pltpu.SemaphoreType.DMA((2 * n,)),
            pltpu.SemaphoreType.DMA((2 * n,)),
            pltpu.SemaphoreType.DMA((14,)),
            pltpu.SemaphoreType.DMA((14,)),
            pltpu.SemaphoreType.DMA((10,)),
            pltpu.SemaphoreType.DMA((10,)),
            pltpu.SemaphoreType.DMA((4,)),
            pltpu.VMEM((2, n_experts, CAP, D), BF),
            pltpu.SemaphoreType.DMA((GROUP,)),
        ],
        12 << 30,
    )
    return out[0], out[2], out[3 : 3 + n], out[3 + n :]


def hand_out_kernel(outer, steps, pos_ref, na_ref, nb_ref, n_ref, *refs):
    n_steps = len(steps)
    from_left, refs = refs[:n_steps], refs[n_steps:]
    from_right, refs = refs[:n_steps], refs[n_steps:]
    x_out, refs = refs[0], refs[1:]
    to_left, refs = refs[:n_steps], refs[n_steps:]
    to_right, refs = refs[:n_steps], refs[n_steps:]
    held, s_hop, r_hop, l_sem, x_ref, o_sem = refs
    leave = [pltpu.make_async_copy(x_ref.at[s % 2], x_out.at[s], o_sem.at[s]) for s in range(GROUP)]
    height = na_ref.shape[0]
    n_experts = x_ref.shape[1]
    greet(outer, (), False)
    hops = Hops(
        outer,
        [(k, a, b, l, r) for k, a, b, l, r in zip(steps, from_left, from_right, to_left, to_right, strict=True)],
        s_hop,
        r_hop,
    )
    hops.start()

    def load(s):
        pieces = [na_ref, n_ref.at[0, 1], nb_ref, n_ref.at[0, 3]] if s == 0 else [n_ref.at[s, p] for p in range(4)]
        return [
            pltpu.make_async_copy(piece, held.at[s % 2, pl.ds(p * height, height)], l_sem.at[s % 2, p])
            for p, piece in enumerate(pieces)
        ]

    for c in load(0):
        c.start()
    for s in range(GROUP):
        if s + 1 < GROUP:
            for c in load(s + 1):
                c.start()
        for c in load(s):
            c.wait()
        if s >= 2:
            leave[s - 2].wait()

        def one(j, carry, s=s):
            rank = lax.broadcasted_iota(jnp.int32, (CAP, 4 * height), 0)
            one_hot = jnp.where(rank == pos_ref[s, pl.ds(j, 1), :], 1.0, 0.0).astype(BF)
            x_ref[s % 2, j] = mm(one_hot, held[s % 2]).astype(BF)
            return carry

        lax.fori_loop(0, n_experts, one, 0)
        leave[s].start()
    for s in range(2, GROUP):
        leave[s].wait()
    hops.wait()


def hand_out(outer, pos, normed, gathered, steps, from_left, from_right):
    height = normed[0].shape[0]
    n, n_experts = len(steps), pos.shape[1]
    weights = [jax.ShapeDtypeStruct(s.shape, BF) for s in from_left]
    out = remote_call(
        functools.partial(hand_out_kernel, outer, steps),
        "hand_out",
        3,
        [jax.ShapeDtypeStruct((GROUP, n_experts, CAP, D), BF)] + weights * 2,
        [VM] + [ANY] * (3 + 2 * n),
        [ANY] * (1 + 2 * n),
        (pos, *normed, gathered, *from_left, *from_right),
        [
            pltpu.VMEM((2, 4 * height, D), BF),
            pltpu.SemaphoreType.DMA((2 * n,)),
            pltpu.SemaphoreType.DMA((2 * n,)),
            pltpu.SemaphoreType.DMA((2, 4)),
            pltpu.VMEM((2, n_experts, CAP, D), BF),
            pltpu.SemaphoreType.DMA((GROUP,)),
        ],
        12 << 30,
    )
    return out[0], out[1 : 1 + n], out[1 + n :]


def expert_step_kernel(j, outer, in_rows, down_rows, steps, sum_steps, x_ref, g_ref, own, *refs):
    n_hops, n_steps, n_sums = outer - 1, len(steps), len(sum_steps)
    lefts, refs = refs[:n_hops], refs[n_hops:]
    rights, refs = refs[:n_hops], refs[n_hops:]
    from_left, refs = refs[:n_steps], refs[n_steps:]
    from_right, refs = refs[:n_steps], refs[n_steps:]
    dws, refs = refs[:n_sums], refs[n_sums:]
    was_l, refs = refs[:n_sums], refs[n_sums:]
    was_r, refs = refs[:n_sums], refs[n_sums:]
    y_out, dx_out, dw_out = refs[:3]
    refs = refs[3:]
    to_left, refs = refs[:n_steps], refs[n_steps:]
    to_right, refs = refs[:n_steps], refs[n_steps:]
    sum_left, refs = refs[:n_sums], refs[n_sums:]
    sum_right, refs = refs[:n_sums], refs[n_sums:]
    x_all, g_all, w_in, w_down, act_all, gug_all, sem_x, sem_g, sem_w, sem_d, s_hop, r_hop = refs[:12]
    (y_ref, dx_ref, dw_ref, o_sem), refs = refs[12:16], refs[16:]
    _, _, o, i = place()
    greet(outer, (), False)
    sums = Sums(outer, sum_steps, dws, was_l, was_r, sum_left, sum_right, *refs)
    if n_steps:
        hops = Hops(
            outer,
            [(k, a, b, l, r) for k, a, b, l, r in zip(steps, from_left, from_right, to_left, to_right, strict=True)],
            s_hop,
            r_hop,
        )
        hops.start()

    def rows_of(source, held, sems):
        return [
            pltpu.make_async_copy(source.at[n, j], held.at[pl.ds(n * CAP, CAP)], sems.at[n]) for n in range(GROUP)
        ]

    def weight_copies(source, at, slot):
        made = []
        for m in range(GROUP):
            where = at * GROUP + flip(i, m)
            made.append(
                pltpu.make_async_copy(
                    source.at[m, pl.ds(0, in_rows)],
                    w_in.at[pl.ds(pl.multiple_of(where * in_rows, in_rows), in_rows)],
                    sem_w.at[slot * GROUP + m],
                )
            )
            made.append(
                pltpu.make_async_copy(
                    source.at[m, pl.ds(in_rows, down_rows)],
                    w_down.at[pl.ds(pl.multiple_of(where * down_rows, down_rows), down_rows)],
                    sem_d.at[slot * GROUP + m],
                )
            )
        return made

    def each_weight(act):
        act(weight_copies(own, o, 0))
        for k in range(1, outer):

            @pl.when(o >= k)
            def _():
                act(weight_copies(lefts[k - 1], o - k, k))

            @pl.when(o + k < outer)
            def _():
                act(weight_copies(rights[k - 1], o + k, n_hops + k))

    def start(made):
        for c in made:
            c.start()

    def wait(made):
        for c in made:
            c.wait()

    sums.load()
    each_weight(start)
    copy_x, copy_g = rows_of(x_ref, x_all, sem_x), rows_of(g_ref, g_all, sem_g)
    start(copy_x)
    start(copy_g)
    sums.send()
    each_weight(wait)
    wait(copy_x)
    wait(copy_g)

    def per_slot(s, carry):
        at = pl.ds(pl.multiple_of(s * CAP, CAP), CAP)
        gate_up = mm(x_all[at, :], w_in[...])
        g, u = gate_up[:, :FF], gate_up[:, FF:]
        sigma = 1.0 / (1.0 + jnp.exp(-g))
        silu = g * sigma
        act = (silu * u).astype(BF)
        act_all[at, :] = act
        y_ref[s] = mm(act, w_down[...]).astype(BF)
        act_grad = mm_nt(g_all[at, :], w_down[...])
        gug_all[at, :FF] = (act_grad * u * sigma * (1.0 + g * (1.0 - sigma))).astype(BF)
        gug_all[at, FF:] = (act_grad * silu).astype(BF)
        dx_ref[s] = mm_nt(gug_all[at, :], w_in[...]).astype(BF)
        for copy in leaving(s):
            copy.start()
        return carry

    def leaving(s):
        return (
            pltpu.make_async_copy(y_ref.at[s], y_out.at[s], o_sem.at[0, s]),
            pltpu.make_async_copy(dx_ref.at[s], dx_out.at[s], o_sem.at[1, s]),
        )

    def gradient(c):
        return pltpu.make_async_copy(dw_ref.at[c], dw_out.at[c], o_sem.at[2, c])

    lax.fori_loop(0, GROUP, per_slot, 0)
    in_block, down_block = GROUP * in_rows, GROUP * down_rows

    def per_owner(c, carry):
        lanes = pl.ds(pl.multiple_of(c * in_block, in_block), in_block)
        part = mm_tn(x_all[:, lanes], gug_all[...]).astype(BF)
        for r in range(GROUP):
            dw_ref[c, flip(i, r), :in_rows, :] = part[r * in_rows : (r + 1) * in_rows]
        lanes = pl.ds(pl.multiple_of(c * down_block, down_block), down_block)
        part = mm_tn(act_all[:, lanes], g_all[...]).astype(BF)
        for r in range(GROUP):
            dw_ref[c, flip(i, r), in_rows:, :] = part[r * down_rows : (r + 1) * down_rows]
        gradient(c).start()
        return carry

    lax.fori_loop(0, outer, per_owner, 0)
    for s in range(GROUP):
        for copy in leaving(s):
            copy.wait()
    for c in range(outer):
        gradient(c).wait()
    if n_steps:
        hops.wait()
    sums.wait()


def expert_step(j, outer, in_rows, down_rows, x, g, own, lefts, rights, hop_plan, sum_plan):
    (steps, from_left, from_right), (sum_steps, dws, was_l, was_r) = hop_plan, sum_plan
    n_hops, n, n_sums = outer - 1, len(steps), len(sum_steps)
    total = GROUP * CAP
    packed = in_rows + down_rows
    weights = [jax.ShapeDtypeStruct(s.shape, BF) for s in from_left]
    shapes = [
        jax.ShapeDtypeStruct((GROUP, CAP, D), BF),
        jax.ShapeDtypeStruct((GROUP, CAP, D), BF),
        jax.ShapeDtypeStruct((outer, GROUP, packed, D), BF),
    ] + weights * 2 + [jax.ShapeDtypeStruct((GROUP, packed, D), BF)] * (2 * n_sums)
    out = remote_call(
        functools.partial(expert_step_kernel, j, outer, in_rows, down_rows, steps, sum_steps),
        "expert_step",
        4 + j,
        shapes,
        [ANY] * (3 + 2 * n_hops + 2 * n + 3 * n_sums),
        [ANY] * (3 + 2 * n + 2 * n_sums),
        (x, g, own, *lefts, *rights, *from_left, *from_right, *dws, *was_l, *was_r),
        [
            pltpu.VMEM((total, D), BF),
            pltpu.VMEM((total, D), BF),
            pltpu.VMEM((D, 2 * FF), BF),
            pltpu.VMEM((FF, D), BF),
            pltpu.VMEM((total, FF), BF),
            pltpu.VMEM((total, 2 * FF), BF),
            pltpu.SemaphoreType.DMA((GROUP,)),
            pltpu.SemaphoreType.DMA((GROUP,)),
            pltpu.SemaphoreType.DMA(((1 + 2 * n_hops) * GROUP,)),
            pltpu.SemaphoreType.DMA(((1 + 2 * n_hops) * GROUP,)),
            pltpu.SemaphoreType.DMA((max(1, 2 * n),)),
            pltpu.SemaphoreType.DMA((max(1, 2 * n),)),
            pltpu.VMEM((GROUP, CAP, D), BF),
            pltpu.VMEM((GROUP, CAP, D), BF),
            pltpu.VMEM((outer, GROUP, packed, D), BF),
            pltpu.SemaphoreType.DMA((3, max(GROUP, outer))),
            *sums_scratch(n_sums, packed),
        ],
        18 * total * D * FF,
    )
    out, rest = out[:3], out[3:]
    return out, rest[:n], rest[n : 2 * n], rest[2 * n : 2 * n + n_sums], rest[2 * n + n_sums :]


class Sums:
    def __init__(self, outer, steps, dws, was_left, was_right, to_left, to_right, message, term, loaded, added, sent, came):
        d, t, o, _ = place()
        back = outer - 1 - o
        self.moves = []
        for n, s in enumerate(steps):
            for side, near, target, was, to, peer in (
                (0, o, outer - s + o, was_left, to_left, d + GROUP),
                (1, back, s - 1 - back, was_right, to_right, d - GROUP),
            ):
                k = 2 * n + side
                own = pltpu.make_async_copy(dws[n].at[target], message.at[k], loaded.at[k])
                before = None if s == 1 else pltpu.make_async_copy(was[n], term.at[side], added.at[k])
                move = pltpu.make_async_remote_copy(
                    message.at[k], to[n], sent.at[k], came.at[k], device_id=(peer, t), device_id_type=MESH
                )
                sends, adds = near <= s - 1, (near <= s - 1) & (near >= 1)
                receives = (near >= 1) & (near <= s)
                self.moves.append((own, before, move, sends, adds, receives, message.at[k], term.at[side]))

    def load(self):
        for own, _, _, sends, *_ in self.moves:
            pl.when(sends)(own.start)

    def send(self):
        for n in range(0, len(self.moves), 2):
            pair = self.moves[n : n + 2]
            for _, before, _, _, adds, *_ in pair:
                if before is not None:
                    pl.when(adds)(before.start)
            for own, before, move, sends, adds, _, message, term in pair:
                pl.when(sends)(own.wait)
                if before is not None:

                    @pl.when(adds)
                    def _(before=before, message=message, term=term):
                        before.wait()

                        def one(m, carry):
                            message[m] = (message[m].astype(F32) + term[m].astype(F32)).astype(BF)
                            return carry

                        lax.fori_loop(0, GROUP, one, 0)

                pl.when(sends)(move.start)

    def wait(self):
        for _, _, move, sends, _, receives, *_ in self.moves:
            pl.when(sends)(move.wait_send)
            pl.when(receives)(move.wait_recv)


def sums_scratch(n, packed):
    n = max(1, n)
    return [
        pltpu.VMEM((2 * n, GROUP, packed, D), BF),
        pltpu.VMEM((2, GROUP, packed, D), BF),
        pltpu.SemaphoreType.DMA((2 * n,)),
        pltpu.SemaphoreType.DMA((2 * n,)),
        pltpu.SemaphoreType.DMA((2 * n,)),
        pltpu.SemaphoreType.DMA((2 * n,)),
    ]


def again(scratch):
    return [pltpu.SemaphoreType.DMA(s.shape) for s in scratch[2:]]


class Final:
    def __init__(self, outer, dw, left, right, mine, term, target, loaded, sent, came, kept):
        _, _, o, _ = place()
        self.from_left, self.from_right = o >= 1, o < outer - 1
        self.mine, self.term = mine, term
        self.own = pltpu.make_async_copy(dw.at[o], mine, loaded.at[0])
        self.left = pltpu.make_async_copy(left, term.at[0], loaded.at[1])
        self.right = pltpu.make_async_copy(right, term.at[1], loaded.at[2])
        self.moves = [to_dp(m, mine.at[m], target.at[m], sent.at[m - 1], came.at[m - 1]) for m in range(1, GROUP)]
        self.keep = pltpu.make_async_copy(mine.at[0], target.at[0], kept)

    def send(self):
        self.own.start()
        pl.when(self.from_left)(self.left.start)
        pl.when(self.from_right)(self.right.start)
        self.own.wait()

        def add(k):
            def one(m, carry):
                self.mine[m] = (self.mine[m].astype(F32) + self.term[k, m].astype(F32)).astype(BF)
                return carry

            lax.fori_loop(0, GROUP, one, 0)

        @pl.when(self.from_left)
        def _():
            self.left.wait()
            add(0)

        @pl.when(self.from_right)
        def _():
            self.right.wait()
            add(1)

        for move in self.moves:
            move.start()
        self.keep.start()

    def wait(self):
        for move in self.moves:
            move.wait()
        self.keep.wait()


def final_scratch(packed):
    return [
        pltpu.VMEM((GROUP, packed, D), BF),
        pltpu.SemaphoreType.DMA((3,)),
        pltpu.SemaphoreType.DMA((GROUP - 1,)),
        pltpu.SemaphoreType.DMA((GROUP - 1,)),
        pltpu.SemaphoreType.DMA,
    ]


class Mixer:
    def __init__(self, sources, pos_ref, gate_ref, held, sems):
        self.sources, self.pos, self.gate, self.held, self.sems = sources, pos_ref, gate_ref, held, sems

    def copies(self, slot, buffer):
        return [
            pltpu.make_async_copy(
                source.at[slot], self.held.at[buffer, pl.ds(j * CAP, CAP)], self.sems.at[buffer * len(self.sources) + j]
            )
            for j, source in enumerate(self.sources)
        ]

    def load(self, slot, buffer):
        for c in self.copies(slot, buffer):
            c.start()

    def mix(self, slot, buffer, out, add=None):
        for c in self.copies(slot, buffer):
            c.wait()
        n_experts = len(self.sources)
        width = n_experts * CAP
        block = 256

        def one(b, carry):
            at = pl.ds(pl.multiple_of(b * block, block), block)
            targets = []
            for j in range(n_experts):
                target = self.pos[slot, at, j : j + 1]
                targets.append(jnp.where(target >= 0, target + j * CAP, -1))
            tiles = []
            for first in range(0, width, LANES):
                size = min(LANES, width - first)
                lane = first + lax.broadcasted_iota(jnp.int32, (block, size), 1)
                tile = jnp.zeros((block, size), F32)
                for j in range(first // CAP, (first + size - 1) // CAP + 1):
                    value = 1.0 if self.gate is None else self.gate[slot, at, j : j + 1]
                    tile = jnp.where(lane == targets[j], value, tile)
                tiles.append(tile.astype(BF))
            total = mm(jnp.concatenate(tiles, axis=1), self.held[buffer])
            if add is not None:
                total = total + add[at, :].astype(F32)
            out[at, :] = total.astype(BF)
            return carry

        lax.fori_loop(0, out.shape[0] // block, one, 0)


class GroupSum:
    def __init__(self, near, q, middle, mine, come_ab, last_ab, sent, came):
        self.middle, self.mine, self.come_ab, self.last_ab, self.q = middle, mine, come_ab, last_ab, q
        self.a = [
            to_dp(2, near.at[1, pl.ds(s * q, q)], come_ab.at[0, pl.ds(s * q, q)], sent.at[s], came.at[s]) for s in range(2)
        ]
        self.b = [
            to_x(near.at[s, pl.ds(3 * q, q)], come_ab.at[1, pl.ds(s * q, q)], sent.at[2 + s], came.at[2 + s])
            for s in range(2)
        ]
        self.last = [
            to_x(middle[0], last_ab.at[0], sent.at[4], came.at[4]),
            to_dp(2, middle[1], last_ab.at[1], sent.at[5], came.at[5]),
        ]

    def second(self):
        q = self.q
        for p, first in enumerate((self.a[1], self.b[1])):
            first.wait_recv()
            self.middle[p][...] = (
                self.middle[p][...].astype(F32) + self.come_ab[p, q : 2 * q].astype(F32)
            ).astype(BF)
            self.last[p].start()

    def terms(self, p):
        (self.a, self.b)[p][0].wait_recv()
        self.last[p].wait_recv()
        return (
            self.mine[p][...].astype(F32) + self.come_ab[p, : self.q].astype(F32) + self.last_ab[p].astype(F32)
        )

    def sent(self):
        for copy in (*self.a, *self.b, *self.last):
            copy.wait_send()


def group_scratch(rows):
    return [
        pltpu.VMEM((2, rows // 2, D), BF),
        pltpu.VMEM((2, rows // 4, D), BF),
        pltpu.SemaphoreType.DMA((6,)),
        pltpu.SemaphoreType.DMA((6,)),
    ]


def rows_back_kernel(outer, first, then, pos_ref, gate_ref, valid_ref, hidden_ref, cot_ref, gain_ref, w_any, *refs):
    n_experts, n1, n2 = pos_ref.shape[2], len(first), len(then)
    sources, refs = refs[:n_experts], refs[n_experts:]
    ys, refs = refs[:n_experts], refs[n_experts:]
    dws, refs = refs[: n1 + 1], refs[n1 + 1 :]
    was_l, refs = refs[:n1], refs[n1:]
    was_r, refs = refs[:n1], refs[n1:]
    f_dw, f_left, f_right, refs = *refs[:3], refs[3:]
    grad_ref, low_ref, gain_grad_ref, own_ref, come_ref, mixed, fin_ref = refs[:7]
    refs = refs[7:]
    to_l, refs = refs[: n1 + n2], refs[n1 + n2 :]
    to_r, refs = refs[: n1 + n2], refs[n1 + n2 :]
    (held, far, come, mixed_come, near, l_sem, s_core, r_core), refs = refs[:8], refs[8:]
    (come_ab, last_ab, s_sem, r_sem), refs = refs[:4], refs[4:]
    sums_a, refs = refs[:6], refs[6:]
    sums_b, refs = (*sums_a[:2], *refs[:4]), refs[4:]
    send_ref, s_at, r_at, w_ref, w_sem = refs[:5]
    final_refs = refs[5:]
    heads = w_ref.shape[1] // 2
    w_copy = pltpu.make_async_copy(w_any.at[:, pl.ds(2 * heads, 2 * heads)], w_ref, w_sem)
    w_copy.start()
    mixer = Mixer(sources, pos_ref, None, held, l_sem)
    mixer.load(3, 0)
    mixer.load(2, 1)
    greet(outer, (1, 2, 3), True)
    one = Sums(outer, first, dws[:n1], was_l, was_r, to_l[:n1], to_r[:n1], *sums_a)
    final = Final(outer, f_dw, f_left, f_right, final_refs[0], sums_a[1], fin_ref, *final_refs[1:])
    two = Sums(
        outer,
        [s for s, _ in then],
        [dws[k] for _, k in then],
        [None if s == 1 else to_l[k] for s, k in then],
        [None if s == 1 else to_r[k] for s, k in then],
        to_l[n1:],
        to_r[n1:],
        *sums_b,
    )
    q = near.shape[1] // 4
    group = GroupSum(
        near,
        q,
        [near.at[0, pl.ds(q, q)], near.at[1, pl.ds(2 * q, q)]],
        [near.at[0, pl.ds(0, q)], near.at[0, pl.ds(2 * q, q)]],
        come_ab,
        last_ab,
        s_sem,
        r_sem,
    )
    def core(s):
        return to_dp(1, far.at[s], come.at[s], s_core.at[s], r_core.at[s])

    def mixed_core(s):
        return to_dp(1, far.at[s], mixed_come.at[s], s_core.at[2 + s], r_core.at[2 + s])

    outputs = Mixer(ys, pos_ref, gate_ref, held, l_sem)
    rows = hidden_ref.shape[0] // 2
    aways = [
        to_x(
            send_ref.at[pl.ds(p * rows, rows)], come_ref.at[pl.ds(p * rows, rows)], s_at.at[p], r_at.at[p]
        )
        for p in range(2)
    ]

    def phase(mixer, base, target, add, ahead, behind):
        def body(k, carry):
            s = 1 - k
            ahead(s, k)
            mixer.mix(base + s, k, target.at[s], None if add is None else add.at[s])
            behind(s, k)
            return carry

        lax.fori_loop(0, 2, body, 0)

    def far_behind(s, k):
        core(s).start()
        mixer.load(s, k)

    def near_behind(s, k):
        @pl.when(s == 1)
        def _():
            group.a[1].start()
            group.b[1].start()
            group.a[0].start()

        pl.when(s == 0)(group.b[0].start)
        outputs.load(2 + s, k)

    def mixed_ahead(s, k):
        core(s).wait_send()
        pl.when(k == 1)(group.second)

    def mixed_behind(s, k):
        mixed_core(s).start()
        outputs.load(s, k)

    def back():
        gain = gain_ref[...]
        gain_grad = jnp.zeros((1, D), F32)
        for p in range(2):
            at = slice(p * rows, (p + 1) * rows)
            hidden = hidden_ref[at]
            normed_grad = group.terms(p)
            inverse = lax.rsqrt(jnp.mean(hidden * hidden, axis=-1, keepdims=True) + EPSILON)
            gain_grad = gain_grad + jnp.sum(normed_grad * (hidden * inverse), axis=0, keepdims=True)
            scaled = normed_grad * gain
            back = inverse * scaled - hidden * (
                inverse * inverse * inverse * jnp.mean(scaled * hidden, axis=-1, keepdims=True)
            )
            dy = jnp.where(valid_ref[at] > 0, cot_ref[at].astype(F32), 0.0)
            total = dy + back
            grad_ref[at] = total
            low = total.astype(BF)
            low_ref[at] = low
            send_ref[at] = mm(low, w_ref[:, heads:]).astype(BF)
            aways[p].start()
        gain_grad_ref[...] = gain_grad

    def last_ahead(s, k):
        mixed_core(s).wait_recv()
        pl.when(k == 1)(back)

    one.load()
    one.send()
    final.send()
    phase(mixer, 2, far, None, lambda s, k: None, far_behind)
    phase(mixer, 0, near, come, lambda s, k: core(s).wait_recv(), near_behind)
    phase(outputs, 2, far, None, mixed_ahead, mixed_behind)
    one.wait()
    two.load()
    two.send()
    w_copy.wait()
    phase(outputs, 0, mixed, mixed_come, last_ahead, lambda s, k: None)
    own_ref[...] = mm(low_ref[...], w_ref[:, :heads]).astype(BF)
    group.sent()
    for s in range(2):
        mixed_core(s).wait_send()
    for away in aways:
        away.wait()
    final.wait()
    two.wait()


def rows_back(
    outer, pos, gate, valid, hidden, cotangent, gain, weights_full, sources, ys, first, then, dws, was_l, was_r, final
):
    rows, heads = hidden.shape[0], weights_full.shape[1] // 4
    n, n_experts = len(first) + len(then), len(sources)
    packed = dws[0].shape[2]
    hop = [jax.ShapeDtypeStruct((GROUP, packed, D), BF)] * (2 * n)
    half = jax.ShapeDtypeStruct((rows, heads), BF)
    most = max(len(first), len(then))
    slots = pltpu.VMEM((2, 2 * rows, D), BF)
    out = remote_call(
        functools.partial(rows_back_kernel, outer, first, then),
        "rows_back",
        10,
        [
            jax.ShapeDtypeStruct((rows, D), F32),
            jax.ShapeDtypeStruct((rows, D), BF),
            jax.ShapeDtypeStruct((1, D), F32),
            half,
            half,
            jax.ShapeDtypeStruct((2, 2 * rows, D), BF),
        ]
        + hop[:1]
        + hop,
        [VM] * 6 + [ANY] * (4 + 2 * n_experts + len(dws) + 2 * len(first)),
        [VM] * 6 + [ANY] * (1 + 2 * n),
        (pos, gate, valid, hidden, cotangent, gain.reshape(1, D), weights_full, *sources, *ys, *dws, *was_l, *was_r, *final),
        [
            pltpu.VMEM((2, n_experts * CAP, D), BF),
            slots,
            slots,
            slots,
            slots,
            pltpu.SemaphoreType.DMA((2 * n_experts,)),
            pltpu.SemaphoreType.DMA((4,)),
            pltpu.SemaphoreType.DMA((4,)),
            *group_scratch(2 * rows),
            *sums_scratch(most, packed),
            *again(sums_scratch(most, packed)),
            pltpu.VMEM((rows, heads), BF),
            pltpu.SemaphoreType.DMA((2,)),
            pltpu.SemaphoreType.DMA((2,)),
            pltpu.VMEM((D, 2 * heads), BF),
            pltpu.SemaphoreType.DMA,
            *final_scratch(packed),
        ],
        30 << 30,
    )
    return out[:6], out[6], out[7 : 7 + n], out[7 + n :]


def attention_back_kernel(
    outer, q_block, steps, len_ref, qkv_ref, lse_ref, cos_ref, sin_ref, own_ref, other_ref, hidden_ref, valid_ref, *refs
):
    n = len(steps)
    mixed, refs = refs[0], refs[1:]
    dws, refs = refs[:n], refs[n:]
    was_l, refs = refs[:n], refs[n:]
    was_r, refs = refs[:n], refs[n:]
    outs, out_ref, refs = refs[:2], refs[2], refs[3:]
    to_l, refs = refs[:n], refs[n:]
    to_r, refs = refs[:n], refs[n:]
    do_ref, dq_ref, dk_ref, dv_ref = refs[:4]
    sums_refs, refs = refs[4:10], refs[10:]
    middle, mine, l_sem, come_ab, last_ab, s_sem, r_sem = refs
    _, t, _, _ = place()
    q = middle.shape[1]
    loads = [
        pltpu.make_async_copy(mixed.at[0, pl.ds(q, q)], middle.at[0], l_sem.at[0]),
        pltpu.make_async_copy(mixed.at[1, pl.ds(2 * q, q)], middle.at[1], l_sem.at[1]),
        pltpu.make_async_copy(mixed.at[0, pl.ds(0, q)], mine.at[0], l_sem.at[2]),
        pltpu.make_async_copy(mixed.at[0, pl.ds(2 * q, q)], mine.at[1], l_sem.at[3]),
    ]
    for c in loads:
        c.start()
    greet(outer, (2,), True)
    group = GroupSum(
        mixed, q, [middle.at[0], middle.at[1]], [mine.at[0], mine.at[1]], come_ab, last_ab, s_sem, r_sem
    )
    for copy in (group.a[1], group.b[1], group.a[0], group.b[0]):
        copy.start()
    sums = Sums(outer, steps, dws, was_l, was_r, to_l, to_r, *sums_refs)
    sums.load()
    sums.send()
    length = len_ref[0]
    rows, own_rows = qkv_ref.shape[0], own_ref.shape[0]
    groups = own_ref.shape[1] // LANES
    scale = 1.0 / math.sqrt(HD)

    def per_group(g, carry):
        q_lanes = pl.ds(pl.multiple_of(g * 2 * LANES, LANES), LANES)
        kv_lanes = pl.ds(pl.multiple_of(g * 2 * LANES + LANES, LANES), LANES)
        o_lanes = pl.ds(pl.multiple_of(g * LANES, LANES), LANES)
        for half, grad_ref in ((t, own_ref), (1 - t, other_ref)):
            do_ref[pl.ds(pl.multiple_of(half * own_rows, own_rows), own_rows), :] = grad_ref[:, o_lanes]
        keys, values = doubled(qkv_ref[:, kv_lanes])
        dk_ref[...] = jnp.zeros_like(dk_ref)
        dv_ref[...] = jnp.zeros_like(dv_ref)
        for b in range(rows // q_block):
            start, n_keys = b * q_block, (b + 1) * q_block
            q = head_pair(qkv_ref[start : start + q_block, q_lanes])
            grad = head_pair(do_ref[start : start + q_block, :])
            scores = mm_nt(keys[:n_keys], q) * scale
            probs = jnp.where(
                allowed(n_keys, q_block, start, length), jnp.exp(scores - lse_ref[g, b : b + 1, :]), 0.0
            )
            prob_grad = mm_nt(values[:n_keys], grad)
            center = jnp.sum(probs * prob_grad, axis=0, keepdims=True)
            score_grad = (probs * (prob_grad - center)).astype(BF)
            dq_ref[start : start + q_block, :] = head_join(mm_tn(score_grad, keys[:n_keys])) * scale
            dk_ref[:n_keys, :] += mm(score_grad, q)
            dv_ref[:n_keys, :] += mm(probs.astype(BF), grad)
        for p, half in enumerate((t, 1 - t)):
            at = pl.ds(pl.multiple_of(half * own_rows, own_rows), own_rows)
            cosine, sine = cos_ref[at, :], sin_ref[at, :]
            dq = dq_ref[at, :]
            outs[p][:, q_lanes] = (dq * cosine - swap_halves(dq) * sine).astype(BF)
            dk, dv = dk_ref[at, :] * scale, dv_ref[at, :]
            dk = dk + pltpu.roll(dk, HD, 1)
            dv = dv + pltpu.roll(dv, HD, 1)
            dk = dk * cosine - swap_halves(dk) * sine
            first = lax.broadcasted_iota(jnp.int32, dk.shape, 1) < HD
            outs[p][:, kv_lanes] = jnp.where(first, dk, dv).astype(BF)

        @pl.when(g == groups // 2)
        def _():
            for c in loads:
                c.wait()
            group.second()

        return carry

    lax.fori_loop(0, groups, per_group, 0)
    for p in range(2):
        at = slice(p * q, (p + 1) * q)
        out_ref[at] = jnp.where(valid_ref[at] > 0, hidden_ref[at] + group.terms(p), 0.0).astype(BF)
    group.sent()
    sums.wait()


def attention_back(
    outer, q_block, length, qkv, lse, cosine, sine, grads, hidden, valid, mixed, steps, dws, was_l, was_r
):
    rows, width = qkv.shape
    n = len(steps)
    packed = dws[0].shape[2]
    hop = jax.ShapeDtypeStruct((GROUP, packed, D), BF)
    out = remote_call(
        functools.partial(attention_back_kernel, outer, q_block, steps),
        "attention_back",
        12,
        [jax.ShapeDtypeStruct((rows // 2, width), BF)] * 2
        + [jax.ShapeDtypeStruct((rows // 2, D), BF)]
        + [hop] * (2 * n),
        [SMEM] + [VM] * 8 + [ANY] * (3 * n + 1),
        [VM] * 3 + [ANY] * (2 * n),
        (length, qkv, lse, cosine, sine, *grads, hidden, valid, mixed, *dws, *was_l, *was_r),
        [
            pltpu.VMEM((rows, LANES), BF),
            pltpu.VMEM((rows, LANES), F32),
            pltpu.VMEM((rows, LANES), F32),
            pltpu.VMEM((rows, LANES), F32),
            *sums_scratch(n, packed),
            pltpu.VMEM((2, rows // 4, D), BF),
            pltpu.VMEM((2, rows // 4, D), BF),
            pltpu.SemaphoreType.DMA((4,)),
            *group_scratch(rows),
        ],
        30 << 30,
    )
    return out[:3], out[3 : 3 + n], out[3 + n :]


def over_outer(outer, source, target, sent, came, base):
    _, t, o, i = place()
    return [
        pltpu.make_async_remote_copy(
            source((o + k) % outer),
            target(k),
            sent.at[base + k],
            came.at[base + k],
            device_id=((o + k) % outer * GROUP + i, t),
            device_id_type=MESH,
        )
        for k in range(1, outer)
    ]


class Spread:
    def __init__(self, outer, terms, come_core, come_y, come_z, sent, came):
        _, _, self.o, i = place()
        self.outer, self.terms, self.come_core, self.come_y, self.come_z = outer, terms, come_core, come_y, come_z
        y, c = i // 2, i % 2
        self.y, self.c = y, c
        self.core = to_dp(1, terms.at[:, :, 1 - c], come_core, sent.at[0], came.at[0])
        self.side = to_dp(2, terms.at[:, 1 - y, c], come_y, sent.at[1], came.at[1])
        self.moves = over_outer(outer, lambda peer: terms.at[peer, y, c], lambda k: come_z.at[k - 1], sent, came, 1)

    def over_core(self):
        self.core.start()

    def over_y(self):
        self.core.wait()

        def add(k, carry):
            for r in range(2):
                self.terms[k, r, self.c] = (
                    self.terms[k, r, self.c].astype(F32) + self.come_core[k, r].astype(F32)
                ).astype(BF)
            return carry

        lax.fori_loop(0, self.outer, add, 0)
        self.side.start()

    def over_z(self):
        self.side.wait()

        def add(k, carry):
            self.terms[k, self.y, self.c] = (
                self.terms[k, self.y, self.c].astype(F32) + self.come_y[k].astype(F32)
            ).astype(BF)
            return carry

        lax.fori_loop(0, self.outer, add, 0)
        for move in self.moves:
            move.start()

    def total(self):
        for move in self.moves:
            move.wait()
        total = self.terms[self.o, self.y, self.c].astype(F32)
        for k in range(1, self.outer):
            total = total + self.come_z[k - 1].astype(F32)
        return total


def spread_scratch(outer, each, columns):
    return [
        pltpu.VMEM((outer, 2, 2, each, columns), BF),
        pltpu.VMEM((outer, 2, each, columns), BF),
        pltpu.VMEM((outer, each, columns), BF),
        pltpu.VMEM((outer - 1, each, columns), BF),
        pltpu.SemaphoreType.DMA((1 + outer,)),
        pltpu.SemaphoreType.DMA((1 + outer,)),
    ]


def finish_kernel(outer, hgrad_ref, x_ref, gain_ref, w_any, *refs):
    (no_ref, nx_ref, po_ref, px_ref, oo_ref, ox_ref, sg_ref), refs = refs[:7], refs[7:]
    dws, refs = refs[:3], refs[3:]
    done, refs = refs[:2], refs[2:]
    was_l, refs = refs[:2], refs[2:]
    was_r, refs = refs[:2], refs[2:]
    tgrad_ref, gains_ref, qkv_ref, outw_ref = refs[:4]
    fins, to_l, to_r, refs = refs[4:7], refs[7:9], refs[9:11], refs[11:]
    sums_refs, refs = [refs[:6], refs[6:12]], refs[12:]
    final_refs, refs = [refs[5 * k : 5 * k + 5] for k in range(3)], refs[15:]
    part_ref, theirs_ref, p_send, p_recv, out_ref, come_ref, c_send, c_recv = refs[:8]
    q_refs, o_refs, refs = refs[8:14], refs[14:20], refs[20:]
    g_buf, g_come, g_z, g_send, g_recv, w_ref, w_sem = refs
    d, t, o, i = place()
    rows = hgrad_ref.shape[0]
    width = w_ref.shape[1]
    w_copy = pltpu.make_async_copy(w_any.at[:, pl.ds(0, width)], w_ref, w_sem)
    w_copy.start()
    greet_all(outer)
    sums = [
        Sums(outer, (3,), [dws[1 + k]], [was_l[k]], [was_r[k]], [to_l[k]], [to_r[k]], *sums_refs[k]) for k in range(2)
    ]
    came = [done, (to_l[0], to_r[0]), (to_l[1], to_r[1])]
    finals = [
        Final(outer, dws[k], *came[k], final_refs[k][0], sums_refs[0][1], fins[k], *final_refs[k][1:]) for k in range(3)
    ]
    for one in sums:
        one.load()
    for one in sums:
        one.send()
    whole, part = Spread(outer, *q_refs), Spread(outer, *o_refs)
    each, heads = outw_ref.shape

    def out_block(k, carry):
        for r in range(GROUP):
            at = pl.ds(pl.multiple_of((k * GROUP + r) * each, each), each)
            part.terms[k, r // 2, r % 2, :, :heads] = oo_ref[at, :]
            part.terms[k, r // 2, r % 2, :, heads:] = ox_ref[at, :]
        return carry

    lax.fori_loop(0, outer, out_block, 0)
    part.over_core()

    w_copy.wait()
    part_ref[...] = mm_nt(px_ref[...], w_ref[...]).astype(BF)
    exchange = to_x(part_ref, theirs_ref, p_send, p_recv)
    exchange.start()

    def weights_block(k, carry):
        lanes = pl.ds(pl.multiple_of(k * GROUP * each, GROUP * each), GROUP * each)
        total = (mm_tn(no_ref[:, lanes], po_ref[...]) + mm_tn(nx_ref[:, lanes], px_ref[...])).astype(BF)
        for r in range(GROUP):
            whole.terms[k, r // 2, r % 2] = total[r * each : (r + 1) * each]
        return carry

    part.over_y()
    lax.fori_loop(0, outer, weights_block, 0)
    whole.over_core()
    finals[0].send()
    whole.over_y()
    part.over_z()
    sums[0].wait()
    finals[1].send()

    exchange.wait()
    quarter = rows // 4

    def norm_rows(p, gain_grad):
        at = pl.ds(pl.multiple_of(p * quarter, quarter), quarter)
        normed_grad = mm_nt(po_ref[at, :], w_ref[...]).astype(BF).astype(F32) + theirs_ref[at, :].astype(F32)
        x = x_ref[at, :].astype(F32)
        inverse = lax.rsqrt(jnp.mean(x * x, axis=-1, keepdims=True) + EPSILON)
        scaled = normed_grad * gain_ref[...]
        tgrad_ref[at, :] = (
            hgrad_ref[at, :]
            + inverse * scaled
            - x * (inverse * inverse * inverse * jnp.mean(scaled * x, axis=-1, keepdims=True))
        )
        return gain_grad + jnp.sum(normed_grad * (x * inverse), axis=0, keepdims=True)

    g_buf[0, 0:1, :] = lax.fori_loop(0, 4, norm_rows, jnp.zeros((1, D), F32))
    g_buf[0, 1:2, :] = sg_ref[...]
    g_buf[0, 2:8, :] = jnp.zeros((6, D), F32)
    g_moves = [
        to_dp(1, g_buf.at[0], g_come.at[0], g_send.at[0], g_recv.at[0]),
        to_dp(2, g_buf.at[1], g_come.at[1], g_send.at[1], g_recv.at[1]),
        to_x(g_buf.at[2], g_come.at[2], g_send.at[2], g_recv.at[2]),
    ]
    g_moves[0].start()
    whole.over_z()
    g_moves[0].wait()
    g_buf[1] = g_buf[0] + g_come[0]
    g_moves[1].start()
    sums[1].wait()
    finals[2].send()
    g_moves[1].wait()
    g_buf[2] = g_buf[1] + g_come[1]
    g_moves[2].start()
    out = part.total()
    outw_ref[...] = out[:, :heads]
    out_ref[...] = out[:, heads:].astype(BF)
    to_other = to_x(out_ref, come_ref, c_send, c_recv)
    to_other.start()
    g_moves[2].wait()
    g_z[0] = g_buf[2] + g_come[2]
    gz_moves = over_outer(outer, lambda peer: g_z.at[0], lambda k: g_z.at[k], g_send, g_recv, 2)
    for move in gz_moves:
        move.start()
    qkv_ref[...] = whole.total()
    to_other.wait()
    outw_ref[...] = outw_ref[...] + come_ref[...].astype(F32)
    for move in gz_moves:
        move.wait()
    gains = g_z[(o + outer) % outer]
    for k in range(1, outer):
        gains = gains + g_z[(o - k + outer) % outer]
    gains_ref[...] = gains
    for final in finals:
        final.wait()


def finish(outer, hgrad, x, gain, weights_full, extra, dws, done, was_l, was_r):
    rows = hgrad.shape[0]
    packed = dws[0].shape[2]
    width = weights_full.shape[1] // 2
    heads = width // 2
    each = D // (outer * GROUP)
    hop = jax.ShapeDtypeStruct((GROUP, packed, D), BF)
    return remote_call(
        functools.partial(finish_kernel, outer),
        "finish",
        11,
        [
            jax.ShapeDtypeStruct((rows, D), F32),
            jax.ShapeDtypeStruct((8, D), F32),
            jax.ShapeDtypeStruct((each, width), F32),
            jax.ShapeDtypeStruct((each, heads), F32),
        ]
        + [hop] * 7,
        [VM] * 3 + [ANY] + [VM] * 7 + [ANY] * 9,
        [VM] * 4 + [ANY] * 7,
        (hgrad, x, gain.reshape(1, D), weights_full, *extra, *dws, *done, *was_l, *was_r),
        [
            *sums_scratch(1, packed) * 2,
            *final_scratch(packed) * 3,
            pltpu.VMEM((rows, D), BF),
            pltpu.VMEM((rows, D), BF),
            pltpu.SemaphoreType.DMA,
            pltpu.SemaphoreType.DMA,
            pltpu.VMEM((each, heads), BF),
            pltpu.VMEM((each, heads), BF),
            pltpu.SemaphoreType.DMA,
            pltpu.SemaphoreType.DMA,
            *spread_scratch(outer, each, width),
            *spread_scratch(outer, each, 2 * heads),
            pltpu.VMEM((3, 8, D), F32),
            pltpu.VMEM((3, 8, D), F32),
            pltpu.VMEM((outer, 8, D), F32),
            pltpu.SemaphoreType.DMA((2 + outer,)),
            pltpu.SemaphoreType.DMA((2 + outer,)),
            pltpu.VMEM((D, width), BF),
            pltpu.SemaphoreType.DMA,
        ],
        30 << 30,
    )


def settle_kernel(in_rows, idx_ref, *refs):
    n = len(refs) - 7
    sources, (in_ref, down_ref, held, wide_in, wide_down, l_sem, s_sem) = refs[:n], refs[n:]
    loads = [pltpu.make_async_copy(source, held.at[j], l_sem.at[j]) for j, source in enumerate(sources)]
    for c in loads:
        c.start()
    stores = []
    for j in range(n):
        loads[j].wait()
        for m in range(GROUP):
            k = j * GROUP + m
            at = (idx_ref[1] ^ m) * n + j
            wide_in[k] = held[j, m, :in_rows, :].astype(F32)
            wide_down[k] = held[j, m, in_rows:, :].astype(F32)
            stores.append(pltpu.make_async_copy(wide_in.at[k], in_ref.at[at], s_sem.at[2 * k]))
            stores.append(pltpu.make_async_copy(wide_down.at[k], down_ref.at[at], s_sem.at[2 * k + 1]))
            for c in stores[-2:]:
                c.start()
    for c in stores:
        c.wait()


def settle_experts(idx, fins, in_rows):
    n = len(fins)
    _, packed, _ = fins[0].shape
    experts, down_rows = n * GROUP, packed - in_rows
    return call(
        functools.partial(settle_kernel, in_rows),
        "settle_experts",
        [jax.ShapeDtypeStruct((experts, in_rows, D), F32), jax.ShapeDtypeStruct((experts, down_rows, D), F32)],
        [SMEM] + [ANY] * n,
        [ANY] * 2,
        (idx, *fins),
        scratch=[
            pltpu.VMEM((n, GROUP, packed, D), BF),
            pltpu.VMEM((experts, in_rows, D), F32),
            pltpu.VMEM((experts, down_rows, D), F32),
            pltpu.SemaphoreType.DMA((n,)),
            pltpu.SemaphoreType.DMA((2 * experts,)),
        ],
        moved=9 << 20,
    )


def layer(
    tokens,
    cotangent,
    lengths,
    expert_ids,
    gate_values,
    first_gain,
    qkv_weight,
    attn_out_weight,
    second_gain,
    expert_in_weight,
    expert_out_weight,
):
    rows = tokens.shape[0]
    n_tensor, n_dp = lax.axis_size("tensor"), lax.axis_size("dp")
    outer = n_dp // GROUP
    slot_rows = rows * n_tensor
    d, t = lax.axis_index("dp"), lax.axis_index("tensor")
    o, i = d // GROUP, d % GROUP
    length = lengths[0]
    idx = jnp.stack([o, i, t, length]).astype(jnp.int32)
    width = qkv_weight.shape[1] * qkv_weight.shape[2]
    experts_local, in_rows, _ = expert_in_weight.shape
    down_rows = expert_out_weight.shape[1]
    own_experts = experts_local // GROUP
    pair = n_tensor == 2
    q_block = 256
    half = rows // 2

    def across(v, m):
        return lax.ppermute(v, "dp", [(a, a ^ m) for a in range(n_dp)])

    def beside(v):
        return lax.ppermute(v, "tensor", [(0, 1), (1, 0)])

    def hop(pairs):
        up = [(a, a + GROUP) for a in range(n_dp - GROUP)]
        down = [(b, a) for a, b in up]
        return [(lax.ppermute(a, "dp", up), lax.ppermute(b, "dp", down)) for a, b in pairs]

    def gather_group(pieces):
        if pair:
            a, b = pieces
            ax, by, ay, bx = beside(a), across(b, 2), across(a, 2), beside(b)
            axy, bxy = across(ax, 2), beside(by)
            slots = [[a, ax, b, bx], [ay, axy, by, bxy]]
        else:
            slot = lax.all_gather(pieces[0], "tensor", axis=0, tiled=True)
            slots = [[slot], [across(slot, 2)]]
        return slots + [[across(p, 1) for p in s] for s in slots]

    positions = t * rows + jnp.arange(rows, dtype=jnp.int32)
    valid_rows = positions < length
    n_experts = experts_local * n_tensor
    chosen = expert_ids.T[None] == jnp.arange(n_experts, dtype=jnp.int32)[:, None, None]
    gates = jnp.sum(jnp.where(chosen, gate_values.T[None].astype(F32), 0.0), axis=1)
    gates = jnp.where(valid_rows[None, :], gates, 0.0).astype(BF)
    x = tokens.astype(F32)
    inverse_one = lax.rsqrt(jnp.mean(x * x, axis=-1, keepdims=True) + EPSILON)
    normed_one = (x * inverse_one * first_gain).astype(BF)
    expert_outs, row_grads, weight_grads = [], [], []
    if pair and outer == 4:
        frequency = THETA ** (-(jnp.arange(HD // 2).astype(F32) * 2.0 / HD))
        shard = jnp.concatenate([qkv_weight.reshape(-1, width), attn_out_weight.T], axis=1)
        main, ready, packed, first_l, first_r = collect(
            outer, shard, normed_one, gates, jnp.tile(frequency, 4)[None, :], expert_in_weight, expert_out_weight
        )
        weights_full, other, cosine, sine, pos, own_gates, pos_columns, gate_columns = main
        main, dy_moved, later, one_l, one_r = attention(
            outer,
            q_block,
            lengths,
            normed_one,
            other,
            weights_full,
            cosine,
            sine,
            tokens,
            second_gain,
            cotangent,
            ready[1],
            packed,
        )
        own_weights = [*ready, *later]
        one_l, one_r = [first_l, *one_l], [first_r, *one_r]
        qkv, lse, attn_own, attn_other, hidden, *normed_two = main
        attn_parts = [attn_own, attn_other]
        gathered, out_grads, moved_l, moved_r = spread(
            outer,
            pos,
            own_gates,
            normed_two,
            [cotangent, *dy_moved],
            (2, 2, 2),
            one_l[:3],
            one_r[:3],
        )
        two_l, two_r = [*moved_l], [*moved_r]
        expert_rows, moved_l, moved_r = hand_out(
            outer, pos, normed_two, gathered, (3, 2), [two_l[0], one_l[3]], [two_r[0], one_r[3]]
        )
        three_l, three_r = [moved_l[0]], [moved_r[0]]
        two_l.append(moved_l[1])
        two_r.append(moved_r[1])
        hop_plans = [
            lambda: ((3,), [two_l[1]], [two_r[1]]),
            lambda: ((3,), [two_l[2]], [two_r[2]]),
            lambda: ((3,), [two_l[3]], [two_r[3]]),
            lambda: ((), [], []),
        ]
        sums_l, sums_r = [], []
        for j in range(own_experts):
            first_grad = weight_grads[:1]
            sum_plan = ((j,), first_grad, sums_l or first_grad, sums_r or first_grad) if j else ((), [], [], [])
            if j == own_experts - 1:
                second_grad = weight_grads[1]
                sum_plan = ((j, 1), weight_grads[:2], [*sums_l, second_grad], [*sums_r, second_grad])
            (y, dx, dw), moved_l, moved_r, sums_l, sums_r = expert_step(
                j,
                outer,
                in_rows,
                down_rows,
                expert_rows,
                out_grads,
                own_weights[j],
                [one_l[j], two_l[j], three_l[j]],
                [one_r[j], two_r[j], three_r[j]],
                hop_plans[j](),
                sum_plan,
            )
            three_l.extend(moved_l[:1])
            three_r.extend(moved_r[:1])
            expert_outs.append(y)
            row_grads.append(dx)
            weight_grads.append(dw)
        valid_column = valid_rows.astype(F32)[:, None]
        _, dw_b, dw_c, dw_d = weight_grads
        main, fin_a, sum_l, sum_r = rows_back(
            outer,
            pos_columns,
            gate_columns,
            valid_column,
            hidden,
            cotangent,
            second_gain,
            weights_full,
            row_grads,
            expert_outs,
            (2, 1),
            ((2, 1), (1, 2)),
            [dw_b, dw_c, dw_d],
            [sums_l[1], dw_c],
            [sums_r[1], dw_c],
            [weight_grads[0], sums_l[0], sums_r[0]],
        )
        hidden_grad, branch_grad, second_gain_part, attn_grad_own, attn_grad_other, mixed = main
        (projected_own, projected_other, output), three_l, three_r = attention_back(
            outer,
            q_block,
            lengths,
            qkv,
            lse,
            cosine,
            sine,
            [attn_grad_own, attn_grad_other],
            hidden,
            valid_column,
            mixed,
            (3, 2),
            [dw_b, dw_d],
            [sum_l[0], sum_l[3]],
            [sum_r[0], sum_r[3]],
        )
        out_own, out_other = (mm_tn(branch_grad, part).astype(BF) for part in attn_parts)
        tokens_grad, gains, qkv_grad, attn_out_grad, *fins = finish(
            outer,
            hidden_grad,
            tokens,
            first_gain,
            weights_full,
            [normed_one, other, projected_own, projected_other, out_own, out_other, second_gain_part],
            [dw_b, dw_c, dw_d],
            [three_l[0], three_r[0]],
            [sum_l[2], three_l[1]],
            [sum_r[2], three_r[1]],
        )
        expert_in_grad, expert_out_grad = settle_experts(idx, [fin_a, *fins[:3]], in_rows)
        return (
            output,
            tokens_grad,
            gains[0],
            qkv_grad.reshape(qkv_weight.shape),
            attn_out_grad.T,
            gains[1],
            expert_in_grad,
            expert_out_grad,
        )
    else:
        if pair:
            gates_x = beside(gates)
            slot_gates = jnp.concatenate(
                [gates[:, :half], gates_x[:, :half], gates[:, half:], gates_x[:, half:]], axis=1
            )
        else:
            slot_gates = lax.all_gather(gates, "tensor", axis=1, tiled=True)
        gates_y = across(slot_gates, 2)
        all_gates = jnp.stack([slot_gates, gates_y, across(slot_gates, 1), across(gates_y, 1)])
        own_gates = lax.dynamic_slice_in_dim(
            all_gates, t * experts_local + i * own_experts, own_experts, axis=1
        ).astype(F32)
        named = own_gates > 0
        before = (
            lax.broadcasted_iota(jnp.int32, (slot_rows, slot_rows), 0)
            < lax.broadcasted_iota(jnp.int32, (slot_rows, slot_rows), 1)
        ).astype(BF)
        ranks = jnp.dot(
            named.astype(BF).reshape(GROUP * own_experts, slot_rows), before, preferred_element_type=F32
        ).reshape(GROUP, own_experts, slot_rows)
        pos = jnp.where(named, ranks, -1.0).astype(jnp.int32)
        pos_columns, gate_columns = jnp.swapaxes(pos, 1, 2), jnp.swapaxes(own_gates, 1, 2)

        cosine, sine = rope_tables(slot_rows)
        dy = jnp.where(valid_rows[:, None], cotangent, jnp.zeros_like(cotangent))
        qkv_full = lax.all_gather(qkv_weight.reshape(qkv_weight.shape[0], width), "dp", axis=0, tiled=True)
        out_full = lax.all_gather(attn_out_weight.T, "dp", axis=0, tiled=True)
        by_distance = pack_weights(idx, expert_in_weight, expert_out_weight)
        by_distance = [by_distance[0]] + [across(by_distance[m], m) for m in range(1, GROUP)]
        own_weights = [jnp.stack([v[j] for v in by_distance]) for j in range(own_experts)]
        hops = [hop([(own, own) for own in own_weights])]
        if pair:
            out_parts = [out_full, beside(out_full)]
        else:
            gathered = lax.all_gather(out_full, "tensor", axis=0)
            out_parts = [gathered[k] for k in range(n_tensor)]

        if pair:
            other = beside(normed_one)
            normed_all = jnp.where(
                t == 0,
                jnp.concatenate([normed_one, other], axis=0),
                jnp.concatenate([other, normed_one], axis=0),
            )
        else:
            normed_all = lax.all_gather(normed_one, "tensor", axis=0, tiled=True)
        qkv = qkv_project(normed_all, qkv_full, cosine, sine)
        *attended, lse = attend(idx, qkv, 2 if pair else 1, q_block)
        if pair:
            attn_parts = [attended[0], beside(attended[1])]
        else:
            heads = attended[0].shape[1]
            exchanged = lax.all_to_all(attended[0].reshape(n_tensor, rows, heads), "tensor", 0, 0)
            attn_parts = [exchanged[k] for k in range(n_tensor)]
        attn_parts, hops[0] = lax.optimization_barrier((attn_parts, hops[0]))
        if outer > 2:
            hops.append(hop(hops[0]))
        hidden, *normed_two = project_out(tokens, second_gain, attn_parts, out_parts, 2 if pair else 1)

        dy_slots = gather_group([dy[:half], dy[half:]] if pair else [dy])
        out_grads = [dispatch(pos[s], own_gates[s], dy_slots[s], True) for s in range(GROUP)]
        normed_slots = gather_group(normed_two)
        normed_slots, out_grads, hops = lax.optimization_barrier((normed_slots, out_grads, hops))
        while len(hops) < outer - 1:
            hops.append(hop(hops[-1]))
        expert_rows = [dispatch(pos[s], own_gates[s], normed_slots[s], False) for s in range(GROUP)]

        for j in range(own_experts):
            if j:
                idx, expert_outs[-1] = lax.optimization_barrier((idx, expert_outs[-1]))
            y, dx, dw = expert(
                idx,
                j,
                outer,
                in_rows,
                down_rows,
                expert_rows,
                out_grads,
                own_weights[j],
                [h[j][0] for h in hops],
                [h[j][1] for h in hops],
            )
            expert_outs.append(y)
            row_grads.append(dx)
            weight_grads.append(dw)

    def sum_group(sources, scaled):
        def part(s, add, n_outs):
            return combine(pos_columns[s], gate_columns[s], sources, s, scaled, add, n_outs)

        far = [part(2, None, 1)[0], part(3, None, 1)[0]]
        near = [across(v, 1) for v in far]
        if pair:
            ay, axy, by, bxy = part(1, near[1], 4)
            a, ax, b, bx = part(0, near[0], 4)

            def add(p, q):
                return (p.astype(F32) + q.astype(F32)).astype(BF)

            a, ax = add(a, across(ay, 2)), add(ax, across(axy, 2))
            b, by = add(b, beside(bx)), add(by, beside(bxy))
            return [[a, beside(ax)], [b, across(by, 2)]]
        (y,) = part(1, near[1], 1)
        (v,) = part(0, near[0], 1)
        v = (v.astype(F32) + across(y, 2).astype(F32)).astype(BF)
        return [[lax.psum_scatter(v, "tensor", scatter_dimension=0, tiled=True)]]

    valid_column = valid_rows.astype(F32)[:, None]
    normed_two_grad = sum_group(row_grads, False)
    hidden_grad, branch_grad, second_gain_part, *attn_grads = hidden_back(
        valid_column, hidden, cotangent, second_gain, normed_two_grad, out_parts
    )
    if pair:
        attn_grads = [attn_grads[0], beside(attn_grads[1])]
    else:
        attn_grads = [
            lax.all_to_all(jnp.stack(attn_grads), "tensor", 0, 0).reshape(slot_rows, attn_grads[0].shape[1])
        ]
    projected_grads = attend_back(idx, qkv, lse, cosine, sine, attn_grads, q_block)

    def first_norm_part(v):
        return lax.dot_general(v, qkv_full, (((1,), (1,)), ((), ())), preferred_element_type=F32).astype(BF)

    if pair:
        theirs = beside(first_norm_part(projected_grads[1]))
        normed_one_grad = first_norm_part(projected_grads[0]).astype(F32) + theirs.astype(F32)
        qkv_part = mm_tn(normed_one, projected_grads[0]) + mm_tn(other, projected_grads[1])
    else:
        normed_one_grad = lax.psum_scatter(
            first_norm_part(projected_grads[0]), "tensor", scatter_dimension=0, tiled=True
        ).astype(F32)
        qkv_part = mm_tn(normed_all, projected_grads[0])
    first_gain_part = jnp.sum(normed_one_grad * (x * inverse_one), axis=0)
    scaled = normed_one_grad * first_gain
    tokens_grad = (
        hidden_grad
        + inverse_one * scaled
        - x * (inverse_one * inverse_one * inverse_one * jnp.mean(scaled * x, axis=-1, keepdims=True))
    )

    mixture = sum_group(expert_outs, True)
    mixture = jnp.concatenate([sum(v.astype(F32) for v in terms) for terms in mixture], axis=0)
    output = jnp.where(valid_rows[:, None], hidden + mixture, 0.0).astype(BF)

    outer_groups = [[a * GROUP + b for a in range(outer)] for b in range(GROUP)]
    received = [[] for _ in range(GROUP)]
    for dw in weight_grads:
        mine = lax.psum_scatter(dw, "dp", scatter_dimension=0, tiled=True, axis_index_groups=outer_groups)
        for m in range(GROUP):
            block = mine[0, m]
            received[m].append(block if m == 0 else across(block, m))
    by_distance = jnp.stack([jnp.stack(v) for v in received])
    by_source = jnp.take(by_distance, jnp.arange(GROUP) ^ i, axis=0).reshape(
        experts_local, in_rows + down_rows, D
    )
    expert_in_grad = by_source[:, :in_rows].astype(F32)
    expert_out_grad = by_source[:, in_rows:].astype(F32)

    attn_out_parts = [mm_tn(branch_grad, part).astype(BF) for part in attn_parts]
    if pair:
        attn_out_part = (attn_out_parts[0].astype(F32) + beside(attn_out_parts[1]).astype(F32)).astype(BF)
    else:
        attn_out_part = lax.psum_scatter(jnp.stack(attn_out_parts), "tensor", scatter_dimension=0, tiled=True)[0]
    qkv_grad = lax.psum_scatter(qkv_part.astype(BF), "dp", scatter_dimension=0, tiled=True).astype(F32)
    attn_out_grad = lax.psum_scatter(attn_out_part, "dp", scatter_dimension=0, tiled=True).astype(F32).T

    gains = jnp.stack([first_gain_part, second_gain_part[0]])
    if pair:
        gains = gains + beside(gains)
    else:
        gains = lax.psum(gains, "tensor")
    step = 1
    while step < n_dp:
        gains = gains + across(gains, step)
        step *= 2
    return (
        output,
        tokens_grad,
        gains[0],
        qkv_grad.reshape(qkv_weight.shape),
        attn_out_grad,
        gains[1],
        expert_in_grad,
        expert_out_grad,
    )


def solution(mesh):
    placed = (
        P(("dp", "tensor"), None),
        P(("dp", "tensor"), None),
        P("dp"),
        P(("dp", "tensor"), None),
        P(("dp", "tensor"), None),
        P(),
        P("dp", "tensor", None),
        P("tensor", "dp"),
        P(),
        P("tensor", "dp", None),
        P("tensor", "dp", None),
    )
    return jax.shard_map(
        layer,
        mesh=mesh,
        in_specs=placed,
        out_specs=(
            P(("dp", "tensor"), None),
            P(("dp", "tensor"), None),
            P(),
            P("dp", "tensor", None),
            P("tensor", "dp"),
            P(),
            P("tensor", "dp", None),
            P("tensor", "dp", None),
        ),
        check_vma=False,
    )
```

```python
import functools
import math

import jax
import jax.numpy as jnp
from jax import lax
from jax.experimental import pallas as pl
from jax.experimental.pallas import tpu as pltpu
from jax.sharding import PartitionSpec as P

D = 1024
HD = 64
FF = 512
G = 2
CAP = 288
GROUP = 4
LANES = 128

EPSILON = 1e-06
THETA = 10000.0
NEGATIVE = -1e30
BF = jnp.bfloat16
F32 = jnp.float32
VMEM_LIMIT = 60 * 1024 * 1024
MESH = pl.DeviceIdType.MESH

ANY = pl.BlockSpec(memory_space=pl.ANY)
SMEM = pl.BlockSpec(memory_space=pltpu.SMEM)
VM = pl.BlockSpec(memory_space=pltpu.VMEM)


def mm(a, b):
    return lax.dot_general(a, b, (((1,), (0,)), ((), ())), preferred_element_type=F32)


def mm_nt(a, b):
    return lax.dot_general(a, b, (((1,), (1,)), ((), ())), preferred_element_type=F32)


def mm_tn(a, b):
    return lax.dot_general(a, b, (((0,), (0,)), ((), ())), preferred_element_type=F32)


def call(kernel, name, out_shape, in_specs, out_specs, args, scratch=(), flops=0, moved=0, **more):
    return pl.pallas_call(
        kernel,
        name=name,
        out_shape=out_shape,
        in_specs=in_specs,
        out_specs=out_specs,
        scratch_shapes=list(scratch),
        compiler_params=pltpu.CompilerParams(vmem_limit_bytes=VMEM_LIMIT),
        cost_estimate=pl.CostEstimate(flops=flops, bytes_accessed=moved, transcendentals=0),
        **more,
    )(*args)


def rope_tables(total_rows):
    half = HD // 2
    positions = jnp.arange(total_rows).astype(F32)
    frequency = THETA ** (-(jnp.arange(half).astype(F32) * 2.0 / HD))
    angles = positions[:, None] * frequency[None, :]
    cosine, sine = jnp.cos(angles), jnp.sin(angles)
    return (
        jnp.concatenate([cosine] * 4, axis=1),
        jnp.concatenate([-sine, sine, -sine, sine], axis=1),
    )


def swap_halves(v):
    lane = lax.broadcasted_iota(jnp.int32, v.shape, 1)
    return jnp.where(lane % HD < HD // 2, pltpu.roll(v, LANES - HD // 2, 1), pltpu.roll(v, HD // 2, 1))


def qkv_kernel(n_ref, w_ref, cos_ref, sin_ref, out_ref):
    projected = mm(n_ref[...], w_ref[...])
    cosine, sine = cos_ref[...], sin_ref[...]
    key_lanes = lax.broadcasted_iota(jnp.int32, cosine.shape, 1) < HD
    for g in range(projected.shape[1] // (2 * LANES)):
        q = projected[:, g * 2 * LANES : g * 2 * LANES + LANES]
        kv = projected[:, g * 2 * LANES + LANES : (g + 1) * 2 * LANES]
        q = q * cosine + swap_halves(q) * sine
        kv = jnp.where(key_lanes, kv * cosine + swap_halves(kv) * sine, kv)
        out_ref[:, g * 2 * LANES : g * 2 * LANES + LANES] = q.astype(BF)
        out_ref[:, g * 2 * LANES + LANES : (g + 1) * 2 * LANES] = kv.astype(BF)


def qkv_project(normed, weight, cosine, sine):
    rows, width = normed.shape[0], weight.shape[1]
    block = 256
    return pl.pallas_call(
        qkv_kernel,
        name="qkv_rope",
        grid=(rows // block,),
        out_shape=jax.ShapeDtypeStruct((rows, width), BF),
        in_specs=[
            pl.BlockSpec((block, D), lambda b: (b, 0)),
            pl.BlockSpec((D, width), lambda b: (0, 0)),
            pl.BlockSpec((block, LANES), lambda b: (b, 0)),
            pl.BlockSpec((block, LANES), lambda b: (b, 0)),
        ],
        out_specs=pl.BlockSpec((block, width), lambda b: (b, 0)),
        compiler_params=pltpu.CompilerParams(vmem_limit_bytes=VMEM_LIMIT),
        cost_estimate=pl.CostEstimate(flops=2 * rows * D * width, bytes_accessed=6 << 20, transcendentals=0),
    )(normed, weight, cosine, sine)


def head_pair(v):
    first = lax.broadcasted_iota(jnp.int32, v.shape, 1) < HD
    zero = jnp.zeros_like(v)
    return jnp.concatenate([jnp.where(first, v, zero), jnp.where(first, zero, v)], axis=0)


def head_join(v):
    n = v.shape[0] // 2
    first = lax.broadcasted_iota(jnp.int32, (n, LANES), 1) < HD
    return jnp.where(first, v[:n], v[n:])


def doubled(kv):
    first = lax.broadcasted_iota(jnp.int32, kv.shape, 1) < HD
    other = pltpu.roll(kv.astype(F32), HD, 1).astype(BF)
    return jnp.where(first, kv, other), jnp.where(first, other, kv)


def allowed(n_keys, q_block, q_start, length):
    key = lax.broadcasted_iota(jnp.int32, (n_keys, 2 * q_block), 0)
    lane = lax.broadcasted_iota(jnp.int32, (n_keys, 2 * q_block), 1)
    query = q_start + jnp.where(lane < q_block, lane, lane - q_block)
    return (key <= query) & (key < length)


def attend_kernel(q_block, idx_ref, qkv_ref, *out_refs):
    outs, lse_ref = out_refs[:-1], out_refs[-1]
    rows = qkv_ref.shape[0]
    length = idx_ref[3]
    keys, values = doubled(qkv_ref[:, LANES:])
    for b in range(rows // q_block):
        start, n_keys = b * q_block, (b + 1) * q_block
        q = head_pair(qkv_ref[start : start + q_block, :LANES])
        scores = mm_nt(keys[:n_keys], q) * (1.0 / math.sqrt(HD))
        scores = jnp.where(allowed(n_keys, q_block, start, length), scores, NEGATIVE)
        largest = jnp.max(scores, axis=0, keepdims=True)
        expon = jnp.exp(scores - largest)
        totals = jnp.sum(expon, axis=0, keepdims=True)
        probs = (expon * (1.0 / totals)).astype(BF)
        mixed = head_join(mm_tn(probs, values[:n_keys])).astype(BF)
        lse_ref[0, b : b + 1, :] = largest + jnp.log(totals)
        if len(outs) == 1:
            outs[0][start : start + q_block] = mixed
        else:
            own_rows = rows // 2
            half, at = start // own_rows, start % own_rows
            mine = idx_ref[2] == half

            @pl.when(mine)
            def _():
                outs[0][at : at + q_block] = mixed

            @pl.when(jnp.logical_not(mine))
            def _():
                outs[1][at : at + q_block] = mixed


def attend(idx, qkv, parts, q_block):
    rows, groups = qkv.shape[0], qkv.shape[1] // (2 * LANES)
    out = jax.ShapeDtypeStruct((rows // parts, groups * LANES), BF)
    return pl.pallas_call(
        functools.partial(attend_kernel, q_block),
        name="attend",
        grid=(groups,),
        out_shape=[out] * parts + [jax.ShapeDtypeStruct((groups, rows // q_block, 2 * q_block), F32)],
        in_specs=[SMEM, pl.BlockSpec((rows, 2 * LANES), lambda g: (0, g))],
        out_specs=[pl.BlockSpec((rows // parts, LANES), lambda g: (0, g))] * parts
        + [pl.BlockSpec((1, rows // q_block, 2 * q_block), lambda g: (g, 0, 0))],
        compiler_params=pltpu.CompilerParams(vmem_limit_bytes=VMEM_LIMIT),
        cost_estimate=pl.CostEstimate(flops=14 << 30, bytes_accessed=4 << 20, transcendentals=0),
    )(idx, qkv)


def attend_back_kernel(q_block, n_grads, idx_ref, qkv_ref, lse_ref, cos_ref, sin_ref, *refs):
    grads, outs = refs[:n_grads], refs[n_grads : 2 * n_grads]
    do_ref, dq_ref, dk_ref, dv_ref = refs[2 * n_grads :]
    rows = qkv_ref.shape[0]
    own_rows = rows // n_grads
    length = idx_ref[3]
    for p in range(n_grads):
        at = pl.multiple_of((p ^ idx_ref[2] if n_grads == 2 else 0) * own_rows, own_rows)
        do_ref[pl.ds(at, own_rows), :] = grads[p][...]
    keys, values = doubled(qkv_ref[:, LANES:])
    dk_ref[...] = jnp.zeros_like(dk_ref)
    dv_ref[...] = jnp.zeros_like(dv_ref)
    scale = 1.0 / math.sqrt(HD)
    for b in range(rows // q_block):
        start, n_keys = b * q_block, (b + 1) * q_block
        q = head_pair(qkv_ref[start : start + q_block, :LANES])
        grad = head_pair(do_ref[start : start + q_block, :])
        scores = mm_nt(keys[:n_keys], q) * scale
        probs = jnp.where(
            allowed(n_keys, q_block, start, length), jnp.exp(scores - lse_ref[0, b : b + 1, :]), 0.0
        )
        prob_grad = mm_nt(values[:n_keys], grad)
        center = jnp.sum(probs * prob_grad, axis=0, keepdims=True)
        score_grad = (probs * (prob_grad - center)).astype(BF)
        dq_ref[start : start + q_block, :] = head_join(mm_tn(score_grad, keys[:n_keys])) * scale
        dk_ref[:n_keys, :] += mm(score_grad, q)
        dv_ref[:n_keys, :] += mm(probs.astype(BF), grad)
    cosine, sine = cos_ref[...], sin_ref[...]
    dq = dq_ref[...]
    dq = (dq * cosine - swap_halves(dq) * sine).astype(BF)
    dk, dv = dk_ref[...] * scale, dv_ref[...]
    dk = dk + pltpu.roll(dk, HD, 1)
    dv = dv + pltpu.roll(dv, HD, 1)
    dk = dk * cosine - swap_halves(dk) * sine
    first = lax.broadcasted_iota(jnp.int32, dk.shape, 1) < HD
    dkv = jnp.where(first, dk, dv).astype(BF)
    if n_grads == 1:
        outs[0][:, :LANES] = dq
        outs[0][:, LANES:] = dkv
    else:
        do_ref[...] = dq
        for p in range(2):
            at = pl.multiple_of((p ^ idx_ref[2]) * own_rows, own_rows)
            outs[p][:, :LANES] = do_ref[pl.ds(at, own_rows), :]
        do_ref[...] = dkv
        for p in range(2):
            at = pl.multiple_of((p ^ idx_ref[2]) * own_rows, own_rows)
            outs[p][:, LANES:] = do_ref[pl.ds(at, own_rows), :]


def attend_back(idx, qkv, lse, cosine, sine, grads, q_block):
    rows, groups, parts = qkv.shape[0], qkv.shape[1] // (2 * LANES), len(grads)
    return pl.pallas_call(
        functools.partial(attend_back_kernel, q_block, parts),
        name="attend_back",
        grid=(groups,),
        out_shape=[jax.ShapeDtypeStruct((rows // parts, groups * 2 * LANES), BF)] * parts,
        in_specs=[
            SMEM,
            pl.BlockSpec((rows, 2 * LANES), lambda g: (0, g)),
            pl.BlockSpec((1, rows // q_block, 2 * q_block), lambda g: (g, 0, 0)),
            pl.BlockSpec((rows, LANES), lambda g: (0, 0)),
            pl.BlockSpec((rows, LANES), lambda g: (0, 0)),
        ]
        + [pl.BlockSpec((rows // parts, LANES), lambda g: (0, g))] * parts,
        out_specs=[pl.BlockSpec((rows // parts, 2 * LANES), lambda g: (0, g))] * parts,
        scratch_shapes=[pltpu.VMEM((rows, LANES), BF)] + [pltpu.VMEM((rows, LANES), F32)] * 3,
        compiler_params=pltpu.CompilerParams(vmem_limit_bytes=VMEM_LIMIT),
        cost_estimate=pl.CostEstimate(flops=30 << 30, bytes_accessed=6 << 20, transcendentals=0),
    )(idx, qkv, lse, cosine, sine, *grads)


def project_out_kernel(n_parts, pieces, x_ref, gain_ref, *refs):
    attns, weights = refs[:n_parts], refs[n_parts : 2 * n_parts]
    hidden_ref, normed_refs = refs[2 * n_parts], refs[2 * n_parts + 1 :]
    rows = x_ref.shape[0] // pieces
    for p in range(pieces):
        at = slice(p * rows, (p + 1) * rows)
        hidden = x_ref[at].astype(F32)
        for a, w in zip(attns, weights, strict=True):
            hidden = hidden + mm_nt(a[at], w[...])
        inverse = lax.rsqrt(jnp.mean(hidden * hidden, axis=-1, keepdims=True) + EPSILON)
        hidden_ref[at] = hidden
        normed_refs[p][...] = (hidden * inverse * gain_ref[...]).astype(BF)


def project_out(x, gain, attns, weights, pieces):
    rows = x.shape[0]
    n = len(attns)
    return call(
        functools.partial(project_out_kernel, n, pieces),
        "project_out",
        [jax.ShapeDtypeStruct((rows, D), F32)] + [jax.ShapeDtypeStruct((rows // pieces, D), BF)] * pieces,
        [VM] * (2 + 2 * n),
        [VM] * (1 + pieces),
        (x, gain.reshape(1, D), *attns, *weights),
        flops=2 * rows * D * D,
        moved=7 << 20,
    )


def hidden_back_kernel(n_parts, pieces, n_sums, valid_ref, hidden_ref, cot_ref, gain_ref, *refs):
    sums, refs = refs[: pieces * n_sums], refs[pieces * n_sums :]
    weights, refs = refs[:n_parts], refs[n_parts:]
    grad_ref, low_ref, gain_grad_ref, attn_refs = refs[0], refs[1], refs[2], refs[3:]
    rows = hidden_ref.shape[0] // pieces
    gain = gain_ref[...]
    gain_grad = jnp.zeros((1, D), F32)
    for p in range(pieces):
        at = slice(p * rows, (p + 1) * rows)
        hidden = hidden_ref[at]
        normed_grad = sums[p * n_sums][...].astype(F32)
        for s in sums[p * n_sums + 1 : (p + 1) * n_sums]:
            normed_grad = normed_grad + s[...].astype(F32)
        inverse = lax.rsqrt(jnp.mean(hidden * hidden, axis=-1, keepdims=True) + EPSILON)
        gain_grad = gain_grad + jnp.sum(normed_grad * (hidden * inverse), axis=0, keepdims=True)
        scaled = normed_grad * gain
        back = inverse * scaled - hidden * (
            inverse * inverse * inverse * jnp.mean(scaled * hidden, axis=-1, keepdims=True)
        )
        dy = jnp.where(valid_ref[at] > 0, cot_ref[at].astype(F32), 0.0)
        total = dy + back
        grad_ref[at] = total
        low = total.astype(BF)
        low_ref[at] = low
        for a, w in zip(attn_refs, weights, strict=True):
            a[at] = mm(low, w[...]).astype(BF)
    gain_grad_ref[...] = gain_grad


def hidden_back(valid, hidden, cotangent, gain, sums, weights):
    rows, pieces, n_sums, n = hidden.shape[0], len(sums), len(sums[0]), len(weights)
    heads = weights[0].shape[1]
    return call(
        functools.partial(hidden_back_kernel, n, pieces, n_sums),
        "hidden_back",
        [
            jax.ShapeDtypeStruct((rows, D), F32),
            jax.ShapeDtypeStruct((rows, D), BF),
            jax.ShapeDtypeStruct((1, D), F32),
        ]
        + [jax.ShapeDtypeStruct((rows, heads), BF)] * n,
        [VM] * (4 + pieces * n_sums + n),
        [VM] * (3 + n),
        (valid, hidden, cotangent, gain.reshape(1, D), *[s for piece in sums for s in piece], *weights),
        flops=2 * rows * D * D,
        moved=10 << 20,
    )


def dispatch_kernel(n_pieces, scaled, pos_ref, gate_ref, *refs):
    pieces, out_ref, rows_ref, sems = refs[:n_pieces], refs[n_pieces], refs[n_pieces + 1], refs[n_pieces + 2]
    height = rows_ref.shape[0] // n_pieces
    copies = [
        pltpu.make_async_copy(piece, rows_ref.at[pl.ds(p * height, height)], sems.at[p])
        for p, piece in enumerate(pieces)
    ]
    for c in copies:
        c.start()
    rank = lax.broadcasted_iota(jnp.int32, (CAP, rows_ref.shape[0]), 0)
    for c in copies:
        c.wait()
    for j in range(out_ref.shape[0]):
        chosen = rank == pos_ref[j : j + 1, :]
        value = gate_ref[j : j + 1, :] if scaled else 1.0
        one_hot = jnp.where(chosen, value, 0.0).astype(BF)
        out_ref[j] = mm(one_hot, rows_ref[...]).astype(BF)


def dispatch(pos, gate, pieces, scaled):
    experts, rows = pos.shape
    return call(
        functools.partial(dispatch_kernel, len(pieces), scaled),
        "dispatch_scaled" if scaled else "dispatch",
        jax.ShapeDtypeStruct((experts, CAP, D), BF),
        [VM, VM] + [ANY] * len(pieces),
        VM,
        (pos, gate, *pieces),
        scratch=[pltpu.VMEM((rows, D), BF), pltpu.SemaphoreType.DMA((len(pieces),))],
        flops=2 * experts * CAP * rows * D,
        moved=5 << 20,
    )


def combine_kernel(n_experts, slot, scaled, n_adds, n_outs, pos_ref, gate_ref, *refs):
    sources, refs = refs[:n_experts], refs[n_experts:]
    adds, outs, (held, sems) = refs[:n_adds], refs[n_adds : n_adds + n_outs], refs[n_adds + n_outs :]
    copies = [
        pltpu.make_async_copy(source.at[slot], held.at[pl.ds(j * CAP, CAP)], sems.at[j])
        for j, source in enumerate(sources)
    ]
    for c in copies:
        c.start()
    for c in copies:
        c.wait()
    width = n_experts * CAP
    rows = pos_ref.shape[0]
    block = 256
    per_out = rows // n_outs
    for b in range(rows // block):
        at = slice(b * block, (b + 1) * block)
        tiles = []
        for first in range(0, width, LANES):
            size = min(LANES, width - first)
            lane = first + lax.broadcasted_iota(jnp.int32, (block, size), 1)
            tile = jnp.zeros((block, size), F32)
            for j in range(first // CAP, (first + size - 1) // CAP + 1):
                target = pos_ref[at, j : j + 1]
                target = jnp.where(target >= 0, target + j * CAP, -1)
                tile = jnp.where(lane == target, gate_ref[at, j : j + 1] if scaled else 1.0, tile)
            tiles.append(tile.astype(BF))
        total = mm(jnp.concatenate(tiles, axis=1), held[...])
        out, inner = outs[b * block // per_out], slice(b * block % per_out, b * block % per_out + block)
        if n_adds:
            total = total + adds[0][at].astype(F32)
        out[inner] = total.astype(BF)


def combine(pos, gate, sources, slot, scaled, add, n_outs):
    rows, n_experts = pos.shape
    adds = [] if add is None else [add]
    return call(
        functools.partial(combine_kernel, n_experts, slot, scaled, len(adds), n_outs),
        "combine_scaled" if scaled else "combine",
        [jax.ShapeDtypeStruct((rows // n_outs, D), BF)] * n_outs,
        [VM, VM] + [ANY] * n_experts + [VM] * len(adds),
        [VM] * n_outs,
        (pos, gate, *sources, *adds),
        scratch=[pltpu.VMEM((n_experts * CAP, D), BF), pltpu.SemaphoreType.DMA((n_experts,))],
        flops=2 * n_experts * CAP * rows * D,
        moved=5 << 20,
    )


def expert_kernel(j, outer, in_rows, down_rows, idx_ref, *refs):
    n_hops = outer - 1
    xs, refs = refs[:GROUP], refs[GROUP:]
    gs, refs = refs[:GROUP], refs[GROUP:]
    own, refs = refs[0], refs[1:]
    lefts, refs = refs[:n_hops], refs[n_hops:]
    rights, refs = refs[:n_hops], refs[n_hops:]
    y_ref, dx_ref, dw_ref = refs[:3]
    x_all, g_all, w_in, w_down, act_all, gug_all, sem_x, sem_g, sem_w, sem_d = refs[3:]
    o, i = idx_ref[0], idx_ref[1]

    def rows_of(sources, held, sems):
        return [
            pltpu.make_async_copy(s.at[j], held.at[pl.ds(n * CAP, CAP)], sems.at[n])
            for n, s in enumerate(sources)
        ]

    def weight_copies(source, at, slot):
        made = []
        for m in range(GROUP):
            place = at * GROUP + (i ^ m)
            made.append(
                pltpu.make_async_copy(
                    source.at[m, pl.ds(0, in_rows)],
                    w_in.at[pl.ds(pl.multiple_of(place * in_rows, in_rows), in_rows)],
                    sem_w.at[slot * GROUP + m],
                )
            )
            made.append(
                pltpu.make_async_copy(
                    source.at[m, pl.ds(in_rows, down_rows)],
                    w_down.at[pl.ds(pl.multiple_of(place * down_rows, down_rows), down_rows)],
                    sem_d.at[slot * GROUP + m],
                )
            )
        return made

    def each_weight(act):
        act(weight_copies(own, o, 0))
        for k in range(1, outer):

            @pl.when(o >= k)
            def _():
                act(weight_copies(lefts[k - 1], o - k, k))

            @pl.when(o + k < outer)
            def _():
                act(weight_copies(rights[k - 1], o + k, n_hops + k))

    def start(made):
        for c in made:
            c.start()

    def wait(made):
        for c in made:
            c.wait()

    each_weight(start)
    copy_x, copy_g = rows_of(xs, x_all, sem_x), rows_of(gs, g_all, sem_g)
    start(copy_x)
    start(copy_g)
    each_weight(wait)
    wait(copy_x)
    wait(copy_g)

    def per_slot(s, carry):
        at = pl.ds(pl.multiple_of(s * CAP, CAP), CAP)
        gate_up = mm(x_all[at, :], w_in[...])
        g, u = gate_up[:, :FF], gate_up[:, FF:]
        sigma = 1.0 / (1.0 + jnp.exp(-g))
        silu = g * sigma
        act = (silu * u).astype(BF)
        act_all[at, :] = act
        y_ref[s] = mm(act, w_down[...]).astype(BF)
        act_grad = mm_nt(g_all[at, :], w_down[...])
        gug_all[at, :FF] = (act_grad * u * sigma * (1.0 + g * (1.0 - sigma))).astype(BF)
        gug_all[at, FF:] = (act_grad * silu).astype(BF)
        dx_ref[s] = mm_nt(gug_all[at, :], w_in[...]).astype(BF)
        return carry

    lax.fori_loop(0, GROUP, per_slot, 0)
    for c in range(outer):
        part = mm_tn(x_all[:, c * GROUP * in_rows : (c + 1) * GROUP * in_rows], gug_all[...]).astype(BF)
        for r in range(GROUP):
            dw_ref[c, i ^ r, :in_rows, :] = part[r * in_rows : (r + 1) * in_rows]
        part = mm_tn(act_all[:, c * GROUP * down_rows : (c + 1) * GROUP * down_rows], g_all[...]).astype(BF)
        for r in range(GROUP):
            dw_ref[c, i ^ r, in_rows:, :] = part[r * down_rows : (r + 1) * down_rows]


def expert(idx, j, outer, in_rows, down_rows, xs, gs, own, lefts, rights):
    n_hops = outer - 1
    total = GROUP * CAP
    packed = in_rows + down_rows
    return call(
        functools.partial(expert_kernel, j, outer, in_rows, down_rows),
        "expert",
        [
            jax.ShapeDtypeStruct((GROUP, CAP, D), BF),
            jax.ShapeDtypeStruct((GROUP, CAP, D), BF),
            jax.ShapeDtypeStruct((outer, GROUP, packed, D), BF),
        ],
        [SMEM] + [ANY] * (2 * GROUP + 1 + 2 * n_hops),
        [VM] * 3,
        (idx, *xs, *gs, own, *lefts, *rights),
        scratch=[
            pltpu.VMEM((total, D), BF),
            pltpu.VMEM((total, D), BF),
            pltpu.VMEM((D, 2 * FF), BF),
            pltpu.VMEM((FF, D), BF),
            pltpu.VMEM((total, FF), BF),
            pltpu.VMEM((total, 2 * FF), BF),
            pltpu.SemaphoreType.DMA((GROUP,)),
            pltpu.SemaphoreType.DMA((GROUP,)),
            pltpu.SemaphoreType.DMA(((1 + 2 * n_hops) * GROUP,)),
            pltpu.SemaphoreType.DMA(((1 + 2 * n_hops) * GROUP,)),
        ],
        flops=18 * total * D * FF,
        moved=15 << 20,
    )


def pack_kernel(n_experts, in_rows, down_rows, idx_ref, in_ref, down_ref, *refs):
    outs, sems = refs[:-1], refs[-1]
    i = idx_ref[1]
    copies = []
    for j in range(n_experts):
        for m in range(GROUP):
            n = j * GROUP + m
            source = (i ^ m) * n_experts + j
            copies.append(
                pltpu.make_async_copy(in_ref.at[source], outs[m].at[j, pl.ds(0, in_rows)], sems.at[2 * n])
            )
            copies.append(
                pltpu.make_async_copy(
                    down_ref.at[source], outs[m].at[j, pl.ds(in_rows, down_rows)], sems.at[2 * n + 1]
                )
            )
    for c in copies:
        c.start()
    for c in copies:
        c.wait()


def pack_weights(idx, expert_in, expert_down):
    experts, in_rows, _ = expert_in.shape
    down_rows = expert_down.shape[1]
    n = experts // GROUP
    return call(
        functools.partial(pack_kernel, n, in_rows, down_rows),
        "pack_weights",
        [jax.ShapeDtypeStruct((n, in_rows + down_rows, D), BF)] * GROUP,
        [SMEM, ANY, ANY],
        [VM] * GROUP,
        (idx, expert_in, expert_down),
        scratch=[pltpu.SemaphoreType.DMA((2 * experts,))],
        moved=6 << 20,
    )


def place():
    d, t = lax.axis_index("dp"), lax.axis_index("tensor")
    return d, t, d // GROUP, d % GROUP


def flip(v, m):
    first, second = v % 2, (v // 2) % 2
    if m & 1:
        v = v + 1 - 2 * first
    if m & 2:
        v = v + 2 - 4 * second
    return v


def greet(outer, distances, tensor):
    d, t, o, _ = place()
    barrier = pltpu.get_barrier_semaphore()
    count = 0
    for m in distances:
        pl.semaphore_signal(barrier, inc=1, device_id=(flip(d, m), t), device_id_type=MESH)
        count += 1
    if tensor:
        pl.semaphore_signal(barrier, inc=1, device_id=(d, 1 - t), device_id_type=MESH)
        count += 1

    @pl.when(o > 0)
    def _():
        pl.semaphore_signal(barrier, inc=1, device_id=(d - GROUP, t), device_id_type=MESH)

    @pl.when(o < outer - 1)
    def _():
        pl.semaphore_signal(barrier, inc=1, device_id=(d + GROUP, t), device_id_type=MESH)

    neighbours = (o + outer - 1) // outer + (2 * outer - 2 - o) // outer
    pl.semaphore_wait(barrier, count + neighbours)


class Hops:
    def __init__(self, outer, steps, sent, came):
        d, t, o, _ = place()
        self.moves = []
        for n, (k, from_left, from_right, to_left, to_right) in enumerate(steps):
            back = outer - 1 - o
            right = pltpu.make_async_remote_copy(
                from_left, to_left, sent.at[2 * n], came.at[2 * n], device_id=(d + GROUP, t), device_id_type=MESH
            )
            left = pltpu.make_async_remote_copy(
                from_right,
                to_right,
                sent.at[2 * n + 1],
                came.at[2 * n + 1],
                device_id=(d - GROUP, t),
                device_id_type=MESH,
            )
            self.moves.append((right, (o >= k - 1) & (back >= 1), o >= k))
            self.moves.append((left, (back >= k - 1) & (o >= 1), back >= k))

    def start(self):
        for copy, sends, _ in self.moves:
            pl.when(sends)(copy.start)

    def wait(self):
        for copy, sends, receives in self.moves:
            pl.when(sends)(copy.wait_send)
            pl.when(receives)(copy.wait_recv)


def greet_all(outer):
    d, t, o, i = place()
    barrier = pltpu.get_barrier_semaphore()
    for m in range(1, GROUP):
        pl.semaphore_signal(barrier, inc=1, device_id=(flip(d, m), t), device_id_type=MESH)
    pl.semaphore_signal(barrier, inc=1, device_id=(d, 1 - t), device_id_type=MESH)
    for k in range(1, outer):
        pl.semaphore_signal(barrier, inc=1, device_id=((o + k) % outer * GROUP + i, t), device_id_type=MESH)
    pl.semaphore_wait(barrier, GROUP - 1 + outer)


def to_x(src, dst, sent, came):
    d, t, _, _ = place()
    return pltpu.make_async_remote_copy(src, dst, sent, came, device_id=(d, 1 - t), device_id_type=MESH)


def to_dp(m, src, dst, sent, came):
    d, t, _, _ = place()
    return pltpu.make_async_remote_copy(src, dst, sent, came, device_id=(flip(d, m), t), device_id_type=MESH)


def remote_call(kernel, name, collective_id, out_shape, in_specs, out_specs, args, scratch, flops):
    return pl.pallas_call(
        kernel,
        name=name,
        out_shape=out_shape,
        in_specs=in_specs,
        out_specs=out_specs,
        scratch_shapes=list(scratch),
        compiler_params=pltpu.CompilerParams(
            vmem_limit_bytes=VMEM_LIMIT, collective_id=collective_id, has_side_effects=True
        ),
        cost_estimate=pl.CostEstimate(flops=flops, bytes_accessed=8 << 20, transcendentals=0),
    )(*args)


def collect_kernel(outer, in_rows, down_rows, shard_ref, normed_ref, gates_ref, freq_ref, in_ref, down_ref, *refs):
    w_ref, other_ref, cos_ref, sin_ref, pos_ref, gate_ref, posc_ref, gatec_ref = refs[:8]
    own_refs, packed_refs, to_left, to_right = refs[8:10], refs[10:12], refs[12], refs[13]
    packed, gates_all, before, l_w, l_in, l_down, l_own = refs[14:21]
    s_z, r_z, s_y, r_y, s_c, r_c, s_x, r_x, s_g, r_g, s_a, r_a, s_hop, r_hop = refs[21:]
    d, t, o, i = place()
    each = shard_ref.shape[0]
    width = w_ref.shape[1] // 2
    own_width = shard_ref.shape[1]
    n_local = in_ref.shape[0]
    n = n_local // GROUP
    slot_rows = gates_all.shape[2]
    half = slot_rows // 4

    def block(which, index):
        return pl.ds(pl.multiple_of((which * GROUP + index) * each, each), each)

    def lanes(h):
        return pl.ds(h * width, width)

    local = pltpu.make_async_copy(shard_ref, w_ref.at[block(o, i), pl.ds(0, own_width)], l_w)
    local.start()
    packs = []
    for j in range(n):
        for m in range(GROUP):
            source, k = flip(i, m) * n + j, j * GROUP + m
            packs.append(
                (
                    pltpu.make_async_copy(in_ref.at[source], packed.at[j, m, pl.ds(0, in_rows)], l_in.at[k]),
                    pltpu.make_async_copy(down_ref.at[source], packed.at[j, m, pl.ds(in_rows, down_rows)], l_down.at[k]),
                )
            )
    for pair in packs:
        for c in pair:
            c.start()
    greet_all(outer)

    x_moves = [
        to_x(shard_ref.at[:, pl.ds(width, own_width - width)], w_ref.at[block(o, i), pl.ds(own_width, 2 * width - own_width)], s_x.at[0], r_x.at[0]),
        to_x(normed_ref, other_ref, s_x.at[1], r_x.at[1]),
    ]
    g_x = [
        to_x(
            gates_ref.at[:, pl.ds(p * half, half)],
            gates_all.at[0, :, pl.ds((2 * p + 1) * half, half)],
            s_g.at[p],
            r_g.at[p],
        )
        for p in range(2)
    ]
    g_y = to_dp(2, gates_all.at[0], gates_all.at[1], s_g.at[2], r_g.at[2])
    g_c = [to_dp(1, gates_all.at[s], gates_all.at[2 + s], s_g.at[3 + s], r_g.at[3 + s]) for s in range(2)]

    def z_move(k, h):
        peer = (o + k) % outer
        source = shard_ref.at[:, pl.ds(0, width)] if h == 0 else w_ref.at[block(o, i), lanes(1)]
        return pltpu.make_async_remote_copy(
            source,
            w_ref.at[block(o, i), lanes(h)],
            s_z.at[2 * k - 2 + h],
            r_z.at[2 * k - 2 + h],
            device_id=(peer * GROUP + i, t),
            device_id_type=MESH,
        )

    def near_source(b, h):
        if b == 0 and h == 0:
            return shard_ref.at[:, pl.ds(0, width)]
        return w_ref.at[block((o + outer - b) % outer, i), lanes(h)]

    def y_move(b, h):
        target = w_ref.at[block((o + outer - b) % outer, i), lanes(h)]
        return to_dp(2, near_source(b, h), target, s_y.at[2 * b + h], r_y.at[2 * b + h])

    def c_move(b, far, h):
        target = w_ref.at[block((o + outer - b) % outer, flip(i, 2) if far else i), lanes(h)]
        source = target if far else near_source(b, h)
        k = (2 * b + far) * 2 + h
        return to_dp(1, source, target, s_c.at[k], r_c.at[k])

    def weights_move(j, m):
        return to_dp(m, packed.at[j, m], own_refs[j].at[m], s_a.at[3 * j + m - 1], r_a.at[3 * j + m - 1])

    keeps = [pltpu.make_async_copy(packed.at[j, 0], own_refs[j].at[0], l_own.at[j]) for j in range(2)]
    stays = [pltpu.make_async_copy(packed.at[2 + j], packed_refs[j], l_own.at[2 + j]) for j in range(2)]
    hops = Hops(outer, [(1, own_refs[0], own_refs[0], to_left, to_right)], s_hop, r_hop)

    def packed_there(j):
        for pair in packs[j * GROUP : (j + 1) * GROUP]:
            for c in pair:
                c.wait()

    x_moves[0].start()
    for c in g_x:
        c.start()
    for k in range(1, outer):
        z_move(k, 0).start()
    y_move(0, 0).start()
    c_move(0, 0, 0).start()
    packed_there(0)
    for m in range(1, GROUP):
        weights_move(0, m).start()
    keeps[0].start()
    x_moves[1].start()
    local.wait()
    x_moves[0].wait()
    for k in range(1, outer):
        z_move(k, 1).start()
    packed_there(1)
    keeps[1].start()
    for j in range(2):
        packed_there(2 + j)
        stays[j].start()
    gates_all[0, :, 0:half] = gates_ref[:, 0:half]
    gates_all[0, :, 2 * half : 3 * half] = gates_ref[:, half:]
    block_rows = 128

    def table(b, carry):
        at = pl.ds(pl.multiple_of(b * block_rows, block_rows), block_rows)
        row = b * block_rows + lax.broadcasted_iota(jnp.int32, (block_rows, LANES), 0)
        angles = row.astype(F32) * freq_ref[...]
        lane = lax.broadcasted_iota(jnp.int32, (block_rows, LANES), 1)
        sine = jnp.sin(angles)
        cos_ref[at, :] = jnp.cos(angles)
        sin_ref[at, :] = jnp.where(lane % HD < HD // 2, -sine, sine)
        return carry

    lax.fori_loop(0, slot_rows // block_rows, table, 0)
    for c in g_x:
        c.wait()
    g_y.start()
    g_c[0].start()
    for k in range(1, outer):
        z_move(k, 0).wait_recv()
        y_move(k, 0).start()
        c_move(k, 0, 0).start()
    for m in range(1, GROUP):
        weights_move(1, m).start()
    for b in range(1):
        y_move(b, 1).start()
        c_move(b, 0, 1).start()
    before[...] = (
        lax.broadcasted_iota(jnp.int32, before.shape, 0) < lax.broadcasted_iota(jnp.int32, before.shape, 1)
    ).astype(F32).astype(BF)
    keeps[0].wait()
    for m in range(1, GROUP):
        weights_move(0, m).wait_recv()
    hops.start()
    g_y.wait()
    g_c[1].start()
    for k in range(1, outer):
        z_move(k, 1).wait_recv()
        y_move(k, 1).start()
        c_move(k, 0, 1).start()
    for b in range(outer):
        y_move(b, 0).wait_recv()
        c_move(b, 1, 0).start()
    for c in g_c:
        c.wait()
    n_all = gates_all.shape[1]
    first = t * n_local + i * n
    pick = (
        lax.broadcasted_iota(jnp.int32, (8, n_all), 1) == lax.broadcasted_iota(jnp.int32, (8, n_all), 0) + first
    ).astype(F32).astype(BF)
    for s in range(GROUP):
        gate = mm(pick, gates_all[s])
        rank = mm((gate > 0).astype(F32).astype(BF), before[...])
        gate_ref[s] = gate[:n]
        pos_ref[s] = jnp.where(gate > 0, rank, -1.0).astype(jnp.int32)[:n]
        gate = lax.dot_general(gates_all[s], pick, (((0,), (1,)), ((), ())), preferred_element_type=F32)
        rank = mm_tn(before[...], (gate > 0).astype(F32).astype(BF))
        gatec_ref[s] = gate[:, :n]
        posc_ref[s] = jnp.where(gate > 0, rank, -1.0).astype(jnp.int32)[:, :n]
    for b in range(outer):
        y_move(b, 1).wait_recv()
        c_move(b, 1, 1).start()
    for k in range(1, outer):
        for h in range(2):
            z_move(k, h).wait_send()
    for b in range(outer):
        for h in range(2):
            y_move(b, h).wait_send()
            c_move(b, 0, h).wait()
            c_move(b, 1, h).wait()
    for m in range(1, GROUP):
        weights_move(0, m).wait_send()
        weights_move(1, m).wait()
    x_moves[1].wait()
    keeps[1].wait()
    for c in stays:
        c.wait()
    hops.wait()


def collect(outer, shard, normed, gates, frequency, expert_in, expert_down):
    each, own_width = shard.shape
    width = own_width * 2 // 3
    rows = normed.shape[0]
    experts, in_rows, _ = expert_in.shape
    down_rows = expert_down.shape[1]
    n = experts // GROUP
    packed = in_rows + down_rows
    hop = jax.ShapeDtypeStruct((GROUP, packed, D), BF)
    dma = pltpu.SemaphoreType.DMA
    out = remote_call(
        functools.partial(collect_kernel, outer, in_rows, down_rows),
        "collect",
        13,
        [
            jax.ShapeDtypeStruct((D, 2 * width), BF),
            jax.ShapeDtypeStruct((rows, D), BF),
            jax.ShapeDtypeStruct((2 * rows, LANES), F32),
            jax.ShapeDtypeStruct((2 * rows, LANES), F32),
            jax.ShapeDtypeStruct((GROUP, n, 2 * rows), jnp.int32),
            jax.ShapeDtypeStruct((GROUP, n, 2 * rows), F32),
            jax.ShapeDtypeStruct((GROUP, 2 * rows, n), jnp.int32),
            jax.ShapeDtypeStruct((GROUP, 2 * rows, n), F32),
        ]
        + [hop] * 6,
        [VM] * 4 + [ANY] * 2,
        [VM] * 8 + [ANY] * 6,
        (shard, normed, gates, frequency, expert_in, expert_down),
        [
            pltpu.VMEM((n, GROUP, packed, D), BF),
            pltpu.VMEM((GROUP, gates.shape[0], 2 * rows), BF),
            pltpu.VMEM((2 * rows, 2 * rows), BF),
            dma,
            dma((experts,)),
            dma((experts,)),
            dma((4,)),
            dma((2 * outer - 2,)),
            dma((2 * outer - 2,)),
            dma((2 * outer,)),
            dma((2 * outer,)),
            dma((4 * outer,)),
            dma((4 * outer,)),
            dma((2,)),
            dma((2,)),
            dma((5,)),
            dma((5,)),
            dma((6,)),
            dma((6,)),
            dma((2,)),
            dma((2,)),
        ],
        4 << 30,
    )
    return out[:8], out[8:10], out[10:12], out[12], out[13]


def attention_kernel(outer, q_block, n_steps, len_ref, own_ref, other_ref, w_ref, cos_ref, sin_ref, x_ref, gain_ref, *refs):
    width = w_ref.shape[1] // 2
    heads = width // 2
    cot_ref, ready, packed_refs, refs = refs[0], refs[1], refs[2:4], refs[4:]
    qkv_out, lse_ref, attn_ref, come_ref, hidden_out, na_ref, nb_ref = refs[:7]
    refs = refs[7:]
    dy_outs, own_refs, refs = refs[:4], refs[4:6], refs[6:]
    to_left, refs = refs[:n_steps], refs[n_steps:]
    to_right, refs = refs[:n_steps], refs[n_steps:]
    send_ref, s_hop, r_hop, s_later, r_later, s_dy, r_dy, s_at, r_at, s_a, r_a, l_own, qkv_ref, hidden_ref, o_sem = refs
    qkv_copy = pltpu.make_async_copy(qkv_ref, qkv_out, o_sem.at[0])
    hidden_copy = pltpu.make_async_copy(hidden_ref, hidden_out, o_sem.at[1])
    d, t, o, i = place()
    length = len_ref[0]
    rows = own_ref.shape[0]
    groups = width // (2 * LANES)
    greet(outer, (1, 2, 3), True)
    hops = Hops(outer, [(1, ready, ready, to_left[0], to_right[0])], s_hop, r_hop)
    later = [
        Hops(outer, [(1, own_refs[k], own_refs[k], to_left[1 + k], to_right[1 + k])], s_later.at[k], r_later.at[k])
        for k in range(2)
    ]
    keeps = [pltpu.make_async_copy(packed_refs[k].at[0], own_refs[k].at[0], l_own.at[k]) for k in range(2)]
    weights = [
        to_dp(m, packed_refs[k].at[m], own_refs[k].at[m], s_a.at[3 * k + m - 1], r_a.at[3 * k + m - 1])
        for k in range(2)
        for m in range(1, GROUP)
    ]
    hops.start()
    for copy in (*weights, *keeps):
        copy.start()
    ax, bx, ay, by = dy_outs
    dy_a, dy_b = (cot_ref.at[pl.ds(p * rows // 2, rows // 2)] for p in range(2))
    dys = [
        to_x(dy_a, ax, s_dy.at[0], r_dy.at[0]),
        to_dp(2, dy_b, by, s_dy.at[1], r_dy.at[1]),
        to_x(dy_b, bx, s_dy.at[2], r_dy.at[2]),
        to_dp(2, dy_a, ay, s_dy.at[3], r_dy.at[3]),
    ]

    block = 256
    key_lanes = lax.broadcasted_iota(jnp.int32, (block, LANES), 1) < HD
    for part, source in enumerate((own_ref, other_ref)):

        def project(b, carry, part=part, source=source):
            here = pl.ds(pl.multiple_of(b * block, block), block)
            at = pl.multiple_of((t if part == 0 else 1 - t) * rows + b * block, block)
            projected = mm(source[here, :], w_ref[:, :width])
            cosine, sine = cos_ref[pl.ds(at, block), :], sin_ref[pl.ds(at, block), :]
            for g in range(groups):
                q = projected[:, g * 2 * LANES : g * 2 * LANES + LANES]
                kv = projected[:, g * 2 * LANES + LANES : (g + 1) * 2 * LANES]
                q = q * cosine + swap_halves(q) * sine
                kv = jnp.where(key_lanes, kv * cosine + swap_halves(kv) * sine, kv)
                qkv_ref[pl.ds(at, block), g * 2 * LANES : g * 2 * LANES + LANES] = q.astype(BF)
                qkv_ref[pl.ds(at, block), g * 2 * LANES + LANES : (g + 1) * 2 * LANES] = kv.astype(BF)
            return carry

        lax.fori_loop(0, rows // block, project, 0)

    for copy in dys:
        copy.start()

    def exchange(g):
        lanes = pl.ds(pl.multiple_of(g * LANES, LANES), LANES)
        return to_x(send_ref.at[:, lanes], come_ref.at[:, lanes], s_at.at[g], r_at.at[g])

    def per_group(g, carry):
        q_lanes = pl.ds(pl.multiple_of(g * 2 * LANES, LANES), LANES)
        kv_lanes = pl.ds(pl.multiple_of(g * 2 * LANES + LANES, LANES), LANES)
        o_lanes = pl.ds(pl.multiple_of(g * LANES, LANES), LANES)
        keys, values = doubled(qkv_ref[:, kv_lanes])
        for b in range(2 * rows // q_block):
            start, n_keys = b * q_block, (b + 1) * q_block
            q = head_pair(qkv_ref[start : start + q_block, q_lanes])
            scores = mm_nt(keys[:n_keys], q) * (1.0 / math.sqrt(HD))
            scores = jnp.where(allowed(n_keys, q_block, start, length), scores, NEGATIVE)
            largest = jnp.max(scores, axis=0, keepdims=True)
            expon = jnp.exp(scores - largest)
            totals = jnp.sum(expon, axis=0, keepdims=True)
            probs = (expon * (1.0 / totals)).astype(BF)
            mixed = head_join(mm_tn(probs, values[:n_keys])).astype(BF)
            lse_ref[g, b : b + 1, :] = largest + jnp.log(totals)
            half, inner = start // rows, start % rows

            @pl.when(t == half)
            def _():
                attn_ref[inner : inner + q_block, o_lanes] = mixed

            @pl.when(t != half)
            def _():
                send_ref[inner : inner + q_block, o_lanes] = mixed

        exchange(g).start()

        for k in range(2):

            @pl.when(g == k)
            def _(k=k):
                for copy in (*weights[(GROUP - 1) * k : (GROUP - 1) * (k + 1)], keeps[k]):
                    copy.wait()
                later[k].start()

        return carry

    lax.fori_loop(0, groups, per_group, 0)

    qkv_copy.start()

    def settle(g, carry):
        exchange(g).wait()
        return carry

    for p, normed_ref in enumerate((na_ref, nb_ref)):
        at = slice(p * rows // 2, (p + 1) * rows // 2)
        hidden_ref[at] = x_ref[at].astype(F32) + mm_nt(attn_ref[at], w_ref[:, width : width + heads])
    lax.fori_loop(0, groups, settle, 0)
    for p, normed_ref in enumerate((na_ref, nb_ref)):
        at = slice(p * rows // 2, (p + 1) * rows // 2)
        hidden = hidden_ref[at] + mm_nt(come_ref[at], w_ref[:, width + heads :])
        inverse = lax.rsqrt(jnp.mean(hidden * hidden, axis=-1, keepdims=True) + EPSILON)
        hidden_ref[at] = hidden
        normed_ref[...] = (hidden * inverse * gain_ref[...]).astype(BF)
    hidden_copy.start()
    for copy in dys:
        copy.wait()
    hops.wait()
    for one in later:
        one.wait()
    qkv_copy.wait()
    hidden_copy.wait()


def attention(outer, q_block, length, own, other, weights_full, cosine, sine, x, gain, cotangent, ready, packed):
    rows, groups = own.shape[0], weights_full.shape[1] // (4 * LANES)
    n = 3
    piece = jax.ShapeDtypeStruct((rows // 2, D), BF)
    hop = jax.ShapeDtypeStruct(ready.shape, BF)
    out = remote_call(
        functools.partial(attention_kernel, outer, q_block, n),
        "attention",
        1,
        [
            jax.ShapeDtypeStruct((2 * rows, groups * 2 * LANES), BF),
            jax.ShapeDtypeStruct((groups, 2 * rows // q_block, 2 * q_block), F32),
            jax.ShapeDtypeStruct((rows, groups * LANES), BF),
            jax.ShapeDtypeStruct((rows, groups * LANES), BF),
            jax.ShapeDtypeStruct((rows, D), F32),
            piece,
            piece,
        ]
        + [piece] * 4
        + [hop] * (2 + 2 * n),
        [SMEM] + [VM] * 7 + [ANY] * 4,
        [ANY] + [VM] * 3 + [ANY] + [VM] * 2 + [ANY] * (6 + 2 * n),
        (length, own, other, weights_full, cosine, sine, x, gain.reshape(1, D), cotangent, ready, *packed),
        [
            pltpu.VMEM((rows, groups * LANES), BF),
            pltpu.SemaphoreType.DMA((2,)),
            pltpu.SemaphoreType.DMA((2,)),
            pltpu.SemaphoreType.DMA((2, 2)),
            pltpu.SemaphoreType.DMA((2, 2)),
            pltpu.SemaphoreType.DMA((4,)),
            pltpu.SemaphoreType.DMA((4,)),
            pltpu.SemaphoreType.DMA((groups,)),
            pltpu.SemaphoreType.DMA((groups,)),
            pltpu.SemaphoreType.DMA((6,)),
            pltpu.SemaphoreType.DMA((6,)),
            pltpu.SemaphoreType.DMA((2,)),
            pltpu.VMEM((2 * rows, groups * 2 * LANES), BF),
            pltpu.VMEM((rows, D), F32),
            pltpu.SemaphoreType.DMA((2,)),
        ],
        30 << 30,
    )
    return out[:7], out[7:11], out[11:13], out[13 : 13 + n], out[13 + n :]


def one_hot_rows(pos, gate, j, n_rows):
    rank = lax.broadcasted_iota(jnp.int32, (CAP, n_rows), 0)
    chosen = rank == pos[j : j + 1, :]
    return jnp.where(chosen, 1.0 if gate is None else gate[j : j + 1, :], 0.0).astype(BF)


def spread_kernel(outer, steps, pos_ref, gate_ref, na_ref, nb_ref, *refs):
    n_steps = len(steps)
    cot_ref, dy_refs, refs = refs[0], refs[1:5], refs[5:]
    from_left, refs = refs[:n_steps], refs[n_steps:]
    from_right, refs = refs[:n_steps], refs[n_steps:]
    n_ref, dyx_ref, og_out = refs[:3]
    refs = refs[3:]
    to_left, refs = refs[:n_steps], refs[n_steps:]
    to_right, refs = refs[:n_steps], refs[n_steps:]
    held, s_hop, r_hop, s_n, r_n, s_d, r_d, l_sem, og_ref, o_sem = refs
    height = na_ref.shape[0]
    n_experts = og_ref.shape[1]
    leave = [pltpu.make_async_copy(og_ref.at[s % 2], og_out.at[s], o_sem.at[s]) for s in range(GROUP)]
    greet(outer, (1, 2), True)
    n_ax = to_x(na_ref, n_ref.at[0, 1], s_n.at[0], r_n.at[0])
    n_by = to_dp(2, nb_ref, n_ref.at[1, 2], s_n.at[1], r_n.at[1])
    n_bx = to_x(nb_ref, n_ref.at[0, 3], s_n.at[2], r_n.at[2])
    n_ay = to_dp(2, na_ref, n_ref.at[1, 0], s_n.at[3], r_n.at[3])
    n_axy = to_dp(2, n_ref.at[0, 1], n_ref.at[1, 1], s_n.at[4], r_n.at[4])
    n_bxy = to_x(n_ref.at[1, 2], n_ref.at[1, 3], s_n.at[5], r_n.at[5])
    core = {}
    for n, (s, p) in enumerate([(s, p) for s in range(2) for p in range(4)]):
        source = na_ref if (s, p) == (0, 0) else nb_ref if (s, p) == (0, 2) else n_ref.at[s, p]
        core[s, p] = to_dp(1, source, n_ref.at[2 + s, p], s_n.at[6 + n], r_n.at[6 + n])
    for copy in (n_ax, n_by, n_bx, n_ay):
        copy.start()
    d_a, d_b = (cot_ref.at[pl.ds(p * height, height)] for p in range(2))
    d_ax, d_bx, d_ay, d_by = dy_refs
    d_axy = to_dp(2, d_ax, dyx_ref.at[0, 1], s_d.at[0], r_d.at[0])
    d_bxy = to_x(d_by, dyx_ref.at[0, 3], s_d.at[1], r_d.at[1])
    d_axy.start()
    d_bxy.start()
    d_near = [[d_a, d_ax, d_b, d_bx], [d_ay, dyx_ref.at[0, 1], d_by, dyx_ref.at[0, 3]]]
    d_core = {}
    for n, (s, p) in enumerate([(s, p) for s in range(2) for p in range(4)]):
        d_core[s, p] = to_dp(1, d_near[s][p], dyx_ref.at[1 + s, p], s_d.at[2 + n], r_d.at[2 + n])
    for key in ((0, 0), (0, 1), (0, 2), (0, 3), (1, 0), (1, 2)):
        d_core[key].start()
    core[0, 0].start()
    core[0, 2].start()
    hops = Hops(
        outer,
        [(k, a, b, l, r) for k, a, b, l, r in zip(steps, from_left, from_right, to_left, to_right, strict=True)],
        s_hop,
        r_hop,
    )
    hops.start()

    def load(s):
        pieces = d_near[s] if s < 2 else [dyx_ref.at[s - 1, p] for p in range(4)]
        return [
            pltpu.make_async_copy(piece, held.at[pl.ds(p * height, height)], l_sem.at[p])
            for p, piece in enumerate(pieces)
        ]

    def give(s):
        copies = load(s)
        for c in copies:
            c.start()
        for c in copies:
            c.wait()
        if s >= 2:
            leave[s - 2].wait()

        def one(j, carry):
            rank = lax.broadcasted_iota(jnp.int32, (CAP, 4 * height), 0)
            chosen = rank == pos_ref[s, pl.ds(j, 1), :]
            one_hot = jnp.where(chosen, gate_ref[s, pl.ds(j, 1), :], 0.0).astype(BF)
            og_ref[s % 2, j] = mm(one_hot, held[...]).astype(BF)
            return carry

        lax.fori_loop(0, n_experts, one, 0)
        leave[s].start()

    give(0)
    n_ax.wait()
    n_by.wait()
    n_axy.start()
    n_bxy.start()
    core[0, 1].start()
    core[1, 2].start()
    d_axy.wait()
    d_bxy.wait()
    d_core[1, 1].start()
    d_core[1, 3].start()
    give(1)
    n_bx.wait()
    n_ay.wait()
    core[0, 3].start()
    core[1, 0].start()
    for p in range(4):
        d_core[0, p].wait()
    give(2)
    n_axy.wait()
    n_bxy.wait()
    core[1, 1].start()
    core[1, 3].start()
    for p in range(4):
        d_core[1, p].wait()
    give(3)
    for key in core:
        core[key].wait()
    for s in range(2, GROUP):
        leave[s].wait()
    hops.wait()


def spread(outer, pos, gate, normed, dys, steps, from_left, from_right):
    height = normed[0].shape[0]
    n, n_experts = len(steps), pos.shape[1]
    weights = [jax.ShapeDtypeStruct(s.shape, BF) for s in from_left]
    out = remote_call(
        functools.partial(spread_kernel, outer, steps),
        "spread",
        2,
        [
            jax.ShapeDtypeStruct((GROUP, 4, height, D), BF),
            jax.ShapeDtypeStruct((3, 4, height, D), BF),
            jax.ShapeDtypeStruct((GROUP, n_experts, CAP, D), BF),
        ]
        + weights * 2,
        [VM] * 2 + [ANY] * (2 + 5 + 2 * n),
        [ANY] * (3 + 2 * n),
        (pos, gate, *normed, *dys, *from_left, *from_right),
        [
            pltpu.VMEM((4 * height, D), BF),
            pltpu.SemaphoreType.DMA((2 * n,)),
            pltpu.SemaphoreType.DMA((2 * n,)),
            pltpu.SemaphoreType.DMA((14,)),
            pltpu.SemaphoreType.DMA((14,)),
            pltpu.SemaphoreType.DMA((10,)),
            pltpu.SemaphoreType.DMA((10,)),
            pltpu.SemaphoreType.DMA((4,)),
            pltpu.VMEM((2, n_experts, CAP, D), BF),
            pltpu.SemaphoreType.DMA((GROUP,)),
        ],
        12 << 30,
    )
    return out[0], out[2], out[3 : 3 + n], out[3 + n :]


def hand_out_kernel(outer, steps, pos_ref, na_ref, nb_ref, n_ref, *refs):
    n_steps = len(steps)
    from_left, refs = refs[:n_steps], refs[n_steps:]
    from_right, refs = refs[:n_steps], refs[n_steps:]
    x_out, refs = refs[0], refs[1:]
    to_left, refs = refs[:n_steps], refs[n_steps:]
    to_right, refs = refs[:n_steps], refs[n_steps:]
    held, s_hop, r_hop, l_sem, x_ref, o_sem = refs
    leave = [pltpu.make_async_copy(x_ref.at[s % 2], x_out.at[s], o_sem.at[s]) for s in range(GROUP)]
    height = na_ref.shape[0]
    n_experts = x_ref.shape[1]
    greet(outer, (), False)
    hops = Hops(
        outer,
        [(k, a, b, l, r) for k, a, b, l, r in zip(steps, from_left, from_right, to_left, to_right, strict=True)],
        s_hop,
        r_hop,
    )
    hops.start()

    def load(s):
        pieces = [na_ref, n_ref.at[0, 1], nb_ref, n_ref.at[0, 3]] if s == 0 else [n_ref.at[s, p] for p in range(4)]
        return [
            pltpu.make_async_copy(piece, held.at[s % 2, pl.ds(p * height, height)], l_sem.at[s % 2, p])
            for p, piece in enumerate(pieces)
        ]

    for c in load(0):
        c.start()
    for s in range(GROUP):
        if s + 1 < GROUP:
            for c in load(s + 1):
                c.start()
        for c in load(s):
            c.wait()
        if s >= 2:
            leave[s - 2].wait()

        def one(j, carry, s=s):
            rank = lax.broadcasted_iota(jnp.int32, (CAP, 4 * height), 0)
            one_hot = jnp.where(rank == pos_ref[s, pl.ds(j, 1), :], 1.0, 0.0).astype(BF)
            x_ref[s % 2, j] = mm(one_hot, held[s % 2]).astype(BF)
            return carry

        lax.fori_loop(0, n_experts, one, 0)
        leave[s].start()
    for s in range(2, GROUP):
        leave[s].wait()
    hops.wait()


def hand_out(outer, pos, normed, gathered, steps, from_left, from_right):
    height = normed[0].shape[0]
    n, n_experts = len(steps), pos.shape[1]
    weights = [jax.ShapeDtypeStruct(s.shape, BF) for s in from_left]
    out = remote_call(
        functools.partial(hand_out_kernel, outer, steps),
        "hand_out",
        3,
        [jax.ShapeDtypeStruct((GROUP, n_experts, CAP, D), BF)] + weights * 2,
        [VM] + [ANY] * (3 + 2 * n),
        [ANY] * (1 + 2 * n),
        (pos, *normed, gathered, *from_left, *from_right),
        [
            pltpu.VMEM((2, 4 * height, D), BF),
            pltpu.SemaphoreType.DMA((2 * n,)),
            pltpu.SemaphoreType.DMA((2 * n,)),
            pltpu.SemaphoreType.DMA((2, 4)),
            pltpu.VMEM((2, n_experts, CAP, D), BF),
            pltpu.SemaphoreType.DMA((GROUP,)),
        ],
        12 << 30,
    )
    return out[0], out[1 : 1 + n], out[1 + n :]


def expert_step_kernel(j, outer, in_rows, down_rows, steps, sum_steps, x_ref, g_ref, own, *refs):
    n_hops, n_steps, n_sums = outer - 1, len(steps), len(sum_steps)
    lefts, refs = refs[:n_hops], refs[n_hops:]
    rights, refs = refs[:n_hops], refs[n_hops:]
    from_left, refs = refs[:n_steps], refs[n_steps:]
    from_right, refs = refs[:n_steps], refs[n_steps:]
    dws, refs = refs[:n_sums], refs[n_sums:]
    was_l, refs = refs[:n_sums], refs[n_sums:]
    was_r, refs = refs[:n_sums], refs[n_sums:]
    y_out, dx_out, dw_out = refs[:3]
    refs = refs[3:]
    to_left, refs = refs[:n_steps], refs[n_steps:]
    to_right, refs = refs[:n_steps], refs[n_steps:]
    sum_left, refs = refs[:n_sums], refs[n_sums:]
    sum_right, refs = refs[:n_sums], refs[n_sums:]
    x_all, g_all, w_in, w_down, act_all, gug_all, sem_x, sem_g, sem_w, sem_d, s_hop, r_hop = refs[:12]
    (y_ref, dx_ref, dw_ref, o_sem), refs = refs[12:16], refs[16:]
    _, _, o, i = place()
    greet(outer, (), False)
    sums = Sums(outer, sum_steps, dws, was_l, was_r, sum_left, sum_right, *refs)
    if n_steps:
        hops = Hops(
            outer,
            [(k, a, b, l, r) for k, a, b, l, r in zip(steps, from_left, from_right, to_left, to_right, strict=True)],
            s_hop,
            r_hop,
        )
        hops.start()

    def rows_of(source, held, sems):
        return [
            pltpu.make_async_copy(source.at[n, j], held.at[pl.ds(n * CAP, CAP)], sems.at[n]) for n in range(GROUP)
        ]

    def weight_copies(source, at, slot):
        made = []
        for m in range(GROUP):
            where = at * GROUP + flip(i, m)
            made.append(
                pltpu.make_async_copy(
                    source.at[m, pl.ds(0, in_rows)],
                    w_in.at[pl.ds(pl.multiple_of(where * in_rows, in_rows), in_rows)],
                    sem_w.at[slot * GROUP + m],
                )
            )
            made.append(
                pltpu.make_async_copy(
                    source.at[m, pl.ds(in_rows, down_rows)],
                    w_down.at[pl.ds(pl.multiple_of(where * down_rows, down_rows), down_rows)],
                    sem_d.at[slot * GROUP + m],
                )
            )
        return made

    def each_weight(act):
        act(weight_copies(own, o, 0))
        for k in range(1, outer):

            @pl.when(o >= k)
            def _():
                act(weight_copies(lefts[k - 1], o - k, k))

            @pl.when(o + k < outer)
            def _():
                act(weight_copies(rights[k - 1], o + k, n_hops + k))

    def start(made):
        for c in made:
            c.start()

    def wait(made):
        for c in made:
            c.wait()

    sums.load()
    each_weight(start)
    copy_x, copy_g = rows_of(x_ref, x_all, sem_x), rows_of(g_ref, g_all, sem_g)
    start(copy_x)
    start(copy_g)
    sums.send()
    each_weight(wait)
    wait(copy_x)
    wait(copy_g)

    def per_slot(s, carry):
        at = pl.ds(pl.multiple_of(s * CAP, CAP), CAP)
        gate_up = mm(x_all[at, :], w_in[...])
        g, u = gate_up[:, :FF], gate_up[:, FF:]
        sigma = 1.0 / (1.0 + jnp.exp(-g))
        silu = g * sigma
        act = (silu * u).astype(BF)
        act_all[at, :] = act
        y_ref[s] = mm(act, w_down[...]).astype(BF)
        act_grad = mm_nt(g_all[at, :], w_down[...])
        gug_all[at, :FF] = (act_grad * u * sigma * (1.0 + g * (1.0 - sigma))).astype(BF)
        gug_all[at, FF:] = (act_grad * silu).astype(BF)
        dx_ref[s] = mm_nt(gug_all[at, :], w_in[...]).astype(BF)
        for copy in leaving(s):
            copy.start()
        return carry

    def leaving(s):
        return (
            pltpu.make_async_copy(y_ref.at[s], y_out.at[s], o_sem.at[0, s]),
            pltpu.make_async_copy(dx_ref.at[s], dx_out.at[s], o_sem.at[1, s]),
        )

    def gradient(c):
        return pltpu.make_async_copy(dw_ref.at[c], dw_out.at[c], o_sem.at[2, c])

    lax.fori_loop(0, GROUP, per_slot, 0)
    in_block, down_block = GROUP * in_rows, GROUP * down_rows

    def per_owner(c, carry):
        lanes = pl.ds(pl.multiple_of(c * in_block, in_block), in_block)
        part = mm_tn(x_all[:, lanes], gug_all[...]).astype(BF)
        for r in range(GROUP):
            dw_ref[c, flip(i, r), :in_rows, :] = part[r * in_rows : (r + 1) * in_rows]
        lanes = pl.ds(pl.multiple_of(c * down_block, down_block), down_block)
        part = mm_tn(act_all[:, lanes], g_all[...]).astype(BF)
        for r in range(GROUP):
            dw_ref[c, flip(i, r), in_rows:, :] = part[r * down_rows : (r + 1) * down_rows]
        gradient(c).start()
        return carry

    lax.fori_loop(0, outer, per_owner, 0)
    for s in range(GROUP):
        for copy in leaving(s):
            copy.wait()
    for c in range(outer):
        gradient(c).wait()
    if n_steps:
        hops.wait()
    sums.wait()


def expert_step(j, outer, in_rows, down_rows, x, g, own, lefts, rights, hop_plan, sum_plan):
    (steps, from_left, from_right), (sum_steps, dws, was_l, was_r) = hop_plan, sum_plan
    n_hops, n, n_sums = outer - 1, len(steps), len(sum_steps)
    total = GROUP * CAP
    packed = in_rows + down_rows
    weights = [jax.ShapeDtypeStruct(s.shape, BF) for s in from_left]
    shapes = [
        jax.ShapeDtypeStruct((GROUP, CAP, D), BF),
        jax.ShapeDtypeStruct((GROUP, CAP, D), BF),
        jax.ShapeDtypeStruct((outer, GROUP, packed, D), BF),
    ] + weights * 2 + [jax.ShapeDtypeStruct((GROUP, packed, D), BF)] * (2 * n_sums)
    out = remote_call(
        functools.partial(expert_step_kernel, j, outer, in_rows, down_rows, steps, sum_steps),
        "expert_step",
        4 + j,
        shapes,
        [ANY] * (3 + 2 * n_hops + 2 * n + 3 * n_sums),
        [ANY] * (3 + 2 * n + 2 * n_sums),
        (x, g, own, *lefts, *rights, *from_left, *from_right, *dws, *was_l, *was_r),
        [
            pltpu.VMEM((total, D), BF),
            pltpu.VMEM((total, D), BF),
            pltpu.VMEM((D, 2 * FF), BF),
            pltpu.VMEM((FF, D), BF),
            pltpu.VMEM((total, FF), BF),
            pltpu.VMEM((total, 2 * FF), BF),
            pltpu.SemaphoreType.DMA((GROUP,)),
            pltpu.SemaphoreType.DMA((GROUP,)),
            pltpu.SemaphoreType.DMA(((1 + 2 * n_hops) * GROUP,)),
            pltpu.SemaphoreType.DMA(((1 + 2 * n_hops) * GROUP,)),
            pltpu.SemaphoreType.DMA((max(1, 2 * n),)),
            pltpu.SemaphoreType.DMA((max(1, 2 * n),)),
            pltpu.VMEM((GROUP, CAP, D), BF),
            pltpu.VMEM((GROUP, CAP, D), BF),
            pltpu.VMEM((outer, GROUP, packed, D), BF),
            pltpu.SemaphoreType.DMA((3, max(GROUP, outer))),
            *sums_scratch(n_sums, packed),
        ],
        18 * total * D * FF,
    )
    out, rest = out[:3], out[3:]
    return out, rest[:n], rest[n : 2 * n], rest[2 * n : 2 * n + n_sums], rest[2 * n + n_sums :]


class Sums:
    def __init__(self, outer, steps, dws, was_left, was_right, to_left, to_right, message, term, loaded, added, sent, came):
        d, t, o, _ = place()
        back = outer - 1 - o
        self.moves = []
        for n, s in enumerate(steps):
            for side, near, target, was, to, peer in (
                (0, o, outer - s + o, was_left, to_left, d + GROUP),
                (1, back, s - 1 - back, was_right, to_right, d - GROUP),
            ):
                k = 2 * n + side
                own = pltpu.make_async_copy(dws[n].at[target], message.at[k], loaded.at[k])
                before = None if s == 1 else pltpu.make_async_copy(was[n], term.at[side], added.at[k])
                move = pltpu.make_async_remote_copy(
                    message.at[k], to[n], sent.at[k], came.at[k], device_id=(peer, t), device_id_type=MESH
                )
                sends, adds = near <= s - 1, (near <= s - 1) & (near >= 1)
                receives = (near >= 1) & (near <= s)
                self.moves.append((own, before, move, sends, adds, receives, message.at[k], term.at[side]))

    def load(self):
        for own, _, _, sends, *_ in self.moves:
            pl.when(sends)(own.start)

    def send(self):
        for n in range(0, len(self.moves), 2):
            pair = self.moves[n : n + 2]
            for _, before, _, _, adds, *_ in pair:
                if before is not None:
                    pl.when(adds)(before.start)
            for own, before, move, sends, adds, _, message, term in pair:
                pl.when(sends)(own.wait)
                if before is not None:

                    @pl.when(adds)
                    def _(before=before, message=message, term=term):
                        before.wait()

                        def one(m, carry):
                            message[m] = (message[m].astype(F32) + term[m].astype(F32)).astype(BF)
                            return carry

                        lax.fori_loop(0, GROUP, one, 0)

                pl.when(sends)(move.start)

    def wait(self):
        for _, _, move, sends, _, receives, *_ in self.moves:
            pl.when(sends)(move.wait_send)
            pl.when(receives)(move.wait_recv)


def sums_scratch(n, packed):
    n = max(1, n)
    return [
        pltpu.VMEM((2 * n, GROUP, packed, D), BF),
        pltpu.VMEM((2, GROUP, packed, D), BF),
        pltpu.SemaphoreType.DMA((2 * n,)),
        pltpu.SemaphoreType.DMA((2 * n,)),
        pltpu.SemaphoreType.DMA((2 * n,)),
        pltpu.SemaphoreType.DMA((2 * n,)),
    ]


def again(scratch):
    return [pltpu.SemaphoreType.DMA(s.shape) for s in scratch[2:]]


class Final:
    def __init__(self, outer, dw, left, right, mine, term, target, loaded, sent, came, kept):
        _, _, o, _ = place()
        self.from_left, self.from_right = o >= 1, o < outer - 1
        self.mine, self.term = mine, term
        self.own = pltpu.make_async_copy(dw.at[o], mine, loaded.at[0])
        self.left = pltpu.make_async_copy(left, term.at[0], loaded.at[1])
        self.right = pltpu.make_async_copy(right, term.at[1], loaded.at[2])
        self.moves = [to_dp(m, mine.at[m], target.at[m], sent.at[m - 1], came.at[m - 1]) for m in range(1, GROUP)]
        self.keep = pltpu.make_async_copy(mine.at[0], target.at[0], kept)

    def send(self):
        self.own.start()
        pl.when(self.from_left)(self.left.start)
        pl.when(self.from_right)(self.right.start)
        self.own.wait()

        def add(k):
            def one(m, carry):
                self.mine[m] = (self.mine[m].astype(F32) + self.term[k, m].astype(F32)).astype(BF)
                return carry

            lax.fori_loop(0, GROUP, one, 0)

        @pl.when(self.from_left)
        def _():
            self.left.wait()
            add(0)

        @pl.when(self.from_right)
        def _():
            self.right.wait()
            add(1)

        for move in self.moves:
            move.start()
        self.keep.start()

    def wait(self):
        for move in self.moves:
            move.wait()
        self.keep.wait()


def final_scratch(packed):
    return [
        pltpu.VMEM((GROUP, packed, D), BF),
        pltpu.SemaphoreType.DMA((3,)),
        pltpu.SemaphoreType.DMA((GROUP - 1,)),
        pltpu.SemaphoreType.DMA((GROUP - 1,)),
        pltpu.SemaphoreType.DMA,
    ]


class Mixer:
    def __init__(self, sources, pos_ref, gate_ref, held, sems):
        self.sources, self.pos, self.gate, self.held, self.sems = sources, pos_ref, gate_ref, held, sems

    def copies(self, slot, buffer):
        return [
            pltpu.make_async_copy(
                source.at[slot], self.held.at[buffer, pl.ds(j * CAP, CAP)], self.sems.at[buffer * len(self.sources) + j]
            )
            for j, source in enumerate(self.sources)
        ]

    def load(self, slot, buffer):
        for c in self.copies(slot, buffer):
            c.start()

    def mix(self, slot, buffer, out, add=None):
        for c in self.copies(slot, buffer):
            c.wait()
        n_experts = len(self.sources)
        width = n_experts * CAP
        block = 256

        def one(b, carry):
            at = pl.ds(pl.multiple_of(b * block, block), block)
            targets = []
            for j in range(n_experts):
                target = self.pos[slot, at, j : j + 1]
                targets.append(jnp.where(target >= 0, target + j * CAP, -1))
            tiles = []
            for first in range(0, width, LANES):
                size = min(LANES, width - first)
                lane = first + lax.broadcasted_iota(jnp.int32, (block, size), 1)
                tile = jnp.zeros((block, size), F32)
                for j in range(first // CAP, (first + size - 1) // CAP + 1):
                    value = 1.0 if self.gate is None else self.gate[slot, at, j : j + 1]
                    tile = jnp.where(lane == targets[j], value, tile)
                tiles.append(tile.astype(BF))
            total = mm(jnp.concatenate(tiles, axis=1), self.held[buffer])
            if add is not None:
                total = total + add[at, :].astype(F32)
            out[at, :] = total.astype(BF)
            return carry

        lax.fori_loop(0, out.shape[0] // block, one, 0)


class GroupSum:
    def __init__(self, near, q, middle, mine, come_ab, last_ab, sent, came):
        self.middle, self.mine, self.come_ab, self.last_ab, self.q = middle, mine, come_ab, last_ab, q
        self.a = [
            to_dp(2, near.at[1, pl.ds(s * q, q)], come_ab.at[0, pl.ds(s * q, q)], sent.at[s], came.at[s]) for s in range(2)
        ]
        self.b = [
            to_x(near.at[s, pl.ds(3 * q, q)], come_ab.at[1, pl.ds(s * q, q)], sent.at[2 + s], came.at[2 + s])
            for s in range(2)
        ]
        self.last = [
            to_x(middle[0], last_ab.at[0], sent.at[4], came.at[4]),
            to_dp(2, middle[1], last_ab.at[1], sent.at[5], came.at[5]),
        ]

    def second(self):
        q = self.q
        for p, first in enumerate((self.a[1], self.b[1])):
            first.wait_recv()
            self.middle[p][...] = (
                self.middle[p][...].astype(F32) + self.come_ab[p, q : 2 * q].astype(F32)
            ).astype(BF)
            self.last[p].start()

    def terms(self, p):
        (self.a, self.b)[p][0].wait_recv()
        self.last[p].wait_recv()
        return (
            self.mine[p][...].astype(F32) + self.come_ab[p, : self.q].astype(F32) + self.last_ab[p].astype(F32)
        )

    def sent(self):
        for copy in (*self.a, *self.b, *self.last):
            copy.wait_send()


def group_scratch(rows):
    return [
        pltpu.VMEM((2, rows // 2, D), BF),
        pltpu.VMEM((2, rows // 4, D), BF),
        pltpu.SemaphoreType.DMA((6,)),
        pltpu.SemaphoreType.DMA((6,)),
    ]


def rows_back_kernel(outer, first, then, pos_ref, gate_ref, valid_ref, hidden_ref, cot_ref, gain_ref, w_any, *refs):
    n_experts, n1, n2 = pos_ref.shape[2], len(first), len(then)
    sources, refs = refs[:n_experts], refs[n_experts:]
    ys, refs = refs[:n_experts], refs[n_experts:]
    dws, refs = refs[: n1 + 1], refs[n1 + 1 :]
    was_l, refs = refs[:n1], refs[n1:]
    was_r, refs = refs[:n1], refs[n1:]
    f_dw, f_left, f_right, refs = *refs[:3], refs[3:]
    grad_ref, low_ref, gain_grad_ref, own_ref, come_ref, mixed_out, fin_ref = refs[:7]
    refs = refs[7:]
    to_l, refs = refs[: n1 + n2], refs[n1 + n2 :]
    to_r, refs = refs[: n1 + n2], refs[n1 + n2 :]
    (held, far, come, mixed_come, near, l_sem, s_core, r_core), refs = refs[:8], refs[8:]
    (come_ab, last_ab, s_sem, r_sem), refs = refs[:4], refs[4:]
    sums_a, refs = refs[:6], refs[6:]
    sums_b, refs = (*sums_a[:2], *refs[:4]), refs[4:]
    send_ref, s_at, r_at, w_ref, w_sem = refs[:5]
    mixed, m_sem, final_refs = refs[5], refs[6], refs[7:]
    heads = w_ref.shape[1] // 2
    w_copy = pltpu.make_async_copy(w_any.at[:, pl.ds(2 * heads, 2 * heads)], w_ref, w_sem)
    w_copy.start()
    mixer = Mixer(sources, pos_ref, None, held, l_sem)
    mixer.load(3, 0)
    mixer.load(2, 1)
    greet(outer, (1, 2, 3), True)
    one = Sums(outer, first, dws[:n1], was_l, was_r, to_l[:n1], to_r[:n1], *sums_a)
    final = Final(outer, f_dw, f_left, f_right, final_refs[0], sums_a[1], fin_ref, *final_refs[1:])
    two = Sums(
        outer,
        [s for s, _ in then],
        [dws[k] for _, k in then],
        [None if s == 1 else to_l[k] for s, k in then],
        [None if s == 1 else to_r[k] for s, k in then],
        to_l[n1:],
        to_r[n1:],
        *sums_b,
    )
    q = near.shape[1] // 4
    group = GroupSum(
        near,
        q,
        [near.at[0, pl.ds(q, q)], near.at[1, pl.ds(2 * q, q)]],
        [near.at[0, pl.ds(0, q)], near.at[0, pl.ds(2 * q, q)]],
        come_ab,
        last_ab,
        s_sem,
        r_sem,
    )
    def core(s):
        return to_dp(1, far.at[s], come.at[s], s_core.at[s], r_core.at[s])

    def mixed_core(s):
        return to_dp(1, far.at[s], mixed_come.at[s], s_core.at[2 + s], r_core.at[2 + s])

    def mixed_leave(s):
        return pltpu.make_async_copy(mixed.at[s], mixed_out.at[s], m_sem.at[s])

    outputs = Mixer(ys, pos_ref, gate_ref, held, l_sem)
    rows = hidden_ref.shape[0] // 2
    aways = [
        to_x(
            send_ref.at[pl.ds(p * rows, rows)], come_ref.at[pl.ds(p * rows, rows)], s_at.at[p], r_at.at[p]
        )
        for p in range(2)
    ]

    def phase(mixer, base, target, add, ahead, behind):
        def body(k, carry):
            s = 1 - k
            ahead(s, k)
            mixer.mix(base + s, k, target.at[s], None if add is None else add.at[s])
            behind(s, k)
            return carry

        lax.fori_loop(0, 2, body, 0)

    def far_behind(s, k):
        core(s).start()
        mixer.load(s, k)

    def near_behind(s, k):
        @pl.when(s == 1)
        def _():
            group.a[1].start()
            group.b[1].start()
            group.a[0].start()

        pl.when(s == 0)(group.b[0].start)
        outputs.load(2 + s, k)

    def go_on():
        group.second()
        one.wait()
        two.load()
        two.send()

    def mixed_ahead(s, k):
        core(s).wait_send()
        pl.when(k == 1)(go_on)

    def mixed_behind(s, k):
        mixed_core(s).start()
        outputs.load(s, k)

    def back():
        gain = gain_ref[...]
        gain_grad = jnp.zeros((1, D), F32)
        for p in range(2):
            at = slice(p * rows, (p + 1) * rows)
            hidden = hidden_ref[at]
            normed_grad = group.terms(p)
            inverse = lax.rsqrt(jnp.mean(hidden * hidden, axis=-1, keepdims=True) + EPSILON)
            gain_grad = gain_grad + jnp.sum(normed_grad * (hidden * inverse), axis=0, keepdims=True)
            scaled = normed_grad * gain
            back = inverse * scaled - hidden * (
                inverse * inverse * inverse * jnp.mean(scaled * hidden, axis=-1, keepdims=True)
            )
            dy = jnp.where(valid_ref[at] > 0, cot_ref[at].astype(F32), 0.0)
            total = dy + back
            grad_ref[at] = total
            low = total.astype(BF)
            low_ref[at] = low
            send_ref[at] = mm(low, w_ref[:, heads:]).astype(BF)
            aways[p].start()
        gain_grad_ref[...] = gain_grad

    def last_ahead(s, k):
        mixed_core(s).wait_recv()
        pl.when(k == 1)(back)

    one.load()
    one.send()
    final.send()
    phase(mixer, 2, far, None, lambda s, k: None, far_behind)
    phase(mixer, 0, near, come, lambda s, k: core(s).wait_recv(), near_behind)
    phase(outputs, 2, far, None, mixed_ahead, mixed_behind)
    w_copy.wait()
    phase(outputs, 0, mixed, mixed_come, last_ahead, lambda s, k: mixed_leave(s).start())
    own_ref[...] = mm(low_ref[...], w_ref[:, :heads]).astype(BF)
    group.sent()
    for s in range(2):
        mixed_core(s).wait_send()
    for away in aways:
        away.wait()
    final.wait()
    for s in range(2):
        mixed_leave(s).wait()
    two.wait()


def rows_back(
    outer, pos, gate, valid, hidden, cotangent, gain, weights_full, sources, ys, first, then, dws, was_l, was_r, final
):
    rows, heads = hidden.shape[0], weights_full.shape[1] // 4
    n, n_experts = len(first) + len(then), len(sources)
    packed = dws[0].shape[2]
    hop = [jax.ShapeDtypeStruct((GROUP, packed, D), BF)] * (2 * n)
    half = jax.ShapeDtypeStruct((rows, heads), BF)
    most = max(len(first), len(then))
    slots = pltpu.VMEM((2, 2 * rows, D), BF)
    out = remote_call(
        functools.partial(rows_back_kernel, outer, first, then),
        "rows_back",
        10,
        [
            jax.ShapeDtypeStruct((rows, D), F32),
            jax.ShapeDtypeStruct((rows, D), BF),
            jax.ShapeDtypeStruct((1, D), F32),
            half,
            half,
            jax.ShapeDtypeStruct((2, 2 * rows, D), BF),
        ]
        + hop[:1]
        + hop,
        [VM] * 6 + [ANY] * (4 + 2 * n_experts + len(dws) + 2 * len(first)),
        [VM] * 5 + [ANY] * (2 + 2 * n),
        (pos, gate, valid, hidden, cotangent, gain.reshape(1, D), weights_full, *sources, *ys, *dws, *was_l, *was_r, *final),
        [
            pltpu.VMEM((2, n_experts * CAP, D), BF),
            slots,
            slots,
            slots,
            slots,
            pltpu.SemaphoreType.DMA((2 * n_experts,)),
            pltpu.SemaphoreType.DMA((4,)),
            pltpu.SemaphoreType.DMA((4,)),
            *group_scratch(2 * rows),
            *sums_scratch(most, packed),
            *again(sums_scratch(most, packed)),
            pltpu.VMEM((rows, heads), BF),
            pltpu.SemaphoreType.DMA((2,)),
            pltpu.SemaphoreType.DMA((2,)),
            pltpu.VMEM((D, 2 * heads), BF),
            pltpu.SemaphoreType.DMA,
            slots,
            pltpu.SemaphoreType.DMA((2,)),
            *final_scratch(packed),
        ],
        30 << 30,
    )
    return out[:6], out[6], out[7 : 7 + n], out[7 + n :]


def attention_back_kernel(
    outer, q_block, steps, len_ref, qkv_ref, lse_ref, cos_ref, sin_ref, own_ref, other_ref, hidden_ref, valid_ref, *refs
):
    n = len(steps)
    mixed, refs = refs[0], refs[1:]
    dws, refs = refs[:n], refs[n:]
    was_l, refs = refs[:n], refs[n:]
    was_r, refs = refs[:n], refs[n:]
    outs, out_ref, refs = refs[:2], refs[2], refs[3:]
    to_l, refs = refs[:n], refs[n:]
    to_r, refs = refs[:n], refs[n:]
    do_ref, dq_ref, dk_ref, dv_ref = refs[:4]
    sums_refs, refs = refs[4:10], refs[10:]
    middle, mine, l_sem, come_ab, last_ab, s_sem, r_sem = refs
    _, t, _, _ = place()
    q = middle.shape[1]
    loads = [
        pltpu.make_async_copy(mixed.at[0, pl.ds(q, q)], middle.at[0], l_sem.at[0]),
        pltpu.make_async_copy(mixed.at[1, pl.ds(2 * q, q)], middle.at[1], l_sem.at[1]),
        pltpu.make_async_copy(mixed.at[0, pl.ds(0, q)], mine.at[0], l_sem.at[2]),
        pltpu.make_async_copy(mixed.at[0, pl.ds(2 * q, q)], mine.at[1], l_sem.at[3]),
    ]
    for c in loads:
        c.start()
    greet(outer, (2,), True)
    group = GroupSum(
        mixed, q, [middle.at[0], middle.at[1]], [mine.at[0], mine.at[1]], come_ab, last_ab, s_sem, r_sem
    )
    for copy in (group.a[1], group.b[1], group.a[0], group.b[0]):
        copy.start()
    sums = Sums(outer, steps, dws, was_l, was_r, to_l, to_r, *sums_refs)
    sums.load()
    sums.send()
    length = len_ref[0]
    rows, own_rows = qkv_ref.shape[0], own_ref.shape[0]
    groups = own_ref.shape[1] // LANES
    scale = 1.0 / math.sqrt(HD)

    def per_group(g, carry):
        q_lanes = pl.ds(pl.multiple_of(g * 2 * LANES, LANES), LANES)
        kv_lanes = pl.ds(pl.multiple_of(g * 2 * LANES + LANES, LANES), LANES)
        o_lanes = pl.ds(pl.multiple_of(g * LANES, LANES), LANES)
        for half, grad_ref in ((t, own_ref), (1 - t, other_ref)):
            do_ref[pl.ds(pl.multiple_of(half * own_rows, own_rows), own_rows), :] = grad_ref[:, o_lanes]
        keys, values = doubled(qkv_ref[:, kv_lanes])
        dk_ref[...] = jnp.zeros_like(dk_ref)
        dv_ref[...] = jnp.zeros_like(dv_ref)
        for b in range(rows // q_block):
            start, n_keys = b * q_block, (b + 1) * q_block
            q = head_pair(qkv_ref[start : start + q_block, q_lanes])
            grad = head_pair(do_ref[start : start + q_block, :])
            scores = mm_nt(keys[:n_keys], q) * scale
            probs = jnp.where(
                allowed(n_keys, q_block, start, length), jnp.exp(scores - lse_ref[g, b : b + 1, :]), 0.0
            )
            prob_grad = mm_nt(values[:n_keys], grad)
            center = jnp.sum(probs * prob_grad, axis=0, keepdims=True)
            score_grad = (probs * (prob_grad - center)).astype(BF)
            dq_ref[start : start + q_block, :] = head_join(mm_tn(score_grad, keys[:n_keys])) * scale
            dk_ref[:n_keys, :] += mm(score_grad, q)
            dv_ref[:n_keys, :] += mm(probs.astype(BF), grad)
        for p, half in enumerate((t, 1 - t)):
            at = pl.ds(pl.multiple_of(half * own_rows, own_rows), own_rows)
            cosine, sine = cos_ref[at, :], sin_ref[at, :]
            dq = dq_ref[at, :]
            outs[p][:, q_lanes] = (dq * cosine - swap_halves(dq) * sine).astype(BF)
            dk, dv = dk_ref[at, :] * scale, dv_ref[at, :]
            dk = dk + pltpu.roll(dk, HD, 1)
            dv = dv + pltpu.roll(dv, HD, 1)
            dk = dk * cosine - swap_halves(dk) * sine
            first = lax.broadcasted_iota(jnp.int32, dk.shape, 1) < HD
            outs[p][:, kv_lanes] = jnp.where(first, dk, dv).astype(BF)

        @pl.when(g == groups // 2)
        def _():
            for c in loads:
                c.wait()
            group.second()

        return carry

    lax.fori_loop(0, groups, per_group, 0)
    for p in range(2):
        at = slice(p * q, (p + 1) * q)
        out_ref[at] = jnp.where(valid_ref[at] > 0, hidden_ref[at] + group.terms(p), 0.0).astype(BF)
    group.sent()
    sums.wait()


def attention_back(
    outer, q_block, length, qkv, lse, cosine, sine, grads, hidden, valid, mixed, steps, dws, was_l, was_r
):
    rows, width = qkv.shape
    n = len(steps)
    packed = dws[0].shape[2]
    hop = jax.ShapeDtypeStruct((GROUP, packed, D), BF)
    out = remote_call(
        functools.partial(attention_back_kernel, outer, q_block, steps),
        "attention_back",
        12,
        [jax.ShapeDtypeStruct((rows // 2, width), BF)] * 2
        + [jax.ShapeDtypeStruct((rows // 2, D), BF)]
        + [hop] * (2 * n),
        [SMEM] + [VM] * 8 + [ANY] * (3 * n + 1),
        [VM] * 3 + [ANY] * (2 * n),
        (length, qkv, lse, cosine, sine, *grads, hidden, valid, mixed, *dws, *was_l, *was_r),
        [
            pltpu.VMEM((rows, LANES), BF),
            pltpu.VMEM((rows, LANES), F32),
            pltpu.VMEM((rows, LANES), F32),
            pltpu.VMEM((rows, LANES), F32),
            *sums_scratch(n, packed),
            pltpu.VMEM((2, rows // 4, D), BF),
            pltpu.VMEM((2, rows // 4, D), BF),
            pltpu.SemaphoreType.DMA((4,)),
            *group_scratch(rows),
        ],
        30 << 30,
    )
    return out[:3], out[3 : 3 + n], out[3 + n :]


def over_outer(outer, source, target, sent, came, base):
    _, t, o, i = place()
    return [
        pltpu.make_async_remote_copy(
            source((o + k) % outer),
            target(k),
            sent.at[base + k],
            came.at[base + k],
            device_id=((o + k) % outer * GROUP + i, t),
            device_id_type=MESH,
        )
        for k in range(1, outer)
    ]


class Spread:
    def __init__(self, outer, terms, come_core, come_y, come_z, sent, came):
        _, _, self.o, i = place()
        self.outer, self.terms, self.come_core, self.come_y, self.come_z = outer, terms, come_core, come_y, come_z
        y, c = i // 2, i % 2
        self.y, self.c = y, c
        self.core = to_dp(1, terms.at[:, :, 1 - c], come_core, sent.at[0], came.at[0])
        self.side = to_dp(2, terms.at[:, 1 - y, c], come_y, sent.at[1], came.at[1])
        self.moves = over_outer(outer, lambda peer: terms.at[peer, y, c], lambda k: come_z.at[k - 1], sent, came, 1)

    def over_core(self):
        self.core.start()

    def over_y(self):
        self.core.wait()

        def add(k, carry):
            for r in range(2):
                self.terms[k, r, self.c] = (
                    self.terms[k, r, self.c].astype(F32) + self.come_core[k, r].astype(F32)
                ).astype(BF)
            return carry

        lax.fori_loop(0, self.outer, add, 0)
        self.side.start()

    def over_z(self):
        self.side.wait()

        def add(k, carry):
            self.terms[k, self.y, self.c] = (
                self.terms[k, self.y, self.c].astype(F32) + self.come_y[k].astype(F32)
            ).astype(BF)
            return carry

        lax.fori_loop(0, self.outer, add, 0)
        for move in self.moves:
            move.start()

    def total(self):
        for move in self.moves:
            move.wait()
        total = self.terms[self.o, self.y, self.c].astype(F32)
        for k in range(1, self.outer):
            total = total + self.come_z[k - 1].astype(F32)
        return total


def spread_scratch(outer, each, columns):
    return [
        pltpu.VMEM((outer, 2, 2, each, columns), BF),
        pltpu.VMEM((outer, 2, each, columns), BF),
        pltpu.VMEM((outer, each, columns), BF),
        pltpu.VMEM((outer - 1, each, columns), BF),
        pltpu.SemaphoreType.DMA((1 + outer,)),
        pltpu.SemaphoreType.DMA((1 + outer,)),
    ]


def finish_kernel(outer, hgrad_any, x_any, gain_ref, w_any, *refs):
    (no_ref, nx_ref, po_ref, px_ref, oo_ref, ox_ref, sg_ref), refs = refs[:7], refs[7:]
    dws, refs = refs[:3], refs[3:]
    done, refs = refs[:2], refs[2:]
    was_l, refs = refs[:2], refs[2:]
    was_r, refs = refs[:2], refs[2:]
    tgrad_ref, gains_ref, qkv_ref, outw_ref = refs[:4]
    fins, to_l, to_r, refs = refs[4:7], refs[7:9], refs[9:11], refs[11:]
    sums_refs, refs = [refs[:6], refs[6:12]], refs[12:]
    final_refs, refs = [refs[5 * k : 5 * k + 5] for k in range(3)], refs[15:]
    part_ref, theirs_ref, p_send, p_recv, out_ref, come_ref, c_send, c_recv = refs[:8]
    q_refs, o_refs, refs = refs[8:14], refs[14:20], refs[20:]
    g_buf, g_come, g_z, g_send, g_recv, w_ref, w_sem, hgrad_ref, x_ref, late_sem = refs
    d, t, o, i = place()
    rows = hgrad_ref.shape[0]
    width = w_ref.shape[1]
    w_copy = pltpu.make_async_copy(w_any.at[:, pl.ds(0, width)], w_ref, w_sem)
    w_copy.start()
    late = [
        pltpu.make_async_copy(hgrad_any, hgrad_ref, late_sem.at[0]),
        pltpu.make_async_copy(x_any, x_ref, late_sem.at[1]),
    ]
    for c in late:
        c.start()
    greet_all(outer)
    sums = [
        Sums(outer, (3,), [dws[1 + k]], [was_l[k]], [was_r[k]], [to_l[k]], [to_r[k]], *sums_refs[k]) for k in range(2)
    ]
    came = [done, (to_l[0], to_r[0]), (to_l[1], to_r[1])]
    finals = [
        Final(outer, dws[k], *came[k], final_refs[k][0], sums_refs[0][1], fins[k], *final_refs[k][1:]) for k in range(3)
    ]
    for one in sums:
        one.load()
    for one in sums:
        one.send()
    w_copy.wait()
    part_ref[...] = mm_nt(px_ref[...], w_ref[...]).astype(BF)
    exchange = to_x(part_ref, theirs_ref, p_send, p_recv)
    exchange.start()
    finals[0].send()
    whole, part = Spread(outer, *q_refs), Spread(outer, *o_refs)
    each, heads = outw_ref.shape

    def out_block(k, carry):
        for r in range(GROUP):
            at = pl.ds(pl.multiple_of((k * GROUP + r) * each, each), each)
            part.terms[k, r // 2, r % 2, :, :heads] = oo_ref[at, :]
            part.terms[k, r // 2, r % 2, :, heads:] = ox_ref[at, :]
        return carry

    lax.fori_loop(0, outer, out_block, 0)
    part.over_core()

    def weights_block(k, carry):
        lanes = pl.ds(pl.multiple_of(k * GROUP * each, GROUP * each), GROUP * each)
        total = (mm_tn(no_ref[:, lanes], po_ref[...]) + mm_tn(nx_ref[:, lanes], px_ref[...])).astype(BF)
        for r in range(GROUP):
            whole.terms[k, r // 2, r % 2] = total[r * each : (r + 1) * each]
        return carry

    part.over_y()
    lax.fori_loop(0, outer, weights_block, 0)
    whole.over_core()
    whole.over_y()
    part.over_z()

    exchange.wait()
    for c in late:
        c.wait()
    quarter = rows // 4

    def norm_rows(p, gain_grad):
        at = pl.ds(pl.multiple_of(p * quarter, quarter), quarter)
        normed_grad = mm_nt(po_ref[at, :], w_ref[...]).astype(BF).astype(F32) + theirs_ref[at, :].astype(F32)
        x = x_ref[at, :].astype(F32)
        inverse = lax.rsqrt(jnp.mean(x * x, axis=-1, keepdims=True) + EPSILON)
        scaled = normed_grad * gain_ref[...]
        tgrad_ref[at, :] = (
            hgrad_ref[at, :]
            + inverse * scaled
            - x * (inverse * inverse * inverse * jnp.mean(scaled * x, axis=-1, keepdims=True))
        )
        return gain_grad + jnp.sum(normed_grad * (x * inverse), axis=0, keepdims=True)

    g_buf[0, 0:1, :] = lax.fori_loop(0, 4, norm_rows, jnp.zeros((1, D), F32))
    g_buf[0, 1:2, :] = sg_ref[...]
    g_buf[0, 2:8, :] = jnp.zeros((6, D), F32)
    g_moves = [
        to_dp(1, g_buf.at[0], g_come.at[0], g_send.at[0], g_recv.at[0]),
        to_x(g_buf.at[1], g_come.at[1], g_send.at[1], g_recv.at[1]),
        to_dp(2, g_buf.at[2], g_come.at[2], g_send.at[2], g_recv.at[2]),
    ]
    g_moves[0].start()
    g_moves[0].wait()
    g_buf[1] = g_buf[0] + g_come[0]
    g_moves[1].start()
    g_moves[1].wait()
    g_buf[2] = g_buf[1] + g_come[1]
    g_moves[2].start()
    sums[0].wait()
    finals[1].send()
    whole.over_z()
    sums[1].wait()
    finals[2].send()
    out = part.total()
    outw_ref[...] = out[:, :heads]
    out_ref[...] = out[:, heads:].astype(BF)
    to_other = to_x(out_ref, come_ref, c_send, c_recv)
    to_other.start()
    g_moves[2].wait()
    g_z[0] = g_buf[2] + g_come[2]
    gz_moves = over_outer(outer, lambda peer: g_z.at[0], lambda k: g_z.at[k], g_send, g_recv, 2)
    for move in gz_moves:
        move.start()
    qkv_ref[...] = whole.total()
    to_other.wait()
    outw_ref[...] = outw_ref[...] + come_ref[...].astype(F32)
    for move in gz_moves:
        move.wait()
    gains = g_z[(o + outer) % outer]
    for k in range(1, outer):
        gains = gains + g_z[(o - k + outer) % outer]
    gains_ref[...] = gains
    for final in finals:
        final.wait()


def finish(outer, hgrad, x, gain, weights_full, extra, dws, done, was_l, was_r):
    rows = hgrad.shape[0]
    packed = dws[0].shape[2]
    width = weights_full.shape[1] // 2
    heads = width // 2
    each = D // (outer * GROUP)
    hop = jax.ShapeDtypeStruct((GROUP, packed, D), BF)
    return remote_call(
        functools.partial(finish_kernel, outer),
        "finish",
        11,
        [
            jax.ShapeDtypeStruct((rows, D), F32),
            jax.ShapeDtypeStruct((8, D), F32),
            jax.ShapeDtypeStruct((each, width), F32),
            jax.ShapeDtypeStruct((each, heads), F32),
        ]
        + [hop] * 7,
        [ANY, ANY, VM, ANY] + [VM] * 7 + [ANY] * 9,
        [VM] * 4 + [ANY] * 7,
        (hgrad, x, gain.reshape(1, D), weights_full, *extra, *dws, *done, *was_l, *was_r),
        [
            *sums_scratch(1, packed) * 2,
            *final_scratch(packed) * 3,
            pltpu.VMEM((rows, D), BF),
            pltpu.VMEM((rows, D), BF),
            pltpu.SemaphoreType.DMA,
            pltpu.SemaphoreType.DMA,
            pltpu.VMEM((each, heads), BF),
            pltpu.VMEM((each, heads), BF),
            pltpu.SemaphoreType.DMA,
            pltpu.SemaphoreType.DMA,
            *spread_scratch(outer, each, width),
            *spread_scratch(outer, each, 2 * heads),
            pltpu.VMEM((3, 8, D), F32),
            pltpu.VMEM((3, 8, D), F32),
            pltpu.VMEM((outer, 8, D), F32),
            pltpu.SemaphoreType.DMA((2 + outer,)),
            pltpu.SemaphoreType.DMA((2 + outer,)),
            pltpu.VMEM((D, width), BF),
            pltpu.SemaphoreType.DMA,
            pltpu.VMEM((rows, D), F32),
            pltpu.VMEM((rows, D), BF),
            pltpu.SemaphoreType.DMA((2,)),
        ],
        30 << 30,
    )


def settle_kernel(in_rows, idx_ref, *refs):
    n = len(refs) - 7
    sources, (in_ref, down_ref, held, wide_in, wide_down, l_sem, s_sem) = refs[:n], refs[n:]
    loads = [pltpu.make_async_copy(source, held.at[j], l_sem.at[j]) for j, source in enumerate(sources)]
    for c in loads:
        c.start()
    stores = []
    for j in range(n):
        loads[j].wait()
        for m in range(GROUP):
            k = j * GROUP + m
            at = (idx_ref[1] ^ m) * n + j
            wide_in[k] = held[j, m, :in_rows, :].astype(F32)
            wide_down[k] = held[j, m, in_rows:, :].astype(F32)
            stores.append(pltpu.make_async_copy(wide_in.at[k], in_ref.at[at], s_sem.at[2 * k]))
            stores.append(pltpu.make_async_copy(wide_down.at[k], down_ref.at[at], s_sem.at[2 * k + 1]))
            for c in stores[-2:]:
                c.start()
    for c in stores:
        c.wait()


def settle_experts(idx, fins, in_rows):
    n = len(fins)
    _, packed, _ = fins[0].shape
    experts, down_rows = n * GROUP, packed - in_rows
    return call(
        functools.partial(settle_kernel, in_rows),
        "settle_experts",
        [jax.ShapeDtypeStruct((experts, in_rows, D), F32), jax.ShapeDtypeStruct((experts, down_rows, D), F32)],
        [SMEM] + [ANY] * n,
        [ANY] * 2,
        (idx, *fins),
        scratch=[
            pltpu.VMEM((n, GROUP, packed, D), BF),
            pltpu.VMEM((experts, in_rows, D), F32),
            pltpu.VMEM((experts, down_rows, D), F32),
            pltpu.SemaphoreType.DMA((n,)),
            pltpu.SemaphoreType.DMA((2 * experts,)),
        ],
        moved=9 << 20,
    )


def layer(
    tokens,
    cotangent,
    lengths,
    expert_ids,
    gate_values,
    first_gain,
    qkv_weight,
    attn_out_weight,
    second_gain,
    expert_in_weight,
    expert_out_weight,
):
    rows = tokens.shape[0]
    n_tensor, n_dp = lax.axis_size("tensor"), lax.axis_size("dp")
    outer = n_dp // GROUP
    slot_rows = rows * n_tensor
    d, t = lax.axis_index("dp"), lax.axis_index("tensor")
    o, i = d // GROUP, d % GROUP
    length = lengths[0]
    idx = jnp.stack([o, i, t, length]).astype(jnp.int32)
    width = qkv_weight.shape[1] * qkv_weight.shape[2]
    experts_local, in_rows, _ = expert_in_weight.shape
    down_rows = expert_out_weight.shape[1]
    own_experts = experts_local // GROUP
    pair = n_tensor == 2
    q_block = 256
    half = rows // 2

    def across(v, m):
        return lax.ppermute(v, "dp", [(a, a ^ m) for a in range(n_dp)])

    def beside(v):
        return lax.ppermute(v, "tensor", [(0, 1), (1, 0)])

    def hop(pairs):
        up = [(a, a + GROUP) for a in range(n_dp - GROUP)]
        down = [(b, a) for a, b in up]
        return [(lax.ppermute(a, "dp", up), lax.ppermute(b, "dp", down)) for a, b in pairs]

    def gather_group(pieces):
        if pair:
            a, b = pieces
            ax, by, ay, bx = beside(a), across(b, 2), across(a, 2), beside(b)
            axy, bxy = across(ax, 2), beside(by)
            slots = [[a, ax, b, bx], [ay, axy, by, bxy]]
        else:
            slot = lax.all_gather(pieces[0], "tensor", axis=0, tiled=True)
            slots = [[slot], [across(slot, 2)]]
        return slots + [[across(p, 1) for p in s] for s in slots]

    positions = t * rows + jnp.arange(rows, dtype=jnp.int32)
    valid_rows = positions < length
    n_experts = experts_local * n_tensor
    chosen = expert_ids.T[None] == jnp.arange(n_experts, dtype=jnp.int32)[:, None, None]
    gates = jnp.sum(jnp.where(chosen, gate_values.T[None].astype(F32), 0.0), axis=1)
    gates = jnp.where(valid_rows[None, :], gates, 0.0).astype(BF)
    x = tokens.astype(F32)
    inverse_one = lax.rsqrt(jnp.mean(x * x, axis=-1, keepdims=True) + EPSILON)
    normed_one = (x * inverse_one * first_gain).astype(BF)
    expert_outs, row_grads, weight_grads = [], [], []
    if pair and outer == 4:
        frequency = THETA ** (-(jnp.arange(HD // 2).astype(F32) * 2.0 / HD))
        shard = jnp.concatenate([qkv_weight.reshape(-1, width), attn_out_weight.T], axis=1)
        main, ready, packed, first_l, first_r = collect(
            outer, shard, normed_one, gates, jnp.tile(frequency, 4)[None, :], expert_in_weight, expert_out_weight
        )
        weights_full, other, cosine, sine, pos, own_gates, pos_columns, gate_columns = main
        main, dy_moved, later, one_l, one_r = attention(
            outer,
            q_block,
            lengths,
            normed_one,
            other,
            weights_full,
            cosine,
            sine,
            tokens,
            second_gain,
            cotangent,
            ready[1],
            packed,
        )
        own_weights = [*ready, *later]
        one_l, one_r = [first_l, *one_l], [first_r, *one_r]
        qkv, lse, attn_own, attn_other, hidden, *normed_two = main
        attn_parts = [attn_own, attn_other]
        gathered, out_grads, moved_l, moved_r = spread(
            outer,
            pos,
            own_gates,
            normed_two,
            [cotangent, *dy_moved],
            (2, 2, 2),
            one_l[:3],
            one_r[:3],
        )
        two_l, two_r = [*moved_l], [*moved_r]
        expert_rows, moved_l, moved_r = hand_out(
            outer, pos, normed_two, gathered, (3, 2), [two_l[0], one_l[3]], [two_r[0], one_r[3]]
        )
        three_l, three_r = [moved_l[0]], [moved_r[0]]
        two_l.append(moved_l[1])
        two_r.append(moved_r[1])
        hop_plans = [
            lambda: ((3,), [two_l[1]], [two_r[1]]),
            lambda: ((3,), [two_l[2]], [two_r[2]]),
            lambda: ((3,), [two_l[3]], [two_r[3]]),
            lambda: ((), [], []),
        ]
        sums_l, sums_r = [], []
        for j in range(own_experts):
            first_grad = weight_grads[:1]
            sum_plan = ((j,), first_grad, sums_l or first_grad, sums_r or first_grad) if j else ((), [], [], [])
            if j == own_experts - 1:
                second_grad = weight_grads[1]
                sum_plan = ((j, 1), weight_grads[:2], [*sums_l, second_grad], [*sums_r, second_grad])
            (y, dx, dw), moved_l, moved_r, sums_l, sums_r = expert_step(
                j,
                outer,
                in_rows,
                down_rows,
                expert_rows,
                out_grads,
                own_weights[j],
                [one_l[j], two_l[j], three_l[j]],
                [one_r[j], two_r[j], three_r[j]],
                hop_plans[j](),
                sum_plan,
            )
            three_l.extend(moved_l[:1])
            three_r.extend(moved_r[:1])
            expert_outs.append(y)
            row_grads.append(dx)
            weight_grads.append(dw)
        valid_column = valid_rows.astype(F32)[:, None]
        _, dw_b, dw_c, dw_d = weight_grads
        main, fin_a, sum_l, sum_r = rows_back(
            outer,
            pos_columns,
            gate_columns,
            valid_column,
            hidden,
            cotangent,
            second_gain,
            weights_full,
            row_grads,
            expert_outs,
            (2, 1),
            ((2, 1), (1, 2)),
            [dw_b, dw_c, dw_d],
            [sums_l[1], dw_c],
            [sums_r[1], dw_c],
            [weight_grads[0], sums_l[0], sums_r[0]],
        )
        hidden_grad, branch_grad, second_gain_part, attn_grad_own, attn_grad_other, mixed = main
        (projected_own, projected_other, output), three_l, three_r = attention_back(
            outer,
            q_block,
            lengths,
            qkv,
            lse,
            cosine,
            sine,
            [attn_grad_own, attn_grad_other],
            hidden,
            valid_column,
            mixed,
            (3, 2),
            [dw_b, dw_d],
            [sum_l[0], sum_l[3]],
            [sum_r[0], sum_r[3]],
        )
        out_own, out_other = (mm_tn(branch_grad, part).astype(BF) for part in attn_parts)
        tokens_grad, gains, qkv_grad, attn_out_grad, *fins = finish(
            outer,
            hidden_grad,
            tokens,
            first_gain,
            weights_full,
            [normed_one, other, projected_own, projected_other, out_own, out_other, second_gain_part],
            [dw_b, dw_c, dw_d],
            [three_l[0], three_r[0]],
            [sum_l[2], three_l[1]],
            [sum_r[2], three_r[1]],
        )
        expert_in_grad, expert_out_grad = settle_experts(idx, [fin_a, *fins[:3]], in_rows)
        return (
            output,
            tokens_grad,
            gains[0],
            qkv_grad.reshape(qkv_weight.shape),
            attn_out_grad.T,
            gains[1],
            expert_in_grad,
            expert_out_grad,
        )
    else:
        if pair:
            gates_x = beside(gates)
            slot_gates = jnp.concatenate(
                [gates[:, :half], gates_x[:, :half], gates[:, half:], gates_x[:, half:]], axis=1
            )
        else:
            slot_gates = lax.all_gather(gates, "tensor", axis=1, tiled=True)
        gates_y = across(slot_gates, 2)
        all_gates = jnp.stack([slot_gates, gates_y, across(slot_gates, 1), across(gates_y, 1)])
        own_gates = lax.dynamic_slice_in_dim(
            all_gates, t * experts_local + i * own_experts, own_experts, axis=1
        ).astype(F32)
        named = own_gates > 0
        before = (
            lax.broadcasted_iota(jnp.int32, (slot_rows, slot_rows), 0)
            < lax.broadcasted_iota(jnp.int32, (slot_rows, slot_rows), 1)
        ).astype(BF)
        ranks = jnp.dot(
            named.astype(BF).reshape(GROUP * own_experts, slot_rows), before, preferred_element_type=F32
        ).reshape(GROUP, own_experts, slot_rows)
        pos = jnp.where(named, ranks, -1.0).astype(jnp.int32)
        pos_columns, gate_columns = jnp.swapaxes(pos, 1, 2), jnp.swapaxes(own_gates, 1, 2)

        cosine, sine = rope_tables(slot_rows)
        dy = jnp.where(valid_rows[:, None], cotangent, jnp.zeros_like(cotangent))
        qkv_full = lax.all_gather(qkv_weight.reshape(qkv_weight.shape[0], width), "dp", axis=0, tiled=True)
        out_full = lax.all_gather(attn_out_weight.T, "dp", axis=0, tiled=True)
        by_distance = pack_weights(idx, expert_in_weight, expert_out_weight)
        by_distance = [by_distance[0]] + [across(by_distance[m], m) for m in range(1, GROUP)]
        own_weights = [jnp.stack([v[j] for v in by_distance]) for j in range(own_experts)]
        hops = [hop([(own, own) for own in own_weights])]
        if pair:
            out_parts = [out_full, beside(out_full)]
        else:
            gathered = lax.all_gather(out_full, "tensor", axis=0)
            out_parts = [gathered[k] for k in range(n_tensor)]

        if pair:
            other = beside(normed_one)
            normed_all = jnp.where(
                t == 0,
                jnp.concatenate([normed_one, other], axis=0),
                jnp.concatenate([other, normed_one], axis=0),
            )
        else:
            normed_all = lax.all_gather(normed_one, "tensor", axis=0, tiled=True)
        qkv = qkv_project(normed_all, qkv_full, cosine, sine)
        *attended, lse = attend(idx, qkv, 2 if pair else 1, q_block)
        if pair:
            attn_parts = [attended[0], beside(attended[1])]
        else:
            heads = attended[0].shape[1]
            exchanged = lax.all_to_all(attended[0].reshape(n_tensor, rows, heads), "tensor", 0, 0)
            attn_parts = [exchanged[k] for k in range(n_tensor)]
        attn_parts, hops[0] = lax.optimization_barrier((attn_parts, hops[0]))
        if outer > 2:
            hops.append(hop(hops[0]))
        hidden, *normed_two = project_out(tokens, second_gain, attn_parts, out_parts, 2 if pair else 1)

        dy_slots = gather_group([dy[:half], dy[half:]] if pair else [dy])
        out_grads = [dispatch(pos[s], own_gates[s], dy_slots[s], True) for s in range(GROUP)]
        normed_slots = gather_group(normed_two)
        normed_slots, out_grads, hops = lax.optimization_barrier((normed_slots, out_grads, hops))
        while len(hops) < outer - 1:
            hops.append(hop(hops[-1]))
        expert_rows = [dispatch(pos[s], own_gates[s], normed_slots[s], False) for s in range(GROUP)]

        for j in range(own_experts):
            if j:
                idx, expert_outs[-1] = lax.optimization_barrier((idx, expert_outs[-1]))
            y, dx, dw = expert(
                idx,
                j,
                outer,
                in_rows,
                down_rows,
                expert_rows,
                out_grads,
                own_weights[j],
                [h[j][0] for h in hops],
                [h[j][1] for h in hops],
            )
            expert_outs.append(y)
            row_grads.append(dx)
            weight_grads.append(dw)

    def sum_group(sources, scaled):
        def part(s, add, n_outs):
            return combine(pos_columns[s], gate_columns[s], sources, s, scaled, add, n_outs)

        far = [part(2, None, 1)[0], part(3, None, 1)[0]]
        near = [across(v, 1) for v in far]
        if pair:
            ay, axy, by, bxy = part(1, near[1], 4)
            a, ax, b, bx = part(0, near[0], 4)

            def add(p, q):
                return (p.astype(F32) + q.astype(F32)).astype(BF)

            a, ax = add(a, across(ay, 2)), add(ax, across(axy, 2))
            b, by = add(b, beside(bx)), add(by, beside(bxy))
            return [[a, beside(ax)], [b, across(by, 2)]]
        (y,) = part(1, near[1], 1)
        (v,) = part(0, near[0], 1)
        v = (v.astype(F32) + across(y, 2).astype(F32)).astype(BF)
        return [[lax.psum_scatter(v, "tensor", scatter_dimension=0, tiled=True)]]

    valid_column = valid_rows.astype(F32)[:, None]
    normed_two_grad = sum_group(row_grads, False)
    hidden_grad, branch_grad, second_gain_part, *attn_grads = hidden_back(
        valid_column, hidden, cotangent, second_gain, normed_two_grad, out_parts
    )
    if pair:
        attn_grads = [attn_grads[0], beside(attn_grads[1])]
    else:
        attn_grads = [
            lax.all_to_all(jnp.stack(attn_grads), "tensor", 0, 0).reshape(slot_rows, attn_grads[0].shape[1])
        ]
    projected_grads = attend_back(idx, qkv, lse, cosine, sine, attn_grads, q_block)

    def first_norm_part(v):
        return lax.dot_general(v, qkv_full, (((1,), (1,)), ((), ())), preferred_element_type=F32).astype(BF)

    if pair:
        theirs = beside(first_norm_part(projected_grads[1]))
        normed_one_grad = first_norm_part(projected_grads[0]).astype(F32) + theirs.astype(F32)
        qkv_part = mm_tn(normed_one, projected_grads[0]) + mm_tn(other, projected_grads[1])
    else:
        normed_one_grad = lax.psum_scatter(
            first_norm_part(projected_grads[0]), "tensor", scatter_dimension=0, tiled=True
        ).astype(F32)
        qkv_part = mm_tn(normed_all, projected_grads[0])
    first_gain_part = jnp.sum(normed_one_grad * (x * inverse_one), axis=0)
    scaled = normed_one_grad * first_gain
    tokens_grad = (
        hidden_grad
        + inverse_one * scaled
        - x * (inverse_one * inverse_one * inverse_one * jnp.mean(scaled * x, axis=-1, keepdims=True))
    )

    mixture = sum_group(expert_outs, True)
    mixture = jnp.concatenate([sum(v.astype(F32) for v in terms) for terms in mixture], axis=0)
    output = jnp.where(valid_rows[:, None], hidden + mixture, 0.0).astype(BF)

    outer_groups = [[a * GROUP + b for a in range(outer)] for b in range(GROUP)]
    received = [[] for _ in range(GROUP)]
    for dw in weight_grads:
        mine = lax.psum_scatter(dw, "dp", scatter_dimension=0, tiled=True, axis_index_groups=outer_groups)
        for m in range(GROUP):
            block = mine[0, m]
            received[m].append(block if m == 0 else across(block, m))
    by_distance = jnp.stack([jnp.stack(v) for v in received])
    by_source = jnp.take(by_distance, jnp.arange(GROUP) ^ i, axis=0).reshape(
        experts_local, in_rows + down_rows, D
    )
    expert_in_grad = by_source[:, :in_rows].astype(F32)
    expert_out_grad = by_source[:, in_rows:].astype(F32)

    attn_out_parts = [mm_tn(branch_grad, part).astype(BF) for part in attn_parts]
    if pair:
        attn_out_part = (attn_out_parts[0].astype(F32) + beside(attn_out_parts[1]).astype(F32)).astype(BF)
    else:
        attn_out_part = lax.psum_scatter(jnp.stack(attn_out_parts), "tensor", scatter_dimension=0, tiled=True)[0]
    qkv_grad = lax.psum_scatter(qkv_part.astype(BF), "dp", scatter_dimension=0, tiled=True).astype(F32)
    attn_out_grad = lax.psum_scatter(attn_out_part, "dp", scatter_dimension=0, tiled=True).astype(F32).T

    gains = jnp.stack([first_gain_part, second_gain_part[0]])
    if pair:
        gains = gains + beside(gains)
    else:
        gains = lax.psum(gains, "tensor")
    step = 1
    while step < n_dp:
        gains = gains + across(gains, step)
        step *= 2
    return (
        output,
        tokens_grad,
        gains[0],
        qkv_grad.reshape(qkv_weight.shape),
        attn_out_grad,
        gains[1],
        expert_in_grad,
        expert_out_grad,
    )


def solution(mesh):
    placed = (
        P(("dp", "tensor"), None),
        P(("dp", "tensor"), None),
        P("dp"),
        P(("dp", "tensor"), None),
        P(("dp", "tensor"), None),
        P(),
        P("dp", "tensor", None),
        P("tensor", "dp"),
        P(),
        P("tensor", "dp", None),
        P("tensor", "dp", None),
    )
    return jax.shard_map(
        layer,
        mesh=mesh,
        in_specs=placed,
        out_specs=(
            P(("dp", "tensor"), None),
            P(("dp", "tensor"), None),
            P(),
            P("dp", "tensor", None),
            P("tensor", "dp"),
            P(),
            P("tensor", "dp", None),
            P("tensor", "dp", None),
        ),
        check_vma=False,
    )
```

```python
import functools
import math

import jax
import jax.numpy as jnp
from jax import lax
from jax.experimental import pallas as pl
from jax.experimental.pallas import tpu as pltpu
from jax.sharding import PartitionSpec as P

D = 1024
HD = 64
FF = 512
G = 2
CAP = 288
GROUP = 4
LANES = 128

EPSILON = 1e-06
THETA = 10000.0
NEGATIVE = -1e30
BF = jnp.bfloat16
F32 = jnp.float32
VMEM_LIMIT = 60 * 1024 * 1024
MESH = pl.DeviceIdType.MESH

ANY = pl.BlockSpec(memory_space=pl.ANY)
SMEM = pl.BlockSpec(memory_space=pltpu.SMEM)
VM = pl.BlockSpec(memory_space=pltpu.VMEM)


def mm(a, b):
    return lax.dot_general(a, b, (((1,), (0,)), ((), ())), preferred_element_type=F32)


def mm_nt(a, b):
    return lax.dot_general(a, b, (((1,), (1,)), ((), ())), preferred_element_type=F32)


def mm_tn(a, b):
    return lax.dot_general(a, b, (((0,), (0,)), ((), ())), preferred_element_type=F32)


def call(kernel, name, out_shape, in_specs, out_specs, args, scratch=(), flops=0, moved=0, **more):
    return pl.pallas_call(
        kernel,
        name=name,
        out_shape=out_shape,
        in_specs=in_specs,
        out_specs=out_specs,
        scratch_shapes=list(scratch),
        compiler_params=pltpu.CompilerParams(vmem_limit_bytes=VMEM_LIMIT),
        cost_estimate=pl.CostEstimate(flops=flops, bytes_accessed=moved, transcendentals=0),
        **more,
    )(*args)


def rope_tables(total_rows):
    half = HD // 2
    positions = jnp.arange(total_rows).astype(F32)
    frequency = THETA ** (-(jnp.arange(half).astype(F32) * 2.0 / HD))
    angles = positions[:, None] * frequency[None, :]
    cosine, sine = jnp.cos(angles), jnp.sin(angles)
    return (
        jnp.concatenate([cosine] * 4, axis=1),
        jnp.concatenate([-sine, sine, -sine, sine], axis=1),
    )


def swap_halves(v):
    lane = lax.broadcasted_iota(jnp.int32, v.shape, 1)
    return jnp.where(lane % HD < HD // 2, pltpu.roll(v, LANES - HD // 2, 1), pltpu.roll(v, HD // 2, 1))


def qkv_kernel(n_ref, w_ref, cos_ref, sin_ref, out_ref):
    projected = mm(n_ref[...], w_ref[...])
    cosine, sine = cos_ref[...], sin_ref[...]
    key_lanes = lax.broadcasted_iota(jnp.int32, cosine.shape, 1) < HD
    for g in range(projected.shape[1] // (2 * LANES)):
        q = projected[:, g * 2 * LANES : g * 2 * LANES + LANES]
        kv = projected[:, g * 2 * LANES + LANES : (g + 1) * 2 * LANES]
        q = q * cosine + swap_halves(q) * sine
        kv = jnp.where(key_lanes, kv * cosine + swap_halves(kv) * sine, kv)
        out_ref[:, g * 2 * LANES : g * 2 * LANES + LANES] = q.astype(BF)
        out_ref[:, g * 2 * LANES + LANES : (g + 1) * 2 * LANES] = kv.astype(BF)


def qkv_project(normed, weight, cosine, sine):
    rows, width = normed.shape[0], weight.shape[1]
    block = 256
    return pl.pallas_call(
        qkv_kernel,
        name="qkv_rope",
        grid=(rows // block,),
        out_shape=jax.ShapeDtypeStruct((rows, width), BF),
        in_specs=[
            pl.BlockSpec((block, D), lambda b: (b, 0)),
            pl.BlockSpec((D, width), lambda b: (0, 0)),
            pl.BlockSpec((block, LANES), lambda b: (b, 0)),
            pl.BlockSpec((block, LANES), lambda b: (b, 0)),
        ],
        out_specs=pl.BlockSpec((block, width), lambda b: (b, 0)),
        compiler_params=pltpu.CompilerParams(vmem_limit_bytes=VMEM_LIMIT),
        cost_estimate=pl.CostEstimate(flops=2 * rows * D * width, bytes_accessed=6 << 20, transcendentals=0),
    )(normed, weight, cosine, sine)


def head_pair(v):
    first = lax.broadcasted_iota(jnp.int32, v.shape, 1) < HD
    zero = jnp.zeros_like(v)
    return jnp.concatenate([jnp.where(first, v, zero), jnp.where(first, zero, v)], axis=0)


def head_join(v):
    n = v.shape[0] // 2
    first = lax.broadcasted_iota(jnp.int32, (n, LANES), 1) < HD
    return jnp.where(first, v[:n], v[n:])


def doubled(kv):
    first = lax.broadcasted_iota(jnp.int32, kv.shape, 1) < HD
    other = pltpu.roll(kv.astype(F32), HD, 1).astype(BF)
    return jnp.where(first, kv, other), jnp.where(first, other, kv)


def allowed(n_keys, q_block, q_start, length):
    key = lax.broadcasted_iota(jnp.int32, (n_keys, 2 * q_block), 0)
    lane = lax.broadcasted_iota(jnp.int32, (n_keys, 2 * q_block), 1)
    query = q_start + jnp.where(lane < q_block, lane, lane - q_block)
    return (key <= query) & (key < length)


def attend_kernel(q_block, idx_ref, qkv_ref, *out_refs):
    outs, lse_ref = out_refs[:-1], out_refs[-1]
    rows = qkv_ref.shape[0]
    length = idx_ref[3]
    keys, values = doubled(qkv_ref[:, LANES:])
    for b in range(rows // q_block):
        start, n_keys = b * q_block, (b + 1) * q_block
        q = head_pair(qkv_ref[start : start + q_block, :LANES])
        scores = mm_nt(keys[:n_keys], q) * (1.0 / math.sqrt(HD))
        scores = jnp.where(allowed(n_keys, q_block, start, length), scores, NEGATIVE)
        largest = jnp.max(scores, axis=0, keepdims=True)
        expon = jnp.exp(scores - largest)
        totals = jnp.sum(expon, axis=0, keepdims=True)
        probs = (expon * (1.0 / totals)).astype(BF)
        mixed = head_join(mm_tn(probs, values[:n_keys])).astype(BF)
        lse_ref[0, b : b + 1, :] = largest + jnp.log(totals)
        if len(outs) == 1:
            outs[0][start : start + q_block] = mixed
        else:
            own_rows = rows // 2
            half, at = start // own_rows, start % own_rows
            mine = idx_ref[2] == half

            @pl.when(mine)
            def _():
                outs[0][at : at + q_block] = mixed

            @pl.when(jnp.logical_not(mine))
            def _():
                outs[1][at : at + q_block] = mixed


def attend(idx, qkv, parts, q_block):
    rows, groups = qkv.shape[0], qkv.shape[1] // (2 * LANES)
    out = jax.ShapeDtypeStruct((rows // parts, groups * LANES), BF)
    return pl.pallas_call(
        functools.partial(attend_kernel, q_block),
        name="attend",
        grid=(groups,),
        out_shape=[out] * parts + [jax.ShapeDtypeStruct((groups, rows // q_block, 2 * q_block), F32)],
        in_specs=[SMEM, pl.BlockSpec((rows, 2 * LANES), lambda g: (0, g))],
        out_specs=[pl.BlockSpec((rows // parts, LANES), lambda g: (0, g))] * parts
        + [pl.BlockSpec((1, rows // q_block, 2 * q_block), lambda g: (g, 0, 0))],
        compiler_params=pltpu.CompilerParams(vmem_limit_bytes=VMEM_LIMIT),
        cost_estimate=pl.CostEstimate(flops=14 << 30, bytes_accessed=4 << 20, transcendentals=0),
    )(idx, qkv)


def attend_back_kernel(q_block, n_grads, idx_ref, qkv_ref, lse_ref, cos_ref, sin_ref, *refs):
    grads, outs = refs[:n_grads], refs[n_grads : 2 * n_grads]
    do_ref, dq_ref, dk_ref, dv_ref = refs[2 * n_grads :]
    rows = qkv_ref.shape[0]
    own_rows = rows // n_grads
    length = idx_ref[3]
    for p in range(n_grads):
        at = pl.multiple_of((p ^ idx_ref[2] if n_grads == 2 else 0) * own_rows, own_rows)
        do_ref[pl.ds(at, own_rows), :] = grads[p][...]
    keys, values = doubled(qkv_ref[:, LANES:])
    dk_ref[...] = jnp.zeros_like(dk_ref)
    dv_ref[...] = jnp.zeros_like(dv_ref)
    scale = 1.0 / math.sqrt(HD)
    for b in range(rows // q_block):
        start, n_keys = b * q_block, (b + 1) * q_block
        q = head_pair(qkv_ref[start : start + q_block, :LANES])
        grad = head_pair(do_ref[start : start + q_block, :])
        scores = mm_nt(keys[:n_keys], q) * scale
        probs = jnp.where(
            allowed(n_keys, q_block, start, length), jnp.exp(scores - lse_ref[0, b : b + 1, :]), 0.0
        )
        prob_grad = mm_nt(values[:n_keys], grad)
        center = jnp.sum(probs * prob_grad, axis=0, keepdims=True)
        score_grad = (probs * (prob_grad - center)).astype(BF)
        dq_ref[start : start + q_block, :] = head_join(mm_tn(score_grad, keys[:n_keys])) * scale
        dk_ref[:n_keys, :] += mm(score_grad, q)
        dv_ref[:n_keys, :] += mm(probs.astype(BF), grad)
    cosine, sine = cos_ref[...], sin_ref[...]
    dq = dq_ref[...]
    dq = (dq * cosine - swap_halves(dq) * sine).astype(BF)
    dk, dv = dk_ref[...] * scale, dv_ref[...]
    dk = dk + pltpu.roll(dk, HD, 1)
    dv = dv + pltpu.roll(dv, HD, 1)
    dk = dk * cosine - swap_halves(dk) * sine
    first = lax.broadcasted_iota(jnp.int32, dk.shape, 1) < HD
    dkv = jnp.where(first, dk, dv).astype(BF)
    if n_grads == 1:
        outs[0][:, :LANES] = dq
        outs[0][:, LANES:] = dkv
    else:
        do_ref[...] = dq
        for p in range(2):
            at = pl.multiple_of((p ^ idx_ref[2]) * own_rows, own_rows)
            outs[p][:, :LANES] = do_ref[pl.ds(at, own_rows), :]
        do_ref[...] = dkv
        for p in range(2):
            at = pl.multiple_of((p ^ idx_ref[2]) * own_rows, own_rows)
            outs[p][:, LANES:] = do_ref[pl.ds(at, own_rows), :]


def attend_back(idx, qkv, lse, cosine, sine, grads, q_block):
    rows, groups, parts = qkv.shape[0], qkv.shape[1] // (2 * LANES), len(grads)
    return pl.pallas_call(
        functools.partial(attend_back_kernel, q_block, parts),
        name="attend_back",
        grid=(groups,),
        out_shape=[jax.ShapeDtypeStruct((rows // parts, groups * 2 * LANES), BF)] * parts,
        in_specs=[
            SMEM,
            pl.BlockSpec((rows, 2 * LANES), lambda g: (0, g)),
            pl.BlockSpec((1, rows // q_block, 2 * q_block), lambda g: (g, 0, 0)),
            pl.BlockSpec((rows, LANES), lambda g: (0, 0)),
            pl.BlockSpec((rows, LANES), lambda g: (0, 0)),
        ]
        + [pl.BlockSpec((rows // parts, LANES), lambda g: (0, g))] * parts,
        out_specs=[pl.BlockSpec((rows // parts, 2 * LANES), lambda g: (0, g))] * parts,
        scratch_shapes=[pltpu.VMEM((rows, LANES), BF)] + [pltpu.VMEM((rows, LANES), F32)] * 3,
        compiler_params=pltpu.CompilerParams(vmem_limit_bytes=VMEM_LIMIT),
        cost_estimate=pl.CostEstimate(flops=30 << 30, bytes_accessed=6 << 20, transcendentals=0),
    )(idx, qkv, lse, cosine, sine, *grads)


def project_out_kernel(n_parts, pieces, x_ref, gain_ref, *refs):
    attns, weights = refs[:n_parts], refs[n_parts : 2 * n_parts]
    hidden_ref, normed_refs = refs[2 * n_parts], refs[2 * n_parts + 1 :]
    rows = x_ref.shape[0] // pieces
    for p in range(pieces):
        at = slice(p * rows, (p + 1) * rows)
        hidden = x_ref[at].astype(F32)
        for a, w in zip(attns, weights, strict=True):
            hidden = hidden + mm_nt(a[at], w[...])
        inverse = lax.rsqrt(jnp.mean(hidden * hidden, axis=-1, keepdims=True) + EPSILON)
        hidden_ref[at] = hidden
        normed_refs[p][...] = (hidden * inverse * gain_ref[...]).astype(BF)


def project_out(x, gain, attns, weights, pieces):
    rows = x.shape[0]
    n = len(attns)
    return call(
        functools.partial(project_out_kernel, n, pieces),
        "project_out",
        [jax.ShapeDtypeStruct((rows, D), F32)] + [jax.ShapeDtypeStruct((rows // pieces, D), BF)] * pieces,
        [VM] * (2 + 2 * n),
        [VM] * (1 + pieces),
        (x, gain.reshape(1, D), *attns, *weights),
        flops=2 * rows * D * D,
        moved=7 << 20,
    )


def hidden_back_kernel(n_parts, pieces, n_sums, valid_ref, hidden_ref, cot_ref, gain_ref, *refs):
    sums, refs = refs[: pieces * n_sums], refs[pieces * n_sums :]
    weights, refs = refs[:n_parts], refs[n_parts:]
    grad_ref, low_ref, gain_grad_ref, attn_refs = refs[0], refs[1], refs[2], refs[3:]
    rows = hidden_ref.shape[0] // pieces
    gain = gain_ref[...]
    gain_grad = jnp.zeros((1, D), F32)
    for p in range(pieces):
        at = slice(p * rows, (p + 1) * rows)
        hidden = hidden_ref[at]
        normed_grad = sums[p * n_sums][...].astype(F32)
        for s in sums[p * n_sums + 1 : (p + 1) * n_sums]:
            normed_grad = normed_grad + s[...].astype(F32)
        inverse = lax.rsqrt(jnp.mean(hidden * hidden, axis=-1, keepdims=True) + EPSILON)
        gain_grad = gain_grad + jnp.sum(normed_grad * (hidden * inverse), axis=0, keepdims=True)
        scaled = normed_grad * gain
        back = inverse * scaled - hidden * (
            inverse * inverse * inverse * jnp.mean(scaled * hidden, axis=-1, keepdims=True)
        )
        dy = jnp.where(valid_ref[at] > 0, cot_ref[at].astype(F32), 0.0)
        total = dy + back
        grad_ref[at] = total
        low = total.astype(BF)
        low_ref[at] = low
        for a, w in zip(attn_refs, weights, strict=True):
            a[at] = mm(low, w[...]).astype(BF)
    gain_grad_ref[...] = gain_grad


def hidden_back(valid, hidden, cotangent, gain, sums, weights):
    rows, pieces, n_sums, n = hidden.shape[0], len(sums), len(sums[0]), len(weights)
    heads = weights[0].shape[1]
    return call(
        functools.partial(hidden_back_kernel, n, pieces, n_sums),
        "hidden_back",
        [
            jax.ShapeDtypeStruct((rows, D), F32),
            jax.ShapeDtypeStruct((rows, D), BF),
            jax.ShapeDtypeStruct((1, D), F32),
        ]
        + [jax.ShapeDtypeStruct((rows, heads), BF)] * n,
        [VM] * (4 + pieces * n_sums + n),
        [VM] * (3 + n),
        (valid, hidden, cotangent, gain.reshape(1, D), *[s for piece in sums for s in piece], *weights),
        flops=2 * rows * D * D,
        moved=10 << 20,
    )


def dispatch_kernel(n_pieces, scaled, pos_ref, gate_ref, *refs):
    pieces, out_ref, rows_ref, sems = refs[:n_pieces], refs[n_pieces], refs[n_pieces + 1], refs[n_pieces + 2]
    height = rows_ref.shape[0] // n_pieces
    copies = [
        pltpu.make_async_copy(piece, rows_ref.at[pl.ds(p * height, height)], sems.at[p])
        for p, piece in enumerate(pieces)
    ]
    for c in copies:
        c.start()
    rank = lax.broadcasted_iota(jnp.int32, (CAP, rows_ref.shape[0]), 0)
    for c in copies:
        c.wait()
    for j in range(out_ref.shape[0]):
        chosen = rank == pos_ref[j : j + 1, :]
        value = gate_ref[j : j + 1, :] if scaled else 1.0
        one_hot = jnp.where(chosen, value, 0.0).astype(BF)
        out_ref[j] = mm(one_hot, rows_ref[...]).astype(BF)


def dispatch(pos, gate, pieces, scaled):
    experts, rows = pos.shape
    return call(
        functools.partial(dispatch_kernel, len(pieces), scaled),
        "dispatch_scaled" if scaled else "dispatch",
        jax.ShapeDtypeStruct((experts, CAP, D), BF),
        [VM, VM] + [ANY] * len(pieces),
        VM,
        (pos, gate, *pieces),
        scratch=[pltpu.VMEM((rows, D), BF), pltpu.SemaphoreType.DMA((len(pieces),))],
        flops=2 * experts * CAP * rows * D,
        moved=5 << 20,
    )


def combine_kernel(n_experts, slot, scaled, n_adds, n_outs, pos_ref, gate_ref, *refs):
    sources, refs = refs[:n_experts], refs[n_experts:]
    adds, outs, (held, sems) = refs[:n_adds], refs[n_adds : n_adds + n_outs], refs[n_adds + n_outs :]
    copies = [
        pltpu.make_async_copy(source.at[slot], held.at[pl.ds(j * CAP, CAP)], sems.at[j])
        for j, source in enumerate(sources)
    ]
    for c in copies:
        c.start()
    for c in copies:
        c.wait()
    width = n_experts * CAP
    rows = pos_ref.shape[0]
    block = 256
    per_out = rows // n_outs
    for b in range(rows // block):
        at = slice(b * block, (b + 1) * block)
        tiles = []
        for first in range(0, width, LANES):
            size = min(LANES, width - first)
            lane = first + lax.broadcasted_iota(jnp.int32, (block, size), 1)
            tile = jnp.zeros((block, size), F32)
            for j in range(first // CAP, (first + size - 1) // CAP + 1):
                target = pos_ref[at, j : j + 1]
                target = jnp.where(target >= 0, target + j * CAP, -1)
                tile = jnp.where(lane == target, gate_ref[at, j : j + 1] if scaled else 1.0, tile)
            tiles.append(tile.astype(BF))
        total = mm(jnp.concatenate(tiles, axis=1), held[...])
        out, inner = outs[b * block // per_out], slice(b * block % per_out, b * block % per_out + block)
        if n_adds:
            total = total + adds[0][at].astype(F32)
        out[inner] = total.astype(BF)


def combine(pos, gate, sources, slot, scaled, add, n_outs):
    rows, n_experts = pos.shape
    adds = [] if add is None else [add]
    return call(
        functools.partial(combine_kernel, n_experts, slot, scaled, len(adds), n_outs),
        "combine_scaled" if scaled else "combine",
        [jax.ShapeDtypeStruct((rows // n_outs, D), BF)] * n_outs,
        [VM, VM] + [ANY] * n_experts + [VM] * len(adds),
        [VM] * n_outs,
        (pos, gate, *sources, *adds),
        scratch=[pltpu.VMEM((n_experts * CAP, D), BF), pltpu.SemaphoreType.DMA((n_experts,))],
        flops=2 * n_experts * CAP * rows * D,
        moved=5 << 20,
    )


def expert_kernel(j, outer, in_rows, down_rows, idx_ref, *refs):
    n_hops = outer - 1
    xs, refs = refs[:GROUP], refs[GROUP:]
    gs, refs = refs[:GROUP], refs[GROUP:]
    own, refs = refs[0], refs[1:]
    lefts, refs = refs[:n_hops], refs[n_hops:]
    rights, refs = refs[:n_hops], refs[n_hops:]
    y_ref, dx_ref, dw_ref = refs[:3]
    x_all, g_all, w_in, w_down, act_all, gug_all, sem_x, sem_g, sem_w, sem_d = refs[3:]
    o, i = idx_ref[0], idx_ref[1]

    def rows_of(sources, held, sems):
        return [
            pltpu.make_async_copy(s.at[j], held.at[pl.ds(n * CAP, CAP)], sems.at[n])
            for n, s in enumerate(sources)
        ]

    def weight_copies(source, at, slot):
        made = []
        for m in range(GROUP):
            place = at * GROUP + (i ^ m)
            made.append(
                pltpu.make_async_copy(
                    source.at[m, pl.ds(0, in_rows)],
                    w_in.at[pl.ds(pl.multiple_of(place * in_rows, in_rows), in_rows)],
                    sem_w.at[slot * GROUP + m],
                )
            )
            made.append(
                pltpu.make_async_copy(
                    source.at[m, pl.ds(in_rows, down_rows)],
                    w_down.at[pl.ds(pl.multiple_of(place * down_rows, down_rows), down_rows)],
                    sem_d.at[slot * GROUP + m],
                )
            )
        return made

    def each_weight(act):
        act(weight_copies(own, o, 0))
        for k in range(1, outer):

            @pl.when(o >= k)
            def _():
                act(weight_copies(lefts[k - 1], o - k, k))

            @pl.when(o + k < outer)
            def _():
                act(weight_copies(rights[k - 1], o + k, n_hops + k))

    def start(made):
        for c in made:
            c.start()

    def wait(made):
        for c in made:
            c.wait()

    each_weight(start)
    copy_x, copy_g = rows_of(xs, x_all, sem_x), rows_of(gs, g_all, sem_g)
    start(copy_x)
    start(copy_g)
    each_weight(wait)
    wait(copy_x)
    wait(copy_g)

    def per_slot(s, carry):
        at = pl.ds(pl.multiple_of(s * CAP, CAP), CAP)
        gate_up = mm(x_all[at, :], w_in[...])
        g, u = gate_up[:, :FF], gate_up[:, FF:]
        sigma = 1.0 / (1.0 + jnp.exp(-g))
        silu = g * sigma
        act = (silu * u).astype(BF)
        act_all[at, :] = act
        y_ref[s] = mm(act, w_down[...]).astype(BF)
        act_grad = mm_nt(g_all[at, :], w_down[...])
        gug_all[at, :FF] = (act_grad * u * sigma * (1.0 + g * (1.0 - sigma))).astype(BF)
        gug_all[at, FF:] = (act_grad * silu).astype(BF)
        dx_ref[s] = mm_nt(gug_all[at, :], w_in[...]).astype(BF)
        return carry

    lax.fori_loop(0, GROUP, per_slot, 0)
    for c in range(outer):
        part = mm_tn(x_all[:, c * GROUP * in_rows : (c + 1) * GROUP * in_rows], gug_all[...]).astype(BF)
        for r in range(GROUP):
            dw_ref[c, i ^ r, :in_rows, :] = part[r * in_rows : (r + 1) * in_rows]
        part = mm_tn(act_all[:, c * GROUP * down_rows : (c + 1) * GROUP * down_rows], g_all[...]).astype(BF)
        for r in range(GROUP):
            dw_ref[c, i ^ r, in_rows:, :] = part[r * down_rows : (r + 1) * down_rows]


def expert(idx, j, outer, in_rows, down_rows, xs, gs, own, lefts, rights):
    n_hops = outer - 1
    total = GROUP * CAP
    packed = in_rows + down_rows
    return call(
        functools.partial(expert_kernel, j, outer, in_rows, down_rows),
        "expert",
        [
            jax.ShapeDtypeStruct((GROUP, CAP, D), BF),
            jax.ShapeDtypeStruct((GROUP, CAP, D), BF),
            jax.ShapeDtypeStruct((outer, GROUP, packed, D), BF),
        ],
        [SMEM] + [ANY] * (2 * GROUP + 1 + 2 * n_hops),
        [VM] * 3,
        (idx, *xs, *gs, own, *lefts, *rights),
        scratch=[
            pltpu.VMEM((total, D), BF),
            pltpu.VMEM((total, D), BF),
            pltpu.VMEM((D, 2 * FF), BF),
            pltpu.VMEM((FF, D), BF),
            pltpu.VMEM((total, FF), BF),
            pltpu.VMEM((total, 2 * FF), BF),
            pltpu.SemaphoreType.DMA((GROUP,)),
            pltpu.SemaphoreType.DMA((GROUP,)),
            pltpu.SemaphoreType.DMA(((1 + 2 * n_hops) * GROUP,)),
            pltpu.SemaphoreType.DMA(((1 + 2 * n_hops) * GROUP,)),
        ],
        flops=18 * total * D * FF,
        moved=15 << 20,
    )


def pack_kernel(n_experts, in_rows, down_rows, idx_ref, in_ref, down_ref, *refs):
    outs, sems = refs[:-1], refs[-1]
    i = idx_ref[1]
    copies = []
    for j in range(n_experts):
        for m in range(GROUP):
            n = j * GROUP + m
            source = (i ^ m) * n_experts + j
            copies.append(
                pltpu.make_async_copy(in_ref.at[source], outs[m].at[j, pl.ds(0, in_rows)], sems.at[2 * n])
            )
            copies.append(
                pltpu.make_async_copy(
                    down_ref.at[source], outs[m].at[j, pl.ds(in_rows, down_rows)], sems.at[2 * n + 1]
                )
            )
    for c in copies:
        c.start()
    for c in copies:
        c.wait()


def pack_weights(idx, expert_in, expert_down):
    experts, in_rows, _ = expert_in.shape
    down_rows = expert_down.shape[1]
    n = experts // GROUP
    return call(
        functools.partial(pack_kernel, n, in_rows, down_rows),
        "pack_weights",
        [jax.ShapeDtypeStruct((n, in_rows + down_rows, D), BF)] * GROUP,
        [SMEM, ANY, ANY],
        [VM] * GROUP,
        (idx, expert_in, expert_down),
        scratch=[pltpu.SemaphoreType.DMA((2 * experts,))],
        moved=6 << 20,
    )


def place():
    d, t = lax.axis_index("dp"), lax.axis_index("tensor")
    return d, t, d // GROUP, d % GROUP


def flip(v, m):
    first, second = v % 2, (v // 2) % 2
    if m & 1:
        v = v + 1 - 2 * first
    if m & 2:
        v = v + 2 - 4 * second
    return v


def greet(outer, distances, tensor):
    d, t, o, _ = place()
    barrier = pltpu.get_barrier_semaphore()
    count = 0
    for m in distances:
        pl.semaphore_signal(barrier, inc=1, device_id=(flip(d, m), t), device_id_type=MESH)
        count += 1
    if tensor:
        pl.semaphore_signal(barrier, inc=1, device_id=(d, 1 - t), device_id_type=MESH)
        count += 1

    @pl.when(o > 0)
    def _():
        pl.semaphore_signal(barrier, inc=1, device_id=(d - GROUP, t), device_id_type=MESH)

    @pl.when(o < outer - 1)
    def _():
        pl.semaphore_signal(barrier, inc=1, device_id=(d + GROUP, t), device_id_type=MESH)

    neighbours = (o + outer - 1) // outer + (2 * outer - 2 - o) // outer
    pl.semaphore_wait(barrier, count + neighbours)


class Hops:
    def __init__(self, outer, steps, sent, came):
        d, t, o, _ = place()
        self.moves = []
        for n, (k, from_left, from_right, to_left, to_right) in enumerate(steps):
            back = outer - 1 - o
            right = pltpu.make_async_remote_copy(
                from_left, to_left, sent.at[2 * n], came.at[2 * n], device_id=(d + GROUP, t), device_id_type=MESH
            )
            left = pltpu.make_async_remote_copy(
                from_right,
                to_right,
                sent.at[2 * n + 1],
                came.at[2 * n + 1],
                device_id=(d - GROUP, t),
                device_id_type=MESH,
            )
            self.moves.append((right, (o >= k - 1) & (back >= 1), o >= k))
            self.moves.append((left, (back >= k - 1) & (o >= 1), back >= k))

    def start(self):
        for copy, sends, _ in self.moves:
            pl.when(sends)(copy.start)

    def wait(self):
        for copy, sends, receives in self.moves:
            pl.when(sends)(copy.wait_send)
            pl.when(receives)(copy.wait_recv)


def greet_all(outer):
    d, t, o, i = place()
    barrier = pltpu.get_barrier_semaphore()
    for m in range(1, GROUP):
        pl.semaphore_signal(barrier, inc=1, device_id=(flip(d, m), t), device_id_type=MESH)
    pl.semaphore_signal(barrier, inc=1, device_id=(d, 1 - t), device_id_type=MESH)
    for k in range(1, outer):
        pl.semaphore_signal(barrier, inc=1, device_id=((o + k) % outer * GROUP + i, t), device_id_type=MESH)
    pl.semaphore_wait(barrier, GROUP - 1 + outer)


def to_x(src, dst, sent, came):
    d, t, _, _ = place()
    return pltpu.make_async_remote_copy(src, dst, sent, came, device_id=(d, 1 - t), device_id_type=MESH)


def to_dp(m, src, dst, sent, came):
    d, t, _, _ = place()
    return pltpu.make_async_remote_copy(src, dst, sent, came, device_id=(flip(d, m), t), device_id_type=MESH)


def remote_call(kernel, name, collective_id, out_shape, in_specs, out_specs, args, scratch, flops):
    return pl.pallas_call(
        kernel,
        name=name,
        out_shape=out_shape,
        in_specs=in_specs,
        out_specs=out_specs,
        scratch_shapes=list(scratch),
        compiler_params=pltpu.CompilerParams(
            vmem_limit_bytes=VMEM_LIMIT, collective_id=collective_id, has_side_effects=True
        ),
        cost_estimate=pl.CostEstimate(flops=flops, bytes_accessed=8 << 20, transcendentals=0),
    )(*args)


def collect_kernel(outer, in_rows, down_rows, shard_ref, normed_ref, gates_ref, freq_ref, in_ref, down_ref, *refs):
    w_ref, other_ref, cos_ref, sin_ref, pos_ref, gate_ref, posc_ref, gatec_ref = refs[:8]
    own_refs, packed_refs, to_left, to_right = refs[8:10], refs[10:12], refs[12], refs[13]
    packed, gates_all, before, l_w, l_in, l_down, l_own = refs[14:21]
    s_z, r_z, s_y, r_y, s_c, r_c, s_x, r_x, s_g, r_g, s_a, r_a, s_hop, r_hop = refs[21:]
    d, t, o, i = place()
    each = shard_ref.shape[0]
    width = w_ref.shape[1] // 2
    own_width = shard_ref.shape[1]
    n_local = in_ref.shape[0]
    n = n_local // GROUP
    slot_rows = gates_all.shape[2]
    half = slot_rows // 4

    def block(which, index):
        return pl.ds(pl.multiple_of((which * GROUP + index) * each, each), each)

    def lanes(h):
        return pl.ds(h * width, width)

    local = pltpu.make_async_copy(shard_ref, w_ref.at[block(o, i), pl.ds(0, own_width)], l_w)
    local.start()
    packs = []
    for j in range(n):
        for m in range(GROUP):
            source, k = flip(i, m) * n + j, j * GROUP + m
            packs.append(
                (
                    pltpu.make_async_copy(in_ref.at[source], packed.at[j, m, pl.ds(0, in_rows)], l_in.at[k]),
                    pltpu.make_async_copy(down_ref.at[source], packed.at[j, m, pl.ds(in_rows, down_rows)], l_down.at[k]),
                )
            )
    for pair in packs:
        for c in pair:
            c.start()
    greet_all(outer)

    x_moves = [
        to_x(shard_ref.at[:, pl.ds(width, own_width - width)], w_ref.at[block(o, i), pl.ds(own_width, 2 * width - own_width)], s_x.at[0], r_x.at[0]),
        to_x(normed_ref, other_ref, s_x.at[1], r_x.at[1]),
    ]
    g_x = [
        to_x(
            gates_ref.at[:, pl.ds(p * half, half)],
            gates_all.at[0, :, pl.ds((2 * p + 1) * half, half)],
            s_g.at[p],
            r_g.at[p],
        )
        for p in range(2)
    ]
    g_y = to_dp(2, gates_all.at[0], gates_all.at[1], s_g.at[2], r_g.at[2])
    g_c = [to_dp(1, gates_all.at[s], gates_all.at[2 + s], s_g.at[3 + s], r_g.at[3 + s]) for s in range(2)]

    def z_move(k, h):
        peer = (o + k) % outer
        source = shard_ref.at[:, pl.ds(0, width)] if h == 0 else w_ref.at[block(o, i), lanes(1)]
        return pltpu.make_async_remote_copy(
            source,
            w_ref.at[block(o, i), lanes(h)],
            s_z.at[2 * k - 2 + h],
            r_z.at[2 * k - 2 + h],
            device_id=(peer * GROUP + i, t),
            device_id_type=MESH,
        )

    def near_source(b, h):
        if b == 0 and h == 0:
            return shard_ref.at[:, pl.ds(0, width)]
        return w_ref.at[block((o + outer - b) % outer, i), lanes(h)]

    def y_move(b, h):
        target = w_ref.at[block((o + outer - b) % outer, i), lanes(h)]
        return to_dp(2, near_source(b, h), target, s_y.at[2 * b + h], r_y.at[2 * b + h])

    def c_move(b, far, h):
        target = w_ref.at[block((o + outer - b) % outer, flip(i, 2) if far else i), lanes(h)]
        source = target if far else near_source(b, h)
        k = (2 * b + far) * 2 + h
        return to_dp(1, source, target, s_c.at[k], r_c.at[k])

    def weights_move(j, m):
        return to_dp(m, packed.at[j, m], own_refs[j].at[m], s_a.at[3 * j + m - 1], r_a.at[3 * j + m - 1])

    keeps = [pltpu.make_async_copy(packed.at[j, 0], own_refs[j].at[0], l_own.at[j]) for j in range(2)]
    stays = [pltpu.make_async_copy(packed.at[2 + j], packed_refs[j], l_own.at[2 + j]) for j in range(2)]
    hops = Hops(outer, [(1, own_refs[0], own_refs[0], to_left, to_right)], s_hop, r_hop)

    def packed_there(j):
        for pair in packs[j * GROUP : (j + 1) * GROUP]:
            for c in pair:
                c.wait()

    x_moves[0].start()
    for c in g_x:
        c.start()
    for k in range(1, outer):
        z_move(k, 0).start()
    y_move(0, 0).start()
    c_move(0, 0, 0).start()
    packed_there(0)
    for m in range(1, GROUP):
        weights_move(0, m).start()
    keeps[0].start()
    x_moves[1].start()
    local.wait()
    x_moves[0].wait()
    for k in range(1, outer):
        z_move(k, 1).start()
    packed_there(1)
    keeps[1].start()
    for j in range(2):
        packed_there(2 + j)
        stays[j].start()
    gates_all[0, :, 0:half] = gates_ref[:, 0:half]
    gates_all[0, :, 2 * half : 3 * half] = gates_ref[:, half:]
    block_rows = 128

    def table(b, carry):
        at = pl.ds(pl.multiple_of(b * block_rows, block_rows), block_rows)
        row = b * block_rows + lax.broadcasted_iota(jnp.int32, (block_rows, LANES), 0)
        angles = row.astype(F32) * freq_ref[...]
        lane = lax.broadcasted_iota(jnp.int32, (block_rows, LANES), 1)
        sine = jnp.sin(angles)
        cos_ref[at, :] = jnp.cos(angles)
        sin_ref[at, :] = jnp.where(lane % HD < HD // 2, -sine, sine)
        return carry

    lax.fori_loop(0, slot_rows // block_rows, table, 0)
    for c in g_x:
        c.wait()
    g_y.start()
    g_c[0].start()
    for k in range(1, outer):
        z_move(k, 0).wait_recv()
        y_move(k, 0).start()
        c_move(k, 0, 0).start()
    for m in range(1, GROUP):
        weights_move(1, m).start()
    for b in range(1):
        y_move(b, 1).start()
        c_move(b, 0, 1).start()
    before[...] = (
        lax.broadcasted_iota(jnp.int32, before.shape, 0) < lax.broadcasted_iota(jnp.int32, before.shape, 1)
    ).astype(F32).astype(BF)
    keeps[0].wait()
    for m in range(1, GROUP):
        weights_move(0, m).wait_recv()
    hops.start()
    g_y.wait()
    g_c[1].start()
    for k in range(1, outer):
        z_move(k, 1).wait_recv()
        y_move(k, 1).start()
        c_move(k, 0, 1).start()
    for b in range(outer):
        y_move(b, 0).wait_recv()
        c_move(b, 1, 0).start()
    for c in g_c:
        c.wait()
    n_all = gates_all.shape[1]
    first = t * n_local + i * n
    pick = (
        lax.broadcasted_iota(jnp.int32, (8, n_all), 1) == lax.broadcasted_iota(jnp.int32, (8, n_all), 0) + first
    ).astype(F32).astype(BF)
    for s in range(GROUP):
        gate = mm(pick, gates_all[s])
        rank = mm((gate > 0).astype(F32).astype(BF), before[...])
        gate_ref[s] = gate[:n]
        pos_ref[s] = jnp.where(gate > 0, rank, -1.0).astype(jnp.int32)[:n]
        gate = lax.dot_general(gates_all[s], pick, (((0,), (1,)), ((), ())), preferred_element_type=F32)
        rank = mm_tn(before[...], (gate > 0).astype(F32).astype(BF))
        gatec_ref[s] = gate[:, :n]
        posc_ref[s] = jnp.where(gate > 0, rank, -1.0).astype(jnp.int32)[:, :n]
    for b in range(outer):
        y_move(b, 1).wait_recv()
        c_move(b, 1, 1).start()
    for k in range(1, outer):
        for h in range(2):
            z_move(k, h).wait_send()
    for b in range(outer):
        for h in range(2):
            y_move(b, h).wait_send()
            c_move(b, 0, h).wait()
            c_move(b, 1, h).wait()
    for m in range(1, GROUP):
        weights_move(0, m).wait_send()
        weights_move(1, m).wait()
    x_moves[1].wait()
    keeps[1].wait()
    for c in stays:
        c.wait()
    hops.wait()


def collect(outer, shard, normed, gates, frequency, expert_in, expert_down):
    each, own_width = shard.shape
    width = own_width * 2 // 3
    rows = normed.shape[0]
    experts, in_rows, _ = expert_in.shape
    down_rows = expert_down.shape[1]
    n = experts // GROUP
    packed = in_rows + down_rows
    hop = jax.ShapeDtypeStruct((GROUP, packed, D), BF)
    dma = pltpu.SemaphoreType.DMA
    out = remote_call(
        functools.partial(collect_kernel, outer, in_rows, down_rows),
        "collect",
        13,
        [
            jax.ShapeDtypeStruct((D, 2 * width), BF),
            jax.ShapeDtypeStruct((rows, D), BF),
            jax.ShapeDtypeStruct((2 * rows, LANES), F32),
            jax.ShapeDtypeStruct((2 * rows, LANES), F32),
            jax.ShapeDtypeStruct((GROUP, n, 2 * rows), jnp.int32),
            jax.ShapeDtypeStruct((GROUP, n, 2 * rows), F32),
            jax.ShapeDtypeStruct((GROUP, 2 * rows, n), jnp.int32),
            jax.ShapeDtypeStruct((GROUP, 2 * rows, n), F32),
        ]
        + [hop] * 6,
        [VM] * 4 + [ANY] * 2,
        [VM] * 8 + [ANY] * 6,
        (shard, normed, gates, frequency, expert_in, expert_down),
        [
            pltpu.VMEM((n, GROUP, packed, D), BF),
            pltpu.VMEM((GROUP, gates.shape[0], 2 * rows), BF),
            pltpu.VMEM((2 * rows, 2 * rows), BF),
            dma,
            dma((experts,)),
            dma((experts,)),
            dma((4,)),
            dma((2 * outer - 2,)),
            dma((2 * outer - 2,)),
            dma((2 * outer,)),
            dma((2 * outer,)),
            dma((4 * outer,)),
            dma((4 * outer,)),
            dma((2,)),
            dma((2,)),
            dma((5,)),
            dma((5,)),
            dma((6,)),
            dma((6,)),
            dma((2,)),
            dma((2,)),
        ],
        4 << 30,
    )
    return out[:8], out[8:10], out[10:12], out[12], out[13]


def attention_kernel(outer, q_block, n_steps, len_ref, own_ref, other_ref, w_ref, cos_ref, sin_ref, x_ref, gain_ref, *refs):
    width = w_ref.shape[1] // 2
    heads = width // 2
    cot_ref, ready, packed_refs, refs = refs[0], refs[1], refs[2:4], refs[4:]
    qkv_out, lse_ref, attn_ref, come_ref, hidden_out, na_ref, nb_ref = refs[:7]
    refs = refs[7:]
    dy_outs, own_refs, refs = refs[:4], refs[4:6], refs[6:]
    to_left, refs = refs[:n_steps], refs[n_steps:]
    to_right, refs = refs[:n_steps], refs[n_steps:]
    send_ref, s_hop, r_hop, s_later, r_later, s_dy, r_dy, s_at, r_at, s_a, r_a, l_own, qkv_ref, hidden_ref, o_sem = refs
    qkv_copy = pltpu.make_async_copy(qkv_ref, qkv_out, o_sem.at[0])
    hidden_copy = pltpu.make_async_copy(hidden_ref, hidden_out, o_sem.at[1])
    d, t, o, i = place()
    length = len_ref[0]
    rows = own_ref.shape[0]
    groups = width // (2 * LANES)
    greet(outer, (1, 2, 3), True)
    hops = Hops(outer, [(1, ready, ready, to_left[0], to_right[0])], s_hop, r_hop)
    later = [
        Hops(outer, [(1, own_refs[k], own_refs[k], to_left[1 + k], to_right[1 + k])], s_later.at[k], r_later.at[k])
        for k in range(2)
    ]
    keeps = [pltpu.make_async_copy(packed_refs[k].at[0], own_refs[k].at[0], l_own.at[k]) for k in range(2)]
    weights = [
        to_dp(m, packed_refs[k].at[m], own_refs[k].at[m], s_a.at[3 * k + m - 1], r_a.at[3 * k + m - 1])
        for k in range(2)
        for m in range(1, GROUP)
    ]
    hops.start()
    for copy in (*weights, *keeps):
        copy.start()
    ax, bx, ay, by = dy_outs
    dy_a, dy_b = (cot_ref.at[pl.ds(p * rows // 2, rows // 2)] for p in range(2))
    dys = [
        to_x(dy_a, ax, s_dy.at[0], r_dy.at[0]),
        to_dp(2, dy_b, by, s_dy.at[1], r_dy.at[1]),
        to_x(dy_b, bx, s_dy.at[2], r_dy.at[2]),
        to_dp(2, dy_a, ay, s_dy.at[3], r_dy.at[3]),
    ]

    block = 256
    key_lanes = lax.broadcasted_iota(jnp.int32, (block, LANES), 1) < HD
    for part, source in enumerate((own_ref, other_ref)):

        def project(b, carry, part=part, source=source):
            here = pl.ds(pl.multiple_of(b * block, block), block)
            at = pl.multiple_of((t if part == 0 else 1 - t) * rows + b * block, block)
            projected = mm(source[here, :], w_ref[:, :width])
            cosine, sine = cos_ref[pl.ds(at, block), :], sin_ref[pl.ds(at, block), :]
            for g in range(groups):
                q = projected[:, g * 2 * LANES : g * 2 * LANES + LANES]
                kv = projected[:, g * 2 * LANES + LANES : (g + 1) * 2 * LANES]
                q = q * cosine + swap_halves(q) * sine
                kv = jnp.where(key_lanes, kv * cosine + swap_halves(kv) * sine, kv)
                qkv_ref[pl.ds(at, block), g * 2 * LANES : g * 2 * LANES + LANES] = q.astype(BF)
                qkv_ref[pl.ds(at, block), g * 2 * LANES + LANES : (g + 1) * 2 * LANES] = kv.astype(BF)
            return carry

        lax.fori_loop(0, rows // block, project, 0)

    for copy in dys:
        copy.start()

    def exchange(g):
        lanes = pl.ds(pl.multiple_of(g * LANES, LANES), LANES)
        return to_x(send_ref.at[:, lanes], come_ref.at[:, lanes], s_at.at[g], r_at.at[g])

    def per_group(g, carry):
        q_lanes = pl.ds(pl.multiple_of(g * 2 * LANES, LANES), LANES)
        kv_lanes = pl.ds(pl.multiple_of(g * 2 * LANES + LANES, LANES), LANES)
        o_lanes = pl.ds(pl.multiple_of(g * LANES, LANES), LANES)
        keys, values = doubled(qkv_ref[:, kv_lanes])
        for b in range(2 * rows // q_block):
            start, n_keys = b * q_block, (b + 1) * q_block
            q = head_pair(qkv_ref[start : start + q_block, q_lanes])
            scores = mm_nt(keys[:n_keys], q) * (1.0 / math.sqrt(HD))
            scores = jnp.where(allowed(n_keys, q_block, start, length), scores, NEGATIVE)
            largest = jnp.max(scores, axis=0, keepdims=True)
            expon = jnp.exp(scores - largest)
            totals = jnp.sum(expon, axis=0, keepdims=True)
            probs = (expon * (1.0 / totals)).astype(BF)
            mixed = head_join(mm_tn(probs, values[:n_keys])).astype(BF)
            lse_ref[g, b : b + 1, :] = largest + jnp.log(totals)
            half, inner = start // rows, start % rows

            @pl.when(t == half)
            def _():
                attn_ref[inner : inner + q_block, o_lanes] = mixed

            @pl.when(t != half)
            def _():
                send_ref[inner : inner + q_block, o_lanes] = mixed

        exchange(g).start()

        for k in range(2):

            @pl.when(g == k)
            def _(k=k):
                for copy in (*weights[(GROUP - 1) * k : (GROUP - 1) * (k + 1)], keeps[k]):
                    copy.wait()
                later[k].start()

        return carry

    lax.fori_loop(0, groups, per_group, 0)

    qkv_copy.start()

    def settle(g, carry):
        exchange(g).wait()
        return carry

    for p, normed_ref in enumerate((na_ref, nb_ref)):
        at = slice(p * rows // 2, (p + 1) * rows // 2)
        hidden_ref[at] = x_ref[at].astype(F32) + mm_nt(attn_ref[at], w_ref[:, width : width + heads])
    lax.fori_loop(0, groups, settle, 0)
    for p, normed_ref in enumerate((na_ref, nb_ref)):
        at = slice(p * rows // 2, (p + 1) * rows // 2)
        hidden = hidden_ref[at] + mm_nt(come_ref[at], w_ref[:, width + heads :])
        inverse = lax.rsqrt(jnp.mean(hidden * hidden, axis=-1, keepdims=True) + EPSILON)
        hidden_ref[at] = hidden
        normed_ref[...] = (hidden * inverse * gain_ref[...]).astype(BF)
    hidden_copy.start()
    for copy in dys:
        copy.wait()
    hops.wait()
    for one in later:
        one.wait()
    qkv_copy.wait()
    hidden_copy.wait()


def attention(outer, q_block, length, own, other, weights_full, cosine, sine, x, gain, cotangent, ready, packed):
    rows, groups = own.shape[0], weights_full.shape[1] // (4 * LANES)
    n = 3
    piece = jax.ShapeDtypeStruct((rows // 2, D), BF)
    hop = jax.ShapeDtypeStruct(ready.shape, BF)
    out = remote_call(
        functools.partial(attention_kernel, outer, q_block, n),
        "attention",
        1,
        [
            jax.ShapeDtypeStruct((2 * rows, groups * 2 * LANES), BF),
            jax.ShapeDtypeStruct((groups, 2 * rows // q_block, 2 * q_block), F32),
            jax.ShapeDtypeStruct((rows, groups * LANES), BF),
            jax.ShapeDtypeStruct((rows, groups * LANES), BF),
            jax.ShapeDtypeStruct((rows, D), F32),
            piece,
            piece,
        ]
        + [piece] * 4
        + [hop] * (2 + 2 * n),
        [SMEM] + [VM] * 7 + [ANY] * 4,
        [ANY] + [VM] * 3 + [ANY] + [VM] * 2 + [ANY] * (6 + 2 * n),
        (length, own, other, weights_full, cosine, sine, x, gain.reshape(1, D), cotangent, ready, *packed),
        [
            pltpu.VMEM((rows, groups * LANES), BF),
            pltpu.SemaphoreType.DMA((2,)),
            pltpu.SemaphoreType.DMA((2,)),
            pltpu.SemaphoreType.DMA((2, 2)),
            pltpu.SemaphoreType.DMA((2, 2)),
            pltpu.SemaphoreType.DMA((4,)),
            pltpu.SemaphoreType.DMA((4,)),
            pltpu.SemaphoreType.DMA((groups,)),
            pltpu.SemaphoreType.DMA((groups,)),
            pltpu.SemaphoreType.DMA((6,)),
            pltpu.SemaphoreType.DMA((6,)),
            pltpu.SemaphoreType.DMA((2,)),
            pltpu.VMEM((2 * rows, groups * 2 * LANES), BF),
            pltpu.VMEM((rows, D), F32),
            pltpu.SemaphoreType.DMA((2,)),
        ],
        30 << 30,
    )
    return out[:7], out[7:11], out[11:13], out[13 : 13 + n], out[13 + n :]


def one_hot_rows(pos, gate, j, n_rows):
    rank = lax.broadcasted_iota(jnp.int32, (CAP, n_rows), 0)
    chosen = rank == pos[j : j + 1, :]
    return jnp.where(chosen, 1.0 if gate is None else gate[j : j + 1, :], 0.0).astype(BF)


def spread_kernel(outer, steps, pos_ref, gate_ref, na_ref, nb_ref, *refs):
    n_steps = len(steps)
    cot_ref, dy_refs, refs = refs[0], refs[1:5], refs[5:]
    from_left, refs = refs[:n_steps], refs[n_steps:]
    from_right, refs = refs[:n_steps], refs[n_steps:]
    n_ref, dyx_ref, og_out = refs[:3]
    refs = refs[3:]
    to_left, refs = refs[:n_steps], refs[n_steps:]
    to_right, refs = refs[:n_steps], refs[n_steps:]
    held, s_hop, r_hop, s_n, r_n, s_d, r_d, l_sem, og_ref, o_sem = refs
    height = na_ref.shape[0]
    n_experts = og_ref.shape[1]
    leave = [pltpu.make_async_copy(og_ref.at[s % 2], og_out.at[s], o_sem.at[s]) for s in range(GROUP)]
    greet(outer, (1, 2), True)
    n_ax = to_x(na_ref, n_ref.at[0, 1], s_n.at[0], r_n.at[0])
    n_by = to_dp(2, nb_ref, n_ref.at[1, 2], s_n.at[1], r_n.at[1])
    n_bx = to_x(nb_ref, n_ref.at[0, 3], s_n.at[2], r_n.at[2])
    n_ay = to_dp(2, na_ref, n_ref.at[1, 0], s_n.at[3], r_n.at[3])
    n_axy = to_dp(2, n_ref.at[0, 1], n_ref.at[1, 1], s_n.at[4], r_n.at[4])
    n_bxy = to_x(n_ref.at[1, 2], n_ref.at[1, 3], s_n.at[5], r_n.at[5])
    core = {}
    for n, (s, p) in enumerate([(s, p) for s in range(2) for p in range(4)]):
        source = na_ref if (s, p) == (0, 0) else nb_ref if (s, p) == (0, 2) else n_ref.at[s, p]
        core[s, p] = to_dp(1, source, n_ref.at[2 + s, p], s_n.at[6 + n], r_n.at[6 + n])
    for copy in (n_ax, n_by, n_bx, n_ay):
        copy.start()
    d_a, d_b = (cot_ref.at[pl.ds(p * height, height)] for p in range(2))
    d_ax, d_bx, d_ay, d_by = dy_refs
    d_axy = to_dp(2, d_ax, dyx_ref.at[0, 1], s_d.at[0], r_d.at[0])
    d_bxy = to_x(d_by, dyx_ref.at[0, 3], s_d.at[1], r_d.at[1])
    d_axy.start()
    d_bxy.start()
    d_near = [[d_a, d_ax, d_b, d_bx], [d_ay, dyx_ref.at[0, 1], d_by, dyx_ref.at[0, 3]]]
    d_core = {}
    for n, (s, p) in enumerate([(s, p) for s in range(2) for p in range(4)]):
        d_core[s, p] = to_dp(1, d_near[s][p], dyx_ref.at[1 + s, p], s_d.at[2 + n], r_d.at[2 + n])
    for key in ((0, 0), (0, 1), (0, 2), (0, 3), (1, 0), (1, 2)):
        d_core[key].start()
    core[0, 0].start()
    core[0, 2].start()
    hops = Hops(
        outer,
        [(k, a, b, l, r) for k, a, b, l, r in zip(steps, from_left, from_right, to_left, to_right, strict=True)],
        s_hop,
        r_hop,
    )
    hops.start()

    def load(s):
        pieces = d_near[s] if s < 2 else [dyx_ref.at[s - 1, p] for p in range(4)]
        return [
            pltpu.make_async_copy(piece, held.at[pl.ds(p * height, height)], l_sem.at[p])
            for p, piece in enumerate(pieces)
        ]

    def give(s):
        copies = load(s)
        for c in copies:
            c.start()
        for c in copies:
            c.wait()
        if s >= 2:
            leave[s - 2].wait()

        def one(j, carry):
            rank = lax.broadcasted_iota(jnp.int32, (CAP, 4 * height), 0)
            chosen = rank == pos_ref[s, pl.ds(j, 1), :]
            one_hot = jnp.where(chosen, gate_ref[s, pl.ds(j, 1), :], 0.0).astype(BF)
            og_ref[s % 2, j] = mm(one_hot, held[...]).astype(BF)
            return carry

        lax.fori_loop(0, n_experts, one, 0)
        leave[s].start()

    give(0)
    n_ax.wait()
    n_by.wait()
    n_axy.start()
    n_bxy.start()
    core[0, 1].start()
    core[1, 2].start()
    d_axy.wait()
    d_bxy.wait()
    d_core[1, 1].start()
    d_core[1, 3].start()
    give(1)
    n_bx.wait()
    n_ay.wait()
    core[0, 3].start()
    core[1, 0].start()
    for p in range(4):
        d_core[0, p].wait()
    give(2)
    n_axy.wait()
    n_bxy.wait()
    core[1, 1].start()
    core[1, 3].start()
    for p in range(4):
        d_core[1, p].wait()
    give(3)
    for key in core:
        core[key].wait()
    for s in range(2, GROUP):
        leave[s].wait()
    hops.wait()


def spread(outer, pos, gate, normed, dys, steps, from_left, from_right):
    height = normed[0].shape[0]
    n, n_experts = len(steps), pos.shape[1]
    weights = [jax.ShapeDtypeStruct(s.shape, BF) for s in from_left]
    out = remote_call(
        functools.partial(spread_kernel, outer, steps),
        "spread",
        2,
        [
            jax.ShapeDtypeStruct((GROUP, 4, height, D), BF),
            jax.ShapeDtypeStruct((3, 4, height, D), BF),
            jax.ShapeDtypeStruct((GROUP, n_experts, CAP, D), BF),
        ]
        + weights * 2,
        [VM] * 2 + [ANY] * (2 + 5 + 2 * n),
        [ANY] * (3 + 2 * n),
        (pos, gate, *normed, *dys, *from_left, *from_right),
        [
            pltpu.VMEM((4 * height, D), BF),
            pltpu.SemaphoreType.DMA((2 * n,)),
            pltpu.SemaphoreType.DMA((2 * n,)),
            pltpu.SemaphoreType.DMA((14,)),
            pltpu.SemaphoreType.DMA((14,)),
            pltpu.SemaphoreType.DMA((10,)),
            pltpu.SemaphoreType.DMA((10,)),
            pltpu.SemaphoreType.DMA((4,)),
            pltpu.VMEM((2, n_experts, CAP, D), BF),
            pltpu.SemaphoreType.DMA((GROUP,)),
        ],
        12 << 30,
    )
    return out[0], out[2], out[3 : 3 + n], out[3 + n :]


def hand_out_kernel(outer, steps, pos_ref, na_ref, nb_ref, n_ref, *refs):
    n_steps = len(steps)
    from_left, refs = refs[:n_steps], refs[n_steps:]
    from_right, refs = refs[:n_steps], refs[n_steps:]
    x_out, refs = refs[0], refs[1:]
    to_left, refs = refs[:n_steps], refs[n_steps:]
    to_right, refs = refs[:n_steps], refs[n_steps:]
    held, s_hop, r_hop, l_sem, x_ref, o_sem = refs
    leave = [pltpu.make_async_copy(x_ref.at[s % 2], x_out.at[s], o_sem.at[s]) for s in range(GROUP)]
    height = na_ref.shape[0]
    n_experts = x_ref.shape[1]
    greet(outer, (), False)
    hops = Hops(
        outer,
        [(k, a, b, l, r) for k, a, b, l, r in zip(steps, from_left, from_right, to_left, to_right, strict=True)],
        s_hop,
        r_hop,
    )
    hops.start()

    def load(s):
        pieces = [na_ref, n_ref.at[0, 1], nb_ref, n_ref.at[0, 3]] if s == 0 else [n_ref.at[s, p] for p in range(4)]
        return [
            pltpu.make_async_copy(piece, held.at[s % 2, pl.ds(p * height, height)], l_sem.at[s % 2, p])
            for p, piece in enumerate(pieces)
        ]

    for c in load(0):
        c.start()
    for s in range(GROUP):
        if s + 1 < GROUP:
            for c in load(s + 1):
                c.start()
        for c in load(s):
            c.wait()
        if s >= 2:
            leave[s - 2].wait()

        def one(j, carry, s=s):
            rank = lax.broadcasted_iota(jnp.int32, (CAP, 4 * height), 0)
            one_hot = jnp.where(rank == pos_ref[s, pl.ds(j, 1), :], 1.0, 0.0).astype(BF)
            x_ref[s % 2, j] = mm(one_hot, held[s % 2]).astype(BF)
            return carry

        lax.fori_loop(0, n_experts, one, 0)
        leave[s].start()
    for s in range(2, GROUP):
        leave[s].wait()
    hops.wait()


def hand_out(outer, pos, normed, gathered, steps, from_left, from_right):
    height = normed[0].shape[0]
    n, n_experts = len(steps), pos.shape[1]
    weights = [jax.ShapeDtypeStruct(s.shape, BF) for s in from_left]
    out = remote_call(
        functools.partial(hand_out_kernel, outer, steps),
        "hand_out",
        3,
        [jax.ShapeDtypeStruct((GROUP, n_experts, CAP, D), BF)] + weights * 2,
        [VM] + [ANY] * (3 + 2 * n),
        [ANY] * (1 + 2 * n),
        (pos, *normed, gathered, *from_left, *from_right),
        [
            pltpu.VMEM((2, 4 * height, D), BF),
            pltpu.SemaphoreType.DMA((2 * n,)),
            pltpu.SemaphoreType.DMA((2 * n,)),
            pltpu.SemaphoreType.DMA((2, 4)),
            pltpu.VMEM((2, n_experts, CAP, D), BF),
            pltpu.SemaphoreType.DMA((GROUP,)),
        ],
        12 << 30,
    )
    return out[0], out[1 : 1 + n], out[1 + n :]


def expert_step_kernel(j, outer, in_rows, down_rows, steps, sum_steps, x_ref, g_ref, own, *refs):
    n_hops, n_steps, n_sums = outer - 1, len(steps), len(sum_steps)
    lefts, refs = refs[:n_hops], refs[n_hops:]
    rights, refs = refs[:n_hops], refs[n_hops:]
    from_left, refs = refs[:n_steps], refs[n_steps:]
    from_right, refs = refs[:n_steps], refs[n_steps:]
    dws, refs = refs[:n_sums], refs[n_sums:]
    was_l, refs = refs[:n_sums], refs[n_sums:]
    was_r, refs = refs[:n_sums], refs[n_sums:]
    y_out, dx_out, dw_out = refs[:3]
    refs = refs[3:]
    to_left, refs = refs[:n_steps], refs[n_steps:]
    to_right, refs = refs[:n_steps], refs[n_steps:]
    sum_left, refs = refs[:n_sums], refs[n_sums:]
    sum_right, refs = refs[:n_sums], refs[n_sums:]
    x_all, g_all, w_in, w_down, act_all, gug_all, sem_x, sem_g, sem_w, sem_d, s_hop, r_hop = refs[:12]
    (y_ref, dx_ref, dw_ref, o_sem), refs = refs[12:16], refs[16:]
    _, _, o, i = place()
    greet(outer, (), False)
    sums = Sums(outer, sum_steps, dws, was_l, was_r, sum_left, sum_right, *refs)
    if n_steps:
        hops = Hops(
            outer,
            [(k, a, b, l, r) for k, a, b, l, r in zip(steps, from_left, from_right, to_left, to_right, strict=True)],
            s_hop,
            r_hop,
        )
        hops.start()

    def rows_of(source, held, sems):
        return [
            pltpu.make_async_copy(source.at[n, j], held.at[pl.ds(n * CAP, CAP)], sems.at[n]) for n in range(GROUP)
        ]

    def weight_copies(source, at, slot):
        made = []
        for m in range(GROUP):
            where = at * GROUP + flip(i, m)
            made.append(
                pltpu.make_async_copy(
                    source.at[m, pl.ds(0, in_rows)],
                    w_in.at[pl.ds(pl.multiple_of(where * in_rows, in_rows), in_rows)],
                    sem_w.at[slot * GROUP + m],
                )
            )
            made.append(
                pltpu.make_async_copy(
                    source.at[m, pl.ds(in_rows, down_rows)],
                    w_down.at[pl.ds(pl.multiple_of(where * down_rows, down_rows), down_rows)],
                    sem_d.at[slot * GROUP + m],
                )
            )
        return made

    def each_weight(act):
        act(weight_copies(own, o, 0))
        for k in range(1, outer):

            @pl.when(o >= k)
            def _():
                act(weight_copies(lefts[k - 1], o - k, k))

            @pl.when(o + k < outer)
            def _():
                act(weight_copies(rights[k - 1], o + k, n_hops + k))

    def start(made):
        for c in made:
            c.start()

    def wait(made):
        for c in made:
            c.wait()

    sums.load()
    each_weight(start)
    copy_x, copy_g = rows_of(x_ref, x_all, sem_x), rows_of(g_ref, g_all, sem_g)
    start(copy_x)
    start(copy_g)
    sums.send()
    each_weight(wait)
    wait(copy_x)
    wait(copy_g)

    def per_slot(s, carry):
        at = pl.ds(pl.multiple_of(s * CAP, CAP), CAP)
        gate_up = mm(x_all[at, :], w_in[...])
        g, u = gate_up[:, :FF], gate_up[:, FF:]
        sigma = 1.0 / (1.0 + jnp.exp(-g))
        silu = g * sigma
        act = (silu * u).astype(BF)
        act_all[at, :] = act
        y_ref[s] = mm(act, w_down[...]).astype(BF)
        act_grad = mm_nt(g_all[at, :], w_down[...])
        gug_all[at, :FF] = (act_grad * u * sigma * (1.0 + g * (1.0 - sigma))).astype(BF)
        gug_all[at, FF:] = (act_grad * silu).astype(BF)
        dx_ref[s] = mm_nt(gug_all[at, :], w_in[...]).astype(BF)
        for copy in leaving(s):
            copy.start()
        return carry

    def leaving(s):
        return (
            pltpu.make_async_copy(y_ref.at[s], y_out.at[s], o_sem.at[0, s]),
            pltpu.make_async_copy(dx_ref.at[s], dx_out.at[s], o_sem.at[1, s]),
        )

    def gradient(c):
        return pltpu.make_async_copy(dw_ref.at[c], dw_out.at[c], o_sem.at[2, c])

    lax.fori_loop(0, GROUP, per_slot, 0)
    in_block, down_block = GROUP * in_rows, GROUP * down_rows

    def per_owner(c, carry):
        lanes = pl.ds(pl.multiple_of(c * in_block, in_block), in_block)
        part = mm_tn(x_all[:, lanes], gug_all[...]).astype(BF)
        for r in range(GROUP):
            dw_ref[c, flip(i, r), :in_rows, :] = part[r * in_rows : (r + 1) * in_rows]
        lanes = pl.ds(pl.multiple_of(c * down_block, down_block), down_block)
        part = mm_tn(act_all[:, lanes], g_all[...]).astype(BF)
        for r in range(GROUP):
            dw_ref[c, flip(i, r), in_rows:, :] = part[r * down_rows : (r + 1) * down_rows]
        gradient(c).start()
        return carry

    lax.fori_loop(0, outer, per_owner, 0)
    for s in range(GROUP):
        for copy in leaving(s):
            copy.wait()
    for c in range(outer):
        gradient(c).wait()
    if n_steps:
        hops.wait()
    sums.wait()


def expert_step(j, outer, in_rows, down_rows, x, g, own, lefts, rights, hop_plan, sum_plan):
    (steps, from_left, from_right), (sum_steps, dws, was_l, was_r) = hop_plan, sum_plan
    n_hops, n, n_sums = outer - 1, len(steps), len(sum_steps)
    total = GROUP * CAP
    packed = in_rows + down_rows
    weights = [jax.ShapeDtypeStruct(s.shape, BF) for s in from_left]
    shapes = [
        jax.ShapeDtypeStruct((GROUP, CAP, D), BF),
        jax.ShapeDtypeStruct((GROUP, CAP, D), BF),
        jax.ShapeDtypeStruct((outer, GROUP, packed, D), BF),
    ] + weights * 2 + [jax.ShapeDtypeStruct((GROUP, packed, D), BF)] * (2 * n_sums)
    out = remote_call(
        functools.partial(expert_step_kernel, j, outer, in_rows, down_rows, steps, sum_steps),
        "expert_step",
        4 + j,
        shapes,
        [ANY] * (3 + 2 * n_hops + 2 * n + 3 * n_sums),
        [ANY] * (3 + 2 * n + 2 * n_sums),
        (x, g, own, *lefts, *rights, *from_left, *from_right, *dws, *was_l, *was_r),
        [
            pltpu.VMEM((total, D), BF),
            pltpu.VMEM((total, D), BF),
            pltpu.VMEM((D, 2 * FF), BF),
            pltpu.VMEM((FF, D), BF),
            pltpu.VMEM((total, FF), BF),
            pltpu.VMEM((total, 2 * FF), BF),
            pltpu.SemaphoreType.DMA((GROUP,)),
            pltpu.SemaphoreType.DMA((GROUP,)),
            pltpu.SemaphoreType.DMA(((1 + 2 * n_hops) * GROUP,)),
            pltpu.SemaphoreType.DMA(((1 + 2 * n_hops) * GROUP,)),
            pltpu.SemaphoreType.DMA((max(1, 2 * n),)),
            pltpu.SemaphoreType.DMA((max(1, 2 * n),)),
            pltpu.VMEM((GROUP, CAP, D), BF),
            pltpu.VMEM((GROUP, CAP, D), BF),
            pltpu.VMEM((outer, GROUP, packed, D), BF),
            pltpu.SemaphoreType.DMA((3, max(GROUP, outer))),
            *sums_scratch(n_sums, packed),
        ],
        18 * total * D * FF,
    )
    out, rest = out[:3], out[3:]
    return out, rest[:n], rest[n : 2 * n], rest[2 * n : 2 * n + n_sums], rest[2 * n + n_sums :]


class Sums:
    def __init__(self, outer, steps, dws, was_left, was_right, to_left, to_right, message, term, loaded, added, sent, came):
        d, t, o, _ = place()
        back = outer - 1 - o
        self.moves = []
        for n, s in enumerate(steps):
            for side, near, target, was, to, peer in (
                (0, o, outer - s + o, was_left, to_left, d + GROUP),
                (1, back, s - 1 - back, was_right, to_right, d - GROUP),
            ):
                k = 2 * n + side
                own = pltpu.make_async_copy(dws[n].at[target], message.at[k], loaded.at[k])
                before = None if s == 1 else pltpu.make_async_copy(was[n], term.at[side], added.at[k])
                move = pltpu.make_async_remote_copy(
                    message.at[k], to[n], sent.at[k], came.at[k], device_id=(peer, t), device_id_type=MESH
                )
                sends, adds = near <= s - 1, (near <= s - 1) & (near >= 1)
                receives = (near >= 1) & (near <= s)
                self.moves.append((own, before, move, sends, adds, receives, message.at[k], term.at[side]))

    def load(self):
        for own, _, _, sends, *_ in self.moves:
            pl.when(sends)(own.start)

    def send(self):
        for n in range(0, len(self.moves), 2):
            pair = self.moves[n : n + 2]
            for _, before, _, _, adds, *_ in pair:
                if before is not None:
                    pl.when(adds)(before.start)
            for own, before, move, sends, adds, _, message, term in pair:
                pl.when(sends)(own.wait)
                if before is not None:

                    @pl.when(adds)
                    def _(before=before, message=message, term=term):
                        before.wait()

                        def one(m, carry):
                            message[m] = (message[m].astype(F32) + term[m].astype(F32)).astype(BF)
                            return carry

                        lax.fori_loop(0, GROUP, one, 0)

                pl.when(sends)(move.start)

    def wait(self):
        for _, _, move, sends, _, receives, *_ in self.moves:
            pl.when(sends)(move.wait_send)
            pl.when(receives)(move.wait_recv)


def sums_scratch(n, packed):
    n = max(1, n)
    return [
        pltpu.VMEM((2 * n, GROUP, packed, D), BF),
        pltpu.VMEM((2, GROUP, packed, D), BF),
        pltpu.SemaphoreType.DMA((2 * n,)),
        pltpu.SemaphoreType.DMA((2 * n,)),
        pltpu.SemaphoreType.DMA((2 * n,)),
        pltpu.SemaphoreType.DMA((2 * n,)),
    ]


def again(scratch):
    return [pltpu.SemaphoreType.DMA(s.shape) for s in scratch[2:]]


class Final:
    def __init__(self, outer, dw, left, right, mine, term, target, loaded, sent, came, kept):
        _, _, o, _ = place()
        self.from_left, self.from_right = o >= 1, o < outer - 1
        self.mine, self.term = mine, term
        self.own = pltpu.make_async_copy(dw.at[o], mine, loaded.at[0])
        self.left = pltpu.make_async_copy(left, term.at[0], loaded.at[1])
        self.right = pltpu.make_async_copy(right, term.at[1], loaded.at[2])
        self.moves = [to_dp(m, mine.at[m], target.at[m], sent.at[m - 1], came.at[m - 1]) for m in range(1, GROUP)]
        self.keep = pltpu.make_async_copy(mine.at[0], target.at[0], kept)

    def send(self):
        self.own.start()
        pl.when(self.from_left)(self.left.start)
        pl.when(self.from_right)(self.right.start)
        self.own.wait()

        def add(k):
            def one(m, carry):
                self.mine[m] = (self.mine[m].astype(F32) + self.term[k, m].astype(F32)).astype(BF)
                return carry

            lax.fori_loop(0, GROUP, one, 0)

        @pl.when(self.from_left)
        def _():
            self.left.wait()
            add(0)

        @pl.when(self.from_right)
        def _():
            self.right.wait()
            add(1)

        for move in self.moves:
            move.start()
        self.keep.start()

    def wait(self):
        for move in self.moves:
            move.wait()
        self.keep.wait()


def final_scratch(packed):
    return [
        pltpu.VMEM((GROUP, packed, D), BF),
        pltpu.SemaphoreType.DMA((3,)),
        pltpu.SemaphoreType.DMA((GROUP - 1,)),
        pltpu.SemaphoreType.DMA((GROUP - 1,)),
        pltpu.SemaphoreType.DMA,
    ]


class Mixer:
    def __init__(self, sources, pos_ref, gate_ref, held, sems):
        self.sources, self.pos, self.gate, self.held, self.sems = sources, pos_ref, gate_ref, held, sems

    def copies(self, slot, buffer):
        return [
            pltpu.make_async_copy(
                source.at[slot], self.held.at[buffer, pl.ds(j * CAP, CAP)], self.sems.at[buffer * len(self.sources) + j]
            )
            for j, source in enumerate(self.sources)
        ]

    def load(self, slot, buffer):
        for c in self.copies(slot, buffer):
            c.start()

    def mix(self, slot, buffer, out, add=None):
        for c in self.copies(slot, buffer):
            c.wait()
        n_experts = len(self.sources)
        width = n_experts * CAP
        block = 256

        def one(b, carry):
            at = pl.ds(pl.multiple_of(b * block, block), block)
            targets = []
            for j in range(n_experts):
                target = self.pos[slot, at, j : j + 1]
                targets.append(jnp.where(target >= 0, target + j * CAP, -1))
            tiles = []
            for first in range(0, width, LANES):
                size = min(LANES, width - first)
                lane = first + lax.broadcasted_iota(jnp.int32, (block, size), 1)
                tile = jnp.zeros((block, size), F32)
                for j in range(first // CAP, (first + size - 1) // CAP + 1):
                    value = 1.0 if self.gate is None else self.gate[slot, at, j : j + 1]
                    tile = jnp.where(lane == targets[j], value, tile)
                tiles.append(tile.astype(BF))
            total = mm(jnp.concatenate(tiles, axis=1), self.held[buffer])
            if add is not None:
                total = total + add[at, :].astype(F32)
            out[at, :] = total.astype(BF)
            return carry

        lax.fori_loop(0, out.shape[0] // block, one, 0)


class GroupSum:
    def __init__(self, near, q, middle, mine, come_ab, last_ab, sent, came):
        self.middle, self.mine, self.come_ab, self.last_ab, self.q = middle, mine, come_ab, last_ab, q
        self.a = [
            to_dp(2, near.at[1, pl.ds(s * q, q)], come_ab.at[0, pl.ds(s * q, q)], sent.at[s], came.at[s]) for s in range(2)
        ]
        self.b = [
            to_x(near.at[s, pl.ds(3 * q, q)], come_ab.at[1, pl.ds(s * q, q)], sent.at[2 + s], came.at[2 + s])
            for s in range(2)
        ]
        self.last = [
            to_x(middle[0], last_ab.at[0], sent.at[4], came.at[4]),
            to_dp(2, middle[1], last_ab.at[1], sent.at[5], came.at[5]),
        ]

    def second(self):
        q = self.q
        for p, first in enumerate((self.a[1], self.b[1])):
            first.wait_recv()
            self.middle[p][...] = (
                self.middle[p][...].astype(F32) + self.come_ab[p, q : 2 * q].astype(F32)
            ).astype(BF)
            self.last[p].start()

    def terms(self, p):
        (self.a, self.b)[p][0].wait_recv()
        self.last[p].wait_recv()
        return (
            self.mine[p][...].astype(F32) + self.come_ab[p, : self.q].astype(F32) + self.last_ab[p].astype(F32)
        )

    def sent(self):
        for copy in (*self.a, *self.b, *self.last):
            copy.wait_send()


def group_scratch(rows):
    return [
        pltpu.VMEM((2, rows // 2, D), BF),
        pltpu.VMEM((2, rows // 4, D), BF),
        pltpu.SemaphoreType.DMA((6,)),
        pltpu.SemaphoreType.DMA((6,)),
    ]


def rows_back_kernel(outer, first, then, pos_ref, gate_ref, valid_ref, hidden_ref, cot_ref, gain_ref, w_any, *refs):
    n_experts, n1, n2 = pos_ref.shape[2], len(first), len(then)
    sources, refs = refs[:n_experts], refs[n_experts:]
    ys, refs = refs[:n_experts], refs[n_experts:]
    dws, refs = refs[: n1 + 1], refs[n1 + 1 :]
    was_l, refs = refs[:n1], refs[n1:]
    was_r, refs = refs[:n1], refs[n1:]
    f_dw, f_left, f_right, refs = *refs[:3], refs[3:]
    grad_ref, low_ref, gain_grad_ref, own_ref, come_ref, mixed_out, fin_ref = refs[:7]
    refs = refs[7:]
    to_l, refs = refs[: n1 + n2], refs[n1 + n2 :]
    to_r, refs = refs[: n1 + n2], refs[n1 + n2 :]
    (held, far, come, mixed_come, near, l_sem, s_core, r_core), refs = refs[:8], refs[8:]
    (come_ab, last_ab, s_sem, r_sem), refs = refs[:4], refs[4:]
    sums_a, refs = refs[:6], refs[6:]
    sums_b, refs = (*sums_a[:2], *refs[:4]), refs[4:]
    send_ref, s_at, r_at, w_ref, w_sem = refs[:5]
    mixed, m_sem, final_refs = refs[5], refs[6], refs[7:]
    heads = w_ref.shape[1] // 2
    w_copy = pltpu.make_async_copy(w_any.at[:, pl.ds(2 * heads, 2 * heads)], w_ref, w_sem)
    w_copy.start()
    mixer = Mixer(sources, pos_ref, None, held, l_sem)
    mixer.load(3, 0)
    mixer.load(2, 1)
    greet(outer, (1, 2, 3), True)
    one = Sums(outer, first, dws[:n1], was_l, was_r, to_l[:n1], to_r[:n1], *sums_a)
    final = Final(outer, f_dw, f_left, f_right, final_refs[0], sums_a[1], fin_ref, *final_refs[1:])
    two = Sums(
        outer,
        [s for s, _ in then],
        [dws[k] for _, k in then],
        [None if s == 1 else to_l[k] for s, k in then],
        [None if s == 1 else to_r[k] for s, k in then],
        to_l[n1:],
        to_r[n1:],
        *sums_b,
    )
    q = near.shape[1] // 4
    group = GroupSum(
        near,
        q,
        [near.at[0, pl.ds(q, q)], near.at[1, pl.ds(2 * q, q)]],
        [near.at[0, pl.ds(0, q)], near.at[0, pl.ds(2 * q, q)]],
        come_ab,
        last_ab,
        s_sem,
        r_sem,
    )
    def core(s):
        return to_dp(1, far.at[s], come.at[s], s_core.at[s], r_core.at[s])

    def mixed_core(s):
        return to_dp(1, far.at[s], mixed_come.at[s], s_core.at[2 + s], r_core.at[2 + s])

    def mixed_leave(s):
        return pltpu.make_async_copy(mixed.at[s], mixed_out.at[s], m_sem.at[s])

    outputs = Mixer(ys, pos_ref, gate_ref, held, l_sem)
    rows = hidden_ref.shape[0] // 2
    aways = [
        to_x(
            send_ref.at[pl.ds(p * rows, rows)], come_ref.at[pl.ds(p * rows, rows)], s_at.at[p], r_at.at[p]
        )
        for p in range(2)
    ]

    def phase(mixer, base, target, add, ahead, behind):
        def body(k, carry):
            s = 1 - k
            ahead(s, k)
            mixer.mix(base + s, k, target.at[s], None if add is None else add.at[s])
            behind(s, k)
            return carry

        lax.fori_loop(0, 2, body, 0)

    def far_behind(s, k):
        core(s).start()
        mixer.load(s, k)

    def near_behind(s, k):
        @pl.when(s == 1)
        def _():
            group.a[1].start()
            group.b[1].start()
            group.a[0].start()

        pl.when(s == 0)(group.b[0].start)
        outputs.load(2 + s, k)

    def go_on():
        group.second()
        one.wait()
        two.load()
        two.send()

    def mixed_ahead(s, k):
        core(s).wait_send()
        pl.when(k == 1)(go_on)

    def mixed_behind(s, k):
        mixed_core(s).start()
        outputs.load(s, k)

    def back():
        gain = gain_ref[...]
        gain_grad = jnp.zeros((1, D), F32)
        for p in range(2):
            at = slice(p * rows, (p + 1) * rows)
            hidden = hidden_ref[at]
            normed_grad = group.terms(p)
            inverse = lax.rsqrt(jnp.mean(hidden * hidden, axis=-1, keepdims=True) + EPSILON)
            gain_grad = gain_grad + jnp.sum(normed_grad * (hidden * inverse), axis=0, keepdims=True)
            scaled = normed_grad * gain
            back = inverse * scaled - hidden * (
                inverse * inverse * inverse * jnp.mean(scaled * hidden, axis=-1, keepdims=True)
            )
            dy = jnp.where(valid_ref[at] > 0, cot_ref[at].astype(F32), 0.0)
            total = dy + back
            grad_ref[at] = total
            low = total.astype(BF)
            low_ref[at] = low
            send_ref[at] = mm(low, w_ref[:, heads:]).astype(BF)
            aways[p].start()
        gain_grad_ref[...] = gain_grad

    def last_ahead(s, k):
        mixed_core(s).wait_recv()
        pl.when(k == 1)(back)

    one.load()
    one.send()
    final.send()
    phase(mixer, 2, far, None, lambda s, k: None, far_behind)
    phase(mixer, 0, near, come, lambda s, k: core(s).wait_recv(), near_behind)
    phase(outputs, 2, far, None, mixed_ahead, mixed_behind)
    w_copy.wait()
    phase(outputs, 0, mixed, mixed_come, last_ahead, lambda s, k: mixed_leave(s).start())
    own_ref[...] = mm(low_ref[...], w_ref[:, :heads]).astype(BF)
    group.sent()
    for s in range(2):
        mixed_core(s).wait_send()
    for away in aways:
        away.wait()
    final.wait()
    for s in range(2):
        mixed_leave(s).wait()
    two.wait()


def rows_back(
    outer, pos, gate, valid, hidden, cotangent, gain, weights_full, sources, ys, first, then, dws, was_l, was_r, final
):
    rows, heads = hidden.shape[0], weights_full.shape[1] // 4
    n, n_experts = len(first) + len(then), len(sources)
    packed = dws[0].shape[2]
    hop = [jax.ShapeDtypeStruct((GROUP, packed, D), BF)] * (2 * n)
    half = jax.ShapeDtypeStruct((rows, heads), BF)
    most = max(len(first), len(then))
    slots = pltpu.VMEM((2, 2 * rows, D), BF)
    out = remote_call(
        functools.partial(rows_back_kernel, outer, first, then),
        "rows_back",
        10,
        [
            jax.ShapeDtypeStruct((rows, D), F32),
            jax.ShapeDtypeStruct((rows, D), BF),
            jax.ShapeDtypeStruct((1, D), F32),
            half,
            half,
            jax.ShapeDtypeStruct((2, 2 * rows, D), BF),
        ]
        + hop[:1]
        + hop,
        [VM] * 6 + [ANY] * (4 + 2 * n_experts + len(dws) + 2 * len(first)),
        [VM] * 5 + [ANY] * (2 + 2 * n),
        (pos, gate, valid, hidden, cotangent, gain.reshape(1, D), weights_full, *sources, *ys, *dws, *was_l, *was_r, *final),
        [
            pltpu.VMEM((2, n_experts * CAP, D), BF),
            slots,
            slots,
            slots,
            slots,
            pltpu.SemaphoreType.DMA((2 * n_experts,)),
            pltpu.SemaphoreType.DMA((4,)),
            pltpu.SemaphoreType.DMA((4,)),
            *group_scratch(2 * rows),
            *sums_scratch(most, packed),
            *again(sums_scratch(most, packed)),
            pltpu.VMEM((rows, heads), BF),
            pltpu.SemaphoreType.DMA((2,)),
            pltpu.SemaphoreType.DMA((2,)),
            pltpu.VMEM((D, 2 * heads), BF),
            pltpu.SemaphoreType.DMA,
            slots,
            pltpu.SemaphoreType.DMA((2,)),
            *final_scratch(packed),
        ],
        30 << 30,
    )
    return out[:6], out[6], out[7 : 7 + n], out[7 + n :]


def attention_back_kernel(
    outer, q_block, steps, len_ref, qkv_ref, lse_ref, cos_ref, sin_ref, own_ref, other_ref, hidden_ref, valid_ref, *refs
):
    n = len(steps)
    mixed, low_any, part_anys, refs = refs[0], refs[1], refs[2:4], refs[4:]
    dws, refs = refs[:n], refs[n:]
    was_l, refs = refs[:n], refs[n:]
    was_r, refs = refs[:n], refs[n:]
    outs, out_ref, weight_refs, refs = refs[:2], refs[2], refs[3:5], refs[5:]
    to_l, refs = refs[:n], refs[n:]
    to_r, refs = refs[:n], refs[n:]
    do_ref, dq_ref, dk_ref, dv_ref = refs[:4]
    sums_refs, refs = refs[4:10], refs[10:]
    middle, mine, l_sem, come_ab, last_ab, s_sem, r_sem, low_ref, part_refs, w_sem = refs
    _, t, _, _ = place()
    heads_copies = [
        pltpu.make_async_copy(low_any, low_ref, w_sem.at[0]),
        pltpu.make_async_copy(part_anys[0], part_refs.at[0], w_sem.at[1]),
        pltpu.make_async_copy(part_anys[1], part_refs.at[1], w_sem.at[2]),
    ]
    for c in heads_copies:
        c.start()
    q = middle.shape[1]
    loads = [
        pltpu.make_async_copy(mixed.at[0, pl.ds(q, q)], middle.at[0], l_sem.at[0]),
        pltpu.make_async_copy(mixed.at[1, pl.ds(2 * q, q)], middle.at[1], l_sem.at[1]),
        pltpu.make_async_copy(mixed.at[0, pl.ds(0, q)], mine.at[0], l_sem.at[2]),
        pltpu.make_async_copy(mixed.at[0, pl.ds(2 * q, q)], mine.at[1], l_sem.at[3]),
    ]
    for c in loads:
        c.start()
    greet(outer, (2,), True)
    group = GroupSum(
        mixed, q, [middle.at[0], middle.at[1]], [mine.at[0], mine.at[1]], come_ab, last_ab, s_sem, r_sem
    )
    for copy in (group.a[1], group.b[1], group.a[0], group.b[0]):
        copy.start()
    sums = Sums(outer, steps, dws, was_l, was_r, to_l, to_r, *sums_refs)
    sums.load()
    sums.send()
    length = len_ref[0]
    rows, own_rows = qkv_ref.shape[0], own_ref.shape[0]
    groups = own_ref.shape[1] // LANES
    scale = 1.0 / math.sqrt(HD)

    def per_group(g, carry):
        q_lanes = pl.ds(pl.multiple_of(g * 2 * LANES, LANES), LANES)
        kv_lanes = pl.ds(pl.multiple_of(g * 2 * LANES + LANES, LANES), LANES)
        o_lanes = pl.ds(pl.multiple_of(g * LANES, LANES), LANES)
        for half, grad_ref in ((t, own_ref), (1 - t, other_ref)):
            do_ref[pl.ds(pl.multiple_of(half * own_rows, own_rows), own_rows), :] = grad_ref[:, o_lanes]
        keys, values = doubled(qkv_ref[:, kv_lanes])
        dk_ref[...] = jnp.zeros_like(dk_ref)
        dv_ref[...] = jnp.zeros_like(dv_ref)
        for b in range(rows // q_block):
            start, n_keys = b * q_block, (b + 1) * q_block
            q = head_pair(qkv_ref[start : start + q_block, q_lanes])
            grad = head_pair(do_ref[start : start + q_block, :])
            scores = mm_nt(keys[:n_keys], q) * scale
            probs = jnp.where(
                allowed(n_keys, q_block, start, length), jnp.exp(scores - lse_ref[g, b : b + 1, :]), 0.0
            )
            prob_grad = mm_nt(values[:n_keys], grad)
            center = jnp.sum(probs * prob_grad, axis=0, keepdims=True)
            score_grad = (probs * (prob_grad - center)).astype(BF)
            dq_ref[start : start + q_block, :] = head_join(mm_tn(score_grad, keys[:n_keys])) * scale
            dk_ref[:n_keys, :] += mm(score_grad, q)
            dv_ref[:n_keys, :] += mm(probs.astype(BF), grad)
        for p, half in enumerate((t, 1 - t)):
            at = pl.ds(pl.multiple_of(half * own_rows, own_rows), own_rows)
            cosine, sine = cos_ref[at, :], sin_ref[at, :]
            dq = dq_ref[at, :]
            outs[p][:, q_lanes] = (dq * cosine - swap_halves(dq) * sine).astype(BF)
            dk, dv = dk_ref[at, :] * scale, dv_ref[at, :]
            dk = dk + pltpu.roll(dk, HD, 1)
            dv = dv + pltpu.roll(dv, HD, 1)
            dk = dk * cosine - swap_halves(dk) * sine
            first = lax.broadcasted_iota(jnp.int32, dk.shape, 1) < HD
            outs[p][:, kv_lanes] = jnp.where(first, dk, dv).astype(BF)

        @pl.when(g == groups // 2)
        def _():
            for c in loads:
                c.wait()
            group.second()

        return carry

    lax.fori_loop(0, groups, per_group, 0)
    for c in heads_copies:
        c.wait()
    block = 256

    def out_weights(k, carry):
        at = pl.ds(pl.multiple_of(k * block, block), block)
        for p in range(2):
            weight_refs[p][at, :] = mm_tn(low_ref[:, at], part_refs[p]).astype(BF)
        return carry

    lax.fori_loop(0, D // block, out_weights, 0)
    for p in range(2):
        at = slice(p * q, (p + 1) * q)
        out_ref[at] = jnp.where(valid_ref[at] > 0, hidden_ref[at] + group.terms(p), 0.0).astype(BF)
    group.sent()
    sums.wait()


def attention_back(
    outer, q_block, length, qkv, lse, cosine, sine, grads, hidden, valid, mixed, low, parts, steps, dws, was_l, was_r
):
    rows, width = qkv.shape
    n = len(steps)
    packed = dws[0].shape[2]
    hop = jax.ShapeDtypeStruct((GROUP, packed, D), BF)
    out = remote_call(
        functools.partial(attention_back_kernel, outer, q_block, steps),
        "attention_back",
        12,
        [jax.ShapeDtypeStruct((rows // 2, width), BF)] * 2
        + [jax.ShapeDtypeStruct((rows // 2, D), BF)]
        + [jax.ShapeDtypeStruct((D, width // 2), BF)] * 2
        + [hop] * (2 * n),
        [SMEM] + [VM] * 8 + [ANY] * (3 * n + 4),
        [VM] * 5 + [ANY] * (2 * n),
        (length, qkv, lse, cosine, sine, *grads, hidden, valid, mixed, low, *parts, *dws, *was_l, *was_r),
        [
            pltpu.VMEM((rows, LANES), BF),
            pltpu.VMEM((rows, LANES), F32),
            pltpu.VMEM((rows, LANES), F32),
            pltpu.VMEM((rows, LANES), F32),
            *sums_scratch(n, packed),
            pltpu.VMEM((2, rows // 4, D), BF),
            pltpu.VMEM((2, rows // 4, D), BF),
            pltpu.SemaphoreType.DMA((4,)),
            *group_scratch(rows),
            pltpu.VMEM((rows // 2, D), BF),
            pltpu.VMEM((2, rows // 2, width // 2), BF),
            pltpu.SemaphoreType.DMA((3,)),
        ],
        30 << 30,
    )
    return out[:5], out[5 : 5 + n], out[5 + n :]


def over_outer(outer, source, target, sent, came, base):
    _, t, o, i = place()
    return [
        pltpu.make_async_remote_copy(
            source((o + k) % outer),
            target(k),
            sent.at[base + k],
            came.at[base + k],
            device_id=((o + k) % outer * GROUP + i, t),
            device_id_type=MESH,
        )
        for k in range(1, outer)
    ]


class Spread:
    def __init__(self, outer, terms, come_core, come_y, come_z, sent, came):
        _, _, self.o, i = place()
        self.outer, self.terms, self.come_core, self.come_y, self.come_z = outer, terms, come_core, come_y, come_z
        y, c = i // 2, i % 2
        self.y, self.c = y, c
        self.core = to_dp(1, terms.at[:, :, 1 - c], come_core, sent.at[0], came.at[0])
        self.side = to_dp(2, terms.at[:, 1 - y, c], come_y, sent.at[1], came.at[1])
        self.moves = over_outer(outer, lambda peer: terms.at[peer, y, c], lambda k: come_z.at[k - 1], sent, came, 1)

    def over_core(self):
        self.core.start()

    def over_y(self):
        self.core.wait()

        def add(k, carry):
            for r in range(2):
                self.terms[k, r, self.c] = (
                    self.terms[k, r, self.c].astype(F32) + self.come_core[k, r].astype(F32)
                ).astype(BF)
            return carry

        lax.fori_loop(0, self.outer, add, 0)
        self.side.start()

    def over_z(self):
        self.side.wait()

        def add(k, carry):
            self.terms[k, self.y, self.c] = (
                self.terms[k, self.y, self.c].astype(F32) + self.come_y[k].astype(F32)
            ).astype(BF)
            return carry

        lax.fori_loop(0, self.outer, add, 0)
        for move in self.moves:
            move.start()

    def total(self):
        for move in self.moves:
            move.wait()
        total = self.terms[self.o, self.y, self.c].astype(F32)
        for k in range(1, self.outer):
            total = total + self.come_z[k - 1].astype(F32)
        return total


def spread_scratch(outer, each, columns):
    return [
        pltpu.VMEM((outer, 2, 2, each, columns), BF),
        pltpu.VMEM((outer, 2, each, columns), BF),
        pltpu.VMEM((outer, each, columns), BF),
        pltpu.VMEM((outer - 1, each, columns), BF),
        pltpu.SemaphoreType.DMA((1 + outer,)),
        pltpu.SemaphoreType.DMA((1 + outer,)),
    ]


def finish_kernel(outer, hgrad_any, x_any, gain_ref, w_any, *refs):
    (no_ref, nx_ref, po_ref, px_ref, oo_ref, ox_ref, sg_ref), refs = refs[:7], refs[7:]
    dws, refs = refs[:3], refs[3:]
    done, refs = refs[:2], refs[2:]
    was_l, refs = refs[:2], refs[2:]
    was_r, refs = refs[:2], refs[2:]
    tgrad_ref, gains_ref, qkv_ref, outw_ref = refs[:4]
    fins, to_l, to_r, refs = refs[4:7], refs[7:9], refs[9:11], refs[11:]
    sums_refs, refs = [refs[:6], refs[6:12]], refs[12:]
    final_refs, refs = [refs[5 * k : 5 * k + 5] for k in range(3)], refs[15:]
    part_ref, theirs_ref, p_send, p_recv, out_ref, come_ref, c_send, c_recv = refs[:8]
    q_refs, o_refs, refs = refs[8:14], refs[14:20], refs[20:]
    g_buf, g_come, g_z, g_send, g_recv, w_ref, w_sem, hgrad_ref, x_ref, late_sem = refs
    d, t, o, i = place()
    rows = hgrad_ref.shape[0]
    width = w_ref.shape[1]
    w_copy = pltpu.make_async_copy(w_any.at[:, pl.ds(0, width)], w_ref, w_sem)
    w_copy.start()
    late = [
        pltpu.make_async_copy(hgrad_any, hgrad_ref, late_sem.at[0]),
        pltpu.make_async_copy(x_any, x_ref, late_sem.at[1]),
    ]
    for c in late:
        c.start()
    greet_all(outer)
    sums = [
        Sums(outer, (3,), [dws[1 + k]], [was_l[k]], [was_r[k]], [to_l[k]], [to_r[k]], *sums_refs[k]) for k in range(2)
    ]
    came = [done, (to_l[0], to_r[0]), (to_l[1], to_r[1])]
    finals = [
        Final(outer, dws[k], *came[k], final_refs[k][0], sums_refs[0][1], fins[k], *final_refs[k][1:]) for k in range(3)
    ]
    for one in sums:
        one.load()
    for one in sums:
        one.send()
    w_copy.wait()
    part_ref[...] = mm_nt(px_ref[...], w_ref[...]).astype(BF)
    exchange = to_x(part_ref, theirs_ref, p_send, p_recv)
    exchange.start()
    finals[0].send()
    whole, part = Spread(outer, *q_refs), Spread(outer, *o_refs)
    each, heads = outw_ref.shape

    def out_block(k, carry):
        for r in range(GROUP):
            at = pl.ds(pl.multiple_of((k * GROUP + r) * each, each), each)
            part.terms[k, r // 2, r % 2, :, :heads] = oo_ref[at, :]
            part.terms[k, r // 2, r % 2, :, heads:] = ox_ref[at, :]
        return carry

    lax.fori_loop(0, outer, out_block, 0)
    part.over_core()

    def weights_block(k, carry):
        lanes = pl.ds(pl.multiple_of(k * GROUP * each, GROUP * each), GROUP * each)
        total = (mm_tn(no_ref[:, lanes], po_ref[...]) + mm_tn(nx_ref[:, lanes], px_ref[...])).astype(BF)
        for r in range(GROUP):
            whole.terms[k, r // 2, r % 2] = total[r * each : (r + 1) * each]
        return carry

    part.over_y()
    lax.fori_loop(0, outer, weights_block, 0)
    whole.over_core()
    whole.over_y()
    part.over_z()

    exchange.wait()
    for c in late:
        c.wait()
    quarter = rows // 4

    def norm_rows(p, gain_grad):
        at = pl.ds(pl.multiple_of(p * quarter, quarter), quarter)
        normed_grad = mm_nt(po_ref[at, :], w_ref[...]).astype(BF).astype(F32) + theirs_ref[at, :].astype(F32)
        x = x_ref[at, :].astype(F32)
        inverse = lax.rsqrt(jnp.mean(x * x, axis=-1, keepdims=True) + EPSILON)
        scaled = normed_grad * gain_ref[...]
        tgrad_ref[at, :] = (
            hgrad_ref[at, :]
            + inverse * scaled
            - x * (inverse * inverse * inverse * jnp.mean(scaled * x, axis=-1, keepdims=True))
        )
        return gain_grad + jnp.sum(normed_grad * (x * inverse), axis=0, keepdims=True)

    g_buf[0, 0:1, :] = lax.fori_loop(0, 4, norm_rows, jnp.zeros((1, D), F32))
    g_buf[0, 1:2, :] = sg_ref[...]
    g_buf[0, 2:8, :] = jnp.zeros((6, D), F32)
    g_moves = [
        to_dp(1, g_buf.at[0], g_come.at[0], g_send.at[0], g_recv.at[0]),
        to_x(g_buf.at[1], g_come.at[1], g_send.at[1], g_recv.at[1]),
        to_dp(2, g_buf.at[2], g_come.at[2], g_send.at[2], g_recv.at[2]),
    ]
    g_moves[0].start()
    g_moves[0].wait()
    g_buf[1] = g_buf[0] + g_come[0]
    g_moves[1].start()
    g_moves[1].wait()
    g_buf[2] = g_buf[1] + g_come[1]
    g_moves[2].start()
    sums[0].wait()
    finals[1].send()
    whole.over_z()
    sums[1].wait()
    finals[2].send()
    out = part.total()
    outw_ref[...] = out[:, :heads]
    out_ref[...] = out[:, heads:].astype(BF)
    to_other = to_x(out_ref, come_ref, c_send, c_recv)
    to_other.start()
    g_moves[2].wait()
    g_z[0] = g_buf[2] + g_come[2]
    gz_moves = over_outer(outer, lambda peer: g_z.at[0], lambda k: g_z.at[k], g_send, g_recv, 2)
    for move in gz_moves:
        move.start()
    qkv_ref[...] = whole.total()
    to_other.wait()
    outw_ref[...] = outw_ref[...] + come_ref[...].astype(F32)
    for move in gz_moves:
        move.wait()
    gains = g_z[(o + outer) % outer]
    for k in range(1, outer):
        gains = gains + g_z[(o - k + outer) % outer]
    gains_ref[...] = gains
    for final in finals:
        final.wait()


def finish(outer, hgrad, x, gain, weights_full, extra, dws, done, was_l, was_r):
    rows = hgrad.shape[0]
    packed = dws[0].shape[2]
    width = weights_full.shape[1] // 2
    heads = width // 2
    each = D // (outer * GROUP)
    hop = jax.ShapeDtypeStruct((GROUP, packed, D), BF)
    return remote_call(
        functools.partial(finish_kernel, outer),
        "finish",
        11,
        [
            jax.ShapeDtypeStruct((rows, D), F32),
            jax.ShapeDtypeStruct((8, D), F32),
            jax.ShapeDtypeStruct((each, width), F32),
            jax.ShapeDtypeStruct((each, heads), F32),
        ]
        + [hop] * 7,
        [ANY, ANY, VM, ANY] + [VM] * 7 + [ANY] * 9,
        [VM] * 4 + [ANY] * 7,
        (hgrad, x, gain.reshape(1, D), weights_full, *extra, *dws, *done, *was_l, *was_r),
        [
            *sums_scratch(1, packed) * 2,
            *final_scratch(packed) * 3,
            pltpu.VMEM((rows, D), BF),
            pltpu.VMEM((rows, D), BF),
            pltpu.SemaphoreType.DMA,
            pltpu.SemaphoreType.DMA,
            pltpu.VMEM((each, heads), BF),
            pltpu.VMEM((each, heads), BF),
            pltpu.SemaphoreType.DMA,
            pltpu.SemaphoreType.DMA,
            *spread_scratch(outer, each, width),
            *spread_scratch(outer, each, 2 * heads),
            pltpu.VMEM((3, 8, D), F32),
            pltpu.VMEM((3, 8, D), F32),
            pltpu.VMEM((outer, 8, D), F32),
            pltpu.SemaphoreType.DMA((2 + outer,)),
            pltpu.SemaphoreType.DMA((2 + outer,)),
            pltpu.VMEM((D, width), BF),
            pltpu.SemaphoreType.DMA,
            pltpu.VMEM((rows, D), F32),
            pltpu.VMEM((rows, D), BF),
            pltpu.SemaphoreType.DMA((2,)),
        ],
        30 << 30,
    )


def settle_kernel(in_rows, idx_ref, *refs):
    n = len(refs) - 7
    sources, (in_ref, down_ref, held, wide_in, wide_down, l_sem, s_sem) = refs[:n], refs[n:]
    loads = [pltpu.make_async_copy(source, held.at[j], l_sem.at[j]) for j, source in enumerate(sources)]
    for c in loads:
        c.start()
    stores = []
    for j in range(n):
        loads[j].wait()
        for m in range(GROUP):
            k = j * GROUP + m
            at = (idx_ref[1] ^ m) * n + j
            wide_in[k] = held[j, m, :in_rows, :].astype(F32)
            wide_down[k] = held[j, m, in_rows:, :].astype(F32)
            stores.append(pltpu.make_async_copy(wide_in.at[k], in_ref.at[at], s_sem.at[2 * k]))
            stores.append(pltpu.make_async_copy(wide_down.at[k], down_ref.at[at], s_sem.at[2 * k + 1]))
            for c in stores[-2:]:
                c.start()
    for c in stores:
        c.wait()


def settle_experts(idx, fins, in_rows):
    n = len(fins)
    _, packed, _ = fins[0].shape
    experts, down_rows = n * GROUP, packed - in_rows
    return call(
        functools.partial(settle_kernel, in_rows),
        "settle_experts",
        [jax.ShapeDtypeStruct((experts, in_rows, D), F32), jax.ShapeDtypeStruct((experts, down_rows, D), F32)],
        [SMEM] + [ANY] * n,
        [ANY] * 2,
        (idx, *fins),
        scratch=[
            pltpu.VMEM((n, GROUP, packed, D), BF),
            pltpu.VMEM((experts, in_rows, D), F32),
            pltpu.VMEM((experts, down_rows, D), F32),
            pltpu.SemaphoreType.DMA((n,)),
            pltpu.SemaphoreType.DMA((2 * experts,)),
        ],
        moved=9 << 20,
    )


def layer(
    tokens,
    cotangent,
    lengths,
    expert_ids,
    gate_values,
    first_gain,
    qkv_weight,
    attn_out_weight,
    second_gain,
    expert_in_weight,
    expert_out_weight,
):
    rows = tokens.shape[0]
    n_tensor, n_dp = lax.axis_size("tensor"), lax.axis_size("dp")
    outer = n_dp // GROUP
    slot_rows = rows * n_tensor
    d, t = lax.axis_index("dp"), lax.axis_index("tensor")
    o, i = d // GROUP, d % GROUP
    length = lengths[0]
    idx = jnp.stack([o, i, t, length]).astype(jnp.int32)
    width = qkv_weight.shape[1] * qkv_weight.shape[2]
    experts_local, in_rows, _ = expert_in_weight.shape
    down_rows = expert_out_weight.shape[1]
    own_experts = experts_local // GROUP
    pair = n_tensor == 2
    q_block = 256
    half = rows // 2

    def across(v, m):
        return lax.ppermute(v, "dp", [(a, a ^ m) for a in range(n_dp)])

    def beside(v):
        return lax.ppermute(v, "tensor", [(0, 1), (1, 0)])

    def hop(pairs):
        up = [(a, a + GROUP) for a in range(n_dp - GROUP)]
        down = [(b, a) for a, b in up]
        return [(lax.ppermute(a, "dp", up), lax.ppermute(b, "dp", down)) for a, b in pairs]

    def gather_group(pieces):
        if pair:
            a, b = pieces
            ax, by, ay, bx = beside(a), across(b, 2), across(a, 2), beside(b)
            axy, bxy = across(ax, 2), beside(by)
            slots = [[a, ax, b, bx], [ay, axy, by, bxy]]
        else:
            slot = lax.all_gather(pieces[0], "tensor", axis=0, tiled=True)
            slots = [[slot], [across(slot, 2)]]
        return slots + [[across(p, 1) for p in s] for s in slots]

    positions = t * rows + jnp.arange(rows, dtype=jnp.int32)
    valid_rows = positions < length
    n_experts = experts_local * n_tensor
    chosen = expert_ids.T[None] == jnp.arange(n_experts, dtype=jnp.int32)[:, None, None]
    gates = jnp.sum(jnp.where(chosen, gate_values.T[None].astype(F32), 0.0), axis=1)
    gates = jnp.where(valid_rows[None, :], gates, 0.0).astype(BF)
    x = tokens.astype(F32)
    inverse_one = lax.rsqrt(jnp.mean(x * x, axis=-1, keepdims=True) + EPSILON)
    normed_one = (x * inverse_one * first_gain).astype(BF)
    expert_outs, row_grads, weight_grads = [], [], []
    if pair and outer == 4:
        frequency = THETA ** (-(jnp.arange(HD // 2).astype(F32) * 2.0 / HD))
        shard = jnp.concatenate([qkv_weight.reshape(-1, width), attn_out_weight.T], axis=1)
        main, ready, packed, first_l, first_r = collect(
            outer, shard, normed_one, gates, jnp.tile(frequency, 4)[None, :], expert_in_weight, expert_out_weight
        )
        weights_full, other, cosine, sine, pos, own_gates, pos_columns, gate_columns = main
        main, dy_moved, later, one_l, one_r = attention(
            outer,
            q_block,
            lengths,
            normed_one,
            other,
            weights_full,
            cosine,
            sine,
            tokens,
            second_gain,
            cotangent,
            ready[1],
            packed,
        )
        own_weights = [*ready, *later]
        one_l, one_r = [first_l, *one_l], [first_r, *one_r]
        qkv, lse, attn_own, attn_other, hidden, *normed_two = main
        attn_parts = [attn_own, attn_other]
        gathered, out_grads, moved_l, moved_r = spread(
            outer,
            pos,
            own_gates,
            normed_two,
            [cotangent, *dy_moved],
            (2, 2, 2),
            one_l[:3],
            one_r[:3],
        )
        two_l, two_r = [*moved_l], [*moved_r]
        expert_rows, moved_l, moved_r = hand_out(
            outer, pos, normed_two, gathered, (3, 2), [two_l[0], one_l[3]], [two_r[0], one_r[3]]
        )
        three_l, three_r = [moved_l[0]], [moved_r[0]]
        two_l.append(moved_l[1])
        two_r.append(moved_r[1])
        hop_plans = [
            lambda: ((3,), [two_l[1]], [two_r[1]]),
            lambda: ((3,), [two_l[2]], [two_r[2]]),
            lambda: ((3,), [two_l[3]], [two_r[3]]),
            lambda: ((), [], []),
        ]
        sums_l, sums_r = [], []
        for j in range(own_experts):
            first_grad = weight_grads[:1]
            sum_plan = ((j,), first_grad, sums_l or first_grad, sums_r or first_grad) if j else ((), [], [], [])
            if j == own_experts - 1:
                second_grad = weight_grads[1]
                sum_plan = ((j, 1), weight_grads[:2], [*sums_l, second_grad], [*sums_r, second_grad])
            (y, dx, dw), moved_l, moved_r, sums_l, sums_r = expert_step(
                j,
                outer,
                in_rows,
                down_rows,
                expert_rows,
                out_grads,
                own_weights[j],
                [one_l[j], two_l[j], three_l[j]],
                [one_r[j], two_r[j], three_r[j]],
                hop_plans[j](),
                sum_plan,
            )
            three_l.extend(moved_l[:1])
            three_r.extend(moved_r[:1])
            expert_outs.append(y)
            row_grads.append(dx)
            weight_grads.append(dw)
        valid_column = valid_rows.astype(F32)[:, None]
        _, dw_b, dw_c, dw_d = weight_grads
        main, fin_a, sum_l, sum_r = rows_back(
            outer,
            pos_columns,
            gate_columns,
            valid_column,
            hidden,
            cotangent,
            second_gain,
            weights_full,
            row_grads,
            expert_outs,
            (2, 1),
            ((2, 1), (1, 2)),
            [dw_b, dw_c, dw_d],
            [sums_l[1], dw_c],
            [sums_r[1], dw_c],
            [weight_grads[0], sums_l[0], sums_r[0]],
        )
        hidden_grad, branch_grad, second_gain_part, attn_grad_own, attn_grad_other, mixed = main
        (projected_own, projected_other, output, out_own, out_other), three_l, three_r = attention_back(
            outer,
            q_block,
            lengths,
            qkv,
            lse,
            cosine,
            sine,
            [attn_grad_own, attn_grad_other],
            hidden,
            valid_column,
            mixed,
            branch_grad,
            attn_parts,
            (3, 2),
            [dw_b, dw_d],
            [sum_l[0], sum_l[3]],
            [sum_r[0], sum_r[3]],
        )
        tokens_grad, gains, qkv_grad, attn_out_grad, *fins = finish(
            outer,
            hidden_grad,
            tokens,
            first_gain,
            weights_full,
            [normed_one, other, projected_own, projected_other, out_own, out_other, second_gain_part],
            [dw_b, dw_c, dw_d],
            [three_l[0], three_r[0]],
            [sum_l[2], three_l[1]],
            [sum_r[2], three_r[1]],
        )
        expert_in_grad, expert_out_grad = settle_experts(idx, [fin_a, *fins[:3]], in_rows)
        return (
            output,
            tokens_grad,
            gains[0],
            qkv_grad.reshape(qkv_weight.shape),
            attn_out_grad.T,
            gains[1],
            expert_in_grad,
            expert_out_grad,
        )
    else:
        if pair:
            gates_x = beside(gates)
            slot_gates = jnp.concatenate(
                [gates[:, :half], gates_x[:, :half], gates[:, half:], gates_x[:, half:]], axis=1
            )
        else:
            slot_gates = lax.all_gather(gates, "tensor", axis=1, tiled=True)
        gates_y = across(slot_gates, 2)
        all_gates = jnp.stack([slot_gates, gates_y, across(slot_gates, 1), across(gates_y, 1)])
        own_gates = lax.dynamic_slice_in_dim(
            all_gates, t * experts_local + i * own_experts, own_experts, axis=1
        ).astype(F32)
        named = own_gates > 0
        before = (
            lax.broadcasted_iota(jnp.int32, (slot_rows, slot_rows), 0)
            < lax.broadcasted_iota(jnp.int32, (slot_rows, slot_rows), 1)
        ).astype(BF)
        ranks = jnp.dot(
            named.astype(BF).reshape(GROUP * own_experts, slot_rows), before, preferred_element_type=F32
        ).reshape(GROUP, own_experts, slot_rows)
        pos = jnp.where(named, ranks, -1.0).astype(jnp.int32)
        pos_columns, gate_columns = jnp.swapaxes(pos, 1, 2), jnp.swapaxes(own_gates, 1, 2)

        cosine, sine = rope_tables(slot_rows)
        dy = jnp.where(valid_rows[:, None], cotangent, jnp.zeros_like(cotangent))
        qkv_full = lax.all_gather(qkv_weight.reshape(qkv_weight.shape[0], width), "dp", axis=0, tiled=True)
        out_full = lax.all_gather(attn_out_weight.T, "dp", axis=0, tiled=True)
        by_distance = pack_weights(idx, expert_in_weight, expert_out_weight)
        by_distance = [by_distance[0]] + [across(by_distance[m], m) for m in range(1, GROUP)]
        own_weights = [jnp.stack([v[j] for v in by_distance]) for j in range(own_experts)]
        hops = [hop([(own, own) for own in own_weights])]
        if pair:
            out_parts = [out_full, beside(out_full)]
        else:
            gathered = lax.all_gather(out_full, "tensor", axis=0)
            out_parts = [gathered[k] for k in range(n_tensor)]

        if pair:
            other = beside(normed_one)
            normed_all = jnp.where(
                t == 0,
                jnp.concatenate([normed_one, other], axis=0),
                jnp.concatenate([other, normed_one], axis=0),
            )
        else:
            normed_all = lax.all_gather(normed_one, "tensor", axis=0, tiled=True)
        qkv = qkv_project(normed_all, qkv_full, cosine, sine)
        *attended, lse = attend(idx, qkv, 2 if pair else 1, q_block)
        if pair:
            attn_parts = [attended[0], beside(attended[1])]
        else:
            heads = attended[0].shape[1]
            exchanged = lax.all_to_all(attended[0].reshape(n_tensor, rows, heads), "tensor", 0, 0)
            attn_parts = [exchanged[k] for k in range(n_tensor)]
        attn_parts, hops[0] = lax.optimization_barrier((attn_parts, hops[0]))
        if outer > 2:
            hops.append(hop(hops[0]))
        hidden, *normed_two = project_out(tokens, second_gain, attn_parts, out_parts, 2 if pair else 1)

        dy_slots = gather_group([dy[:half], dy[half:]] if pair else [dy])
        out_grads = [dispatch(pos[s], own_gates[s], dy_slots[s], True) for s in range(GROUP)]
        normed_slots = gather_group(normed_two)
        normed_slots, out_grads, hops = lax.optimization_barrier((normed_slots, out_grads, hops))
        while len(hops) < outer - 1:
            hops.append(hop(hops[-1]))
        expert_rows = [dispatch(pos[s], own_gates[s], normed_slots[s], False) for s in range(GROUP)]

        for j in range(own_experts):
            if j:
                idx, expert_outs[-1] = lax.optimization_barrier((idx, expert_outs[-1]))
            y, dx, dw = expert(
                idx,
                j,
                outer,
                in_rows,
                down_rows,
                expert_rows,
                out_grads,
                own_weights[j],
                [h[j][0] for h in hops],
                [h[j][1] for h in hops],
            )
            expert_outs.append(y)
            row_grads.append(dx)
            weight_grads.append(dw)

    def sum_group(sources, scaled):
        def part(s, add, n_outs):
            return combine(pos_columns[s], gate_columns[s], sources, s, scaled, add, n_outs)

        far = [part(2, None, 1)[0], part(3, None, 1)[0]]
        near = [across(v, 1) for v in far]
        if pair:
            ay, axy, by, bxy = part(1, near[1], 4)
            a, ax, b, bx = part(0, near[0], 4)

            def add(p, q):
                return (p.astype(F32) + q.astype(F32)).astype(BF)

            a, ax = add(a, across(ay, 2)), add(ax, across(axy, 2))
            b, by = add(b, beside(bx)), add(by, beside(bxy))
            return [[a, beside(ax)], [b, across(by, 2)]]
        (y,) = part(1, near[1], 1)
        (v,) = part(0, near[0], 1)
        v = (v.astype(F32) + across(y, 2).astype(F32)).astype(BF)
        return [[lax.psum_scatter(v, "tensor", scatter_dimension=0, tiled=True)]]

    valid_column = valid_rows.astype(F32)[:, None]
    normed_two_grad = sum_group(row_grads, False)
    hidden_grad, branch_grad, second_gain_part, *attn_grads = hidden_back(
        valid_column, hidden, cotangent, second_gain, normed_two_grad, out_parts
    )
    if pair:
        attn_grads = [attn_grads[0], beside(attn_grads[1])]
    else:
        attn_grads = [
            lax.all_to_all(jnp.stack(attn_grads), "tensor", 0, 0).reshape(slot_rows, attn_grads[0].shape[1])
        ]
    projected_grads = attend_back(idx, qkv, lse, cosine, sine, attn_grads, q_block)

    def first_norm_part(v):
        return lax.dot_general(v, qkv_full, (((1,), (1,)), ((), ())), preferred_element_type=F32).astype(BF)

    if pair:
        theirs = beside(first_norm_part(projected_grads[1]))
        normed_one_grad = first_norm_part(projected_grads[0]).astype(F32) + theirs.astype(F32)
        qkv_part = mm_tn(normed_one, projected_grads[0]) + mm_tn(other, projected_grads[1])
    else:
        normed_one_grad = lax.psum_scatter(
            first_norm_part(projected_grads[0]), "tensor", scatter_dimension=0, tiled=True
        ).astype(F32)
        qkv_part = mm_tn(normed_all, projected_grads[0])
    first_gain_part = jnp.sum(normed_one_grad * (x * inverse_one), axis=0)
    scaled = normed_one_grad * first_gain
    tokens_grad = (
        hidden_grad
        + inverse_one * scaled
        - x * (inverse_one * inverse_one * inverse_one * jnp.mean(scaled * x, axis=-1, keepdims=True))
    )

    mixture = sum_group(expert_outs, True)
    mixture = jnp.concatenate([sum(v.astype(F32) for v in terms) for terms in mixture], axis=0)
    output = jnp.where(valid_rows[:, None], hidden + mixture, 0.0).astype(BF)

    outer_groups = [[a * GROUP + b for a in range(outer)] for b in range(GROUP)]
    received = [[] for _ in range(GROUP)]
    for dw in weight_grads:
        mine = lax.psum_scatter(dw, "dp", scatter_dimension=0, tiled=True, axis_index_groups=outer_groups)
        for m in range(GROUP):
            block = mine[0, m]
            received[m].append(block if m == 0 else across(block, m))
    by_distance = jnp.stack([jnp.stack(v) for v in received])
    by_source = jnp.take(by_distance, jnp.arange(GROUP) ^ i, axis=0).reshape(
        experts_local, in_rows + down_rows, D
    )
    expert_in_grad = by_source[:, :in_rows].astype(F32)
    expert_out_grad = by_source[:, in_rows:].astype(F32)

    attn_out_parts = [mm_tn(branch_grad, part).astype(BF) for part in attn_parts]
    if pair:
        attn_out_part = (attn_out_parts[0].astype(F32) + beside(attn_out_parts[1]).astype(F32)).astype(BF)
    else:
        attn_out_part = lax.psum_scatter(jnp.stack(attn_out_parts), "tensor", scatter_dimension=0, tiled=True)[0]
    qkv_grad = lax.psum_scatter(qkv_part.astype(BF), "dp", scatter_dimension=0, tiled=True).astype(F32)
    attn_out_grad = lax.psum_scatter(attn_out_part, "dp", scatter_dimension=0, tiled=True).astype(F32).T

    gains = jnp.stack([first_gain_part, second_gain_part[0]])
    if pair:
        gains = gains + beside(gains)
    else:
        gains = lax.psum(gains, "tensor")
    step = 1
    while step < n_dp:
        gains = gains + across(gains, step)
        step *= 2
    return (
        output,
        tokens_grad,
        gains[0],
        qkv_grad.reshape(qkv_weight.shape),
        attn_out_grad,
        gains[1],
        expert_in_grad,
        expert_out_grad,
    )


def solution(mesh):
    placed = (
        P(("dp", "tensor"), None),
        P(("dp", "tensor"), None),
        P("dp"),
        P(("dp", "tensor"), None),
        P(("dp", "tensor"), None),
        P(),
        P("dp", "tensor", None),
        P("tensor", "dp"),
        P(),
        P("tensor", "dp", None),
        P("tensor", "dp", None),
    )
    return jax.shard_map(
        layer,
        mesh=mesh,
        in_specs=placed,
        out_specs=(
            P(("dp", "tensor"), None),
            P(("dp", "tensor"), None),
            P(),
            P("dp", "tensor", None),
            P("tensor", "dp"),
            P(),
            P("tensor", "dp", None),
            P("tensor", "dp", None),
        ),
        check_vma=False,
    )
```
